32 devices in a mesh: batch: 8 (over z, x), rows: 4 (over y, core).
Axes of the slice: x: 2, y: 2, z: 4, core: 2. Of those that a mesh axis runs over, the one named last changes fastest.
Arguments:
- pixels: int32 [12, 16, 16, 1024], P(None, 'rows', None, 'batch'), may hold values from 0 to 255
- valid_mask: int32 [16, 16, 1024], P('rows', None, 'batch'), may hold values from 0 to 1, as said below
- vectors: float32 [2960], replicated, may hold values from -0.8 to 0.8
- vectors_first: float32 [2960], replicated, may hold values from -7.6293945e-06 to 7.6293945e-06
- vectors_second: float32 [2960], replicated, may hold values from 6.357699e-14 to 5.0861594e-13
- entry_taps: float32 [9, 18, 512], replicated, may hold values from -0.625 to 0.625
- entry_first: float32 [9, 18, 512], replicated, may hold values from -1.4305115e-06 to 1.4305115e-06
- entry_second: float32 [9, 18, 512], replicated, may hold values from 3.1788496e-15 to 2.5430797e-14
- middle: float32 [2, 512, 512], replicated, may hold values from -0.25 to 0.25
- middle_first: float32 [2, 512, 512], replicated, may hold values from -7.6293945e-06 to 7.6293945e-06
- middle_second: float32 [2, 512, 512], replicated, may hold values from 6.357699e-14 to 5.0861594e-13
- exit_taps: float32 [9, 36, 512], replicated, may hold values from -0.046875 to 0.046875
- exit_first: float32 [9, 36, 512], replicated, may hold values from -7.6293945e-06 to 7.6293945e-06
- exit_second: float32 [9, 36, 512], replicated, may hold values from 6.357699e-14 to 5.0861594e-13
- prior_taps: float32 [9, 48, 24], replicated, may hold values from -0.21875 to 0.21875
- prior_first: float32 [9, 48, 24], replicated, may hold values from -7.6293945e-06 to 7.6293945e-06
- prior_second: float32 [9, 48, 24], replicated, may hold values from 6.357699e-14 to 5.0861594e-13
Outputs:
- loss: float32 [], replicated
- grad_norm: float32 [], replicated
- vectors_new: float32 [2960], replicated
- vectors_grad: float32 [2960], replicated
- vectors_moment: float32 [2960], replicated
- entry_new: float32 [9, 18, 512], replicated
- entry_grad: float32 [9, 18, 512], replicated
- entry_moment: float32 [9, 18, 512], replicated
- middle_new: float32 [2, 512, 512], replicated
- middle_grad: float32 [2, 512, 512], replicated
- middle_moment: float32 [2, 512, 512], replicated
- exit_new: float32 [9, 36, 512], replicated
- exit_grad: float32 [9, 36, 512], replicated
- exit_moment: float32 [9, 36, 512], replicated
- prior_new: float32 [9, 48, 24], replicated
- prior_grad: float32 [9, 48, 24], replicated
- prior_moment: float32 [9, 48, 24], replicated
- bias_grads: float32 [4, 512], replicated
The draws below stay inside these ranges and needn't reach their ends.
Inputs may be any that keep to these rules, and one draw needn't show every extreme that they name: `valid_mask`: 0 or 1; the first pixel (row 0, column 0) of every image is 1.
All inputs are finite; a program needn't handle non-finite values.
Results may differ from the reference program's by a relative error of at most 0.0055.
The reference program's roundings to bfloat16 on the way count: a program that leaves them out, or rounds other values in their place, can miss the bound.
Values may be sent and summed in bfloat16 or wider, within the bound.
No kernel may reach another device: no remote copies, remote signals or barrier semaphores. Data moves between devices by JAX's collectives and lax.ppermute only.
A program may use at most 448 MiB of HBM per device.

```python
import math
import jax
import jax.numpy as jnp
from jax import lax

HID = 512
CH = 12
GRID = 16
IMAGES = 1024
VEC = 2960
PARAMS = 786448


def draw_pixels(key, part):
    key_centre, key_spread, key_offset = jax.random.split(jax.random.fold_in(key, 7), 3)
    centre = jax.random.randint(key_centre, (IMAGES,), 16, 240)
    spread = jax.random.randint(key_spread, (IMAGES,), 8, 65)
    offset = jax.random.randint(key_offset, (CH, GRID, GRID, IMAGES), -64, 65)
    value = centre[None, None, None, :] + offset * spread[None, None, None, :] // 64
    return jnp.clip(value, 0, 255).astype(jnp.int32)


def draw_valid_mask(key, part):
    image_index = jnp.arange(IMAGES, dtype=jnp.int32)
    percent = 25 + 70 * image_index // max(IMAGES - 1, 1)
    random_roll = jax.random.randint(key, (GRID, GRID, IMAGES), 0, 100)
    valid = (random_roll < percent[None, None, :]).astype(jnp.int32)
    corner = (jnp.arange(GRID)[:, None, None] == 0) & (jnp.arange(GRID)[None, :, None] == 0)
    return jnp.where(corner, 1, valid).astype(jnp.int32)


def noise(stream_key, extent, width, reach, kind=jnp.bfloat16):
    array = width * jax.random.normal(stream_key, extent, jnp.float32)
    return jnp.clip(array, min=-reach, max=reach).astype(kind)


def setup_inputs(seed: int = 0) -> dict:
    streams_of = jax.random.split(jax.random.key(seed), 18)
    pixels = draw_pixels(jax.random.fold_in(streams_of[17], 71), 0)
    valid_mask = draw_valid_mask(jax.random.fold_in(streams_of[17], 71), 0)
    vectors = noise(streams_of[2], (VEC,), 0.2, 0.8, jnp.float32)
    vectors_first = noise(streams_of[3], (VEC,), (0.0011 / PARAMS ** 0.5), 7.62939453125e-06, jnp.float32)
    vectors_second = jnp.clip(jnp.exp(jax.random.uniform(streams_of[4], (VEC,), jnp.float32, math.log(6.35769919783008e-14), math.log(5.086159358264064e-13))), 6.35769919783008e-14, 5.086159358264064e-13)
    entry_taps = noise(streams_of[5], (9, 3 * CH // 2, HID), (9 * CH) ** -0.5, 0.625, jnp.float32)
    entry_first = noise(streams_of[6], (9, 3 * CH // 2, HID), (0.0002 / PARAMS ** 0.5), 1.430511474609375e-06, jnp.float32)
    entry_second = jnp.clip(jnp.exp(jax.random.uniform(streams_of[7], (9, 3 * CH // 2, HID), jnp.float32, math.log(3.1788496412666874e-15), math.log(2.54307971301335e-14))), 3.1788496412666874e-15, 2.54307971301335e-14)
    middle = noise(streams_of[8], (2, HID, HID), HID ** -0.5, 0.25, jnp.float32)
    middle_first = noise(streams_of[9], (2, HID, HID), (0.0011 / PARAMS ** 0.5), 7.62939453125e-06, jnp.float32)
    middle_second = jnp.clip(jnp.exp(jax.random.uniform(streams_of[10], (2, HID, HID), jnp.float32, math.log(6.35769919783008e-14), math.log(5.086159358264064e-13))), 6.35769919783008e-14, 5.086159358264064e-13)
    exit_taps = noise(streams_of[11], (9, 3 * CH, HID), (36 * HID) ** -0.5, 0.046875, jnp.float32)
    exit_first = noise(streams_of[12], (9, 3 * CH, HID), (0.0011 / PARAMS ** 0.5), 7.62939453125e-06, jnp.float32)
    exit_second = jnp.clip(jnp.exp(jax.random.uniform(streams_of[13], (9, 3 * CH, HID), jnp.float32, math.log(6.35769919783008e-14), math.log(5.086159358264064e-13))), 6.35769919783008e-14, 5.086159358264064e-13)
    prior_taps = noise(streams_of[14], (9, 4 * CH, 2 * CH), (72 * CH) ** -0.5, 0.21875, jnp.float32)
    prior_first = noise(streams_of[15], (9, 4 * CH, 2 * CH), (0.0011 / PARAMS ** 0.5), 7.62939453125e-06, jnp.float32)
    prior_second = jnp.clip(jnp.exp(jax.random.uniform(streams_of[16], (9, 4 * CH, 2 * CH), jnp.float32, math.log(6.35769919783008e-14), math.log(5.086159358264064e-13))), 6.35769919783008e-14, 5.086159358264064e-13)
    return {"pixels": pixels, "valid_mask": valid_mask, "vectors": vectors, "vectors_first": vectors_first, "vectors_second": vectors_second, "entry_taps": entry_taps, "entry_first": entry_first, "entry_second": entry_second, "middle": middle, "middle_first": middle_first, "middle_second": middle_second, "exit_taps": exit_taps, "exit_first": exit_first, "exit_second": exit_second, "prior_taps": prior_taps, "prior_first": prior_first, "prior_second": prior_second}


HIGH = lax.Precision.HIGHEST
LOG_TWO_PI = math.log(2.0 * math.pi)
LEARN_RATE = 0.05
BETA_ONE = 0.9
BETA_TWO = 0.999
ADAM_EPS = 1e-08
WEIGHT_DECAY = 0.01
CLIP_NORM = 0.01
ADAM_STEP = 10

@jax.custom_vjp
def low(v):
    return lax.optimization_barrier(v.astype(jnp.bfloat16)).astype(jnp.float32)

@jax.custom_vjp
def low_back(v):
    return v

def low_keep(v):
    return (low(v), None)

def low_pass(kept, grad):
    return (grad,)

def back_keep(v):
    return (v, None)

def back_low(kept, grad):
    return (low(grad),)
low.defvjp(low_keep, low_pass)
low_back.defvjp(back_keep, back_low)

def conv_taps(source, weight):
    row_count, col_count = (source.shape[1], source.shape[2])
    padded = jnp.pad(source, ((0, 0), (1, 1), (1, 1), (0, 0)))
    total = jnp.zeros((weight.shape[1], row_count, col_count, source.shape[3]), jnp.float32)
    for tap_index in range(9):
        shift_row, shift_col = (tap_index // 3, tap_index % 3)
        window = padded[:, shift_row:shift_row + row_count, shift_col:shift_col + col_count, :]
        total = total + jnp.einsum('oi,irwb->orwb', weight[tap_index], window, precision=HIGH)
    return total

def level_params(vectors, entry_taps, middle, exit_taps, level_index):
    chans = CH * (level_index + 1)
    half_size = chans // 2
    offset = 0 if level_index == 0 else 4 * CH + 2 * HID + CH * CH
    segment = vectors[offset:offset + 4 * chans + 2 * HID + chans * chans]
    first_in = 0 if level_index == 0 else CH // 2
    first_out = 0 if level_index == 0 else CH
    return {'chan': segment[:4 * chans].reshape(4, chans), 'bias_a': segment[4 * chans:4 * chans + HID], 'bias_b': segment[4 * chans + HID:4 * chans + 2 * HID], 'lu_mix': segment[4 * chans + 2 * HID:].reshape(chans, chans), 'weight_a': jnp.swapaxes(entry_taps[:, first_in:first_in + half_size], 1, 2), 'weight_b': middle[level_index], 'weight_c': exit_taps[:, first_out:first_out + chans]}

def hidden_biases(vector_grad):
    second_start = 4 * CH + 2 * HID + CH * CH
    first_part = vector_grad[4 * CH:4 * CH + 2 * HID]
    second_part = vector_grad[second_start + 8 * CH:second_start + 8 * CH + 2 * HID]
    return jnp.concatenate([first_part, second_part]).reshape(4, HID)

def mix_channels(source, chan, lu_mix):
    chans = lu_mix.shape[0]
    shifted = (source + chan[0][:, None, None, None]) * jnp.exp(chan[1])[:, None, None, None]
    lower = jnp.tril(lu_mix, -1) + jnp.eye(chans, dtype=jnp.float32)
    upper = jnp.triu(lu_mix, 1) + jnp.diag(jnp.exp(chan[2]))
    matrix = jnp.dot(lower, upper, precision=HIGH)[::-1]
    mixed = jnp.tensordot(matrix, shifted, axes=1, precision=HIGH)
    return (mixed, jnp.sum(chan[1]) + jnp.sum(chan[2]))

def affine_head(second_half, output):
    half_size = second_half.shape[0]
    scale_log = jax.nn.log_sigmoid(output[half_size:] + 2.0)
    result = (second_half + output[:half_size]) * jnp.exp(scale_log)
    return (result, lax.optimization_barrier(jnp.sum(scale_log, axis=0)))

def gauss_log(dropped, prior):
    half_size = dropped.shape[0]
    mean_part, log_part = (prior[:half_size], prior[half_size:])
    scaled = (dropped - mean_part) * jnp.exp(-log_part)
    return lax.optimization_barrier(jnp.sum(-0.5 * LOG_TWO_PI - log_part - 0.5 * scaled * scaled, axis=0))

def squeeze(field):
    chans, row_count, col_count = (field.shape[0], field.shape[1], field.shape[2])
    rest = field.shape[3:]
    parted = field.reshape((chans, row_count // 2, 2, col_count // 2, 2) + rest)
    moved = jnp.moveaxis(parted, (2, 4), (1, 2))
    return moved.reshape((chans * 4, row_count // 2, col_count // 2) + rest)

def flow_step(field, params):
    mixed, const = mix_channels(field, params['chan'], params['lu_mix'])
    half_size = mixed.shape[0] // 2
    first_half = mixed[:half_size]
    pre_one = low_back(conv_taps(low(first_half), low(params['weight_a'])) + params['bias_a'][:, None, None, None])
    hidden_one = low(jnp.maximum(pre_one, 0.0))
    pre_two = low_back(jnp.einsum('oi,irwb->orwb', low(params['weight_b']), hidden_one, precision=HIGH) + params['bias_b'][:, None, None, None])
    hidden_two = low(jnp.maximum(pre_two, 0.0))
    output = low_back(conv_taps(hidden_two, low(params['weight_c'])) + params['chan'][3][:, None, None, None])
    result, step_log = affine_head(mixed[half_size:], output)
    return (jnp.concatenate([first_half, result]), const, step_log)

def block_loss(vectors, entry_taps, middle, exit_taps, prior_taps, source, mask_one, coef):
    first = level_params(vectors, entry_taps, middle, exit_taps, 0)
    out_one, const_one, step_one = flow_step(source, first)
    folded = squeeze(out_one)
    keep_part, drop_part = (folded[:2 * CH], folded[2 * CH:])
    row_count, col_count = (mask_one.shape[0], mask_one.shape[1])
    mask_two = lax.optimization_barrier(jnp.min(mask_one.reshape(row_count // 2, 2, col_count // 2, 2, -1), axis=(1, 3)))
    prior = low_back(conv_taps(low(keep_part), low(prior_taps)) + vectors[-4 * CH:][:, None, None, None])
    drop_log = gauss_log(drop_part, prior)
    second = level_params(vectors, entry_taps, middle, exit_taps, 1)
    out_two, const_two, step_two = flow_step(keep_part, second)
    top_log = lax.optimization_barrier(jnp.sum(-0.5 * (LOG_TWO_PI + out_two * out_two), axis=0))
    total = jnp.sum(mask_one * (const_one + step_one)) + jnp.sum(mask_two * (const_two + step_two + drop_log + top_log))
    return coef * total

def adamw(weight, grad, first, second):
    first_new = BETA_ONE * first + (1.0 - BETA_ONE) * grad
    second_new = BETA_TWO * second + (1.0 - BETA_TWO) * grad * grad
    first_hat = first_new / (1.0 - BETA_ONE ** ADAM_STEP)
    second_hat = second_new / (1.0 - BETA_TWO ** ADAM_STEP)
    updated = weight - LEARN_RATE * (first_hat / (jnp.sqrt(second_hat) + ADAM_EPS) + WEIGHT_DECAY * weight)
    return (updated, second_new)

def reference(pixels, valid_mask, vectors, vectors_first, vectors_second, entry_taps, entry_first, entry_second, middle, middle_first, middle_second, exit_taps, exit_first, exit_second, prior_taps, prior_first, prior_second):
    source = (pixels.astype(jnp.float32) + 0.5) / 256.0 - 0.5
    mask_one = valid_mask.astype(jnp.float32)
    coef = -1.0 / (CH * jnp.sum(mask_one) * math.log(2.0))
    block_size = math.gcd(IMAGES, 16)
    block_count = IMAGES // block_size
    sources = jnp.moveaxis(source.reshape(CH, GRID, GRID, block_count, block_size), 3, 0)
    masks = jnp.moveaxis(mask_one.reshape(GRID, GRID, block_count, block_size), 2, 0)
    weights = (vectors, entry_taps, middle, exit_taps, prior_taps)

    def one_block(carry, item):
        value, back = jax.vjp(lambda *params: block_loss(*params, item[0], item[1], coef), *weights)
        grads = back(jnp.ones((), jnp.float32))
        summed = tuple((old_grad + new_grad for old_grad, new_grad in zip(carry[1], grads)))
        return ((carry[0] + value, summed), None)
    start = (jnp.zeros((), jnp.float32), tuple((jnp.zeros_like(weight) for weight in weights)))
    (total, grads), unused = lax.scan(one_block, start, (sources, masks))
    loss = total + 8.0
    grad_norm = jnp.sqrt(sum((jnp.sum(grad * grad) for grad in grads)))
    clip = jnp.minimum(1.0, CLIP_NORM / (grad_norm + 1e-06))
    firsts = (vectors_first, entry_first, middle_first, exit_first, prior_first)
    seconds = (vectors_second, entry_second, middle_second, exit_second, prior_second)
    results = [loss, grad_norm]
    for weight, grad, first, second in zip(weights, grads, firsts, seconds):
        clipped = grad * clip
        updated, second_new = adamw(weight, clipped, first, second)
        results.extend([updated, clipped, second_new])
    results.append(hidden_biases(grads[0] * clip))
    return tuple(results)
```

```python
import functools
import math

import jax
import jax.numpy as jnp
from jax import lax
from jax.experimental import pallas as pl
from jax.experimental.pallas import tpu as pltpu
from jax.sharding import PartitionSpec as P

HID = 512
CH = 12

F32 = jnp.float32
BF16 = jnp.bfloat16
HIGH = lax.Precision.HIGHEST
LOG_TWO_PI = math.log(2.0 * math.pi)
LEARN_RATE = 0.05
BETA_ONE = 0.9
BETA_TWO = 0.999
ADAM_EPS = 1e-08
WEIGHT_DECAY = 0.01
CLIP_NORM = 0.01
ADAM_STEP = 10
LANES = 128
VMEM_LIMIT = 60 * 2**20


def dot(left, right):
    return lax.dot_general(left, right, (((1,), (0,)), ((), ())), preferred_element_type=F32)


def dot_nt(left, right):
    return lax.dot_general(left, right, (((1,), (1,)), ((), ())), preferred_element_type=F32)


def lane_band(bands, height=1):
    return lax.broadcasted_iota(jnp.int32, (height, LANES), 1) // (LANES // bands)


def pack_kernel(bands, index_ref, pixels_ref, mask_ref, *out_refs):
    own = index_ref[0]
    width = LANES // bands
    rows = pixels_ref.shape[0] // bands
    extra = mask_ref.shape[0] // bands
    band = lane_band(bands)
    parts = [pixels_ref[pl.ds(e, rows, stride=bands), :].astype(F32) for e in range(bands)]
    masks = [mask_ref[pl.ds(e, extra, stride=bands), :].astype(F32) for e in range(bands)]
    for d, out_ref in enumerate(out_refs):
        target = own ^ d
        for source, first, size in ((parts, 0, rows), (masks, rows, extra)):
            total = jnp.zeros((size, LANES), F32)
            for e in range(bands):
                shift = lax.rem(e - target + bands, bands) * width
                total = jnp.where(band == e, pltpu.roll(source[e], shift, 1), total)
            out_ref[first : first + size, :] = total.astype(BF16)


def fill_ext(ext_ref, field, rows, cols, bands, pattern):
    width = LANES // bands
    band = lane_band(bands)
    stride = (cols + 2) * LANES
    height = ext_ref.shape[0]
    pads = jnp.broadcast_to(pattern, (height, LANES))
    for block in range(ext_ref.shape[1] // LANES):
        ext_ref[:, block * LANES : (block + 1) * LANES] = pads
    for row in range(rows):
        start = (row + 1) * stride + LANES
        ext_ref[:, start : start + cols * LANES] = field[:, row * cols * LANES : (row + 1) * cols * LANES]
    last = (rows - 1) * cols * LANES
    for col in range(cols):
        above = pltpu.roll(field[:, last + col * LANES : last + (col + 1) * LANES], width, 1)
        start = LANES + col * LANES
        ext_ref[:, start : start + LANES] = jnp.where(band >= 1, above, pads)
        below = pltpu.roll(field[:, col * LANES : (col + 1) * LANES], LANES - width, 1)
        start = (rows + 1) * stride + LANES + col * LANES
        ext_ref[:, start : start + LANES] = jnp.where(band < bands - 1, below, pads)


def fold_ext(ext_ref, rows, cols, bands):
    width = LANES // bands
    band = lane_band(bands)
    stride = (cols + 2) * LANES
    pieces = []
    for row in range(rows):
        start = (row + 1) * stride + LANES
        piece = ext_ref[:, start : start + cols * LANES]
        if row == 0:
            blocks = []
            for col in range(cols):
                start = (rows + 1) * stride + LANES + col * LANES
                moved = pltpu.roll(ext_ref[:, start : start + LANES], width, 1)
                blocks.append(jnp.where(band >= 1, moved, 0.0))
            piece = piece + jnp.concatenate(blocks, axis=1)
        if row == rows - 1:
            blocks = []
            for col in range(cols):
                start = LANES + col * LANES
                moved = pltpu.roll(ext_ref[:, start : start + LANES], LANES - width, 1)
                blocks.append(jnp.where(band < bands - 1, moved, 0.0))
            piece = piece + jnp.concatenate(blocks, axis=1)
        pieces.append(piece)
    return pieces


def window(cols, row, first_col, tap, turned=False):
    dy, dx = tap // 3, tap % 3
    if turned:
        dy, dx = 2 - dy, 2 - dx
    return ((row + dy) * (cols + 2) + first_col + dx) * LANES


def gather_cols(ext_ref, cols, row, first_col, size, turned=False):
    starts = [window(cols, row, first_col, tap, turned) for tap in range(9)]
    starts = [s if isinstance(s, int) else pl.multiple_of(s, LANES) for s in starts]
    return jnp.concatenate([ext_ref[:, pl.ds(s, size)] for s in starts], axis=0).astype(BF16)


def scatter_cols(ext_ref, values, cols, row, first_col, size, turned=False):
    height = ext_ref.shape[0]
    for tap in range(9):
        start = window(cols, row, first_col, tap, turned)
        if not isinstance(start, int):
            start = pl.multiple_of(start, LANES)
        at = pl.ds(start, size)
        ext_ref[:, at] = ext_ref[:, at] + values[tap * height : (tap + 1) * height]


def mix(matrix_ref, field_ref, start, size, pairs):
    total = None
    for j in pairs:
        term = matrix_ref[:, j : j + 1] * field_ref[j : j + 1, start : start + size]
        total = term if total is None else total + term
    return total


def log_sigmoid(value):
    return jnp.minimum(value, 0.0) - jnp.log1p(jnp.exp(-jnp.abs(value)))


def sigmoid_minus(value):
    power = jnp.exp(-jnp.abs(value))
    return jnp.where(value >= 0.0, power, 1.0) / (1.0 + power)


def row_mask(height, period, valid):
    return lax.rem(lax.broadcasted_iota(jnp.int32, (height, 1), 0), period) < valid


def fold_lanes(value):
    total = value[:, :LANES]
    for start in range(LANES, value.shape[1], LANES):
        total = total + value[:, start : start + LANES]
    return total


def couple_two_forward(
    dims,
    index_ref,
    b0,
    b1,
    b2,
    b3,
    chan1_ref,
    m1_ref,
    chan2_ref,
    m2_ref,
    et_ref,
    wb_ref,
    f_ref,
    bias_ref,
    y1_ref,
    mix1_ref,
    mask_ref,
    mask2_ref,
    keep_ref,
    y2_ref,
    out2_ref,
    t2_ref,
    xcol_ref,
    h1_ref,
    h2_ref,
    loss_ref,
    bufs,
    xs,
    ext,
    oacc,
):
    rows, cols, bands = dims
    own = index_ref[0]
    width = LANES // bands
    band = lane_band(bands)
    groups = cols // bands
    for d, ref in enumerate((b0, b1, b2, b3)):
        bufs[d, :, :] = ref[...].astype(F32)
    xs[...] = jnp.zeros_like(xs)
    for s in range(rows):
        for a in range(groups):
            loads = [bufs[d, pl.ds(s * groups + a, CH + 1, stride=rows * groups), :] for d in range(bands)]
            for e in range(bands):
                total = jnp.zeros((CH + 1, LANES), F32)
                for d in range(bands):
                    origin = own ^ d
                    shift = lax.rem(origin - e + bands, bands) * width
                    total = jnp.where(band == origin, pltpu.roll(loads[d], shift, 1), total)
                start = (s * cols + bands * a + e) * LANES
                xs[0 : CH + 1, start : start + LANES] = total
    line = cols * LANES
    for s in range(rows):
        at = slice(s * line, (s + 1) * line)
        mask_ref[:, at] = xs[CH : CH + 1, at]
        raw = xs[:, at]
        source = (raw + 0.5) / 256.0 - 0.5
        y1_ref[:, at] = (source + chan1_ref[:, 0:1]) * chan1_ref[:, 1:2]
    for s in range(rows):
        at = slice(s * line, (s + 1) * line)
        mix1_ref[:, at] = mix(m1_ref, y1_ref, s * line, line, range(CH))
    half_rows, half_cols = rows // 2, cols // 2
    for i in range(half_rows):
        for j in range(half_cols):
            at = slice((i * half_cols + j) * LANES, (i * half_cols + j + 1) * LANES)
            masks = None
            for p in range(4):
                di, dj = p // 2, p % 2
                start = ((2 * i + di) * cols + 2 * j + dj) * LANES
                keep_ref[p * 8 : p * 8 + 8, at] = mix1_ref[0:8, start : start + LANES]
                block = mask_ref[:, start : start + LANES]
                masks = block if masks is None else jnp.minimum(masks, block)
            mask2_ref[:, at] = masks
    size = half_rows * half_cols * LANES
    y2_ref[...] = (keep_ref[...] + chan2_ref[:, 0:1]) * chan2_ref[:, 1:2]
    pairs = [j for j in range(32) if j % 8 < 6]
    mixed = mix(m2_ref, y2_ref, 0, size, pairs)
    out2_ref[...] = mixed
    iota = lax.broadcasted_iota(jnp.int32, (16, 1), 0)
    ones = jnp.where(iota == CH, 1.0, 0.0)
    fill_ext(ext, mixed[:16] + ones, half_rows, half_cols, bands, ones)
    oacc[...] = jnp.zeros_like(oacc)
    chunk = half_cols * LANES
    for i in range(half_rows):
        at = slice(i * chunk, (i + 1) * chunk)
        xcol = gather_cols(ext, half_cols, i, 0, chunk)
        xcol_ref[:, at] = xcol
        hidden = jnp.maximum(dot(et_ref[...], xcol), 0.0).astype(BF16)
        h1_ref[:, at] = hidden
        hidden = jnp.maximum(dot(wb_ref[...], hidden) + bias_ref[...], 0.0).astype(BF16)
        h2_ref[:, at] = hidden
        scatter_cols(oacc, dot(f_ref[...], hidden), half_cols, i, 0, chunk, True)
    output = jnp.concatenate(fold_ext(oacc, half_rows, half_cols, bands), axis=1) + chan2_ref[:, 2:3]
    second = output[16:] + 2.0
    t2_ref[...] = second
    scale_log = log_sigmoid(second)
    result = (mixed[16:] + output[:16]) * jnp.exp(scale_log)
    out2_ref[16:, :] = result
    valid = row_mask(16, 16, CH)
    per_pixel = jnp.where(valid, scale_log - 0.5 * (mixed[:16] * mixed[:16] + result * result), 0.0)
    mask2 = mask2_ref[...]
    loss_ref[...] = jnp.zeros_like(loss_ref)
    loss_ref[0:1, :] = jnp.sum(fold_lanes(per_pixel * mask2), axis=0, keepdims=True)
    loss_ref[1:2, :] = fold_lanes(mask2)
    loss_ref[2:3, :] = fold_lanes(mask_ref[...])


def gram(left, right_ref, pairs, acc_ref):
    for j in pairs:
        acc_ref[j, :, :] = acc_ref[j, :, :] + fold_lanes(left * right_ref[j : j + 1, :])


def couple_two_backward(
    dims,
    coef_ref,
    mask2_ref,
    y2_ref,
    out2_ref,
    t2_ref,
    xcol_ref,
    h1_ref,
    h2_ref,
    chan2_ref,
    m2t_ref,
    e_ref,
    wbt_ref,
    ft_ref,
    ge_ref,
    gwb_ref,
    gf_ref,
    gbb_ref,
    gm_ref,
    gsum_ref,
    gbc_ref,
    gkeep_ref,
    ext,
    gacc,
    gmix,
    bacc,
):
    rows, cols, bands = dims
    coef = coef_ref[0]
    mask2 = mask2_ref[...]
    weight = coef * mask2
    second = t2_ref[...]
    result = out2_ref[16:, :]
    g_result = -weight * result
    g_log = g_result * result + weight
    g_second = g_log * sigmoid_minus(second)
    g_half = g_result * jnp.exp(log_sigmoid(second))
    gmix[0:16, :] = -weight * out2_ref[0:16, :]
    gmix[16:32, :] = g_half
    valid = row_mask(16, 16, CH)
    g_out = jnp.concatenate([g_half, jnp.where(valid, g_second, 0.0)], axis=0)
    g_out = g_out.astype(BF16).astype(F32)
    gbc_ref[...] = fold_lanes(g_out)
    fill_ext(ext, g_out, rows, cols, bands, jnp.zeros((32, 1), F32))
    gacc[...] = jnp.zeros_like(gacc)
    chunk = cols * LANES
    for i in range(rows):
        at = slice(i * chunk, (i + 1) * chunk)
        gcol = gather_cols(ext, cols, i, 0, chunk, True)
        hidden_two = h2_ref[:, at]
        hidden_one = h1_ref[:, at]
        g_pre = jnp.where(hidden_two > 0, dot(ft_ref[...], gcol), 0.0).astype(BF16)
        g_f = dot_nt(gcol, hidden_two)
        g_wb = dot_nt(g_pre, hidden_one)
        folded = fold_lanes(g_pre.astype(F32))
        g_pre = jnp.where(hidden_one > 0, dot(wbt_ref[...], g_pre), 0.0).astype(BF16)
        g_e = dot_nt(xcol_ref[:, at], g_pre)
        scatter_cols(gacc, dot(e_ref[...], g_pre), cols, i, 0, chunk)
        if i == 0:
            gf_ref[...], gwb_ref[...], ge_ref[...], bacc[...] = g_f, g_wb, g_e, folded
        else:
            gf_ref[...] += g_f
            gwb_ref[...] += g_wb
            ge_ref[...] += g_e
            bacc[...] += folded
    gbb_ref[...] = lax.dot_general(
        jnp.ones((8, LANES), F32), bacc[...], (((1,), (1,)), ((), ())), precision=HIGH, preferred_element_type=F32
    )
    gmix[0:16, :] += jnp.concatenate(fold_ext(gacc, rows, cols, bands), axis=1)
    pairs = [j for j in range(32) if j % 8 < 6]
    g_mixed = gmix[...]
    gm_ref[...] = jnp.zeros_like(gm_ref)
    gram(g_mixed, y2_ref, pairs, gm_ref)
    gsum_ref[...] = fold_lanes(g_mixed)
    valid_rows = [j for j in range(32) if j % 16 < CH]
    gkeep_ref[...] = mix(m2t_ref, gmix, 0, rows * chunk, valid_rows) * chan2_ref[:, 1:2]


def couple_one_forward(
    dims,
    chunk,
    coef_ref,
    mix1_ref,
    mask_ref,
    mask2_ref,
    keep_ref,
    gkeep_in_ref,
    chan1_ref,
    et_ref,
    wb_ref,
    f_ref,
    bias_ref,
    wp_ref,
    wpt_ref,
    pbias_ref,
    xcol_ref,
    h1_ref,
    h2_ref,
    res_ref,
    t_ref,
    gout_ref,
    gwp_ref,
    gpb_ref,
    loss_ref,
    ext,
    oacc,
    kext,
    kcol,
    gkacc,
    drop,
):
    rows, cols, bands = dims
    step = pl.program_id(0)
    per_row = cols * LANES // chunk
    iota = lax.broadcasted_iota(jnp.int32, (8, 1), 0)
    ones = jnp.where(iota == CH // 2, 1.0, 0.0)

    @pl.when(step == 0)
    def _():
        fill_ext(ext, mix1_ref[0:8, :] + ones, rows, cols, bands, ones)
        oacc[...] = jnp.zeros_like(oacc)

    row = step // per_row
    col = (step % per_row) * (chunk // LANES)
    xcol = gather_cols(ext, cols, row, col, chunk)
    xcol_ref[...] = xcol
    hidden = jnp.maximum(dot(et_ref[...], xcol), 0.0).astype(BF16)
    h1_ref[...] = hidden
    hidden = jnp.maximum(dot(wb_ref[...], hidden) + bias_ref[...], 0.0).astype(BF16)
    h2_ref[...] = hidden
    scatter_cols(oacc, dot(f_ref[...], hidden), cols, row, col, chunk, True)

    @pl.when(step == pl.num_programs(0) - 1)
    def _():
        line = cols * LANES
        valid = row_mask(8, 8, CH // 2)
        step_total = None
        half_rows, half_cols = rows // 2, cols // 2
        for s, piece in enumerate(fold_ext(oacc, rows, cols, bands)):
            at = slice(s * line, (s + 1) * line)
            output = piece + chan1_ref[:, 2:3]
            second = output[8:] + 2.0
            t_ref[:, at] = second
            scale_log = log_sigmoid(second)
            result = (mix1_ref[8:16, at] + output[:8]) * jnp.exp(scale_log)
            res_ref[:, at] = result
            part = fold_lanes(jnp.where(valid, scale_log, 0.0) * mask_ref[:, at])
            step_total = part if step_total is None else step_total + part
        for i in range(half_rows):
            for j in range(half_cols):
                at = slice((i * half_cols + j) * LANES, (i * half_cols + j + 1) * LANES)
                for p in range(4):
                    start = ((2 * i + p // 2) * cols + 2 * j + p % 2) * LANES
                    drop[p * 8 : p * 8 + 8, at] = res_ref[:, start : start + LANES]
        part_iota = lax.broadcasted_iota(jnp.int32, (32, 1), 0)
        part_ones = jnp.where(part_iota == CH // 2, 1.0, 0.0)
        fill_ext(kext, keep_ref[...] + part_ones, half_rows, half_cols, bands, part_ones)
        part_line = half_cols * LANES
        gkacc[...] = jnp.zeros_like(gkacc)
        weight = coef_ref[0] * mask2_ref[...]
        valid = row_mask(32, 8, CH // 2)
        prior_total = None
        for i in range(half_rows):
            at = slice(i * part_line, (i + 1) * part_line)
            columns = gather_cols(kext, half_cols, i, 0, part_line)
            kcol[...] = columns
            prior = dot(wp_ref[...], columns) + pbias_ref[...]
            mean, logs = prior[:32], prior[32:]
            inverse = jnp.exp(-logs)
            scaled = (drop[:, at] - mean) * inverse
            part = fold_lanes((-logs - 0.5 * scaled * scaled) * mask2_ref[:, at])
            prior_total = part if prior_total is None else prior_total + part
            g_mean = weight[:, at] * scaled * inverse
            g_logs = jnp.where(valid, weight[:, at] * (scaled * scaled - 1.0), 0.0)
            drop[:, at] = -g_mean
            g_prior = jnp.concatenate([g_mean, g_logs], axis=0).astype(BF16)
            g_wp = dot_nt(g_prior, kcol[...])
            if i == 0:
                gwp_ref[...] = g_wp
                gpb_ref[...] = fold_lanes(g_prior.astype(F32))
            else:
                gwp_ref[...] += g_wp
                gpb_ref[...] += fold_lanes(g_prior.astype(F32))
            scatter_cols(gkacc, dot(wpt_ref[...], g_prior), half_cols, i, 0, part_line)
        loss_ref[...] = jnp.zeros_like(loss_ref)
        loss_ref[0:1, :] = jnp.sum(step_total, axis=0, keepdims=True) + jnp.sum(prior_total, axis=0, keepdims=True)
        for i, piece in enumerate(fold_ext(gkacc, half_rows, half_cols, bands)):
            at = slice(i * part_line, (i + 1) * part_line)
            g_keep = piece + gkeep_in_ref[:, at]
            g_drop = drop[:, at]
            for j in range(half_cols):
                inner = slice(j * LANES, (j + 1) * LANES)
                for p in range(4):
                    start = ((2 * i + p // 2) * cols + 2 * j + p % 2) * LANES
                    gout_ref[0:8, start : start + LANES] = g_keep[p * 8 : p * 8 + 8, inner]
                    gout_ref[8:16, start : start + LANES] = g_drop[p * 8 : p * 8 + 8, inner]


def couple_one_backward(
    dims,
    chunk,
    coef_ref,
    mask_ref,
    y1_ref,
    res_ref,
    t_ref,
    gout_ref,
    e_ref,
    wbt_ref,
    ft_ref,
    xcol_ref,
    h1_ref,
    h2_ref,
    ge_ref,
    gwb_ref,
    gf_ref,
    gbb_ref,
    gm_ref,
    gsum_ref,
    gbc_ref,
    ext,
    gacc,
    gmix,
    bacc,
):
    rows, cols, bands = dims
    step = pl.program_id(0)
    per_row = cols * LANES // chunk

    @pl.when(step == 0)
    def _():
        weight = coef_ref[0] * mask_ref[...]
        second = t_ref[...]
        result = res_ref[...]
        g_result = gout_ref[8:16, :]
        g_log = g_result * result + weight
        g_second = g_log * sigmoid_minus(second)
        g_half = g_result * jnp.exp(log_sigmoid(second))
        gmix[0:8, :] = gout_ref[0:8, :]
        gmix[8:16, :] = g_half
        valid = row_mask(8, 8, CH // 2)
        g_out = jnp.concatenate([g_half, jnp.where(valid, g_second, 0.0)], axis=0)
        g_out = g_out.astype(BF16).astype(F32)
        gbc_ref[...] = fold_lanes(g_out)
        fill_ext(ext, g_out, rows, cols, bands, jnp.zeros((16, 1), F32))
        gacc[...] = jnp.zeros_like(gacc)
        gf_ref[...] = jnp.zeros_like(gf_ref)
        gwb_ref[...] = jnp.zeros_like(gwb_ref)
        ge_ref[...] = jnp.zeros_like(ge_ref)
        bacc[...] = jnp.zeros_like(bacc)

    row = step // per_row
    col = (step % per_row) * (chunk // LANES)
    gcol = gather_cols(ext, cols, row, col, chunk, True)
    hidden_two = h2_ref[...]
    hidden_one = h1_ref[...]
    g_pre = jnp.where(hidden_two > 0, dot(ft_ref[...], gcol), 0.0).astype(BF16)
    gf_ref[...] += dot_nt(gcol, hidden_two)
    gwb_ref[...] += dot_nt(g_pre, hidden_one)
    bacc[...] += fold_lanes(g_pre.astype(F32))
    g_pre = jnp.where(hidden_one > 0, dot(wbt_ref[...], g_pre), 0.0).astype(BF16)
    ge_ref[...] += dot_nt(xcol_ref[...], g_pre)
    scatter_cols(gacc, dot(e_ref[...], g_pre), cols, row, col, chunk)

    @pl.when(step == pl.num_programs(0) - 1)
    def _():
        gbb_ref[...] = lax.dot_general(
            jnp.ones((8, LANES), F32), bacc[...], (((1,), (1,)), ((), ())), precision=HIGH, preferred_element_type=F32
        )
        gmix[0:8, :] += jnp.concatenate(fold_ext(gacc, rows, cols, bands), axis=1)
        g_mixed = gmix[...]
        gm_ref[...] = jnp.zeros_like(gm_ref)
        gram(g_mixed, y1_ref, range(CH), gm_ref)
        gsum_ref[...] = fold_lanes(g_mixed)


def call(kernel, inputs, outputs, scratch, flops, grid=None, in_specs=None, out_specs=None):
    whole = pl.BlockSpec(memory_space=pltpu.VMEM)
    smem = pl.BlockSpec(memory_space=pltpu.SMEM)
    if in_specs is None:
        in_specs = [smem if x.ndim == 1 else whole for x in inputs]
        out_specs = [whole for _ in outputs]
    spec = {} if grid is None else {"grid": grid}
    traffic = sum(x.size * x.dtype.itemsize for x in list(inputs) + list(outputs))
    return pl.pallas_call(
        kernel,
        out_shape=outputs,
        in_specs=in_specs,
        out_specs=out_specs,
        scratch_shapes=scratch,
        compiler_params=pltpu.CompilerParams(vmem_limit_bytes=VMEM_LIMIT),
        cost_estimate=pl.CostEstimate(flops=flops, bytes_accessed=traffic, transcendentals=0),
        **spec,
    )(*inputs)


def shape(dims, dtype=F32):
    return jax.ShapeDtypeStruct(tuple(dims), dtype)


def split_three(value):
    high = lax.reduce_precision(value, 8, 7)
    middle = lax.reduce_precision(value - high, 8, 7)
    return high, middle, value - high - middle


def mixing_matrix(chan, lu_mix):
    chans = lu_mix.shape[0]
    lower = jnp.tril(lu_mix, -1) + jnp.eye(chans, dtype=F32)
    upper = jnp.triu(lu_mix, 1) + jnp.diag(jnp.exp(chan[2]))
    return jnp.dot(lower, upper, precision=HIGH)[::-1]


def spread_one(value):
    parted = value.reshape((2, CH // 2) + value.shape[1:])
    return jnp.pad(parted, ((0, 0), (0, 2)) + ((0, 0),) * (value.ndim - 1)).reshape((16,) + value.shape[1:])


def spread_two(value):
    parted = value.reshape((2, CH) + value.shape[1:])
    return jnp.pad(parted, ((0, 0), (0, 4)) + ((0, 0),) * (value.ndim - 1)).reshape((32,) + value.shape[1:])


def spread_keep(value):
    parted = jnp.swapaxes(value.reshape((CH // 2, 4) + value.shape[1:]), 0, 1)
    return jnp.pad(parted, ((0, 0), (0, 2)) + ((0, 0),) * (value.ndim - 1)).reshape((32,) + value.shape[1:])


def gather_keep(value):
    parted = value.reshape((4, 8) + value.shape[1:])[:, : CH // 2]
    return jnp.swapaxes(parted, 0, 1).reshape((24,) + value.shape[1:])


def entry_matrix(taps, bias, height):
    count = taps.shape[1]
    padded = jnp.pad(taps, ((0, 0), (0, height - count), (0, 0)))
    for tap, piece in enumerate(split_three(bias)):
        padded = padded.at[tap, count].set(piece)
    return padded.reshape(9 * height, HID).astype(BF16)


def exit_matrix(taps, height):
    half = taps.shape[1] // 2
    parted = jnp.pad(taps.reshape(9, 2, half, HID), ((0, 0), (0, 0), (0, height - half), (0, 0)))
    return parted.reshape(18 * height, HID).astype(BF16)


def level_params(vectors, entry_taps, middle, exit_taps, level_index):
    chans = CH * (level_index + 1)
    half_size = chans // 2
    offset = 0 if level_index == 0 else 4 * CH + 2 * HID + CH * CH
    segment = vectors[offset : offset + 4 * chans + 2 * HID + chans * chans]
    first_in = 0 if level_index == 0 else CH // 2
    first_out = 0 if level_index == 0 else CH
    return {
        "chan": segment[: 4 * chans].reshape(4, chans),
        "bias_a": segment[4 * chans : 4 * chans + HID],
        "bias_b": segment[4 * chans + HID : 4 * chans + 2 * HID],
        "lu_mix": segment[4 * chans + 2 * HID :].reshape(chans, chans),
        "taps_a": entry_taps[:, first_in : first_in + half_size],
        "weight_b": middle[level_index].astype(BF16),
        "taps_c": exit_taps[:, first_out : first_out + chans],
    }


def hidden_biases(vector_grad):
    second_start = 4 * CH + 2 * HID + CH * CH
    first_part = vector_grad[4 * CH : 4 * CH + 2 * HID]
    second_part = vector_grad[second_start + 8 * CH : second_start + 8 * CH + 2 * HID]
    return jnp.concatenate([first_part, second_part]).reshape(4, HID)


def adamw(weight, grad, first, second):
    first_new = BETA_ONE * first + (1.0 - BETA_ONE) * grad
    second_new = BETA_TWO * second + (1.0 - BETA_TWO) * grad * grad
    first_hat = first_new / (1.0 - BETA_ONE**ADAM_STEP)
    second_hat = second_new / (1.0 - BETA_TWO**ADAM_STEP)
    updated = weight - LEARN_RATE * (first_hat / (jnp.sqrt(second_hat) + ADAM_EPS) + WEIGHT_DECAY * weight)
    return (updated, second_new)


def chan_grads(params, grad_matrix, grad_mixed_sum, output_bias, coef_mask):
    chan, lu_mix = params["chan"], params["lu_mix"]
    matrix, back = jax.vjp(mixing_matrix, chan, lu_mix)
    from_matrix, lu_grad = back(grad_matrix)
    shifted_sum = jnp.dot(grad_mixed_sum, matrix, precision=HIGH)
    bias = shifted_sum * jnp.exp(chan[1])
    scale = jnp.sum(matrix * grad_matrix, axis=0) + coef_mask
    rows = jnp.stack([bias, scale, from_matrix[2] + coef_mask, output_bias])
    return rows, lu_grad


def total_over(value, axes):
    for axis in axes:
        size = lax.axis_size(axis)
        distance = 1
        while distance < size:
            value = value + lax.ppermute(value, axis, [(i, i ^ distance) for i in range(size)])
            distance *= 2
    return value


def on_device(
    pixels,
    valid_mask,
    vectors,
    vectors_first,
    vectors_second,
    entry_taps,
    entry_first,
    entry_second,
    middle,
    middle_first,
    middle_second,
    exit_taps,
    exit_first,
    exit_second,
    prior_taps,
    prior_first,
    prior_second,
):
    bands = lax.axis_size("rows")
    rows, cols = valid_mask.shape[0], valid_mask.shape[1]
    dims = (rows, cols, bands)
    half_dims = (rows // 2, cols // 2, bands)
    size = rows * cols * LANES
    part = size // 4
    local_count = jnp.sum(valid_mask.astype(F32))
    own = lax.axis_index("rows").astype(jnp.int32).reshape(1)
    piece_rows = (CH + 1) * rows * cols // bands
    pieces = call(
        functools.partial(pack_kernel, bands),
        (own, pixels.reshape(-1, LANES), valid_mask.reshape(-1, LANES)),
        [shape((piece_rows, LANES), BF16)] * bands,
        [],
        1000,
    )
    count = total_over(local_count, ("batch", "rows"))
    bufs = [pieces[0]]
    for d in range(1, bands):
        bufs.append(lax.ppermute(pieces[d], "rows", [(i, i ^ d) for i in range(bands)]))
    coef = (-1.0 / (CH * count * math.log(2.0))).reshape(1)

    one = level_params(vectors, entry_taps, middle, exit_taps, 0)
    two = level_params(vectors, entry_taps, middle, exit_taps, 1)
    e_one = entry_matrix(one["taps_a"], one["bias_a"], 8)
    e_two = entry_matrix(two["taps_a"], two["bias_a"], 16)
    f_one = exit_matrix(one["taps_c"], 8)
    f_two = exit_matrix(two["taps_c"], 16)
    m_one = jnp.pad(spread_one(mixing_matrix(one["chan"], one["lu_mix"])), ((0, 0), (0, 4)))
    m_two = spread_keep(spread_two(mixing_matrix(two["chan"], two["lu_mix"])).T).T
    chan_one = jnp.stack(
        [
            jnp.pad(one["chan"][0], (0, 4)),
            jnp.pad(jnp.exp(one["chan"][1]), (0, 4)),
            spread_one(one["chan"][3]),
        ],
        axis=1,
    )
    chan_two = jnp.stack(
        [spread_keep(two["chan"][0]), spread_keep(jnp.exp(two["chan"][1])), spread_two(two["chan"][3])], axis=1
    )
    prior_parts = prior_taps.astype(BF16).reshape(9, 2, CH // 2, 4, CH // 2, 4)
    prior_parts = jnp.pad(
        prior_parts.transpose(1, 3, 2, 0, 5, 4), ((0, 0), (0, 0), (0, 2), (0, 0), (0, 0), (0, 2))
    )
    wp = prior_parts.reshape(64, 288)
    prior_bias = vectors[-4 * CH :].reshape(2, 24)
    prior_bias = jnp.concatenate([spread_keep(prior_bias[0]), spread_keep(prior_bias[1])])[:, None]

    ext_lanes = (rows // 2 + 2) * (cols // 2 + 2) * LANES
    (y1, mixed_one, mask, mask2, keep, y2, out_two, t_two, xcol_two, h1_two, h2_two, loss_two) = call(
        functools.partial(couple_two_forward, dims),
        (
            own,
            *bufs,
            chan_one,
            m_one,
            chan_two,
            m_two,
            e_two.T,
            two["weight_b"],
            f_two,
            two["bias_b"][:, None],
        ),
        [
            shape((16, size)),
            shape((16, size)),
            shape((1, size)),
            shape((1, part)),
            shape((32, part)),
            shape((32, part)),
            shape((32, part)),
            shape((16, part)),
            shape((144, part), BF16),
            shape((HID, part), BF16),
            shape((HID, part), BF16),
            shape((8, LANES)),
        ],
        [
            pltpu.VMEM((bands, piece_rows, LANES), F32),
            pltpu.VMEM((16, size), F32),
            pltpu.VMEM((16, ext_lanes), F32),
            pltpu.VMEM((32, ext_lanes), F32),
        ],
        2 * HID * part * (144 + HID + 288),
    )
    (ge_two, gwb_two, gf_two, gbb_two, gm_two, gsum_two, gbc_two, gkeep_two) = call(
        functools.partial(couple_two_backward, half_dims),
        (
            coef,
            mask2,
            y2,
            out_two,
            t_two,
            xcol_two,
            h1_two,
            h2_two,
            chan_two,
            m_two.T,
            e_two,
            two["weight_b"].T,
            f_two.T,
        ),
        [
            shape((144, HID)),
            shape((HID, HID)),
            shape((288, HID)),
            shape((8, HID)),
            shape((32, 32, LANES)),
            shape((32, LANES)),
            shape((32, LANES)),
            shape((32, part)),
        ],
        [
            pltpu.VMEM((32, ext_lanes), F32),
            pltpu.VMEM((16, ext_lanes), F32),
            pltpu.VMEM((32, part), F32),
            pltpu.VMEM((HID, LANES), F32),
        ],
        4 * HID * part * (144 + HID + 288),
    )
    whole_lanes = (rows + 2) * (cols + 2) * LANES
    chunk = 1024
    steps = size // chunk
    vmem = pl.BlockSpec(memory_space=pltpu.VMEM)
    smem = pl.BlockSpec(memory_space=pltpu.SMEM)

    def fixed(value):
        rank = len(value.shape)
        return pl.BlockSpec(value.shape, lambda j: (0,) * rank)

    def moving(height):
        return pl.BlockSpec((height, chunk), lambda j: (0, j))

    fwd_in = (
        coef,
        mixed_one,
        mask,
        mask2,
        keep,
        gkeep_two,
        chan_one,
        e_one.T,
        one["weight_b"],
        f_one,
        one["bias_b"][:, None],
        wp,
        wp.T,
        prior_bias,
    )
    fwd_out = [
        shape((72, size), BF16),
        shape((HID, size), BF16),
        shape((HID, size), BF16),
        shape((8, size)),
        shape((8, size)),
        shape((16, size)),
        shape((64, 288)),
        shape((64, LANES)),
        shape((8, LANES)),
    ]
    (xcol_one, h1_one, h2_one, res_one, t_one, gout_one, gwp, gpb, loss_one) = call(
        functools.partial(couple_one_forward, dims, chunk),
        fwd_in,
        fwd_out,
        [
            pltpu.VMEM((8, whole_lanes), F32),
            pltpu.VMEM((16, whole_lanes), F32),
            pltpu.VMEM((32, ext_lanes), F32),
            pltpu.VMEM((288, cols // 2 * LANES), BF16),
            pltpu.VMEM((32, ext_lanes), F32),
            pltpu.VMEM((32, part), F32),
        ],
        2 * HID * size * (72 + HID + 144),
        grid=(steps,),
        in_specs=[smem] + [fixed(x) for x in fwd_in[1:]],
        out_specs=[moving(72), moving(HID), moving(HID)] + [fixed(x) for x in fwd_out[3:]],
    )
    bwd_in = (
        coef,
        mask,
        y1,
        res_one,
        t_one,
        gout_one,
        e_one,
        one["weight_b"].T,
        f_one.T,
        xcol_one,
        h1_one,
        h2_one,
    )
    bwd_out = [
        shape((72, HID)),
        shape((HID, HID)),
        shape((144, HID)),
        shape((8, HID)),
        shape((CH, 16, LANES)),
        shape((16, LANES)),
        shape((16, LANES)),
    ]
    (ge_one, gwb_one, gf_one, gbb_one, gm_one, gsum_one, gbc_one) = call(
        functools.partial(couple_one_backward, dims, chunk),
        bwd_in,
        bwd_out,
        [
            pltpu.VMEM((16, whole_lanes), F32),
            pltpu.VMEM((8, whole_lanes), F32),
            pltpu.VMEM((16, size), F32),
            pltpu.VMEM((HID, LANES), F32),
        ],
        4 * HID * size * (72 + HID + 144),
        grid=(steps,),
        in_specs=[smem] + [fixed(x) for x in bwd_in[1:9]] + [moving(72), moving(HID), moving(HID)],
        out_specs=[fixed(x) for x in bwd_out],
    )

    def unpad_one(value, axis=0):
        parted = value.reshape(value.shape[:axis] + (2, 8) + value.shape[axis + 1 :])
        parted = lax.slice_in_dim(parted, 0, 6, axis=axis + 1)
        return parted.reshape(value.shape[:axis] + (12,) + value.shape[axis + 1 :])

    def unpad_two(value, axis=0):
        parted = value.reshape(value.shape[:axis] + (2, 16) + value.shape[axis + 1 :])
        parted = lax.slice_in_dim(parted, 0, 12, axis=axis + 1)
        return parted.reshape(value.shape[:axis] + (24,) + value.shape[axis + 1 :])

    entry_one = ge_one.reshape(9, 8, HID)
    entry_two = ge_two.reshape(9, 16, HID)
    exit_one = unpad_one(gf_one.reshape(9, 16, HID), 1)
    exit_two = unpad_two(gf_two.reshape(9, 32, HID), 1)
    prior_grad = gwp.reshape(2, 4, 8, 9, 4, 8)[:, :, :6, :, :, :6].transpose(3, 0, 2, 1, 5, 4).reshape(9, 48, 24)
    pieces_small = (
        unpad_one(jnp.sum(gm_one, axis=2).T),
        unpad_one(jnp.sum(gsum_one, axis=1)),
        unpad_one(jnp.sum(gbc_one, axis=1)),
        gather_keep(unpad_two(jnp.sum(gm_two, axis=2).T).T).T,
        unpad_two(jnp.sum(gsum_two, axis=1)),
        unpad_two(jnp.sum(gbc_two, axis=1)),
        gather_keep(jnp.sum(gpb[:32], axis=1)),
        gather_keep(jnp.sum(gpb[32:], axis=1)),
        entry_one[0, 6],
        gbb_one[0],
        entry_two[0, 12],
        gbb_two[0],
        jnp.sum(loss_one[0]) + jnp.sum(loss_two[0]),
        jnp.sum(loss_two[1]),
    )
    big = (entry_one[:, :6], gwb_one, exit_one, entry_two[:, :12], gwb_two, exit_two, prior_grad)
    pieces_small, big = lax.psum((pieces_small, big), ("batch", "rows"))
    (gm1, gs1, gc1, gm2, gs2, gc2, gp0, gp1, ga1, gb1, ga2, gb2, log_total, count_two) = pieces_small
    (entry_one, middle_one, exit_one, entry_two, middle_two, exit_two, prior_grad) = big
    const_one = jnp.sum(one["chan"][1]) + jnp.sum(one["chan"][2])
    const_two = jnp.sum(two["chan"][1]) + jnp.sum(two["chan"][2])
    total = log_total + const_one * count + count_two * (const_two - 48 * 0.5 * LOG_TWO_PI)
    loss = coef[0] * total + 8.0
    chan1, lu1 = chan_grads(one, gm1, gs1, gc1, coef[0] * count)
    chan2, lu2 = chan_grads(two, gm2, gs2, gc2, coef[0] * count_two)
    vector_grad = jnp.concatenate(
        [chan1.reshape(-1), ga1, gb1, lu1.reshape(-1), chan2.reshape(-1), ga2, gb2, lu2.reshape(-1), gp0, gp1]
    )
    grads = (
        vector_grad,
        jnp.concatenate([entry_one, entry_two], axis=1),
        jnp.stack([middle_one, middle_two]),
        jnp.concatenate([exit_one, exit_two], axis=1),
        prior_grad,
    )
    grad_norm = jnp.sqrt(sum((jnp.sum(grad * grad) for grad in grads)))
    clip = jnp.minimum(1.0, CLIP_NORM / (grad_norm + 1e-06))
    weights = (vectors, entry_taps, middle, exit_taps, prior_taps)
    firsts = (vectors_first, entry_first, middle_first, exit_first, prior_first)
    seconds = (vectors_second, entry_second, middle_second, exit_second, prior_second)
    results = [loss, grad_norm]
    for weight, grad, first, second in zip(weights, grads, firsts, seconds):
        clipped = grad * clip
        updated, second_new = adamw(weight, clipped, first, second)
        results.extend([updated, clipped, second_new])
    results.append(hidden_biases(grads[0] * clip))
    return tuple(results)


def solution(mesh):
    replicated = (P(),) * 15
    return jax.shard_map(
        on_device,
        mesh=mesh,
        in_specs=(P(None, "rows", None, "batch"), P("rows", None, "batch")) + replicated,
        out_specs=(P(),) * 18,
        check_vma=False,
    )
```

```python
import functools
import math

import jax
import jax.numpy as jnp
from jax import lax
from jax.experimental import pallas as pl
from jax.experimental.pallas import tpu as pltpu
from jax.sharding import PartitionSpec as P

HID = 512
CH = 12

F32 = jnp.float32
BF16 = jnp.bfloat16
HIGH = lax.Precision.HIGHEST
LOG_TWO_PI = math.log(2.0 * math.pi)
LEARN_RATE = 0.05
BETA_ONE = 0.9
BETA_TWO = 0.999
ADAM_EPS = 1e-08
WEIGHT_DECAY = 0.01
CLIP_NORM = 0.01
ADAM_STEP = 10
LANES = 128
VMEM_LIMIT = 20 * 2**20
ONE_START = 4 * CH
TWO_START = 4 * CH + 2 * HID + CH * CH
PRIOR_START = TWO_START + 8 * CH + 2 * HID + 4 * CH * CH
VEC = PRIOR_START + 4 * CH
FLAT_ROWS = -(-VEC // (8 * LANES)) * 8
WB_ROWS = 4 * HID
TWO_F, TWO_E = WB_ROWS, WB_ROWS + 4 * 216
TWO_B = TWO_E + 4 * 144
TWO_SMALL = TWO_B + 8
TWO_ROWS = 3584
ONE_F = WB_ROWS
ONE_P = ONE_F + 4 * 112
ONE_B = ONE_P + 3 * 64
ONE_LOSS = ONE_B + 8
ONE_ROWS = 2816
PART_A = 1536
REST_A = 4 * 56
REST_SMALL = REST_A + 8
REST_ROWS = 256


def dot(left, right):
    return lax.dot_general(left, right, (((1,), (0,)), ((), ())), preferred_element_type=F32)


def dot_nt(left, right):
    return lax.dot_general(left, right, (((1,), (1,)), ((), ())), preferred_element_type=F32)


def lane_band(bands, height=1):
    return lax.broadcasted_iota(jnp.int32, (height, LANES), 1) // (LANES // bands)


def pack_kernel(bands, index_ref, pixels_ref, mask_ref, *out_refs):
    own = index_ref[0]
    count = jnp.sum(mask_ref[...].astype(F32), axis=0, keepdims=True)
    count = jnp.where(lax.broadcasted_iota(jnp.int32, (16, 1), 0) == 0, count, 0.0).astype(BF16)
    width = LANES // bands
    rows = pixels_ref.shape[0] // bands
    extra = mask_ref.shape[0] // bands
    band = lane_band(bands)
    parts = [pixels_ref[pl.ds(e, rows, stride=bands), :].astype(F32) for e in range(bands)]
    masks = [mask_ref[pl.ds(e, extra, stride=bands), :].astype(F32) for e in range(bands)]
    for d, out_ref in enumerate(out_refs):
        target = own ^ d
        for source, first, size in ((parts, 0, rows), (masks, rows, extra)):
            total = jnp.zeros((size, LANES), F32)
            for e in range(bands):
                shift = lax.rem(e - target + bands, bands) * width
                total = jnp.where(band == e, pltpu.roll(source[e], shift, 1), total)
            out_ref[first : first + size, :] = total.astype(BF16)
        out_ref[rows + extra :, :] = count


def fill_ext(ext_ref, field, rows, cols, bands, pattern):
    width = LANES // bands
    band = lane_band(bands)
    stride = (cols + 2) * LANES
    height = ext_ref.shape[0]
    pads = jnp.broadcast_to(pattern, (height, LANES))
    for block in range(ext_ref.shape[1] // LANES):
        ext_ref[:, block * LANES : (block + 1) * LANES] = pads
    for row in range(rows):
        start = (row + 1) * stride + LANES
        ext_ref[:, start : start + cols * LANES] = field[:, row * cols * LANES : (row + 1) * cols * LANES]
    last = (rows - 1) * cols * LANES
    for col in range(cols):
        above = pltpu.roll(field[:, last + col * LANES : last + (col + 1) * LANES], width, 1)
        start = LANES + col * LANES
        ext_ref[:, start : start + LANES] = jnp.where(band >= 1, above, pads)
        below = pltpu.roll(field[:, col * LANES : (col + 1) * LANES], LANES - width, 1)
        start = (rows + 1) * stride + LANES + col * LANES
        ext_ref[:, start : start + LANES] = jnp.where(band < bands - 1, below, pads)


def fold_ext(ext_ref, rows, cols, bands):
    width = LANES // bands
    band = lane_band(bands)
    stride = (cols + 2) * LANES
    pieces = []
    for row in range(rows):
        start = (row + 1) * stride + LANES
        piece = ext_ref[:, start : start + cols * LANES]
        if row == 0:
            blocks = []
            for col in range(cols):
                start = (rows + 1) * stride + LANES + col * LANES
                moved = pltpu.roll(ext_ref[:, start : start + LANES], width, 1)
                blocks.append(jnp.where(band >= 1, moved, 0.0))
            piece = piece + jnp.concatenate(blocks, axis=1)
        if row == rows - 1:
            blocks = []
            for col in range(cols):
                start = LANES + col * LANES
                moved = pltpu.roll(ext_ref[:, start : start + LANES], LANES - width, 1)
                blocks.append(jnp.where(band < bands - 1, moved, 0.0))
            piece = piece + jnp.concatenate(blocks, axis=1)
        pieces.append(piece)
    return pieces


def window(cols, row, first_col, tap, turned=False):
    dy, dx = tap // 3, tap % 3
    if turned:
        dy, dx = 2 - dy, 2 - dx
    return ((row + dy) * (cols + 2) + first_col + dx) * LANES


def gather_cols(ext_ref, cols, row, first_col, size, turned=False):
    starts = [window(cols, row, first_col, tap, turned) for tap in range(9)]
    starts = [s if isinstance(s, int) else pl.multiple_of(s, LANES) for s in starts]
    return jnp.concatenate([ext_ref[:, pl.ds(s, size)] for s in starts], axis=0).astype(BF16)


def scatter_cols(ext_ref, values, cols, row, first_col, size, turned=False):
    height = ext_ref.shape[0]
    for tap in range(9):
        start = window(cols, row, first_col, tap, turned)
        if not isinstance(start, int):
            start = pl.multiple_of(start, LANES)
        at = pl.ds(start, size)
        ext_ref[:, at] = ext_ref[:, at] + values[tap * height : (tap + 1) * height]


def mix(matrix_ref, field_ref, start, size, pairs):
    total = None
    for j in pairs:
        term = matrix_ref[:, j : j + 1] * field_ref[j : j + 1, start : start + size]
        total = term if total is None else total + term
    return total


def log_sigmoid(value):
    return jnp.minimum(value, 0.0) - jnp.log1p(jnp.exp(-jnp.abs(value)))


def sigmoid_minus(value):
    power = jnp.exp(-jnp.abs(value))
    return jnp.where(value >= 0.0, power, 1.0) / (1.0 + power)


def row_mask(height, period, valid):
    return lax.rem(lax.broadcasted_iota(jnp.int32, (height, 1), 0), period) < valid


def fold_lanes(value):
    total = value[:, :LANES]
    for start in range(LANES, value.shape[1], LANES):
        total = total + value[:, start : start + LANES]
    return total


def coef_of(count_ref):
    return -1.0 / (CH * jnp.sum(count_ref[...], keepdims=True) * math.log(2.0))


def unpack_kernel(
    dims,
    index_ref,
    b0,
    b1,
    b2,
    b3,
    chan1_ref,
    m1_ref,
    chan2_ref,
    m2_ref,
    y1_ref,
    mix1_ref,
    mask_ref,
    mask2_ref,
    keep_ref,
    y2_ref,
    mix2_ref,
    bufs,
    xs,
):
    rows, cols, bands = dims
    own = index_ref[0]
    width = LANES // bands
    band = lane_band(bands)
    groups = cols // bands
    for d, ref in enumerate((b0, b1, b2, b3)):
        bufs[d, :, :] = ref[...].astype(F32)
    xs[...] = jnp.zeros_like(xs)
    for s in range(rows):
        for a in range(groups):
            loads = [bufs[d, pl.ds(s * groups + a, CH + 1, stride=rows * groups), :] for d in range(bands)]
            for e in range(bands):
                total = jnp.zeros((CH + 1, LANES), F32)
                for d in range(bands):
                    origin = own ^ d
                    shift = lax.rem(origin - e + bands, bands) * width
                    total = jnp.where(band == origin, pltpu.roll(loads[d], shift, 1), total)
                start = (s * cols + bands * a + e) * LANES
                xs[0 : CH + 1, start : start + LANES] = total
    line = cols * LANES
    for s in range(rows):
        at = slice(s * line, (s + 1) * line)
        mask_ref[:, at] = xs[CH : CH + 1, at]
        raw = xs[:, at]
        source = (raw + 0.5) / 256.0 - 0.5
        y1_ref[:, at] = (source + chan1_ref[:, 0:1]) * chan1_ref[:, 1:2]
    for s in range(rows):
        at = slice(s * line, (s + 1) * line)
        mix1_ref[:, at] = mix(m1_ref, y1_ref, s * line, line, range(CH))
    half_rows, half_cols = rows // 2, cols // 2
    for i in range(half_rows):
        for j in range(half_cols):
            at = slice((i * half_cols + j) * LANES, (i * half_cols + j + 1) * LANES)
            masks = None
            for p in range(4):
                di, dj = p // 2, p % 2
                start = ((2 * i + di) * cols + 2 * j + dj) * LANES
                keep_ref[p * 8 : p * 8 + 8, at] = mix1_ref[0:8, start : start + LANES]
                block = mask_ref[:, start : start + LANES]
                masks = block if masks is None else jnp.minimum(masks, block)
            mask2_ref[:, at] = masks
    size = half_rows * half_cols * LANES
    y2_ref[...] = (keep_ref[...] + chan2_ref[:, 0:1]) * chan2_ref[:, 1:2]
    pairs = [j for j in range(32) if j % 8 < 6]
    mix2_ref[...] = mix(m2_ref, y2_ref, 0, size, pairs)


def couple_two_forward(
    dims,
    mix2_ref,
    mask_ref,
    mask2_ref,
    chan2_ref,
    et_ref,
    wb_ref,
    f_ref,
    bias_ref,
    out2_ref,
    t2_ref,
    xcol_ref,
    h1_ref,
    h2_ref,
    loss_ref,
    ext,
    oacc,
):
    half_rows, half_cols, bands = dims
    mixed = mix2_ref[...]
    out2_ref[0:16, :] = mixed[:16]
    iota = lax.broadcasted_iota(jnp.int32, (16, 1), 0)
    ones = jnp.where(iota == CH, 1.0, 0.0)
    fill_ext(ext, mixed[:16] + ones, half_rows, half_cols, bands, ones)
    oacc[...] = jnp.zeros_like(oacc)
    chunk = half_cols * LANES
    for i in range(half_rows):
        at = slice(i * chunk, (i + 1) * chunk)
        xcol = gather_cols(ext, half_cols, i, 0, chunk)
        xcol_ref[:, at] = xcol
        hidden = jnp.maximum(dot(et_ref[...], xcol), 0.0).astype(BF16)
        h1_ref[:, at] = hidden
        hidden = jnp.maximum(dot(wb_ref[...], hidden) + bias_ref[...], 0.0).astype(BF16)
        h2_ref[:, at] = hidden
        scatter_cols(oacc, dot(f_ref[...], hidden), half_cols, i, 0, chunk, True)
    output = jnp.concatenate(fold_ext(oacc, half_rows, half_cols, bands), axis=1) + chan2_ref[:, 2:3]
    second = output[16:] + 2.0
    t2_ref[...] = second
    scale_log = log_sigmoid(second)
    result = (mixed[16:] + output[:16]) * jnp.exp(scale_log)
    out2_ref[16:, :] = result
    valid = row_mask(16, 16, CH)
    per_pixel = jnp.where(valid, scale_log - 0.5 * (mixed[:16] * mixed[:16] + result * result), 0.0)
    mask2 = mask2_ref[...]
    loss_ref[...] = jnp.zeros_like(loss_ref)
    loss_ref[0:1, :] = jnp.sum(fold_lanes(per_pixel * mask2), axis=0, keepdims=True)
    loss_ref[1:2, :] = fold_lanes(mask2)
    loss_ref[2:3, :] = fold_lanes(mask_ref[...])


def part_out(slab_ref, first, size, index, bit, kept_ref, sent_ref):
    half = size // 2
    high = lax.rem(index // bit, 2)
    kept_ref[...] = slab_ref[pl.ds(pl.multiple_of(first + high * half, 8), half), :]
    sent_ref[...] = slab_ref[pl.ds(pl.multiple_of(first + (1 - high) * half, 8), half), :]


def gram(left, right_ref, pairs, acc_ref):
    for j in pairs:
        acc_ref[j, :, :] = acc_ref[j, :, :] + fold_lanes(left * right_ref[j : j + 1, :])


def couple_two_backward(
    dims,
    index_ref,
    count_ref,
    mask2_ref,
    y2_ref,
    out2_ref,
    t2_ref,
    xcol_ref,
    h1_ref,
    h2_ref,
    chan2_ref,
    m2t_ref,
    e_ref,
    wbt_ref,
    ft_ref,
    kept_ref,
    sent_ref,
    gkeep_ref,
    ext,
    gacc,
    gmix,
    bacc,
    ge,
    gf,
    acc,
    slab_ref,
):
    rows, cols, bands = dims
    coef = coef_of(count_ref)
    mask2 = mask2_ref[...]
    weight = coef * mask2
    second = t2_ref[...]
    result = out2_ref[16:, :]
    g_result = -weight * result
    g_log = g_result * result + weight
    g_second = g_log * sigmoid_minus(second)
    g_half = g_result * jnp.exp(log_sigmoid(second))
    gmix[0:16, :] = -weight * out2_ref[0:16, :]
    gmix[16:32, :] = g_half
    valid = row_mask(16, 16, CH)
    g_out = jnp.concatenate([g_half, jnp.where(valid, g_second, 0.0)], axis=0)
    g_out = g_out.astype(BF16).astype(F32)
    out_sums = fold_lanes(g_out)
    fill_ext(ext, g_out, rows, cols, bands, jnp.zeros((32, 1), F32))
    gacc[...] = jnp.zeros_like(gacc)
    chunk = cols * LANES
    for i in range(rows):
        at = slice(i * chunk, (i + 1) * chunk)
        gcol = gather_cols(ext, cols, i, 0, chunk, True)
        hidden_two = h2_ref[:, at]
        hidden_one = h1_ref[:, at]
        g_pre = jnp.where(hidden_two > 0, dot(ft_ref[...], gcol), 0.0).astype(BF16)
        g_f = dot_nt(gcol, hidden_two)
        g_wb = dot_nt(g_pre, hidden_one)
        folded = fold_lanes(g_pre.astype(F32))
        g_pre = jnp.where(hidden_one > 0, dot(wbt_ref[...], g_pre), 0.0).astype(BF16)
        g_e = dot_nt(xcol_ref[:, at], g_pre)
        scatter_cols(gacc, dot(e_ref[...], g_pre), cols, i, 0, chunk)
        if i == 0:
            gf[...], ge[...], bacc[...] = g_f, g_e, folded
        else:
            gf[...] += g_f
            ge[...] += g_e
            bacc[...] += folded
        for block in range(HID // LANES):
            at = slice(block * HID, (block + 1) * HID)
            part = g_wb[:, block * LANES : (block + 1) * LANES]
            slab_ref[at, :] = part if i == 0 else slab_ref[at, :] + part
    slab_ref[TWO_B:TWO_ROWS, :] = jnp.zeros((TWO_ROWS - TWO_B, LANES), F32)
    put_rows(slab_ref, lambda block: TWO_B + block, ones_sum(bacc), 0, 1)
    for piece in range(18):
        put_rows(slab_ref, lambda block: TWO_F + block * 216 + piece * CH, gf, piece * 16, CH)
    put_rows(slab_ref, lambda block: TWO_E + block * 144, ge, 0, 144)
    gmix[0:16, :] += jnp.concatenate(fold_ext(gacc, rows, cols, bands), axis=1)
    pairs = [j for j in range(32) if j % 8 < 6]
    g_mixed = gmix[...]
    acc[...] = jnp.zeros_like(acc)
    gram(g_mixed, y2_ref, pairs, acc)
    stack = [(j, acc[j]) for j in pairs] + [(32, fold_lanes(g_mixed)), (33, out_sums)]
    slab_ref[TWO_SMALL : TWO_SMALL + 32, :] = lane_sums(stack, 32)
    part_out(slab_ref, 0, TWO_ROWS, index_ref[1], 1, kept_ref, sent_ref)
    valid_rows = [j for j in range(32) if j % 16 < CH]
    gkeep_ref[...] = mix(m2t_ref, gmix, 0, rows * chunk, valid_rows) * chan2_ref[:, 1:2]


def couple_one_forward(
    dims,
    chunk,
    count_ref,
    mix1_ref,
    mask_ref,
    mask2_ref,
    keep_ref,
    gkeep_in_ref,
    chan1_ref,
    et_ref,
    wb_ref,
    f_ref,
    bias_ref,
    wp_ref,
    wpt_ref,
    pbias_ref,
    xcol_ref,
    h1_ref,
    h2_ref,
    res_ref,
    t_ref,
    gout_ref,
    gwp_ref,
    loss_ref,
    ext,
    oacc,
    kext,
    kcol,
    gkacc,
    drop,
):
    rows, cols, bands = dims
    step = pl.program_id(0)
    per_row = cols * LANES // chunk
    iota = lax.broadcasted_iota(jnp.int32, (8, 1), 0)
    ones = jnp.where(iota == CH // 2, 1.0, 0.0)

    @pl.when(step == 0)
    def _():
        fill_ext(ext, mix1_ref[0:8, :] + ones, rows, cols, bands, ones)
        oacc[...] = jnp.zeros_like(oacc)

    row = step // per_row
    col = (step % per_row) * (chunk // LANES)
    xcol = gather_cols(ext, cols, row, col, chunk)
    xcol_ref[...] = xcol
    hidden = jnp.maximum(dot(et_ref[...], xcol), 0.0).astype(BF16)
    h1_ref[...] = hidden
    hidden = jnp.maximum(dot(wb_ref[...], hidden) + bias_ref[...], 0.0).astype(BF16)
    h2_ref[...] = hidden
    scatter_cols(oacc, dot(f_ref[...], hidden), cols, row, col, chunk, True)

    @pl.when(step == pl.num_programs(0) - 1)
    def _():
        line = cols * LANES
        valid = row_mask(8, 8, CH // 2)
        step_total = None
        half_rows, half_cols = rows // 2, cols // 2
        for s, piece in enumerate(fold_ext(oacc, rows, cols, bands)):
            at = slice(s * line, (s + 1) * line)
            output = piece + chan1_ref[:, 2:3]
            second = output[8:] + 2.0
            t_ref[:, at] = second
            scale_log = log_sigmoid(second)
            result = (mix1_ref[8:16, at] + output[:8]) * jnp.exp(scale_log)
            res_ref[:, at] = result
            part = fold_lanes(jnp.where(valid, scale_log, 0.0) * mask_ref[:, at])
            step_total = part if step_total is None else step_total + part
        for i in range(half_rows):
            for j in range(half_cols):
                at = slice((i * half_cols + j) * LANES, (i * half_cols + j + 1) * LANES)
                for p in range(4):
                    start = ((2 * i + p // 2) * cols + 2 * j + p % 2) * LANES
                    drop[p * 8 : p * 8 + 8, at] = res_ref[:, start : start + LANES]
        part_iota = lax.broadcasted_iota(jnp.int32, (32, 1), 0)
        part_ones = jnp.where(part_iota == CH // 2, 1.0, 0.0)
        fill_ext(kext, keep_ref[...] + part_ones, half_rows, half_cols, bands, part_ones)
        part_line = half_cols * LANES
        gkacc[...] = jnp.zeros_like(gkacc)
        weight = coef_of(count_ref) * mask2_ref[...]
        valid = row_mask(32, 8, CH // 2)
        prior_total = None
        for i in range(half_rows):
            at = slice(i * part_line, (i + 1) * part_line)
            columns = gather_cols(kext, half_cols, i, 0, part_line)
            kcol[...] = columns
            prior = dot(wp_ref[...], columns) + pbias_ref[...]
            mean, logs = prior[:32], prior[32:]
            inverse = jnp.exp(-logs)
            scaled = (drop[:, at] - mean) * inverse
            part = fold_lanes((-logs - 0.5 * scaled * scaled) * mask2_ref[:, at])
            prior_total = part if prior_total is None else prior_total + part
            g_mean = weight[:, at] * scaled * inverse
            g_logs = jnp.where(valid, weight[:, at] * (scaled * scaled - 1.0), 0.0)
            drop[:, at] = -g_mean
            g_prior = jnp.concatenate([g_mean, g_logs], axis=0).astype(BF16)
            g_wp = dot_nt(g_prior, kcol[...])
            if i == 0:
                gwp_ref[...] = g_wp
            else:
                gwp_ref[...] += g_wp
            scatter_cols(gkacc, dot(wpt_ref[...], g_prior), half_cols, i, 0, part_line)
        loss_ref[...] = jnp.zeros_like(loss_ref)
        loss_ref[0:1, :] = jnp.sum(step_total, axis=0, keepdims=True) + jnp.sum(prior_total, axis=0, keepdims=True)
        for i, piece in enumerate(fold_ext(gkacc, half_rows, half_cols, bands)):
            at = slice(i * part_line, (i + 1) * part_line)
            g_keep = piece + gkeep_in_ref[:, at]
            g_drop = drop[:, at]
            for j in range(half_cols):
                inner = slice(j * LANES, (j + 1) * LANES)
                for p in range(4):
                    start = ((2 * i + p // 2) * cols + 2 * j + p % 2) * LANES
                    gout_ref[0:8, start : start + LANES] = g_keep[p * 8 : p * 8 + 8, inner]
                    gout_ref[8:16, start : start + LANES] = g_drop[p * 8 : p * 8 + 8, inner]


def put_rows(slab_ref, first, values, row, count):
    for block in range(HID // LANES):
        start = first(block)
        slab_ref[start : start + count, :] = values[row : row + count, block * LANES : (block + 1) * LANES]


def lane_sums(stack, width):
    lane = lax.broadcasted_iota(jnp.int32, (1, LANES), 1)
    total = jnp.zeros(stack[0][1].shape, F32)
    for j, value in stack:
        total = total + jnp.where(lane == j, jnp.sum(value, axis=1, keepdims=True), 0.0)
    return total


def ones_sum(value_ref):
    return lax.dot_general(
        jnp.ones((8, LANES), F32), value_ref[...], (((1,), (1,)), ((), ())), precision=HIGH, preferred_element_type=F32
    )


def one_backward_top(
    dims,
    chunk,
    bits,
    index_ref,
    count_ref,
    mask_ref,
    res_ref,
    t_ref,
    gout_ref,
    ft_ref,
    gwp_ref,
    loss_one_ref,
    loss_two_ref,
    h1_ref,
    h2_ref,
    kept_a,
    sent_a,
    kept_b,
    sent_b,
    ghalf_ref,
    gbc_ref,
    gpre_ref,
    ext,
    gf,
    bacc,
    slab_ref,
):
    rows, cols, bands = dims
    step = pl.program_id(0)
    per_row = cols * LANES // chunk

    @pl.when(step == 0)
    def _():
        weight = coef_of(count_ref) * mask_ref[...]
        second = t_ref[...]
        result = res_ref[...]
        g_result = gout_ref[8:16, :]
        g_log = g_result * result + weight
        g_second = g_log * sigmoid_minus(second)
        g_half = g_result * jnp.exp(log_sigmoid(second))
        ghalf_ref[...] = g_half
        valid = row_mask(8, 8, CH // 2)
        g_out = jnp.concatenate([g_half, jnp.where(valid, g_second, 0.0)], axis=0)
        g_out = g_out.astype(BF16).astype(F32)
        gbc_ref[...] = fold_lanes(g_out)
        fill_ext(ext, g_out, rows, cols, bands, jnp.zeros((16, 1), F32))
        gf[...] = jnp.zeros_like(gf)
        slab_ref[...] = jnp.zeros_like(slab_ref)
        bacc[...] = jnp.zeros_like(bacc)

    row = step // per_row
    col = (step % per_row) * (chunk // LANES)
    gcol = gather_cols(ext, cols, row, col, chunk, True)
    hidden_two = h2_ref[...]
    g_pre = jnp.where(hidden_two > 0, dot(ft_ref[...], gcol), 0.0).astype(BF16)
    gpre_ref[...] = g_pre
    gf[...] += dot_nt(gcol, hidden_two)
    g_wb = dot_nt(g_pre, h1_ref[...])
    for block in range(HID // LANES):
        slab_ref[block * HID : (block + 1) * HID, :] += g_wb[:, block * LANES : (block + 1) * LANES]
    bacc[...] += fold_lanes(g_pre.astype(F32))

    @pl.when(step == pl.num_programs(0) - 1)
    def _():
        bias = ones_sum(bacc)
        put_rows(slab_ref, lambda block: ONE_B + block, bias, 0, 1)
        for piece in range(18):
            put_rows(slab_ref, lambda block: ONE_F + block * 112 + piece * 6, gf, piece * 8, 6)
        for block in range(3):
            width = min(LANES, 288 - block * LANES)
            slab_ref[ONE_P + block * 64 : ONE_P + block * 64 + 64, 0:width] = gwp_ref[
                :, block * LANES : block * LANES + width
            ]
        slab_ref[ONE_LOSS : ONE_LOSS + 1, :] = loss_one_ref[0:1, :] + loss_two_ref[0:1, :]
        slab_ref[ONE_LOSS + 1 : ONE_LOSS + 2, :] = loss_two_ref[1:2, :]
        part_out(slab_ref, 0, PART_A, index_ref[1], bits[0], kept_a, sent_a)
        part_out(slab_ref, PART_A, ONE_ROWS - PART_A, index_ref[1], bits[1], kept_b, sent_b)


def one_backward_bottom(
    dims,
    chunk,
    y1_ref,
    ghalf_ref,
    gbc_ref,
    gout_ref,
    e_ref,
    wbt_ref,
    xcol_ref,
    h1_ref,
    gpre_ref,
    slab_ref,
    gacc,
    gmix,
    ge,
    acc,
):
    rows, cols, bands = dims
    step = pl.program_id(0)
    per_row = cols * LANES // chunk

    @pl.when(step == 0)
    def _():
        gacc[...] = jnp.zeros_like(gacc)
        ge[...] = jnp.zeros_like(ge)
        slab_ref[...] = jnp.zeros_like(slab_ref)

    row = step // per_row
    col = (step % per_row) * (chunk // LANES)
    g_pre = jnp.where(h1_ref[...] > 0, dot(wbt_ref[...], gpre_ref[...]), 0.0).astype(BF16)
    ge[...] += dot_nt(xcol_ref[...], g_pre)
    scatter_cols(gacc, dot(e_ref[...], g_pre), cols, row, col, chunk)

    @pl.when(step == pl.num_programs(0) - 1)
    def _():
        gmix[0:8, :] = gout_ref[0:8, :] + jnp.concatenate(fold_ext(gacc, rows, cols, bands), axis=1)
        gmix[8:16, :] = ghalf_ref[...]
        g_mixed = gmix[...]
        acc[...] = jnp.zeros_like(acc)
        gram(g_mixed, y1_ref, range(CH), acc)
        stack = [(j, acc[j]) for j in range(CH)] + [(16, fold_lanes(g_mixed)), (17, gbc_ref[...])]
        slab_ref[REST_SMALL : REST_SMALL + 16, :] = lane_sums(stack, CH)
        for tap in range(9):
            put_rows(slab_ref, lambda block: block * 56 + tap * 6, ge, tap * 8, 6)
        put_rows(slab_ref, lambda block: REST_A + block, ge, 6, 1)


def call(kernel, inputs, outputs, scratch, flops, grid=None, in_specs=None, out_specs=None):
    whole = pl.BlockSpec(memory_space=pltpu.VMEM)
    smem = pl.BlockSpec(memory_space=pltpu.SMEM)
    if in_specs is None:
        in_specs = [smem if x.dtype == jnp.int32 and x.ndim == 1 else whole for x in inputs]
        out_specs = [whole for _ in outputs]
    spec = {} if grid is None else {"grid": grid}
    traffic = sum(x.size * x.dtype.itemsize for x in list(inputs) + list(outputs))
    return pl.pallas_call(
        kernel,
        out_shape=outputs,
        in_specs=in_specs,
        out_specs=out_specs,
        scratch_shapes=scratch,
        compiler_params=pltpu.CompilerParams(vmem_limit_bytes=VMEM_LIMIT),
        cost_estimate=pl.CostEstimate(flops=flops, bytes_accessed=traffic, transcendentals=0),
        **spec,
    )(*inputs)


def shape(dims, dtype=F32):
    return jax.ShapeDtypeStruct(tuple(dims), dtype)


def high_dot(left, right, contract=(1, 0)):
    return lax.dot_general(
        left, right, (((contract[0],), (contract[1],)), ((), ())), precision=HIGH, preferred_element_type=F32
    )


def iotas(height, width=LANES):
    return (
        lax.broadcasted_iota(jnp.int32, (height, width), 0),
        lax.broadcasted_iota(jnp.int32, (height, width), 1),
    )


def take_flat(flat_ref, start, length):
    row, offset = divmod(start, LANES)
    lane = lax.broadcasted_iota(jnp.int32, (1, LANES), 1)
    value = flat_ref[row : row + 1, :]
    if offset:
        value = pltpu.roll(value, LANES - offset, 1)
        if offset + length > LANES:
            after = pltpu.roll(flat_ref[row + 1 : row + 2, :], LANES - offset, 1)
            value = jnp.where(lane < LANES - offset, value, after)
    return jnp.where(lane < length, value, 0.0) if length < LANES else value


def put_flat(pieces, start, value, length):
    row, offset = divmod(start, LANES)
    lane = lax.broadcasted_iota(jnp.int32, (1, LANES), 1)
    if length < LANES:
        value = jnp.where(lane < length, value, 0.0)
    if offset:
        value = pltpu.roll(value, offset, 1)
    if offset + length > LANES:
        pieces.setdefault(row + 1, []).append(jnp.where(lane < offset, value, 0.0))
        value = jnp.where(lane >= offset, value, 0.0)
    pieces.setdefault(row, []).append(value)


def level_tables(flat_ref, level, lu):
    chans = CH * (level + 1)
    start = ONE_START - 4 * CH if level == 0 else TWO_START
    chan = [take_flat(flat_ref, start + k * chans, chans) for k in range(4)]
    first = start + 4 * chans + 2 * HID
    lu[...] = jnp.zeros_like(lu)
    for i in range(chans):
        lu[i : i + 1, :] = take_flat(flat_ref, first + i * chans, chans)
    row, lane = iotas(LANES)
    value = lu[...]
    inside = row < chans
    lower = jnp.where(row > lane, value, 0.0) + jnp.where((row == lane) & inside, 1.0, 0.0)
    upper = jnp.where(row < lane, value, 0.0) + jnp.where((row == lane) & inside, jnp.exp(chan[2]), 0.0)
    return chans, start, chan, lower, upper


def natural_row(level, row):
    height, half = (8, CH // 2) if level == 0 else (16, CH)
    return (row // height) * half + lax.rem(row, height), lax.rem(row, height) < half


def natural_keep(row):
    return 4 * lax.rem(row, 8) + row // 8, lax.rem(row, 8) < CH // 2


def pick(condition, value):
    return jnp.sum(jnp.where(condition, value, 0.0), axis=1, keepdims=True)


def prior_places():
    row, lane = iotas(64, 4 * CH)
    inner = lax.rem(row, 32)
    natural, valid = natural_keep(inner)
    return ((lane == natural + (row // 32) * 2 * CH) & valid).astype(F32).astype(BF16)


def prior_lanes(tap):
    row, lane = iotas(2 * CH)
    inner = lane - (tap * 32) % LANES
    natural = 4 * lax.rem(inner, 8) + inner // 8
    valid = (inner >= 0) & (inner < 32) & (lax.rem(inner, 8) < CH // 2)
    return ((row == natural) & valid).astype(F32).astype(BF16)


def prepare_level(level, flat_ref, entry_ref, middle_ref, exit_ref, outs, wide):
    e_ref, et_ref, f_ref, ft_ref, wb_ref, wbt_ref, bb_ref = outs
    chans = CH * (level + 1)
    start = 0 if level == 0 else TWO_START
    half, tall = chans // 2, 8 * (level + 1)
    first_in, first_out = (0, 0) if level == 0 else (CH // 2, CH)
    wide[...] = jnp.zeros_like(wide)
    for tap in range(9):
        wide[tap * tall : tap * tall + half, :] = entry_ref[tap, first_in : first_in + half, :]
    row, lane = iotas(LANES)
    for block in range(HID // LANES):
        at = slice(block * LANES, (block + 1) * LANES)
        value = take_flat(flat_ref, start + 4 * chans + block * LANES, LANES)
        for tap in range(3):
            part = value.astype(BF16).astype(F32)
            wide[tap * tall + half : tap * tall + half + 1, at] = part
            value = value - part
        value = take_flat(flat_ref, start + 4 * chans + HID + block * LANES, LANES)
        bb_ref[at, :] = pick(row == lane, value)
    count = 9 * tall
    padded = -(-count // LANES) * LANES
    e_ref[...] = wide[0:count, :].astype(BF16)
    et_ref[...] = wide[0:padded, :].T[:, 0:count].astype(BF16)
    wide[...] = jnp.zeros_like(wide)
    for tap in range(9):
        for side in range(2):
            first = (tap * 2 + side) * tall
            wide[first : first + half, :] = exit_ref[tap, first_out + side * half : first_out + (side + 1) * half, :]
    count = 18 * tall
    padded = -(-count // LANES) * LANES
    f_ref[...] = wide[0:count, :].astype(BF16)
    ft_ref[...] = wide[0:padded, :].T[:, 0:count].astype(BF16)
    wb_ref[...] = middle_ref[level].astype(BF16)
    wbt_ref[...] = middle_ref[level].T.astype(BF16)


def prepare_two_kernel(
    flat_ref, entry_ref, middle_ref, exit_ref, chan1_ref, m1_ref, chan2_ref, m2_ref, m2t_ref, *rest
):
    outs, (lu, wide) = rest[:-2], rest[-2:]
    for level in range(2):
        chans, start, chan, lower, upper = level_tables(flat_ref, level, lu)
        product = high_dot(lower, upper)
        height = 16 * (level + 1)
        row, lane = iotas(height)
        natural, valid = natural_row(level, row)
        spread = ((lane == chans - 1 - natural) & valid).astype(F32)
        matrix = high_dot(spread, product)
        out_bias = pick((lane == natural) & valid, chan[3])
        if level == 0:
            m1_ref[...] = matrix
            shift, scale = pick(lane == row, chan[0]), pick((lane == row) & (row < CH), jnp.exp(chan[1]))
        else:
            source, target = iotas(LANES)
            place, used = natural_keep(target)
            matrix = high_dot(matrix, ((source == place) & used & (target < 32)).astype(F32))
            m2_ref[...] = matrix
            lu[...] = jnp.zeros_like(lu)
            lu[0:32, :] = matrix
            m2t_ref[...] = lu[...].T[0:32, :]
            place, used = natural_keep(row)
            shift = pick((lane == place) & used, chan[0])
            scale = pick((lane == place) & used, jnp.exp(chan[1]))
        chan_ref = chan1_ref if level == 0 else chan2_ref
        chan_ref[...] = (
            jnp.where(lane == 0, shift, 0.0) + jnp.where(lane == 1, scale, 0.0) + jnp.where(lane == 2, out_bias, 0.0)
        )
    prepare_level(1, flat_ref, entry_ref, middle_ref, exit_ref, outs, wide)


def prepare_one_kernel(flat_ref, entry_ref, middle_ref, exit_ref, prior_ref, wp_ref, wpt_ref, pbias_ref, *rest):
    outs, (lu, wide) = rest[:-2], rest[-2:]
    prepare_level(0, flat_ref, entry_ref, middle_ref, exit_ref, outs, wide)
    places = prior_places()
    blocks = [None] * 3
    for tap in range(9):
        moved = dot_nt(places, prior_ref[tap].astype(BF16)).astype(BF16)
        part = dot(moved, prior_lanes(tap))
        block = tap * 32 // LANES
        blocks[block] = part if blocks[block] is None else blocks[block] + part
    lu[...] = jnp.zeros_like(lu)
    for block, value in enumerate(blocks):
        width = min(LANES, 288 - block * LANES)
        at = slice(block * LANES, block * LANES + width)
        wp_ref[:, at] = value[:, 0:width].astype(BF16)
        lu[0:64, :] = value
        wpt_ref[at, :] = lu[...].T[0:width, 0:64].astype(BF16)
    row, lane = iotas(64)
    natural, valid = natural_keep(lax.rem(row, 32))
    pbias_ref[...] = pick((lane == natural + (row // 32) * 2 * CH) & valid, take_flat(flat_ref, PRIOR_START, 4 * CH))


def adamw(weight, grad, first, second):
    first_new = BETA_ONE * first + (1.0 - BETA_ONE) * grad
    second_new = BETA_TWO * second + (1.0 - BETA_TWO) * grad * grad
    first_hat = first_new / (1.0 - BETA_ONE**ADAM_STEP)
    second_hat = second_new / (1.0 - BETA_TWO**ADAM_STEP)
    updated = weight - LEARN_RATE * (first_hat / (jnp.sqrt(second_hat) + ADAM_EPS) + WEIGHT_DECAY * weight)
    return (updated, second_new)


def finish_kernel(
    count_ref,
    two_ref,
    one_ref,
    rest_ref,
    extra_ref,
    flat_ref,
    flat_first,
    flat_second,
    entry_ref,
    entry_first,
    entry_second,
    middle_ref,
    middle_first,
    middle_second,
    exit_ref,
    exit_first,
    exit_second,
    prior_ref,
    prior_first,
    prior_second,
    loss_ref,
    norm_ref,
    flat_new,
    flat_grad,
    flat_moment,
    entry_new,
    entry_grad,
    entry_moment,
    middle_new,
    middle_grad,
    middle_moment,
    exit_new,
    exit_grad,
    exit_moment,
    prior_new,
    prior_grad,
    prior_moment,
    bias_ref,
    two,
    one,
    rest,
    lu,
):
    two[...] = two_ref[WB_ROWS:, :].astype(F32)
    one[...] = one_ref[WB_ROWS:, :].astype(F32)
    rest[...] = rest_ref[...].astype(F32)
    extra = extra_ref[...].astype(F32)
    log_total = jnp.sum(extra[0:3], keepdims=True)
    count_two = jnp.sum(extra[3:6], keepdims=True)
    coef, count = coef_of(count_ref), jnp.sum(count_ref[...], keepdims=True)
    base = WB_ROWS
    squares = []
    pieces = {}
    consts = []
    for level in range(2):
        chans, start, chan, lower, upper = level_tables(flat_ref, level, lu)
        consts.append(jnp.sum(chan[1] + chan[2], keepdims=True))
        weight = coef * count if level == 0 else coef * count_two
        height = 16 * (level + 1)
        small = rest[REST_SMALL : REST_SMALL + 16, :] if level == 0 else two[TWO_SMALL - base : TWO_SMALL - base + 32, :]
        sum_lane = 16 * (level + 1)
        product = high_dot(lower, upper)
        row, lane = iotas(LANES, height)
        natural, valid = natural_row(level, lane)
        turned = high_dot(((row == chans - 1 - natural) & valid).astype(F32), small)
        row, lane = iotas(LANES)
        g_product = jnp.where(lane < sum_lane, turned, 0.0)
        if level == 1:
            place, used = natural_keep(row)
            g_product = high_dot(g_product, ((lane == place) & used & (row < 32)).astype(F32))
        else:
            g_product = jnp.where(lane < chans, g_product, 0.0)
        g_lower = high_dot(g_product, upper, (1, 1))
        g_upper = high_dot(lower.T, g_product)
        g_lu = jnp.where(row > lane, g_lower, 0.0) + jnp.where(row < lane, g_upper, 0.0)
        diagonal = jnp.sum(jnp.where(row == lane, g_upper, 0.0), axis=0, keepdims=True)
        shift = jnp.sum(turned[:, sum_lane : sum_lane + 1] * product, axis=0, keepdims=True)
        scale = jnp.sum(product * g_product, axis=0, keepdims=True)
        row, lane = iotas(height)
        natural, valid = natural_row(level, row)
        out_bias = jnp.where((lane == natural) & valid, small[:, sum_lane + 1 : sum_lane + 2], 0.0)
        put_flat(pieces, start, shift * jnp.exp(chan[1]), chans)
        put_flat(pieces, start + chans, scale + weight, chans)
        put_flat(pieces, start + 2 * chans, diagonal * jnp.exp(chan[2]) + weight, chans)
        put_flat(pieces, start + 3 * chans, jnp.sum(out_bias, axis=0, keepdims=True), chans)
        for i in range(chans):
            put_flat(pieces, start + 4 * chans + 2 * HID + i * chans, g_lu[i : i + 1, :], chans)
        for block in range(HID // LANES):
            if level == 0:
                value_a = rest[REST_A + block : REST_A + block + 1, :]
                value_b = one[ONE_B - base + block : ONE_B - base + block + 1, :]
            else:
                at = TWO_E - base + block * 144 + CH
                value_a = two[at : at + 1, :]
                value_b = two[TWO_B - base + block : TWO_B - base + block + 1, :]
            at = start + 4 * chans + block * LANES
            put_flat(pieces, at, value_a, LANES)
            put_flat(pieces, at + HID, value_b, LANES)
            bias_ref[2 * level : 2 * level + 1, block * LANES : (block + 1) * LANES] = value_a
            bias_ref[2 * level + 1 : 2 * level + 2, block * LANES : (block + 1) * LANES] = value_b
    row, lane = iotas(64)
    natural, valid = natural_keep(lax.rem(row, 32))
    column = one[ONE_P - base : ONE_P - base + 64, CH // 2 : CH // 2 + 1]
    prior_bias = jnp.where((lane == natural + (row // 32) * 2 * CH) & valid, column, 0.0)
    put_flat(pieces, PRIOR_START, jnp.sum(prior_bias, axis=0, keepdims=True), 4 * CH)
    for r in range(FLAT_ROWS):
        parts = pieces.get(r, [jnp.zeros((1, LANES), F32)])
        flat_grad[r : r + 1, :] = functools.reduce(jnp.add, parts)
    for tap in range(9):
        for block in range(HID // LANES):
            at = slice(block * LANES, (block + 1) * LANES)
            first = block * 56 + tap * 6
            entry_grad[tap, 0:6, at] = rest[first : first + 6, :]
            first = TWO_E - base + block * 144 + tap * 16
            entry_grad[tap, 6:18, at] = two[first : first + CH, :]
            first = ONE_F - base + block * 112 + tap * CH
            exit_grad[tap, 0:CH, at] = one[first : first + CH, :]
            first = TWO_F - base + block * 216 + tap * 2 * CH
            exit_grad[tap, CH : 3 * CH, at] = two[first : first + 2 * CH, :]
    places = prior_places()
    for tap in range(9):
        first = ONE_P - base + (tap * 32 // LANES) * 64
        block = one[first : first + 64, :].astype(BF16)
        moved = dot_nt(prior_lanes(tap), block).astype(BF16)
        prior_grad[tap, :, :] = dot(moved, places)
    for ref in (flat_grad, entry_grad, exit_grad, prior_grad):
        value = ref[...]
        squares.append(jnp.sum(value * value, keepdims=True).reshape(1, 1))
    for ref in (one_ref, two_ref):
        total = jnp.zeros((64, LANES), F32)
        for start in range(0, WB_ROWS, 64):
            value = ref[start : start + 64, :].astype(F32)
            total = total + value * value
        squares.append(jnp.sum(total, keepdims=True))
    norm = jnp.sqrt(functools.reduce(jnp.add, squares))
    clip = jnp.minimum(1.0, CLIP_NORM / (norm + 1e-06))
    total = log_total + consts[0] * count + count_two * (consts[1] - 2 * CH * LOG_TWO_PI)
    loss_ref[...] = coef * total + 8.0
    norm_ref[...] = norm
    bias_ref[...] = bias_ref[...] * clip

    def update(at, refs):
        weight, first, second, new, grad, moment = refs
        value = grad[at] * clip
        grad[at] = value
        new[at], moment[at] = adamw(weight[at], value, first[at], second[at])

    update(..., (flat_ref, flat_first, flat_second, flat_new, flat_grad, flat_moment))
    for tap in range(9):
        update(tap, (entry_ref, entry_first, entry_second, entry_new, entry_grad, entry_moment))
        update(tap, (exit_ref, exit_first, exit_second, exit_new, exit_grad, exit_moment))
        update(tap, (prior_ref, prior_first, prior_second, prior_new, prior_grad, prior_moment))
    size = 64
    for level, slab in enumerate((one_ref, two_ref)):

        @pl.loop(0, HID // size)
        def _(j):
            rows = pl.ds(pl.multiple_of(j * size, size), size)
            for block in range(HID // LANES):
                at = (level, rows, slice(block * LANES, (block + 1) * LANES))
                value = slab[pl.ds(pl.multiple_of(block * HID + j * size, size), size), :].astype(F32) * clip
                middle_grad[at] = value
                middle_new[at], middle_moment[at] = adamw(middle_ref[at], value, middle_first[at], middle_second[at])


def total_over(value, axes):
    for axis in axes:
        size = lax.axis_size(axis)
        distance = 1
        while distance < size:
            value = value + lax.ppermute(value, axis, [(i, i ^ distance) for i in range(size)])
            distance *= 2
    return value


def on_device(
    pixels,
    valid_mask,
    vectors,
    vectors_first,
    vectors_second,
    entry_taps,
    entry_first,
    entry_second,
    middle,
    middle_first,
    middle_second,
    exit_taps,
    exit_first,
    exit_second,
    prior_taps,
    prior_first,
    prior_second,
):
    bands = lax.axis_size("rows")
    rows, cols = valid_mask.shape[0], valid_mask.shape[1]
    dims = (rows, cols, bands)
    half_dims = (rows // 2, cols // 2, bands)
    size = rows * cols * LANES
    part = size // 4
    batches = lax.axis_size("batch")
    devices = batches * bands
    bits = [2**k for k in range((devices - 1).bit_length())]
    index = lax.axis_index("batch") * bands + lax.axis_index("rows")
    own = jnp.stack([lax.axis_index("rows"), index]).astype(jnp.int32)

    def trade(value, bit):
        return lax.ppermute(value, ("batch", "rows"), [(i, i ^ bit) for i in range(devices)])

    def after(value, *done):
        return lax.optimization_barrier((value, *done))[0]

    pixel_rows = (CH + 1) * rows * cols // bands
    piece_rows = pixel_rows + 16
    pieces = call(
        functools.partial(pack_kernel, bands),
        (own, pixels.reshape(-1, LANES), valid_mask.reshape(-1, LANES)),
        [shape((piece_rows, LANES), BF16)] * bands,
        [],
        1000,
    )
    bufs = [pieces[0]]
    for d in range(1, bands):
        bufs.append(lax.ppermute(pieces[d], "rows", [(i, i ^ d) for i in range(bands)]))

    def flat(value):
        return jnp.pad(value, (0, FLAT_ROWS * LANES - VEC)).reshape(FLAT_ROWS, LANES)

    vectors_flat = flat(vectors)

    def level_shapes(tall):
        return [
            shape((9 * tall, HID), BF16),
            shape((HID, 9 * tall), BF16),
            shape((18 * tall, HID), BF16),
            shape((HID, 18 * tall), BF16),
            shape((HID, HID), BF16),
            shape((HID, HID), BF16),
            shape((HID, 1)),
        ]

    square, tall_scratch = pltpu.VMEM((LANES, LANES), F32), pltpu.VMEM((384, HID), F32)
    rounds = iter(bits[bands.bit_length() - 1 :])

    def count_round(value, beside):
        bit = next(rounds, None)
        return value if bit is None else value + after(trade(value, bit), beside)

    chan_one, m_one, chan_two, m_two, m_two_t, e_two, e_two_t, f_two, f_two_t, wb_two, wb_two_t, bb_two = call(
        prepare_two_kernel,
        (after(vectors_flat, pieces[0]), entry_taps, middle, exit_taps),
        [shape((16, LANES)), shape((16, LANES)), shape((32, LANES)), shape((32, LANES)), shape((32, LANES))]
        + level_shapes(16),
        [square, tall_scratch],
        10**9,
    )
    bufs = [after(x, m_one) for x in bufs]
    count = sum(x[pixel_rows : pixel_rows + 1].astype(F32) for x in bufs)
    prior_turned = jnp.swapaxes(prior_taps, 1, 2)
    wp, wpt, prior_bias, e_one, e_one_t, f_one, f_one_t, wb_one, wb_one_t, bb_one = call(
        prepare_one_kernel,
        (after(vectors_flat, count), entry_taps, middle, exit_taps, prior_turned),
        [shape((64, 288), BF16), shape((288, 64), BF16), shape((64, 1))] + level_shapes(8),
        [square, tall_scratch],
        10**9,
    )
    count = count_round(count, prior_bias)

    ext_lanes = (rows // 2 + 2) * (cols // 2 + 2) * LANES
    (y1, mixed_one, mask, mask2, keep, y2, mixed_two) = call(
        functools.partial(unpack_kernel, dims),
        (own, *bufs, after(chan_one, count), m_one, chan_two, m_two),
        [
            shape((16, size)),
            shape((16, size)),
            shape((1, size)),
            shape((1, part)),
            shape((32, part)),
            shape((32, part)),
            shape((32, part)),
        ],
        [pltpu.VMEM((bands, piece_rows, LANES), F32), pltpu.VMEM((16, size), F32)],
        10**9,
    )
    count = count_round(count, mask2)
    (out_two, t_two, xcol_two, h1_two, h2_two, loss_two) = call(
        functools.partial(couple_two_forward, half_dims),
        (mixed_two, mask, mask2, after(chan_two, count), e_two_t, wb_two, f_two, bb_two),
        [
            shape((32, part)),
            shape((16, part)),
            shape((144, part), BF16),
            shape((HID, part), BF16),
            shape((HID, part), BF16),
            shape((8, LANES)),
        ],
        [pltpu.VMEM((16, ext_lanes), F32), pltpu.VMEM((32, ext_lanes), F32)],
        2 * HID * part * (144 + HID + 288),
    )
    for _ in bits:
        count = count_round(count, loss_two)
    half_two = shape((TWO_ROWS // 2, LANES))
    (kept_two, sent_two, gkeep_two) = call(
        functools.partial(couple_two_backward, half_dims),
        (own, count, mask2, y2, out_two, t_two, xcol_two, h1_two, h2_two, chan_two, m_two_t, e_two, wb_two_t, f_two_t),
        [half_two, half_two, shape((32, part))],
        [
            pltpu.VMEM((32, ext_lanes), F32),
            pltpu.VMEM((16, ext_lanes), F32),
            pltpu.VMEM((32, part), F32),
            pltpu.VMEM((HID, LANES), F32),
            pltpu.VMEM((144, HID), F32),
            pltpu.VMEM((288, HID), F32),
            pltpu.VMEM((32, 32, LANES), F32),
            pltpu.VMEM((TWO_ROWS, LANES), F32),
        ],
        4 * HID * part * (144 + HID + 288),
    )
    whole_lanes = (rows + 2) * (cols + 2) * LANES
    chunk = 1024
    steps = size // chunk
    smem = pl.BlockSpec(memory_space=pltpu.SMEM)

    def fixed(value):
        rank = len(value.shape)
        return pl.BlockSpec(value.shape, lambda j: (0,) * rank)

    def moving(height):
        return pl.BlockSpec((height, chunk), lambda j: (0, j))

    fwd_in = (
        count,
        mixed_one,
        mask,
        mask2,
        keep,
        gkeep_two,
        chan_one,
        e_one_t,
        wb_one,
        f_one,
        bb_one,
        wp,
        wpt,
        prior_bias,
    )
    fwd_out = [
        shape((72, size), BF16),
        shape((HID, size), BF16),
        shape((HID, size), BF16),
        shape((8, size)),
        shape((8, size)),
        shape((16, size)),
        shape((64, 288)),
        shape((8, LANES)),
    ]
    (xcol_one, h1_one, h2_one, res_one, t_one, gout_one, gwp, loss_one) = call(
        functools.partial(couple_one_forward, dims, chunk),
        fwd_in,
        fwd_out,
        [
            pltpu.VMEM((8, whole_lanes), F32),
            pltpu.VMEM((16, whole_lanes), F32),
            pltpu.VMEM((32, ext_lanes), F32),
            pltpu.VMEM((288, cols // 2 * LANES), BF16),
            pltpu.VMEM((32, ext_lanes), F32),
            pltpu.VMEM((32, part), F32),
        ],
        2 * HID * size * (72 + HID + 144),
        grid=(steps,),
        in_specs=[fixed(x) for x in fwd_in],
        out_specs=[moving(72), moving(HID), moving(HID)] + [fixed(x) for x in fwd_out[3:]],
    )
    first_bit, second_bit, third_bit = bits[0], bits[2], bits[1]
    total_two = kept_two + after(trade(sent_two, first_bit), loss_one)
    top_in = (own, after(count, total_two), mask, res_one, t_one, gout_one, f_one_t, gwp, loss_one, loss_two, h1_one, h2_one)
    half_a, half_b = shape((PART_A // 2, LANES)), shape(((ONE_ROWS - PART_A) // 2, LANES))
    top_out = [half_a, half_a, half_b, half_b] + [shape((8, size)), shape((16, LANES)), shape((HID, size), BF16)]
    (kept_a, sent_a, kept_b, sent_b, ghalf, gbc, gpre) = call(
        functools.partial(one_backward_top, dims, chunk, (second_bit, third_bit)),
        top_in,
        top_out,
        [
            pltpu.VMEM((16, whole_lanes), F32),
            pltpu.VMEM((144, HID), F32),
            pltpu.VMEM((HID, LANES), F32),
            pltpu.VMEM((ONE_ROWS, LANES), F32),
        ],
        2 * HID * size * (144 + HID + 144),
        grid=(steps,),
        in_specs=[smem] + [fixed(x) for x in top_in[1:10]] + [moving(HID), moving(HID)],
        out_specs=[fixed(x) for x in top_out[:6]] + [moving(HID)],
    )

    def halve(parts, bit, *beside):
        high = (index // bit) % 2
        halves = [x.shape[0] // 2 for x in parts]
        sent = [lax.dynamic_slice_in_dim(x, (1 - high) * h, h, 0) for x, h in zip(parts, halves)]
        kept = [lax.dynamic_slice_in_dim(x, high * h, h, 0) for x, h in zip(parts, halves)]
        got = after(trade(jnp.concatenate(sent) if len(sent) > 1 else sent[0], bit), *beside)
        results, first = [], 0
        for x, h in zip(kept, halves):
            results.append(x + got[first : first + h])
            first += h
        return results

    (total_two,) = halve([total_two], second_bit, gbc)
    low_in = (y1, ghalf, after(gbc, total_two), gout_one, e_one, wb_one_t, xcol_one, h1_one, gpre)
    (slab_rest,) = call(
        functools.partial(one_backward_bottom, dims, chunk),
        low_in,
        [shape((REST_ROWS, LANES))],
        [
            pltpu.VMEM((8, whole_lanes), F32),
            pltpu.VMEM((16, size), F32),
            pltpu.VMEM((72, HID), F32),
            pltpu.VMEM((CH, 16, LANES), F32),
        ],
        2 * HID * size * (72 + HID + 72),
        grid=(steps,),
        in_specs=[fixed(x) for x in low_in[:6]] + [moving(72), moving(HID), moving(HID)],
        out_specs=[fixed(shape((REST_ROWS, LANES)))],
    )

    total_a = kept_a + after(trade(sent_a, second_bit), slab_rest)
    total_b = kept_b + after(trade(sent_b, third_bit), slab_rest)
    (total_two,) = halve([total_two], third_bit, slab_rest)
    far = bits[3:]
    total_a, total_b, total_rest = halve([total_a, total_b, slab_rest], first_bit)
    total_a, total_rest = halve([total_a, total_rest], third_bit)
    (total_b,) = halve([total_b], second_bit)
    (total_rest,) = halve([total_rest], second_bit)
    shards = [total_two, total_a, total_b, total_rest]
    for bit in far:
        shards = halve(shards, bit)
    orders = [
        [first_bit, second_bit, third_bit] + far,
        [second_bit, first_bit, third_bit] + far,
        [third_bit, first_bit, second_bit] + far,
        [first_bit, third_bit, second_bit] + far,
    ]
    loss_part = shards[2]
    owner, loss_row = divmod(ONE_LOSS - PART_A, loss_part.shape[0])
    extra = []
    for row in range(2):
        value = loss_part[loss_row + row]
        for _ in range(3):
            high = lax.reduce_precision(value, 8, 7)
            extra.append(high)
            value = value - high
    extra = jnp.pad(jnp.stack(extra), ((0, 10), (0, 0)))
    spread = jnp.concatenate(shards + [extra]).astype(BF16)
    back = bits[::-1]
    for bit in back:
        other = trade(spread, bit)
        spread = jnp.where(
            (index // bit) % 2 == 0, jnp.concatenate([spread, other]), jnp.concatenate([other, spread])
        )
    spread = spread.reshape((2,) * len(bits) + (-1, LANES))
    totals = []
    first = 0
    for shard, order in zip(shards, orders):
        part_rows = spread[..., first : first + shard.shape[0], :]
        first += shard.shape[0]
        axes = [len(bits) - 1 - back.index(bit) for bit in order]
        totals.append(part_rows.transpose(axes + [len(bits), len(bits) + 1]).reshape(-1, LANES))
    place = [0] * len(bits)
    for k, bit in enumerate(orders[2]):
        place[len(bits) - 1 - back.index(bit)] = (owner >> (len(bits) - 1 - k)) & 1
    extra = spread[tuple(place)][first:]
    totals = [totals[0], jnp.concatenate(totals[1:3]), totals[3]]
    taps = [
        (entry_taps, entry_first, entry_second),
        (middle, middle_first, middle_second),
        (exit_taps, exit_first, exit_second),
        (prior_turned, jnp.swapaxes(prior_first, 1, 2), jnp.swapaxes(prior_second, 1, 2)),
    ]
    flats = (vectors_flat, flat(vectors_first), flat(vectors_second))
    outs = [shape((1, 1)), shape((1, 1))] + [shape((FLAT_ROWS, LANES))] * 3
    for group in taps:
        outs += [shape(group[0].shape)] * 3
    outs.append(shape((4, HID)))
    results = call(
        finish_kernel,
        (count, *totals, extra, *flats, *[x for group in taps for x in group]),
        outs,
        [
            pltpu.VMEM((TWO_ROWS - WB_ROWS, LANES), F32),
            pltpu.VMEM((ONE_ROWS - WB_ROWS, LANES), F32),
            pltpu.VMEM((REST_ROWS, LANES), F32),
            pltpu.VMEM((LANES, LANES), F32),
        ],
        10**8,
    )
    results = list(results)
    for k in range(2):
        results[k] = results[k].reshape(())
    for k in range(2, 5):
        results[k] = results[k].reshape(-1)[:VEC]
    for k in range(14, 17):
        results[k] = jnp.swapaxes(results[k], 1, 2)
    return tuple(results)


def solution(mesh):
    replicated = (P(),) * 15
    return jax.shard_map(
        on_device,
        mesh=mesh,
        in_specs=(P(None, "rows", None, "batch"), P("rows", None, "batch")) + replicated,
        out_specs=(P(),) * 18,
        check_vma=False,
    )
```

```python
import functools
import math

import jax
import jax.numpy as jnp
from jax import lax
from jax.experimental import pallas as pl
from jax.experimental.pallas import tpu as pltpu
from jax.sharding import PartitionSpec as P

HID = 512
CH = 12

F32 = jnp.float32
BF16 = jnp.bfloat16
HIGH = lax.Precision.HIGHEST
LOG_TWO_PI = math.log(2.0 * math.pi)
LEARN_RATE = 0.05
BETA_ONE = 0.9
BETA_TWO = 0.999
ADAM_EPS = 1e-08
WEIGHT_DECAY = 0.01
CLIP_NORM = 0.01
ADAM_STEP = 10
LANES = 128
VMEM_LIMIT = 20 * 2**20
ONE_START = 4 * CH
TWO_START = 4 * CH + 2 * HID + CH * CH
PRIOR_START = TWO_START + 8 * CH + 2 * HID + 4 * CH * CH
VEC = PRIOR_START + 4 * CH
FLAT_ROWS = -(-VEC // (8 * LANES)) * 8
WB_ROWS = 4 * HID
TWO_F, TWO_E = WB_ROWS, WB_ROWS + 4 * 216
TWO_B = TWO_E + 4 * 144
TWO_SMALL = TWO_B + 8
TWO_ROWS = 3584
ONE_F = WB_ROWS
ONE_P = ONE_F + 4 * 112
ONE_B = ONE_P + 3 * 64
ONE_LOSS = ONE_B + 8
ONE_ROWS = 2816
PART_A = 1536
REST_A = 4 * 56
REST_SMALL = REST_A + 8
REST_ROWS = 256


def dot(left, right):
    return lax.dot_general(left, right, (((1,), (0,)), ((), ())), preferred_element_type=F32)


def dot_nt(left, right):
    return lax.dot_general(left, right, (((1,), (1,)), ((), ())), preferred_element_type=F32)


def lane_band(bands, height=1):
    return lax.broadcasted_iota(jnp.int32, (height, LANES), 1) // (LANES // bands)


def pack_kernel(bands, index_ref, pixels_ref, mask_ref, *out_refs):
    own = index_ref[0]
    count = jnp.sum(mask_ref[...].astype(F32), axis=0, keepdims=True)
    count = jnp.where(lax.broadcasted_iota(jnp.int32, (16, 1), 0) == 0, count, 0.0).astype(BF16)
    width = LANES // bands
    rows = pixels_ref.shape[0] // bands
    extra = mask_ref.shape[0] // bands
    band = lane_band(bands)
    parts = [pixels_ref[pl.ds(e, rows, stride=bands), :].astype(F32) for e in range(bands)]
    masks = [mask_ref[pl.ds(e, extra, stride=bands), :].astype(F32) for e in range(bands)]
    for d, out_ref in enumerate(out_refs):
        target = own ^ d
        for source, first, size in ((parts, 0, rows), (masks, rows, extra)):
            total = jnp.zeros((size, LANES), F32)
            for e in range(bands):
                shift = lax.rem(e - target + bands, bands) * width
                total = jnp.where(band == e, pltpu.roll(source[e], shift, 1), total)
            out_ref[first : first + size, :] = total.astype(BF16)
        out_ref[rows + extra :, :] = count


def fill_ext(ext_ref, field, rows, cols, bands, pattern):
    width = LANES // bands
    band = lane_band(bands)
    stride = (cols + 2) * LANES
    height = ext_ref.shape[0]
    pads = jnp.broadcast_to(pattern, (height, LANES))
    for block in range(ext_ref.shape[1] // LANES):
        ext_ref[:, block * LANES : (block + 1) * LANES] = pads
    for row in range(rows):
        start = (row + 1) * stride + LANES
        ext_ref[:, start : start + cols * LANES] = field[:, row * cols * LANES : (row + 1) * cols * LANES]
    last = (rows - 1) * cols * LANES
    for col in range(cols):
        above = pltpu.roll(field[:, last + col * LANES : last + (col + 1) * LANES], width, 1)
        start = LANES + col * LANES
        ext_ref[:, start : start + LANES] = jnp.where(band >= 1, above, pads)
        below = pltpu.roll(field[:, col * LANES : (col + 1) * LANES], LANES - width, 1)
        start = (rows + 1) * stride + LANES + col * LANES
        ext_ref[:, start : start + LANES] = jnp.where(band < bands - 1, below, pads)


def fold_ext(ext_ref, rows, cols, bands):
    width = LANES // bands
    band = lane_band(bands)
    stride = (cols + 2) * LANES
    pieces = []
    for row in range(rows):
        start = (row + 1) * stride + LANES
        piece = ext_ref[:, start : start + cols * LANES]
        if row == 0:
            blocks = []
            for col in range(cols):
                start = (rows + 1) * stride + LANES + col * LANES
                moved = pltpu.roll(ext_ref[:, start : start + LANES], width, 1)
                blocks.append(jnp.where(band >= 1, moved, 0.0))
            piece = piece + jnp.concatenate(blocks, axis=1)
        if row == rows - 1:
            blocks = []
            for col in range(cols):
                start = LANES + col * LANES
                moved = pltpu.roll(ext_ref[:, start : start + LANES], LANES - width, 1)
                blocks.append(jnp.where(band < bands - 1, moved, 0.0))
            piece = piece + jnp.concatenate(blocks, axis=1)
        pieces.append(piece)
    return pieces


def window(cols, row, first_col, tap, turned=False):
    dy, dx = tap // 3, tap % 3
    if turned:
        dy, dx = 2 - dy, 2 - dx
    return ((row + dy) * (cols + 2) + first_col + dx) * LANES


def place_of(step, chunk, cols):
    per_row = cols * LANES // chunk
    return step // per_row, lax.rem(step, per_row) * (chunk // LANES), pl.ds(pl.multiple_of(step * chunk, chunk), chunk)


def gather_cols(ext_ref, cols, row, first_col, size, turned=False):
    starts = [window(cols, row, first_col, tap, turned) for tap in range(9)]
    starts = [s if isinstance(s, int) else pl.multiple_of(s, LANES) for s in starts]
    return jnp.concatenate([ext_ref[:, pl.ds(s, size)] for s in starts], axis=0).astype(BF16)


def scatter_cols(ext_ref, values, cols, row, first_col, size, turned=False):
    height = ext_ref.shape[0]
    for tap in range(9):
        start = window(cols, row, first_col, tap, turned)
        if not isinstance(start, int):
            start = pl.multiple_of(start, LANES)
        at = pl.ds(start, size)
        ext_ref[:, at] = ext_ref[:, at] + values[tap * height : (tap + 1) * height]


def mix(matrix_ref, field_ref, start, size, pairs):
    total = None
    for j in pairs:
        term = matrix_ref[:, j : j + 1] * field_ref[j : j + 1, start : start + size]
        total = term if total is None else total + term
    return total


def log_sigmoid(value):
    return jnp.minimum(value, 0.0) - jnp.log1p(jnp.exp(-jnp.abs(value)))


def sigmoid_minus(value):
    power = jnp.exp(-jnp.abs(value))
    return jnp.where(value >= 0.0, power, 1.0) / (1.0 + power)


def row_mask(height, period, valid):
    return lax.rem(lax.broadcasted_iota(jnp.int32, (height, 1), 0), period) < valid


def fold_lanes(value):
    total = value[:, :LANES]
    for start in range(LANES, value.shape[1], LANES):
        total = total + value[:, start : start + LANES]
    return total


def coef_of(count_ref):
    return -1.0 / (CH * jnp.sum(count_ref[...], keepdims=True) * math.log(2.0))


def unpack_kernel(
    dims,
    index_ref,
    b0,
    b1,
    b2,
    b3,
    chan1_ref,
    m1_ref,
    chan2_ref,
    m2_ref,
    y1_ref,
    mix1_ref,
    mask_ref,
    mask2_ref,
    keep_ref,
    y2_ref,
    mix2_ref,
    bufs,
    xs,
):
    rows, cols, bands = dims
    own = index_ref[0]
    width = LANES // bands
    band = lane_band(bands)
    groups = cols // bands
    for d, ref in enumerate((b0, b1, b2, b3)):
        bufs[d, :, :] = ref[...].astype(F32)
    xs[...] = jnp.zeros_like(xs)
    for s in range(rows):
        for a in range(groups):
            loads = [bufs[d, pl.ds(s * groups + a, CH + 1, stride=rows * groups), :] for d in range(bands)]
            for e in range(bands):
                total = jnp.zeros((CH + 1, LANES), F32)
                for d in range(bands):
                    origin = own ^ d
                    shift = lax.rem(origin - e + bands, bands) * width
                    total = jnp.where(band == origin, pltpu.roll(loads[d], shift, 1), total)
                start = (s * cols + bands * a + e) * LANES
                xs[0 : CH + 1, start : start + LANES] = total
    line = cols * LANES
    for s in range(rows):
        at = slice(s * line, (s + 1) * line)
        mask_ref[:, at] = xs[CH : CH + 1, at]
        raw = xs[:, at]
        source = (raw + 0.5) / 256.0 - 0.5
        y1_ref[:, at] = (source + chan1_ref[:, 0:1]) * chan1_ref[:, 1:2]
    for s in range(rows):
        at = slice(s * line, (s + 1) * line)
        mix1_ref[:, at] = mix(m1_ref, y1_ref, s * line, line, range(CH))
    half_rows, half_cols = rows // 2, cols // 2
    for i in range(half_rows):
        for j in range(half_cols):
            at = slice((i * half_cols + j) * LANES, (i * half_cols + j + 1) * LANES)
            masks = None
            for p in range(4):
                di, dj = p // 2, p % 2
                start = ((2 * i + di) * cols + 2 * j + dj) * LANES
                keep_ref[p * 8 : p * 8 + 8, at] = mix1_ref[0:8, start : start + LANES]
                block = mask_ref[:, start : start + LANES]
                masks = block if masks is None else jnp.minimum(masks, block)
            mask2_ref[:, at] = masks
    size = half_rows * half_cols * LANES
    y2_ref[...] = (keep_ref[...] + chan2_ref[:, 0:1]) * chan2_ref[:, 1:2]
    pairs = [j for j in range(32) if j % 8 < 6]
    mix2_ref[...] = mix(m2_ref, y2_ref, 0, size, pairs)


def couple_two_forward(
    dims,
    mix2_ref,
    mask_ref,
    mask2_ref,
    chan2_ref,
    et_ref,
    wb_ref,
    f_ref,
    bias_ref,
    out2_ref,
    t2_ref,
    xcol_ref,
    h1_ref,
    h2_ref,
    loss_ref,
    ext,
    oacc,
):
    half_rows, half_cols, bands = dims
    mixed = mix2_ref[...]
    out2_ref[0:16, :] = mixed[:16]
    iota = lax.broadcasted_iota(jnp.int32, (16, 1), 0)
    ones = jnp.where(iota == CH, 1.0, 0.0)
    fill_ext(ext, mixed[:16] + ones, half_rows, half_cols, bands, ones)
    oacc[...] = jnp.zeros_like(oacc)
    chunk = half_cols * LANES
    for i in range(half_rows):
        at = slice(i * chunk, (i + 1) * chunk)
        xcol = gather_cols(ext, half_cols, i, 0, chunk)
        xcol_ref[:, at] = xcol
        hidden = jnp.maximum(dot(et_ref[...], xcol), 0.0).astype(BF16)
        h1_ref[:, at] = hidden
        hidden = jnp.maximum(dot(wb_ref[...], hidden) + bias_ref[...], 0.0).astype(BF16)
        h2_ref[:, at] = hidden
        scatter_cols(oacc, dot(f_ref[...], hidden), half_cols, i, 0, chunk, True)
    output = jnp.concatenate(fold_ext(oacc, half_rows, half_cols, bands), axis=1) + chan2_ref[:, 2:3]
    second = output[16:] + 2.0
    t2_ref[...] = second
    scale_log = log_sigmoid(second)
    result = (mixed[16:] + output[:16]) * jnp.exp(scale_log)
    out2_ref[16:, :] = result
    valid = row_mask(16, 16, CH)
    per_pixel = jnp.where(valid, scale_log - 0.5 * (mixed[:16] * mixed[:16] + result * result), 0.0)
    mask2 = mask2_ref[...]
    loss_ref[...] = jnp.zeros_like(loss_ref)
    loss_ref[0:1, :] = jnp.sum(fold_lanes(per_pixel * mask2), axis=0, keepdims=True)
    loss_ref[1:2, :] = fold_lanes(mask2)
    loss_ref[2:3, :] = fold_lanes(mask_ref[...])


def part_out(slab_ref, first, size, index, bit, kept_ref, sent_ref):
    half = size // 2
    high = lax.rem(index // bit, 2)
    kept_ref[...] = slab_ref[pl.ds(pl.multiple_of(first + high * half, 8), half), :]
    sent_ref[...] = slab_ref[pl.ds(pl.multiple_of(first + (1 - high) * half, 8), half), :]


def gram(left, right_ref, pairs, acc_ref):
    for j in pairs:
        acc_ref[j, :, :] = acc_ref[j, :, :] + fold_lanes(left * right_ref[j : j + 1, :])


def couple_two_backward(
    dims,
    index_ref,
    count_ref,
    mask2_ref,
    y2_ref,
    out2_ref,
    t2_ref,
    xcol_ref,
    h1_ref,
    h2_ref,
    chan2_ref,
    m2t_ref,
    e_ref,
    wbt_ref,
    ft_ref,
    kept_ref,
    sent_ref,
    gkeep_ref,
    ext,
    gacc,
    gmix,
    bacc,
    ge,
    gf,
    acc,
    slab_ref,
):
    rows, cols, bands = dims
    coef = coef_of(count_ref)
    mask2 = mask2_ref[...]
    weight = coef * mask2
    second = t2_ref[...]
    result = out2_ref[16:, :]
    g_result = -weight * result
    g_log = g_result * result + weight
    g_second = g_log * sigmoid_minus(second)
    g_half = g_result * jnp.exp(log_sigmoid(second))
    gmix[0:16, :] = -weight * out2_ref[0:16, :]
    gmix[16:32, :] = g_half
    valid = row_mask(16, 16, CH)
    g_out = jnp.concatenate([g_half, jnp.where(valid, g_second, 0.0)], axis=0)
    g_out = g_out.astype(BF16).astype(F32)
    out_sums = fold_lanes(g_out)
    fill_ext(ext, g_out, rows, cols, bands, jnp.zeros((32, 1), F32))
    gacc[...] = jnp.zeros_like(gacc)
    chunk = cols * LANES
    for i in range(rows):
        at = slice(i * chunk, (i + 1) * chunk)
        gcol = gather_cols(ext, cols, i, 0, chunk, True)
        hidden_two = h2_ref[:, at]
        hidden_one = h1_ref[:, at]
        g_pre = jnp.where(hidden_two > 0, dot(ft_ref[...], gcol), 0.0).astype(BF16)
        g_f = dot_nt(gcol, hidden_two)
        g_wb = dot_nt(g_pre, hidden_one)
        folded = fold_lanes(g_pre.astype(F32))
        g_pre = jnp.where(hidden_one > 0, dot(wbt_ref[...], g_pre), 0.0).astype(BF16)
        g_e = dot_nt(xcol_ref[:, at], g_pre)
        scatter_cols(gacc, dot(e_ref[...], g_pre), cols, i, 0, chunk)
        if i == 0:
            gf[...], ge[...], bacc[...] = g_f, g_e, folded
        else:
            gf[...] += g_f
            ge[...] += g_e
            bacc[...] += folded
        for block in range(HID // LANES):
            at = slice(block * HID, (block + 1) * HID)
            part = g_wb[:, block * LANES : (block + 1) * LANES]
            slab_ref[at, :] = part if i == 0 else slab_ref[at, :] + part
    slab_ref[TWO_B:TWO_ROWS, :] = jnp.zeros((TWO_ROWS - TWO_B, LANES), F32)
    put_rows(slab_ref, lambda block: TWO_B + block, ones_sum(bacc), 0, 1)
    for piece in range(18):
        put_rows(slab_ref, lambda block: TWO_F + block * 216 + piece * CH, gf, piece * 16, CH)
    put_rows(slab_ref, lambda block: TWO_E + block * 144, ge, 0, 144)
    gmix[0:16, :] += jnp.concatenate(fold_ext(gacc, rows, cols, bands), axis=1)
    pairs = [j for j in range(32) if j % 8 < 6]
    g_mixed = gmix[...]
    acc[...] = jnp.zeros_like(acc)
    gram(g_mixed, y2_ref, pairs, acc)
    stack = [(j, acc[j]) for j in pairs] + [(32, fold_lanes(g_mixed)), (33, out_sums)]
    slab_ref[TWO_SMALL : TWO_SMALL + 32, :] = lane_sums(stack, 32)
    part_out(slab_ref, 0, TWO_ROWS, index_ref[1], 1, kept_ref, sent_ref)
    valid_rows = [j for j in range(32) if j % 16 < CH]
    gkeep_ref[...] = mix(m2t_ref, gmix, 0, rows * chunk, valid_rows) * chan2_ref[:, 1:2]


def couple_one_forward(
    dims,
    chunk,
    count_ref,
    mix1_ref,
    mask_ref,
    mask2_ref,
    keep_ref,
    gkeep_in_ref,
    chan1_ref,
    et_ref,
    wb_ref,
    f_ref,
    bias_ref,
    wp_ref,
    wpt_ref,
    pbias_ref,
    xcol_ref,
    h1_ref,
    h2_ref,
    res_ref,
    t_ref,
    gout_ref,
    gwp_ref,
    loss_ref,
    ext,
    oacc,
    kext,
    kcol,
    gkacc,
    drop,
):
    rows, cols, bands = dims
    iota = lax.broadcasted_iota(jnp.int32, (8, 1), 0)
    ones = jnp.where(iota == CH // 2, 1.0, 0.0)
    fill_ext(ext, mix1_ref[0:8, :] + ones, rows, cols, bands, ones)
    oacc[...] = jnp.zeros_like(oacc)

    @pl.loop(0, rows * cols * LANES // chunk)
    def _(step):
        row, col, at = place_of(step, chunk, cols)
        xcol = gather_cols(ext, cols, row, col, chunk)
        xcol_ref[:, at] = xcol
        hidden = jnp.maximum(dot(et_ref[...], xcol), 0.0).astype(BF16)
        h1_ref[:, at] = hidden
        hidden = jnp.maximum(dot(wb_ref[...], hidden) + bias_ref[...], 0.0).astype(BF16)
        h2_ref[:, at] = hidden
        scatter_cols(oacc, dot(f_ref[...], hidden), cols, row, col, chunk, True)

    line = cols * LANES
    valid = row_mask(8, 8, CH // 2)
    step_total = None
    half_rows, half_cols = rows // 2, cols // 2
    for s, piece in enumerate(fold_ext(oacc, rows, cols, bands)):
        at = slice(s * line, (s + 1) * line)
        output = piece + chan1_ref[:, 2:3]
        second = output[8:] + 2.0
        t_ref[:, at] = second
        scale_log = log_sigmoid(second)
        result = (mix1_ref[8:16, at] + output[:8]) * jnp.exp(scale_log)
        res_ref[:, at] = result
        part = fold_lanes(jnp.where(valid, scale_log, 0.0) * mask_ref[:, at])
        step_total = part if step_total is None else step_total + part
    for i in range(half_rows):
        for j in range(half_cols):
            at = slice((i * half_cols + j) * LANES, (i * half_cols + j + 1) * LANES)
            for p in range(4):
                start = ((2 * i + p // 2) * cols + 2 * j + p % 2) * LANES
                drop[p * 8 : p * 8 + 8, at] = res_ref[:, start : start + LANES]
    part_iota = lax.broadcasted_iota(jnp.int32, (32, 1), 0)
    part_ones = jnp.where(part_iota == CH // 2, 1.0, 0.0)
    fill_ext(kext, keep_ref[...] + part_ones, half_rows, half_cols, bands, part_ones)
    part_line = half_cols * LANES
    gkacc[...] = jnp.zeros_like(gkacc)
    weight = coef_of(count_ref) * mask2_ref[...]
    valid = row_mask(32, 8, CH // 2)
    prior_total = None
    for i in range(half_rows):
        at = slice(i * part_line, (i + 1) * part_line)
        columns = gather_cols(kext, half_cols, i, 0, part_line)
        kcol[...] = columns
        prior = dot(wp_ref[...], columns) + pbias_ref[...]
        mean, logs = prior[:32], prior[32:]
        inverse = jnp.exp(-logs)
        scaled = (drop[:, at] - mean) * inverse
        part = fold_lanes((-logs - 0.5 * scaled * scaled) * mask2_ref[:, at])
        prior_total = part if prior_total is None else prior_total + part
        g_mean = weight[:, at] * scaled * inverse
        g_logs = jnp.where(valid, weight[:, at] * (scaled * scaled - 1.0), 0.0)
        drop[:, at] = -g_mean
        g_prior = jnp.concatenate([g_mean, g_logs], axis=0).astype(BF16)
        g_wp = dot_nt(g_prior, kcol[...])
        if i == 0:
            gwp_ref[...] = g_wp
        else:
            gwp_ref[...] += g_wp
        scatter_cols(gkacc, dot(wpt_ref[...], g_prior), half_cols, i, 0, part_line)
    loss_ref[...] = jnp.zeros_like(loss_ref)
    loss_ref[0:1, :] = jnp.sum(step_total, axis=0, keepdims=True) + jnp.sum(prior_total, axis=0, keepdims=True)
    for i, piece in enumerate(fold_ext(gkacc, half_rows, half_cols, bands)):
        at = slice(i * part_line, (i + 1) * part_line)
        g_keep = piece + gkeep_in_ref[:, at]
        g_drop = drop[:, at]
        for j in range(half_cols):
            inner = slice(j * LANES, (j + 1) * LANES)
            for p in range(4):
                start = ((2 * i + p // 2) * cols + 2 * j + p % 2) * LANES
                gout_ref[0:8, start : start + LANES] = g_keep[p * 8 : p * 8 + 8, inner]
                gout_ref[8:16, start : start + LANES] = g_drop[p * 8 : p * 8 + 8, inner]


def put_rows(slab_ref, first, values, row, count):
    for block in range(HID // LANES):
        start = first(block)
        slab_ref[start : start + count, :] = values[row : row + count, block * LANES : (block + 1) * LANES]


def lane_sums(stack, width):
    lane = lax.broadcasted_iota(jnp.int32, (1, LANES), 1)
    total = jnp.zeros(stack[0][1].shape, F32)
    for j, value in stack:
        total = total + jnp.where(lane == j, jnp.sum(value, axis=1, keepdims=True), 0.0)
    return total


def ones_sum(value_ref):
    return lax.dot_general(
        jnp.ones((8, LANES), F32), value_ref[...], (((1,), (1,)), ((), ())), precision=HIGH, preferred_element_type=F32
    )


def one_backward_top(
    dims,
    chunk,
    bits,
    index_ref,
    count_ref,
    mask_ref,
    res_ref,
    t_ref,
    gout_ref,
    ft_ref,
    gwp_ref,
    loss_one_ref,
    loss_two_ref,
    h1_ref,
    h2_ref,
    gpre_ref,
    kept_a,
    sent_a,
    kept_b,
    sent_b,
    ghalf_ref,
    gbc_ref,
    ext,
    gf,
    bacc,
    slab_ref,
):
    rows, cols, bands = dims
    weight = coef_of(count_ref) * mask_ref[...]
    second = t_ref[...]
    result = res_ref[...]
    g_result = gout_ref[8:16, :]
    g_log = g_result * result + weight
    g_second = g_log * sigmoid_minus(second)
    g_half = g_result * jnp.exp(log_sigmoid(second))
    ghalf_ref[...] = g_half
    valid = row_mask(8, 8, CH // 2)
    g_out = jnp.concatenate([g_half, jnp.where(valid, g_second, 0.0)], axis=0)
    g_out = g_out.astype(BF16).astype(F32)
    gbc_ref[...] = fold_lanes(g_out)
    fill_ext(ext, g_out, rows, cols, bands, jnp.zeros((16, 1), F32))
    gf[...] = jnp.zeros_like(gf)
    slab_ref[...] = jnp.zeros_like(slab_ref)
    bacc[...] = jnp.zeros_like(bacc)

    @pl.loop(0, rows * cols * LANES // chunk)
    def _(step):
        row, col, at = place_of(step, chunk, cols)
        gcol = gather_cols(ext, cols, row, col, chunk, True)
        hidden_two = h2_ref[:, at]
        g_pre = jnp.where(hidden_two > 0, dot(ft_ref[...], gcol), 0.0).astype(BF16)
        gf[...] += dot_nt(gcol, hidden_two)
        gpre_ref[:, at] = g_pre
        g_wb = dot_nt(g_pre, h1_ref[:, at])
        for block in range(HID // LANES):
            slab_ref[block * HID : (block + 1) * HID, :] += g_wb[:, block * LANES : (block + 1) * LANES]
        bacc[...] += fold_lanes(g_pre.astype(F32))

    bias = ones_sum(bacc)
    put_rows(slab_ref, lambda block: ONE_B + block, bias, 0, 1)
    for piece in range(18):
        put_rows(slab_ref, lambda block: ONE_F + block * 112 + piece * 6, gf, piece * 8, 6)
    for block in range(3):
        width = min(LANES, 288 - block * LANES)
        slab_ref[ONE_P + block * 64 : ONE_P + block * 64 + 64, 0:width] = gwp_ref[
            :, block * LANES : block * LANES + width
        ]
    slab_ref[ONE_LOSS : ONE_LOSS + 1, :] = loss_one_ref[0:1, :] + loss_two_ref[0:1, :]
    slab_ref[ONE_LOSS + 1 : ONE_LOSS + 2, :] = loss_two_ref[1:2, :]
    part_out(slab_ref, 0, PART_A, index_ref[1], bits[0], kept_a, sent_a)
    part_out(slab_ref, PART_A, ONE_ROWS - PART_A, index_ref[1], bits[1], kept_b, sent_b)


def one_backward_bottom(
    dims,
    chunk,
    y1_ref,
    ghalf_ref,
    gbc_ref,
    gout_ref,
    e_ref,
    wbt_ref,
    xcol_ref,
    h1_ref,
    gpre_ref,
    slab_ref,
    gacc,
    gmix,
    ge,
    acc,
):
    rows, cols, bands = dims
    gacc[...] = jnp.zeros_like(gacc)
    ge[...] = jnp.zeros_like(ge)
    slab_ref[...] = jnp.zeros_like(slab_ref)

    @pl.loop(0, rows * cols * LANES // chunk)
    def _(step):
        row, col, at = place_of(step, chunk, cols)
        g_pre = jnp.where(h1_ref[:, at] > 0, dot(wbt_ref[...], gpre_ref[:, at]), 0.0).astype(BF16)
        ge[...] += dot_nt(xcol_ref[:, at], g_pre)
        scatter_cols(gacc, dot(e_ref[...], g_pre), cols, row, col, chunk)

    gmix[0:8, :] = gout_ref[0:8, :] + jnp.concatenate(fold_ext(gacc, rows, cols, bands), axis=1)
    gmix[8:16, :] = ghalf_ref[...]
    g_mixed = gmix[...]
    acc[...] = jnp.zeros_like(acc)
    gram(g_mixed, y1_ref, range(CH), acc)
    stack = [(j, acc[j]) for j in range(CH)] + [(16, fold_lanes(g_mixed)), (17, gbc_ref[...])]
    slab_ref[REST_SMALL : REST_SMALL + 16, :] = lane_sums(stack, CH)
    for tap in range(9):
        put_rows(slab_ref, lambda block: block * 56 + tap * 6, ge, tap * 8, 6)
    put_rows(slab_ref, lambda block: REST_A + block, ge, 6, 1)


def call(kernel, inputs, outputs, scratch, flops, aliases=None):
    whole = pl.BlockSpec(memory_space=pltpu.VMEM)
    smem = pl.BlockSpec(memory_space=pltpu.SMEM)
    traffic = sum(x.size * x.dtype.itemsize for x in list(inputs) + list(outputs))
    return pl.pallas_call(
        kernel,
        out_shape=outputs,
        in_specs=[smem if x.dtype == jnp.int32 and x.ndim == 1 else whole for x in inputs],
        out_specs=[whole for _ in outputs],
        scratch_shapes=scratch,
        input_output_aliases=aliases or {},
        compiler_params=pltpu.CompilerParams(vmem_limit_bytes=VMEM_LIMIT),
        cost_estimate=pl.CostEstimate(flops=flops, bytes_accessed=traffic, transcendentals=0),
    )(*inputs)


def shape(dims, dtype=F32):
    return jax.ShapeDtypeStruct(tuple(dims), dtype)


def high_dot(left, right, contract=(1, 0)):
    return lax.dot_general(
        left, right, (((contract[0],), (contract[1],)), ((), ())), precision=HIGH, preferred_element_type=F32
    )


def iotas(height, width=LANES):
    return (
        lax.broadcasted_iota(jnp.int32, (height, width), 0),
        lax.broadcasted_iota(jnp.int32, (height, width), 1),
    )


def take_flat(flat_ref, start, length):
    row, offset = divmod(start, LANES)
    lane = lax.broadcasted_iota(jnp.int32, (1, LANES), 1)
    value = flat_ref[row : row + 1, :]
    if offset:
        value = pltpu.roll(value, LANES - offset, 1)
        if offset + length > LANES:
            after = pltpu.roll(flat_ref[row + 1 : row + 2, :], LANES - offset, 1)
            value = jnp.where(lane < LANES - offset, value, after)
    return jnp.where(lane < length, value, 0.0) if length < LANES else value


def put_flat(pieces, start, value, length):
    row, offset = divmod(start, LANES)
    lane = lax.broadcasted_iota(jnp.int32, (1, LANES), 1)
    if length < LANES:
        value = jnp.where(lane < length, value, 0.0)
    if offset:
        value = pltpu.roll(value, offset, 1)
    if offset + length > LANES:
        pieces.setdefault(row + 1, []).append(jnp.where(lane < offset, value, 0.0))
        value = jnp.where(lane >= offset, value, 0.0)
    pieces.setdefault(row, []).append(value)


def level_tables(flat_ref, level, lu):
    chans = CH * (level + 1)
    start = ONE_START - 4 * CH if level == 0 else TWO_START
    chan = [take_flat(flat_ref, start + k * chans, chans) for k in range(4)]
    first = start + 4 * chans + 2 * HID
    lu[...] = jnp.zeros_like(lu)
    for i in range(chans):
        lu[i : i + 1, :] = take_flat(flat_ref, first + i * chans, chans)
    row, lane = iotas(LANES)
    value = lu[...]
    inside = row < chans
    lower = jnp.where(row > lane, value, 0.0) + jnp.where((row == lane) & inside, 1.0, 0.0)
    upper = jnp.where(row < lane, value, 0.0) + jnp.where((row == lane) & inside, jnp.exp(chan[2]), 0.0)
    return chans, start, chan, lower, upper


def natural_row(level, row):
    height, half = (8, CH // 2) if level == 0 else (16, CH)
    return (row // height) * half + lax.rem(row, height), lax.rem(row, height) < half


def natural_keep(row):
    return 4 * lax.rem(row, 8) + row // 8, lax.rem(row, 8) < CH // 2


def pick(condition, value):
    return jnp.sum(jnp.where(condition, value, 0.0), axis=1, keepdims=True)


def prior_places():
    row, lane = iotas(64, 4 * CH)
    inner = lax.rem(row, 32)
    natural, valid = natural_keep(inner)
    return ((lane == natural + (row // 32) * 2 * CH) & valid).astype(F32).astype(BF16)


def prior_lanes(tap):
    row, lane = iotas(2 * CH)
    inner = lane - (tap * 32) % LANES
    natural = 4 * lax.rem(inner, 8) + inner // 8
    valid = (inner >= 0) & (inner < 32) & (lax.rem(inner, 8) < CH // 2)
    return ((row == natural) & valid).astype(F32).astype(BF16)


def prepare_level(level, flat_ref, entry_ref, middle_ref, exit_ref, outs, wide):
    e_ref, et_ref, f_ref, ft_ref, wb_ref, wbt_ref, bb_ref = outs
    chans = CH * (level + 1)
    start = 0 if level == 0 else TWO_START
    half, tall = chans // 2, 8 * (level + 1)
    first_in, first_out = (0, 0) if level == 0 else (CH // 2, CH)
    wide[...] = jnp.zeros_like(wide)
    for tap in range(9):
        wide[tap * tall : tap * tall + half, :] = entry_ref[tap, first_in : first_in + half, :]
    row, lane = iotas(LANES)
    for block in range(HID // LANES):
        at = slice(block * LANES, (block + 1) * LANES)
        value = take_flat(flat_ref, start + 4 * chans + block * LANES, LANES)
        for tap in range(3):
            part = value.astype(BF16).astype(F32)
            wide[tap * tall + half : tap * tall + half + 1, at] = part
            value = value - part
        value = take_flat(flat_ref, start + 4 * chans + HID + block * LANES, LANES)
        bb_ref[at, :] = pick(row == lane, value)
    count = 9 * tall
    padded = -(-count // LANES) * LANES
    e_ref[...] = wide[0:count, :].astype(BF16)
    et_ref[...] = wide[0:padded, :].T[:, 0:count].astype(BF16)
    wide[...] = jnp.zeros_like(wide)
    for tap in range(9):
        for side in range(2):
            first = (tap * 2 + side) * tall
            wide[first : first + half, :] = exit_ref[tap, first_out + side * half : first_out + (side + 1) * half, :]
    count = 18 * tall
    padded = -(-count // LANES) * LANES
    f_ref[...] = wide[0:count, :].astype(BF16)
    ft_ref[...] = wide[0:padded, :].T[:, 0:count].astype(BF16)
    wb_ref[...] = middle_ref[level].astype(BF16)
    wbt_ref[...] = middle_ref[level].T.astype(BF16)


def prepare_two_kernel(
    flat_ref, entry_ref, middle_ref, exit_ref, chan1_ref, m1_ref, chan2_ref, m2_ref, m2t_ref, *rest
):
    outs, (lu, wide) = rest[:-2], rest[-2:]
    for level in range(2):
        chans, start, chan, lower, upper = level_tables(flat_ref, level, lu)
        product = high_dot(lower, upper)
        height = 16 * (level + 1)
        row, lane = iotas(height)
        natural, valid = natural_row(level, row)
        spread = ((lane == chans - 1 - natural) & valid).astype(F32)
        matrix = high_dot(spread, product)
        out_bias = pick((lane == natural) & valid, chan[3])
        if level == 0:
            m1_ref[...] = matrix
            shift, scale = pick(lane == row, chan[0]), pick((lane == row) & (row < CH), jnp.exp(chan[1]))
        else:
            source, target = iotas(LANES)
            place, used = natural_keep(target)
            matrix = high_dot(matrix, ((source == place) & used & (target < 32)).astype(F32))
            m2_ref[...] = matrix
            lu[...] = jnp.zeros_like(lu)
            lu[0:32, :] = matrix
            m2t_ref[...] = lu[...].T[0:32, :]
            place, used = natural_keep(row)
            shift = pick((lane == place) & used, chan[0])
            scale = pick((lane == place) & used, jnp.exp(chan[1]))
        chan_ref = chan1_ref if level == 0 else chan2_ref
        chan_ref[...] = (
            jnp.where(lane == 0, shift, 0.0) + jnp.where(lane == 1, scale, 0.0) + jnp.where(lane == 2, out_bias, 0.0)
        )
    prepare_level(1, flat_ref, entry_ref, middle_ref, exit_ref, outs, wide)


def prepare_one_kernel(flat_ref, entry_ref, middle_ref, exit_ref, prior_ref, wp_ref, wpt_ref, pbias_ref, *rest):
    outs, (lu, wide) = rest[:-2], rest[-2:]
    prepare_level(0, flat_ref, entry_ref, middle_ref, exit_ref, outs, wide)
    places = prior_places()
    blocks = [None] * 3
    for tap in range(9):
        moved = dot_nt(places, prior_ref[tap].astype(BF16)).astype(BF16)
        part = dot(moved, prior_lanes(tap))
        block = tap * 32 // LANES
        blocks[block] = part if blocks[block] is None else blocks[block] + part
    lu[...] = jnp.zeros_like(lu)
    for block, value in enumerate(blocks):
        width = min(LANES, 288 - block * LANES)
        at = slice(block * LANES, block * LANES + width)
        wp_ref[:, at] = value[:, 0:width].astype(BF16)
        lu[0:64, :] = value
        wpt_ref[at, :] = lu[...].T[0:width, 0:64].astype(BF16)
    row, lane = iotas(64)
    natural, valid = natural_keep(lax.rem(row, 32))
    pbias_ref[...] = pick((lane == natural + (row // 32) * 2 * CH) & valid, take_flat(flat_ref, PRIOR_START, 4 * CH))


def adamw(weight, grad, first, second):
    first_new = BETA_ONE * first + (1.0 - BETA_ONE) * grad
    second_new = BETA_TWO * second + (1.0 - BETA_TWO) * grad * grad
    first_hat = first_new * (1.0 / (1.0 - BETA_ONE**ADAM_STEP))
    second_hat = second_new * (1.0 / (1.0 - BETA_TWO**ADAM_STEP))
    updated = weight - LEARN_RATE * (first_hat / (jnp.sqrt(second_hat) + ADAM_EPS) + WEIGHT_DECAY * weight)
    return (updated, second_new)


def finish_kernel(
    count_ref,
    two_ref,
    one_ref,
    rest_ref,
    extra_ref,
    flat_ref,
    flat_first,
    flat_second,
    entry_ref,
    entry_first,
    entry_second,
    middle_ref,
    middle_first,
    middle_second,
    exit_ref,
    exit_first,
    exit_second,
    prior_ref,
    prior_first,
    prior_second,
    loss_ref,
    norm_ref,
    flat_new,
    flat_grad,
    flat_moment,
    entry_new,
    entry_grad,
    entry_moment,
    middle_new,
    middle_grad,
    middle_moment,
    exit_new,
    exit_grad,
    exit_moment,
    prior_new,
    prior_grad,
    prior_moment,
    bias_ref,
    two,
    one,
    rest,
    lu,
):
    two[...] = two_ref[WB_ROWS:, :].astype(F32)
    one[...] = one_ref[WB_ROWS:, :].astype(F32)
    rest[...] = rest_ref[...].astype(F32)
    extra = extra_ref[...].astype(F32)
    log_total = jnp.sum(extra[0:3], keepdims=True)
    count_two = jnp.sum(extra[3:6], keepdims=True)
    coef, count = coef_of(count_ref), jnp.sum(count_ref[...], keepdims=True)
    base = WB_ROWS
    squares = []
    pieces = {}
    consts = []
    for level in range(2):
        chans, start, chan, lower, upper = level_tables(flat_ref, level, lu)
        consts.append(jnp.sum(chan[1] + chan[2], keepdims=True))
        weight = coef * count if level == 0 else coef * count_two
        height = 16 * (level + 1)
        small = rest[REST_SMALL : REST_SMALL + 16, :] if level == 0 else two[TWO_SMALL - base : TWO_SMALL - base + 32, :]
        sum_lane = 16 * (level + 1)
        product = high_dot(lower, upper)
        row, lane = iotas(LANES, height)
        natural, valid = natural_row(level, lane)
        turned = high_dot(((row == chans - 1 - natural) & valid).astype(F32), small)
        row, lane = iotas(LANES)
        g_product = jnp.where(lane < sum_lane, turned, 0.0)
        if level == 1:
            place, used = natural_keep(row)
            g_product = high_dot(g_product, ((lane == place) & used & (row < 32)).astype(F32))
        else:
            g_product = jnp.where(lane < chans, g_product, 0.0)
        g_lower = high_dot(g_product, upper, (1, 1))
        g_upper = high_dot(lower.T, g_product)
        g_lu = jnp.where(row > lane, g_lower, 0.0) + jnp.where(row < lane, g_upper, 0.0)
        diagonal = jnp.sum(jnp.where(row == lane, g_upper, 0.0), axis=0, keepdims=True)
        shift = jnp.sum(turned[:, sum_lane : sum_lane + 1] * product, axis=0, keepdims=True)
        scale = jnp.sum(product * g_product, axis=0, keepdims=True)
        row, lane = iotas(height)
        natural, valid = natural_row(level, row)
        out_bias = jnp.where((lane == natural) & valid, small[:, sum_lane + 1 : sum_lane + 2], 0.0)
        put_flat(pieces, start, shift * jnp.exp(chan[1]), chans)
        put_flat(pieces, start + chans, scale + weight, chans)
        put_flat(pieces, start + 2 * chans, diagonal * jnp.exp(chan[2]) + weight, chans)
        put_flat(pieces, start + 3 * chans, jnp.sum(out_bias, axis=0, keepdims=True), chans)
        for i in range(chans):
            put_flat(pieces, start + 4 * chans + 2 * HID + i * chans, g_lu[i : i + 1, :], chans)
        for block in range(HID // LANES):
            if level == 0:
                value_a = rest[REST_A + block : REST_A + block + 1, :]
                value_b = one[ONE_B - base + block : ONE_B - base + block + 1, :]
            else:
                at = TWO_E - base + block * 144 + CH
                value_a = two[at : at + 1, :]
                value_b = two[TWO_B - base + block : TWO_B - base + block + 1, :]
            at = start + 4 * chans + block * LANES
            put_flat(pieces, at, value_a, LANES)
            put_flat(pieces, at + HID, value_b, LANES)
            bias_ref[2 * level : 2 * level + 1, block * LANES : (block + 1) * LANES] = value_a
            bias_ref[2 * level + 1 : 2 * level + 2, block * LANES : (block + 1) * LANES] = value_b
    row, lane = iotas(64)
    natural, valid = natural_keep(lax.rem(row, 32))
    column = one[ONE_P - base : ONE_P - base + 64, CH // 2 : CH // 2 + 1]
    prior_bias = jnp.where((lane == natural + (row // 32) * 2 * CH) & valid, column, 0.0)
    put_flat(pieces, PRIOR_START, jnp.sum(prior_bias, axis=0, keepdims=True), 4 * CH)
    for r in range(FLAT_ROWS):
        parts = pieces.get(r, [jnp.zeros((1, LANES), F32)])
        flat_grad[r : r + 1, :] = functools.reduce(jnp.add, parts)
    for tap in range(9):
        for block in range(HID // LANES):
            at = slice(block * LANES, (block + 1) * LANES)
            first = block * 56 + tap * 6
            entry_grad[tap, 0:6, at] = rest[first : first + 6, :]
            first = TWO_E - base + block * 144 + tap * 16
            entry_grad[tap, 6:18, at] = two[first : first + CH, :]
            first = ONE_F - base + block * 112 + tap * CH
            exit_grad[tap, 0:CH, at] = one[first : first + CH, :]
            first = TWO_F - base + block * 216 + tap * 2 * CH
            exit_grad[tap, CH : 3 * CH, at] = two[first : first + 2 * CH, :]
    places = prior_places()
    for tap in range(9):
        first = ONE_P - base + (tap * 32 // LANES) * 64
        block = one[first : first + 64, :].astype(BF16)
        moved = dot_nt(prior_lanes(tap), block).astype(BF16)
        prior_grad[tap, :, :] = dot(moved, places)
    for ref in (flat_grad, entry_grad, exit_grad, prior_grad):
        value = ref[...]
        squares.append(jnp.sum(value * value, keepdims=True).reshape(1, 1))
    for ref in (one_ref, two_ref):
        total = jnp.zeros((64, LANES), F32)
        for start in range(0, WB_ROWS, 64):
            value = ref[start : start + 64, :].astype(F32)
            total = total + value * value
        squares.append(jnp.sum(total, keepdims=True))
    norm = jnp.sqrt(functools.reduce(jnp.add, squares))
    clip = jnp.minimum(1.0, CLIP_NORM / (norm + 1e-06))
    total = log_total + consts[0] * count + count_two * (consts[1] - 2 * CH * LOG_TWO_PI)
    loss_ref[...] = coef * total + 8.0
    norm_ref[...] = norm
    bias_ref[...] = bias_ref[...] * clip

    def update(at, refs):
        weight, first, second, new, grad, moment = refs
        value = grad[at] * clip
        grad[at] = value
        new[at], moment[at] = adamw(weight[at], value, first[at], second[at])

    update(..., (flat_ref, flat_first, flat_second, flat_new, flat_grad, flat_moment))
    for tap in range(9):
        update(tap, (entry_ref, entry_first, entry_second, entry_new, entry_grad, entry_moment))
        update(tap, (exit_ref, exit_first, exit_second, exit_new, exit_grad, exit_moment))
        update(tap, (prior_ref, prior_first, prior_second, prior_new, prior_grad, prior_moment))
    size = 64
    for level, slab in enumerate((one_ref, two_ref)):

        @pl.loop(0, HID // size)
        def _(j):
            rows = pl.ds(pl.multiple_of(j * size, size), size)
            for block in range(HID // LANES):
                at = (level, rows, slice(block * LANES, (block + 1) * LANES))
                value = slab[pl.ds(pl.multiple_of(block * HID + j * size, size), size), :].astype(F32) * clip
                middle_grad[at] = value
                middle_new[at], middle_moment[at] = adamw(middle_ref[at], value, middle_first[at], middle_second[at])


def total_over(value, axes):
    for axis in axes:
        size = lax.axis_size(axis)
        distance = 1
        while distance < size:
            value = value + lax.ppermute(value, axis, [(i, i ^ distance) for i in range(size)])
            distance *= 2
    return value


def on_device(
    pixels,
    valid_mask,
    vectors,
    vectors_first,
    vectors_second,
    entry_taps,
    entry_first,
    entry_second,
    middle,
    middle_first,
    middle_second,
    exit_taps,
    exit_first,
    exit_second,
    prior_taps,
    prior_first,
    prior_second,
):
    bands = lax.axis_size("rows")
    rows, cols = valid_mask.shape[0], valid_mask.shape[1]
    dims = (rows, cols, bands)
    half_dims = (rows // 2, cols // 2, bands)
    size = rows * cols * LANES
    part = size // 4
    batches = lax.axis_size("batch")
    devices = batches * bands
    bits = [2**k for k in range((devices - 1).bit_length())]
    index = lax.axis_index("batch") * bands + lax.axis_index("rows")
    own = jnp.stack([lax.axis_index("rows"), index]).astype(jnp.int32)

    def trade(value, bit):
        return lax.ppermute(value, ("batch", "rows"), [(i, i ^ bit) for i in range(devices)])

    def in_hbm(value):
        return pltpu.with_memory_space_constraint(value, pltpu.HBM)

    def after(value, *done):
        return lax.optimization_barrier((value, *done))[0]

    pixel_rows = (CH + 1) * rows * cols // bands
    piece_rows = pixel_rows + 16
    pieces = call(
        functools.partial(pack_kernel, bands),
        (own, pixels.reshape(-1, LANES), valid_mask.reshape(-1, LANES)),
        [shape((piece_rows, LANES), BF16)] * bands,
        [],
        1000,
    )
    bufs = [pieces[0]]
    for d in range(1, bands):
        bufs.append(lax.ppermute(pieces[d], "rows", [(i, i ^ d) for i in range(bands)]))

    def flat(value):
        return jnp.pad(value, (0, FLAT_ROWS * LANES - VEC)).reshape(FLAT_ROWS, LANES)

    vectors_flat = flat(vectors)

    def level_shapes(tall):
        return [
            shape((9 * tall, HID), BF16),
            shape((HID, 9 * tall), BF16),
            shape((18 * tall, HID), BF16),
            shape((HID, 18 * tall), BF16),
            shape((HID, HID), BF16),
            shape((HID, HID), BF16),
            shape((HID, 1)),
        ]

    square, tall_scratch = pltpu.VMEM((LANES, LANES), F32), pltpu.VMEM((384, HID), F32)
    rounds = iter(bits[bands.bit_length() - 1 :])

    def count_round(value, beside):
        bit = next(rounds, None)
        return value if bit is None else value + after(trade(value, bit), beside)

    chan_one, m_one, chan_two, m_two, m_two_t, e_two, e_two_t, f_two, f_two_t, wb_two, wb_two_t, bb_two = call(
        prepare_two_kernel,
        (after(vectors_flat, pieces[0]), entry_taps, middle, exit_taps),
        [shape((16, LANES)), shape((16, LANES)), shape((32, LANES)), shape((32, LANES)), shape((32, LANES))]
        + level_shapes(16),
        [square, tall_scratch],
        10**9,
    )
    bufs = [after(x, m_one) for x in bufs]
    count = sum(x[pixel_rows : pixel_rows + 1].astype(F32) for x in bufs)
    prior_turned = jnp.swapaxes(prior_taps, 1, 2)
    wp, wpt, prior_bias, e_one, e_one_t, f_one, f_one_t, wb_one, wb_one_t, bb_one = call(
        prepare_one_kernel,
        (after(vectors_flat, count), entry_taps, middle, exit_taps, prior_turned),
        [shape((64, 288), BF16), shape((288, 64), BF16), shape((64, 1))] + level_shapes(8),
        [square, tall_scratch],
        10**9,
    )
    count = count_round(count, prior_bias)

    ext_lanes = (rows // 2 + 2) * (cols // 2 + 2) * LANES
    (y1, mixed_one, mask, mask2, keep, y2, mixed_two) = call(
        functools.partial(unpack_kernel, dims),
        (own, *bufs, after(chan_one, count), m_one, chan_two, m_two),
        [
            shape((16, size)),
            shape((16, size)),
            shape((1, size)),
            shape((1, part)),
            shape((32, part)),
            shape((32, part)),
            shape((32, part)),
        ],
        [pltpu.VMEM((bands, piece_rows, LANES), F32), pltpu.VMEM((16, size), F32)],
        10**9,
    )
    count = count_round(count, mask2)
    (out_two, t_two, xcol_two, h1_two, h2_two, loss_two) = call(
        functools.partial(couple_two_forward, half_dims),
        (mixed_two, mask, mask2, after(chan_two, count), e_two_t, wb_two, f_two, bb_two),
        [
            shape((32, part)),
            shape((16, part)),
            shape((144, part), BF16),
            shape((HID, part), BF16),
            shape((HID, part), BF16),
            shape((8, LANES)),
        ],
        [pltpu.VMEM((16, ext_lanes), F32), pltpu.VMEM((32, ext_lanes), F32)],
        2 * HID * part * (144 + HID + 288),
    )
    for _ in bits:
        count = count_round(count, loss_two)
    half_two = shape((TWO_ROWS // 2, LANES))
    (kept_two, sent_two, gkeep_two) = call(
        functools.partial(couple_two_backward, half_dims),
        (own, count, mask2, y2, out_two, t_two, xcol_two, h1_two, h2_two, chan_two, m_two_t, e_two, wb_two_t, f_two_t),
        [half_two, half_two, shape((32, part))],
        [
            pltpu.VMEM((32, ext_lanes), F32),
            pltpu.VMEM((16, ext_lanes), F32),
            pltpu.VMEM((32, part), F32),
            pltpu.VMEM((HID, LANES), F32),
            pltpu.VMEM((144, HID), F32),
            pltpu.VMEM((288, HID), F32),
            pltpu.VMEM((32, 32, LANES), F32),
            pltpu.VMEM((TWO_ROWS, LANES), F32),
        ],
        4 * HID * part * (144 + HID + 288),
    )
    whole_lanes = (rows + 2) * (cols + 2) * LANES
    chunk = 1024
    fwd_in = (
        count,
        in_hbm(mixed_one),
        mask,
        mask2,
        in_hbm(keep),
        in_hbm(gkeep_two),
        chan_one,
        in_hbm(e_one_t),
        in_hbm(wb_one),
        in_hbm(f_one),
        in_hbm(bb_one),
        in_hbm(wp),
        in_hbm(wpt),
        in_hbm(prior_bias),
    )
    fwd_out = [
        shape((72, size), BF16),
        shape((HID, size), BF16),
        shape((HID, size), BF16),
        shape((8, size)),
        shape((8, size)),
        shape((16, size)),
        shape((64, 288)),
        shape((8, LANES)),
    ]
    (xcol_one, h1_one, h2_one, res_one, t_one, gout_one, gwp, loss_one) = call(
        functools.partial(couple_one_forward, dims, chunk),
        fwd_in,
        fwd_out,
        [
            pltpu.VMEM((8, whole_lanes), F32),
            pltpu.VMEM((16, whole_lanes), F32),
            pltpu.VMEM((32, ext_lanes), F32),
            pltpu.VMEM((288, cols // 2 * LANES), BF16),
            pltpu.VMEM((32, ext_lanes), F32),
            pltpu.VMEM((32, part), F32),
        ],
        2 * HID * size * (72 + HID + 144),
    )
    first_bit, second_bit, third_bit, fourth_bit = bits[0], bits[2], bits[1], bits[3]
    total_two = kept_two + after(trade(sent_two, first_bit), loss_one)
    top_in = (own, after(count, total_two), mask, res_one, t_one, gout_one, f_one_t, gwp, loss_one, loss_two, h1_one, h2_one)
    half_a, half_b = shape((PART_A // 2, LANES)), shape(((ONE_ROWS - PART_A) // 2, LANES))
    top_out = [shape((HID, size), BF16), half_a, half_a, half_b, half_b, shape((8, size)), shape((16, LANES))]
    (gpre, kept_a, sent_a, kept_b, sent_b, ghalf, gbc) = call(
        functools.partial(one_backward_top, dims, chunk, (second_bit, third_bit)),
        top_in,
        top_out,
        [
            pltpu.VMEM((16, whole_lanes), F32),
            pltpu.VMEM((144, HID), F32),
            pltpu.VMEM((HID, LANES), F32),
            pltpu.VMEM((ONE_ROWS, LANES), F32),
        ],
        2 * HID * size * (144 + HID + 144),
        aliases={11: 0},
    )

    def halve(parts, bit, *beside):
        high = (index // bit) % 2
        halves = [x.shape[0] // 2 for x in parts]
        sent = [lax.dynamic_slice_in_dim(x, (1 - high) * h, h, 0) for x, h in zip(parts, halves)]
        kept = [lax.dynamic_slice_in_dim(x, high * h, h, 0) for x, h in zip(parts, halves)]
        got = after(trade(jnp.concatenate(sent) if len(sent) > 1 else sent[0], bit), *beside)
        results, first = [], 0
        for x, h in zip(kept, halves):
            results.append(x + got[first : first + h])
            first += h
        return results

    (total_two,) = halve([total_two], second_bit, gbc)
    low_in = (y1, ghalf, after(gbc, total_two), gout_one, e_one, wb_one_t, xcol_one, h1_one, gpre)
    (slab_rest,) = call(
        functools.partial(one_backward_bottom, dims, chunk),
        low_in,
        [shape((REST_ROWS, LANES))],
        [
            pltpu.VMEM((8, whole_lanes), F32),
            pltpu.VMEM((16, size), F32),
            pltpu.VMEM((72, HID), F32),
            pltpu.VMEM((CH, 16, LANES), F32),
        ],
        2 * HID * size * (72 + HID + 72),
    )

    total_a = kept_a + after(trade(sent_a, second_bit), slab_rest)
    total_b = kept_b + after(trade(sent_b, third_bit), slab_rest)
    (total_two,) = halve([total_two], fourth_bit, slab_rest)
    far = bits[3:]
    total_a, total_b, total_rest = halve([total_a, total_b, after(slab_rest, total_two)], first_bit)
    (total_two,) = halve([total_two], third_bit)
    total_a, total_rest = halve([total_a, total_rest], third_bit)
    (total_b,) = halve([total_b], second_bit)
    (total_rest,) = halve([total_rest], second_bit)
    shards = halve([total_a, total_b, total_rest], far[0])
    shards = [total_two] + shards
    for bit in far[1:]:
        shards = halve(shards, bit)
    orders = [
        [first_bit, second_bit, fourth_bit, third_bit] + far[1:],
        [second_bit, first_bit, third_bit] + far,
        [third_bit, first_bit, second_bit] + far,
        [first_bit, third_bit, second_bit] + far,
    ]
    loss_part = shards[2]
    owner, loss_row = divmod(ONE_LOSS - PART_A, loss_part.shape[0])
    extra = []
    for row in range(2):
        value = loss_part[loss_row + row]
        for _ in range(3):
            high = lax.reduce_precision(value, 8, 7)
            extra.append(high)
            value = value - high
    extra = jnp.pad(jnp.stack(extra), ((0, 10), (0, 0)))
    spread = [shards[0].astype(BF16), jnp.concatenate(shards[1:] + [extra]).astype(BF16)]
    near = [[third_bit, second_bit, first_bit], [second_bit, third_bit, first_bit]]
    backs = [far[::-1] + near[0], far[::-1] + near[1]]

    def double(values, bit):
        low = (index // bit) % 2 == 0
        joined = jnp.concatenate(values) if len(values) > 1 else values[0]
        other = trade(joined, bit)
        results, first = [], 0
        for value in values:
            got = other[first : first + value.shape[0]]
            first += value.shape[0]
            results.append(jnp.where(low, jnp.concatenate([value, got]), jnp.concatenate([got, value])))
        return results

    for bit in far[::-1]:
        spread = double(spread, bit)
    for k in range(3):
        spread = [double([value], order[k])[0] for value, order in zip(spread, near)]
    count_bits = len(bits)
    spread = [value.reshape((2,) * count_bits + (-1, LANES)) for value in spread]

    def reorder(value, back, order):
        axes = [count_bits - 1 - back.index(bit) for bit in order]
        return value.transpose(axes + [count_bits, count_bits + 1]).reshape(-1, LANES)

    totals = [reorder(spread[0], backs[0], orders[0])]
    first = 0
    for shard, order in zip(shards[1:], orders[1:]):
        totals.append(reorder(spread[1][..., first : first + shard.shape[0], :], backs[1], order))
        first += shard.shape[0]
    place = [0] * count_bits
    for k, bit in enumerate(orders[2]):
        place[count_bits - 1 - backs[1].index(bit)] = (owner >> (count_bits - 1 - k)) & 1
    extra = spread[1][tuple(place)][first:]
    totals = [totals[0], jnp.concatenate(totals[1:3]), totals[3]]
    taps = [
        (entry_taps, entry_first, entry_second),
        (middle, middle_first, middle_second),
        (exit_taps, exit_first, exit_second),
        (prior_turned, jnp.swapaxes(prior_first, 1, 2), jnp.swapaxes(prior_second, 1, 2)),
    ]
    flats = (vectors_flat, flat(vectors_first), flat(vectors_second))
    outs = [shape((1, 1)), shape((1, 1))] + [shape((FLAT_ROWS, LANES))] * 3
    for group in taps:
        outs += [shape(group[0].shape)] * 3
    outs.append(shape((4, HID)))
    results = call(
        finish_kernel,
        (count, *totals, extra, *flats, *[x for group in taps for x in group]),
        outs,
        [
            pltpu.VMEM((TWO_ROWS - WB_ROWS, LANES), F32),
            pltpu.VMEM((ONE_ROWS - WB_ROWS, LANES), F32),
            pltpu.VMEM((REST_ROWS, LANES), F32),
            pltpu.VMEM((LANES, LANES), F32),
        ],
        10**8,
    )
    results = list(results)
    for k in range(2):
        results[k] = results[k].reshape(())
    for k in range(2, 5):
        results[k] = results[k].reshape(-1)[:VEC]
    for k in range(14, 17):
        results[k] = jnp.swapaxes(results[k], 1, 2)
    return tuple(results)


def solution(mesh):
    replicated = (P(),) * 15
    return jax.shard_map(
        on_device,
        mesh=mesh,
        in_specs=(P(None, "rows", None, "batch"), P("rows", None, "batch")) + replicated,
        out_specs=(P(),) * 18,
        check_vma=False,
    )
```

```python
import functools
import math

import jax
import jax.numpy as jnp
from jax import lax
from jax.experimental import pallas as pl
from jax.experimental.pallas import tpu as pltpu
from jax.sharding import PartitionSpec as P

HID = 512
CH = 12

F32 = jnp.float32
BF16 = jnp.bfloat16
HIGH = lax.Precision.HIGHEST
LOG_TWO_PI = math.log(2.0 * math.pi)
LEARN_RATE = 0.05
BETA_ONE = 0.9
BETA_TWO = 0.999
ADAM_EPS = 1e-08
WEIGHT_DECAY = 0.01
CLIP_NORM = 0.01
ADAM_STEP = 10
LANES = 128
VMEM_LIMIT = 20 * 2**20
ONE_START = 4 * CH
TWO_START = 4 * CH + 2 * HID + CH * CH
PRIOR_START = TWO_START + 8 * CH + 2 * HID + 4 * CH * CH
VEC = PRIOR_START + 4 * CH
FLAT_ROWS = -(-VEC // (8 * LANES)) * 8
WB_ROWS = 4 * HID
TWO_F, TWO_E = WB_ROWS, WB_ROWS + 4 * 216
TWO_B = TWO_E + 4 * 144
TWO_SMALL = TWO_B + 8
TWO_ROWS = 3584
ONE_F = WB_ROWS
ONE_P = ONE_F + 4 * 112
ONE_B = ONE_P + 3 * 64
ONE_LOSS = ONE_B + 8
ONE_ROWS = 2816
PART_A = 1536
REST_A = 4 * 56
REST_SMALL = REST_A + 8
REST_ROWS = 256


def dot(left, right):
    return lax.dot_general(left, right, (((1,), (0,)), ((), ())), preferred_element_type=F32)


def dot_nt(left, right):
    return lax.dot_general(left, right, (((1,), (1,)), ((), ())), preferred_element_type=F32)


def lane_band(bands, height=1):
    return lax.broadcasted_iota(jnp.int32, (height, LANES), 1) // (LANES // bands)


def pack_kernel(bands, index_ref, pixels_ref, mask_ref, *out_refs):
    own = index_ref[0]
    width = LANES // bands
    rows = pixels_ref.shape[0] // bands
    extra = mask_ref.shape[0] // bands
    band = lane_band(bands)
    parts = [pixels_ref[pl.ds(e, rows, stride=bands), :].astype(F32) for e in range(bands)]
    masks = [mask_ref[pl.ds(e, extra, stride=bands), :].astype(F32) for e in range(bands)]
    for d, out_ref in enumerate(out_refs):
        target = own ^ d
        for source, first, size in ((parts, 0, rows), (masks, rows, extra)):
            total = jnp.zeros((size, LANES), F32)
            for e in range(bands):
                shift = lax.rem(e - target + bands, bands) * width
                total = jnp.where(band == e, pltpu.roll(source[e], shift, 1), total)
            out_ref[first : first + size, :] = total.astype(BF16)


def fill_ext(ext_ref, field, rows, cols, bands, pattern):
    width = LANES // bands
    band = lane_band(bands)
    stride = (cols + 2) * LANES
    height = ext_ref.shape[0]
    pads = jnp.broadcast_to(pattern, (height, LANES))
    for block in range(ext_ref.shape[1] // LANES):
        ext_ref[:, block * LANES : (block + 1) * LANES] = pads
    for row in range(rows):
        start = (row + 1) * stride + LANES
        ext_ref[:, start : start + cols * LANES] = field[:, row * cols * LANES : (row + 1) * cols * LANES]
    last = (rows - 1) * cols * LANES
    for col in range(cols):
        above = pltpu.roll(field[:, last + col * LANES : last + (col + 1) * LANES], width, 1)
        start = LANES + col * LANES
        ext_ref[:, start : start + LANES] = jnp.where(band >= 1, above, pads)
        below = pltpu.roll(field[:, col * LANES : (col + 1) * LANES], LANES - width, 1)
        start = (rows + 1) * stride + LANES + col * LANES
        ext_ref[:, start : start + LANES] = jnp.where(band < bands - 1, below, pads)


def fold_ext(ext_ref, rows, cols, bands):
    width = LANES // bands
    band = lane_band(bands)
    stride = (cols + 2) * LANES
    pieces = []
    for row in range(rows):
        start = (row + 1) * stride + LANES
        piece = ext_ref[:, start : start + cols * LANES]
        if row == 0:
            blocks = []
            for col in range(cols):
                start = (rows + 1) * stride + LANES + col * LANES
                moved = pltpu.roll(ext_ref[:, start : start + LANES], width, 1)
                blocks.append(jnp.where(band >= 1, moved, 0.0))
            piece = piece + jnp.concatenate(blocks, axis=1)
        if row == rows - 1:
            blocks = []
            for col in range(cols):
                start = LANES + col * LANES
                moved = pltpu.roll(ext_ref[:, start : start + LANES], LANES - width, 1)
                blocks.append(jnp.where(band < bands - 1, moved, 0.0))
            piece = piece + jnp.concatenate(blocks, axis=1)
        pieces.append(piece)
    return pieces


def window(cols, row, first_col, tap, turned=False):
    dy, dx = tap // 3, tap % 3
    if turned:
        dy, dx = 2 - dy, 2 - dx
    return ((row + dy) * (cols + 2) + first_col + dx) * LANES


def place_of(step, chunk, cols):
    per_row = cols * LANES // chunk
    return step // per_row, lax.rem(step, per_row) * (chunk // LANES), pl.ds(pl.multiple_of(step * chunk, chunk), chunk)


def gather_cols(ext_ref, cols, row, first_col, size, turned=False):
    starts = [window(cols, row, first_col, tap, turned) for tap in range(9)]
    starts = [s if isinstance(s, int) else pl.multiple_of(s, LANES) for s in starts]
    return jnp.concatenate([ext_ref[:, pl.ds(s, size)] for s in starts], axis=0).astype(BF16)


def scatter_cols(ext_ref, values, cols, row, first_col, size, turned=False):
    height = ext_ref.shape[0]
    for tap in range(9):
        start = window(cols, row, first_col, tap, turned)
        if not isinstance(start, int):
            start = pl.multiple_of(start, LANES)
        at = pl.ds(start, size)
        ext_ref[:, at] = ext_ref[:, at] + values[tap * height : (tap + 1) * height]


def mix(matrix_ref, field_ref, start, size, pairs):
    total = None
    for j in pairs:
        term = matrix_ref[:, j : j + 1] * field_ref[j : j + 1, start : start + size]
        total = term if total is None else total + term
    return total


def log_sigmoid(value):
    return jnp.minimum(value, 0.0) - jnp.log1p(jnp.exp(-jnp.abs(value)))


def sigmoid_minus(value):
    power = jnp.exp(-jnp.abs(value))
    return jnp.where(value >= 0.0, power, 1.0) / (1.0 + power)


def row_mask(height, period, valid):
    return lax.rem(lax.broadcasted_iota(jnp.int32, (height, 1), 0), period) < valid


def fold_lanes(value):
    total = value[:, :LANES]
    for start in range(LANES, value.shape[1], LANES):
        total = total + value[:, start : start + LANES]
    return total


def unpack_kernel(
    dims,
    index_ref,
    b0,
    b1,
    b2,
    b3,
    chan1_ref,
    m1_ref,
    chan2_ref,
    m2_ref,
    y1_ref,
    mix1_ref,
    mask_ref,
    mask2_ref,
    keep_ref,
    y2_ref,
    mix2_ref,
    bufs,
    xs,
):
    rows, cols, bands = dims
    own = index_ref[0]
    width = LANES // bands
    band = lane_band(bands)
    groups = cols // bands
    for d, ref in enumerate((b0, b1, b2, b3)):
        bufs[d, :, :] = ref[...].astype(F32)
    xs[...] = jnp.zeros_like(xs)
    for s in range(rows):
        for a in range(groups):
            loads = [bufs[d, pl.ds(s * groups + a, CH + 1, stride=rows * groups), :] for d in range(bands)]
            for e in range(bands):
                total = jnp.zeros((CH + 1, LANES), F32)
                for d in range(bands):
                    origin = own ^ d
                    shift = lax.rem(origin - e + bands, bands) * width
                    total = jnp.where(band == origin, pltpu.roll(loads[d], shift, 1), total)
                start = (s * cols + bands * a + e) * LANES
                xs[0 : CH + 1, start : start + LANES] = total
    line = cols * LANES
    for s in range(rows):
        at = slice(s * line, (s + 1) * line)
        mask_ref[:, at] = xs[CH : CH + 1, at]
        raw = xs[:, at]
        source = (raw + 0.5) / 256.0 - 0.5
        y1_ref[:, at] = (source + chan1_ref[:, 0:1]) * chan1_ref[:, 1:2]
    for s in range(rows):
        at = slice(s * line, (s + 1) * line)
        mix1_ref[:, at] = mix(m1_ref, y1_ref, s * line, line, range(CH))
    half_rows, half_cols = rows // 2, cols // 2
    for i in range(half_rows):
        for j in range(half_cols):
            at = slice((i * half_cols + j) * LANES, (i * half_cols + j + 1) * LANES)
            masks = None
            for p in range(4):
                di, dj = p // 2, p % 2
                start = ((2 * i + di) * cols + 2 * j + dj) * LANES
                keep_ref[p * 8 : p * 8 + 8, at] = mix1_ref[0:8, start : start + LANES]
                block = mask_ref[:, start : start + LANES]
                masks = block if masks is None else jnp.minimum(masks, block)
            mask2_ref[:, at] = masks
    size = half_rows * half_cols * LANES
    y2_ref[...] = (keep_ref[...] + chan2_ref[:, 0:1]) * chan2_ref[:, 1:2]
    pairs = [j for j in range(32) if j % 8 < 6]
    mix2_ref[...] = mix(m2_ref, y2_ref, 0, size, pairs)


def couple_two_forward(
    dims,
    mix2_ref,
    mask_ref,
    mask2_ref,
    chan2_ref,
    et_ref,
    wb_ref,
    f_ref,
    bias_ref,
    out2_ref,
    t2_ref,
    xcol_ref,
    h1_ref,
    h2_ref,
    loss_ref,
    ext,
    oacc,
):
    half_rows, half_cols, bands = dims
    mixed = mix2_ref[...]
    out2_ref[0:16, :] = mixed[:16]
    iota = lax.broadcasted_iota(jnp.int32, (16, 1), 0)
    ones = jnp.where(iota == CH, 1.0, 0.0)
    fill_ext(ext, mixed[:16] + ones, half_rows, half_cols, bands, ones)
    oacc[...] = jnp.zeros_like(oacc)
    chunk = half_cols * LANES
    for i in range(half_rows):
        at = slice(i * chunk, (i + 1) * chunk)
        xcol = gather_cols(ext, half_cols, i, 0, chunk)
        xcol_ref[:, at] = xcol
        hidden = jnp.maximum(dot(et_ref[...], xcol), 0.0).astype(BF16)
        h1_ref[:, at] = hidden
        hidden = jnp.maximum(dot(wb_ref[...], hidden) + bias_ref[...], 0.0).astype(BF16)
        h2_ref[:, at] = hidden
        scatter_cols(oacc, dot(f_ref[...], hidden), half_cols, i, 0, chunk, True)
    output = jnp.concatenate(fold_ext(oacc, half_rows, half_cols, bands), axis=1) + chan2_ref[:, 2:3]
    second = output[16:] + 2.0
    t2_ref[...] = second
    scale_log = log_sigmoid(second)
    result = (mixed[16:] + output[:16]) * jnp.exp(scale_log)
    out2_ref[16:, :] = result
    valid = row_mask(16, 16, CH)
    per_pixel = jnp.where(valid, scale_log - 0.5 * (mixed[:16] * mixed[:16] + result * result), 0.0)
    mask2 = mask2_ref[...]
    loss_ref[...] = jnp.zeros_like(loss_ref)
    loss_ref[0:1, :] = jnp.sum(fold_lanes(per_pixel * mask2), axis=0, keepdims=True)
    loss_ref[1:2, :] = fold_lanes(mask2)
    loss_ref[2:3, :] = fold_lanes(mask_ref[...])


def part_out(slab_ref, first, size, index, bit, kept_ref, sent_ref):
    half = size // 2
    high = lax.rem(index // bit, 2)
    kept_ref[...] = slab_ref[pl.ds(pl.multiple_of(first + high * half, 8), half), :]
    sent_ref[...] = slab_ref[pl.ds(pl.multiple_of(first + (1 - high) * half, 8), half), :]


def gram(left, right_ref, pairs, acc_ref):
    for j in pairs:
        acc_ref[j, :, :] = acc_ref[j, :, :] + fold_lanes(left * right_ref[j : j + 1, :])


def couple_two_backward(
    dims,
    bits,
    index_ref,
    mask2_ref,
    y2_ref,
    out2_ref,
    t2_ref,
    xcol_ref,
    h1_ref,
    h2_ref,
    chan2_ref,
    m2t_ref,
    e_ref,
    wbt_ref,
    ft_ref,
    kept_u,
    sent_u,
    kept_v,
    sent_v,
    gkeep_ref,
    ext,
    gacc,
    gmix,
    bacc,
    ge,
    gf,
    acc,
    slab_ref,
):
    rows, cols, bands = dims
    weight = -mask2_ref[...]
    second = t2_ref[...]
    result = out2_ref[16:, :]
    g_result = -weight * result
    g_log = g_result * result + weight
    g_second = g_log * sigmoid_minus(second)
    g_half = g_result * jnp.exp(log_sigmoid(second))
    gmix[0:16, :] = -weight * out2_ref[0:16, :]
    gmix[16:32, :] = g_half
    valid = row_mask(16, 16, CH)
    g_out = jnp.concatenate([g_half, jnp.where(valid, g_second, 0.0)], axis=0)
    g_out = g_out.astype(BF16).astype(F32)
    out_sums = fold_lanes(g_out)
    fill_ext(ext, g_out, rows, cols, bands, jnp.zeros((32, 1), F32))
    gacc[...] = jnp.zeros_like(gacc)
    chunk = cols * LANES
    for i in range(rows):
        at = slice(i * chunk, (i + 1) * chunk)
        gcol = gather_cols(ext, cols, i, 0, chunk, True)
        hidden_two = h2_ref[:, at]
        hidden_one = h1_ref[:, at]
        g_pre = jnp.where(hidden_two > 0, dot(ft_ref[...], gcol), 0.0).astype(BF16)
        g_f = dot_nt(gcol, hidden_two)
        g_wb = dot_nt(g_pre, hidden_one)
        folded = fold_lanes(g_pre.astype(F32))
        g_pre = jnp.where(hidden_one > 0, dot(wbt_ref[...], g_pre), 0.0).astype(BF16)
        g_e = dot_nt(xcol_ref[:, at], g_pre)
        scatter_cols(gacc, dot(e_ref[...], g_pre), cols, i, 0, chunk)
        if i == 0:
            gf[...], ge[...], bacc[...] = g_f, g_e, folded
        else:
            gf[...] += g_f
            ge[...] += g_e
            bacc[...] += folded
        for block in range(HID // LANES):
            at = slice(block * HID, (block + 1) * HID)
            part = g_wb[:, block * LANES : (block + 1) * LANES]
            slab_ref[at, :] = part if i == 0 else slab_ref[at, :] + part
    slab_ref[TWO_B:TWO_ROWS, :] = jnp.zeros((TWO_ROWS - TWO_B, LANES), F32)
    put_rows(slab_ref, lambda block: TWO_B + block, ones_sum(bacc), 0, 1)
    for piece in range(18):
        put_rows(slab_ref, lambda block: TWO_F + block * 216 + piece * CH, gf, piece * 16, CH)
    put_rows(slab_ref, lambda block: TWO_E + block * 144, ge, 0, 144)
    gmix[0:16, :] += jnp.concatenate(fold_ext(gacc, rows, cols, bands), axis=1)
    pairs = [j for j in range(32) if j % 8 < 6]
    g_mixed = gmix[...]
    acc[...] = jnp.zeros_like(acc)
    gram(g_mixed, y2_ref, pairs, acc)
    stack = [(j, acc[j]) for j in pairs] + [(32, fold_lanes(g_mixed)), (33, out_sums)]
    slab_ref[TWO_SMALL : TWO_SMALL + 32, :] = lane_sums(stack, 32)
    part_out(slab_ref, 0, TWO_ROWS // 2, index_ref[1], bits[0], kept_u, sent_u)
    part_out(slab_ref, TWO_ROWS // 2, TWO_ROWS // 2, index_ref[1], bits[1], kept_v, sent_v)
    valid_rows = [j for j in range(32) if j % 16 < CH]
    gkeep_ref[...] = mix(m2t_ref, gmix, 0, rows * chunk, valid_rows) * chan2_ref[:, 1:2]


def level_two_kernel(
    dims,
    bits,
    index_ref,
    b0,
    b1,
    b2,
    b3,
    chan1_ref,
    m1_ref,
    chan2_ref,
    m2_ref,
    m2t_ref,
    e_ref,
    et_ref,
    f_ref,
    ft_ref,
    wb_ref,
    wbt_ref,
    bias_ref,
    y1_ref,
    mix1_ref,
    mask_ref,
    mask2_ref,
    keep_ref,
    loss_ref,
    gkeep_ref,
    kept_u,
    sent_u,
    kept_v,
    sent_v,
    bufs,
    xs,
    y2,
    mix2,
    out2,
    t2,
    xcol,
    h1,
    h2,
    ext_in,
    oacc,
    ext_out,
    gacc,
    gmix,
    bacc,
    ge,
    gf,
    acc,
    slab,
):
    rows, cols, bands = dims
    half = (rows // 2, cols // 2, bands)
    unpack_kernel(
        dims, index_ref, b0, b1, b2, b3, chan1_ref, m1_ref, chan2_ref, m2_ref,
        y1_ref, mix1_ref, mask_ref, mask2_ref, keep_ref, y2, mix2, bufs, xs,
    )
    couple_two_forward(
        half, mix2, mask_ref, mask2_ref, chan2_ref, et_ref, wb_ref, f_ref, bias_ref,
        out2, t2, xcol, h1, h2, loss_ref, ext_in, oacc,
    )
    couple_two_backward(
        half, bits, index_ref, mask2_ref, y2, out2, t2, xcol, h1, h2, chan2_ref, m2t_ref, e_ref, wbt_ref, ft_ref,
        kept_u, sent_u, kept_v, sent_v, gkeep_ref, ext_out, gacc, gmix, bacc, ge, gf, acc, slab,
    )


def couple_one_forward(
    dims,
    chunk,
    mix1_ref,
    mask_ref,
    mask2_ref,
    keep_ref,
    gkeep_in_ref,
    chan1_ref,
    et_ref,
    wb_ref,
    f_ref,
    bias_ref,
    wp_ref,
    wpt_ref,
    pbias_ref,
    xcol_ref,
    h1_ref,
    h2_ref,
    res_ref,
    t_ref,
    gout_ref,
    gwp_ref,
    loss_ref,
    ext,
    oacc,
    kext,
    kcol,
    gkacc,
    drop,
):
    rows, cols, bands = dims
    iota = lax.broadcasted_iota(jnp.int32, (8, 1), 0)
    ones = jnp.where(iota == CH // 2, 1.0, 0.0)
    fill_ext(ext, mix1_ref[0:8, :] + ones, rows, cols, bands, ones)
    oacc[...] = jnp.zeros_like(oacc)

    @pl.loop(0, rows * cols * LANES // chunk)
    def _(step):
        row, col, at = place_of(step, chunk, cols)
        xcol = gather_cols(ext, cols, row, col, chunk)
        xcol_ref[:, at] = xcol
        hidden = jnp.maximum(dot(et_ref[...], xcol), 0.0).astype(BF16)
        h1_ref[:, at] = hidden
        hidden = jnp.maximum(dot(wb_ref[...], hidden) + bias_ref[...], 0.0).astype(BF16)
        h2_ref[:, at] = hidden
        scatter_cols(oacc, dot(f_ref[...], hidden), cols, row, col, chunk, True)

    line = cols * LANES
    valid = row_mask(8, 8, CH // 2)
    step_total = None
    half_rows, half_cols = rows // 2, cols // 2
    for s, piece in enumerate(fold_ext(oacc, rows, cols, bands)):
        at = slice(s * line, (s + 1) * line)
        output = piece + chan1_ref[:, 2:3]
        second = output[8:] + 2.0
        t_ref[:, at] = second
        scale_log = log_sigmoid(second)
        result = (mix1_ref[8:16, at] + output[:8]) * jnp.exp(scale_log)
        res_ref[:, at] = result
        part = fold_lanes(jnp.where(valid, scale_log, 0.0) * mask_ref[:, at])
        step_total = part if step_total is None else step_total + part
    for i in range(half_rows):
        for j in range(half_cols):
            at = slice((i * half_cols + j) * LANES, (i * half_cols + j + 1) * LANES)
            for p in range(4):
                start = ((2 * i + p // 2) * cols + 2 * j + p % 2) * LANES
                drop[p * 8 : p * 8 + 8, at] = res_ref[:, start : start + LANES]
    part_iota = lax.broadcasted_iota(jnp.int32, (32, 1), 0)
    part_ones = jnp.where(part_iota == CH // 2, 1.0, 0.0)
    fill_ext(kext, keep_ref[...] + part_ones, half_rows, half_cols, bands, part_ones)
    part_line = half_cols * LANES
    gkacc[...] = jnp.zeros_like(gkacc)
    weight = -mask2_ref[...]
    valid = row_mask(32, 8, CH // 2)
    prior_total = None
    for i in range(half_rows):
        at = slice(i * part_line, (i + 1) * part_line)
        columns = gather_cols(kext, half_cols, i, 0, part_line)
        kcol[...] = columns
        prior = dot(wp_ref[...], columns) + pbias_ref[...]
        mean, logs = prior[:32], prior[32:]
        inverse = jnp.exp(-logs)
        scaled = (drop[:, at] - mean) * inverse
        part = fold_lanes((-logs - 0.5 * scaled * scaled) * mask2_ref[:, at])
        prior_total = part if prior_total is None else prior_total + part
        g_mean = weight[:, at] * scaled * inverse
        g_logs = jnp.where(valid, weight[:, at] * (scaled * scaled - 1.0), 0.0)
        drop[:, at] = -g_mean
        g_prior = jnp.concatenate([g_mean, g_logs], axis=0).astype(BF16)
        g_wp = dot_nt(g_prior, kcol[...])
        if i == 0:
            gwp_ref[...] = g_wp
        else:
            gwp_ref[...] += g_wp
        scatter_cols(gkacc, dot(wpt_ref[...], g_prior), half_cols, i, 0, part_line)
    loss_ref[...] = jnp.zeros_like(loss_ref)
    loss_ref[0:1, :] = jnp.sum(step_total, axis=0, keepdims=True) + jnp.sum(prior_total, axis=0, keepdims=True)
    for i, piece in enumerate(fold_ext(gkacc, half_rows, half_cols, bands)):
        at = slice(i * part_line, (i + 1) * part_line)
        g_keep = piece + gkeep_in_ref[:, at]
        g_drop = drop[:, at]
        for j in range(half_cols):
            inner = slice(j * LANES, (j + 1) * LANES)
            for p in range(4):
                start = ((2 * i + p // 2) * cols + 2 * j + p % 2) * LANES
                gout_ref[0:8, start : start + LANES] = g_keep[p * 8 : p * 8 + 8, inner]
                gout_ref[8:16, start : start + LANES] = g_drop[p * 8 : p * 8 + 8, inner]


def put_rows(slab_ref, first, values, row, count):
    for block in range(HID // LANES):
        start = first(block)
        slab_ref[start : start + count, :] = values[row : row + count, block * LANES : (block + 1) * LANES]


def lane_sums(stack, width):
    lane = lax.broadcasted_iota(jnp.int32, (1, LANES), 1)
    total = jnp.zeros(stack[0][1].shape, F32)
    for j, value in stack:
        total = total + jnp.where(lane == j, jnp.sum(value, axis=1, keepdims=True), 0.0)
    return total


def ones_sum(value_ref):
    return lax.dot_general(
        jnp.ones((8, LANES), F32), value_ref[...], (((1,), (1,)), ((), ())), precision=HIGH, preferred_element_type=F32
    )


def one_backward_top(
    dims,
    chunk,
    bits,
    index_ref,
    mask_ref,
    res_ref,
    t_ref,
    gout_ref,
    ft_ref,
    gwp_ref,
    loss_one_ref,
    loss_two_ref,
    h1_ref,
    h2_ref,
    gpre_ref,
    kept_a,
    sent_a,
    kept_b,
    sent_b,
    ghalf_ref,
    gbc_ref,
    ext,
    gf,
    bacc,
    slab_ref,
):
    rows, cols, bands = dims
    weight = -mask_ref[...]
    second = t_ref[...]
    result = res_ref[...]
    g_result = gout_ref[8:16, :]
    g_log = g_result * result + weight
    g_second = g_log * sigmoid_minus(second)
    g_half = g_result * jnp.exp(log_sigmoid(second))
    ghalf_ref[...] = g_half
    valid = row_mask(8, 8, CH // 2)
    g_out = jnp.concatenate([g_half, jnp.where(valid, g_second, 0.0)], axis=0)
    g_out = g_out.astype(BF16).astype(F32)
    gbc_ref[...] = fold_lanes(g_out)
    fill_ext(ext, g_out, rows, cols, bands, jnp.zeros((16, 1), F32))
    gf[...] = jnp.zeros_like(gf)
    slab_ref[...] = jnp.zeros_like(slab_ref)
    bacc[...] = jnp.zeros_like(bacc)

    @pl.loop(0, rows * cols * LANES // chunk)
    def _(step):
        row, col, at = place_of(step, chunk, cols)
        gcol = gather_cols(ext, cols, row, col, chunk, True)
        hidden_two = h2_ref[:, at]
        g_pre = jnp.where(hidden_two > 0, dot(ft_ref[...], gcol), 0.0).astype(BF16)
        gf[...] += dot_nt(gcol, hidden_two)
        gpre_ref[:, at] = g_pre
        g_wb = dot_nt(g_pre, h1_ref[:, at])
        for block in range(HID // LANES):
            slab_ref[block * HID : (block + 1) * HID, :] += g_wb[:, block * LANES : (block + 1) * LANES]
        bacc[...] += fold_lanes(g_pre.astype(F32))

    bias = ones_sum(bacc)
    put_rows(slab_ref, lambda block: ONE_B + block, bias, 0, 1)
    for piece in range(18):
        put_rows(slab_ref, lambda block: ONE_F + block * 112 + piece * 6, gf, piece * 8, 6)
    for block in range(3):
        width = min(LANES, 288 - block * LANES)
        slab_ref[ONE_P + block * 64 : ONE_P + block * 64 + 64, 0:width] = gwp_ref[
            :, block * LANES : block * LANES + width
        ]
    slab_ref[ONE_LOSS : ONE_LOSS + 1, :] = loss_one_ref[0:1, :] + loss_two_ref[0:1, :]
    slab_ref[ONE_LOSS + 1 : ONE_LOSS + 3, :] = loss_two_ref[1:3, :]
    part_out(slab_ref, 0, PART_A, index_ref[1], bits[0], kept_a, sent_a)
    part_out(slab_ref, PART_A, ONE_ROWS - PART_A, index_ref[1], bits[1], kept_b, sent_b)


def one_backward_bottom(
    dims,
    chunk,
    y1_ref,
    ghalf_ref,
    gbc_ref,
    gout_ref,
    e_ref,
    wbt_ref,
    xcol_ref,
    h1_ref,
    gpre_ref,
    slab_ref,
    gacc,
    gmix,
    ge,
    acc,
):
    rows, cols, bands = dims
    gacc[...] = jnp.zeros_like(gacc)
    ge[...] = jnp.zeros_like(ge)
    slab_ref[...] = jnp.zeros_like(slab_ref)

    @pl.loop(0, rows * cols * LANES // chunk)
    def _(step):
        row, col, at = place_of(step, chunk, cols)
        g_pre = jnp.where(h1_ref[:, at] > 0, dot(wbt_ref[...], gpre_ref[:, at]), 0.0).astype(BF16)
        ge[...] += dot_nt(xcol_ref[:, at], g_pre)
        scatter_cols(gacc, dot(e_ref[...], g_pre), cols, row, col, chunk)

    gmix[0:8, :] = gout_ref[0:8, :] + jnp.concatenate(fold_ext(gacc, rows, cols, bands), axis=1)
    gmix[8:16, :] = ghalf_ref[...]
    g_mixed = gmix[...]
    acc[...] = jnp.zeros_like(acc)
    gram(g_mixed, y1_ref, range(CH), acc)
    stack = [(j, acc[j]) for j in range(CH)] + [(16, fold_lanes(g_mixed)), (17, gbc_ref[...])]
    slab_ref[REST_SMALL : REST_SMALL + 16, :] = lane_sums(stack, CH)
    for tap in range(9):
        put_rows(slab_ref, lambda block: block * 56 + tap * 6, ge, tap * 8, 6)
    put_rows(slab_ref, lambda block: REST_A + block, ge, 6, 1)


def call(kernel, inputs, outputs, scratch, flops, aliases=None, far_in=(), far_out=()):
    whole = pl.BlockSpec(memory_space=pltpu.VMEM)
    smem = pl.BlockSpec(memory_space=pltpu.SMEM)
    far = pl.BlockSpec(memory_space=pl.ANY)
    traffic = sum(x.size * x.dtype.itemsize for x in list(inputs) + list(outputs))
    return pl.pallas_call(
        kernel,
        out_shape=outputs,
        in_specs=[
            far if k in far_in else smem if x.dtype == jnp.int32 and x.ndim == 1 else whole for k, x in enumerate(inputs)
        ],
        out_specs=[far if k in far_out else whole for k in range(len(outputs))],
        scratch_shapes=scratch,
        input_output_aliases=aliases or {},
        compiler_params=pltpu.CompilerParams(vmem_limit_bytes=VMEM_LIMIT),
        cost_estimate=pl.CostEstimate(flops=flops, bytes_accessed=traffic, transcendentals=0),
    )(*inputs)


def shape(dims, dtype=F32):
    return jax.ShapeDtypeStruct(tuple(dims), dtype)


def high_dot(left, right, contract=(1, 0)):
    return lax.dot_general(
        left, right, (((contract[0],), (contract[1],)), ((), ())), precision=HIGH, preferred_element_type=F32
    )


def iotas(height, width=LANES):
    return (
        lax.broadcasted_iota(jnp.int32, (height, width), 0),
        lax.broadcasted_iota(jnp.int32, (height, width), 1),
    )


def take_flat(flat_ref, start, length):
    row, offset = divmod(start, LANES)
    lane = lax.broadcasted_iota(jnp.int32, (1, LANES), 1)
    value = flat_ref[row : row + 1, :]
    if offset:
        value = pltpu.roll(value, LANES - offset, 1)
        if offset + length > LANES:
            after = pltpu.roll(flat_ref[row + 1 : row + 2, :], LANES - offset, 1)
            value = jnp.where(lane < LANES - offset, value, after)
    return jnp.where(lane < length, value, 0.0) if length < LANES else value


def put_flat(pieces, start, value, length):
    row, offset = divmod(start, LANES)
    lane = lax.broadcasted_iota(jnp.int32, (1, LANES), 1)
    if length < LANES:
        value = jnp.where(lane < length, value, 0.0)
    if offset:
        value = pltpu.roll(value, offset, 1)
    if offset + length > LANES:
        pieces.setdefault(row + 1, []).append(jnp.where(lane < offset, value, 0.0))
        value = jnp.where(lane >= offset, value, 0.0)
    pieces.setdefault(row, []).append(value)


def level_tables(flat_ref, level, lu):
    chans = CH * (level + 1)
    start = ONE_START - 4 * CH if level == 0 else TWO_START
    chan = [take_flat(flat_ref, start + k * chans, chans) for k in range(4)]
    first = start + 4 * chans + 2 * HID
    lu[...] = jnp.zeros_like(lu)
    for i in range(chans):
        lu[i : i + 1, :] = take_flat(flat_ref, first + i * chans, chans)
    row, lane = iotas(LANES)
    value = lu[...]
    inside = row < chans
    lower = jnp.where(row > lane, value, 0.0) + jnp.where((row == lane) & inside, 1.0, 0.0)
    upper = jnp.where(row < lane, value, 0.0) + jnp.where((row == lane) & inside, jnp.exp(chan[2]), 0.0)
    return chans, start, chan, lower, upper


def natural_row(level, row):
    height, half = (8, CH // 2) if level == 0 else (16, CH)
    return (row // height) * half + lax.rem(row, height), lax.rem(row, height) < half


def natural_keep(row):
    return 4 * lax.rem(row, 8) + row // 8, lax.rem(row, 8) < CH // 2


def pick(condition, value):
    return jnp.sum(jnp.where(condition, value, 0.0), axis=1, keepdims=True)


def prior_places():
    row, lane = iotas(64, 4 * CH)
    inner = lax.rem(row, 32)
    natural, valid = natural_keep(inner)
    return ((lane == natural + (row // 32) * 2 * CH) & valid).astype(F32).astype(BF16)


def prior_lanes(tap):
    row, lane = iotas(2 * CH)
    inner = lane - (tap * 32) % LANES
    natural = 4 * lax.rem(inner, 8) + inner // 8
    valid = (inner >= 0) & (inner < 32) & (lax.rem(inner, 8) < CH // 2)
    return ((row == natural) & valid).astype(F32).astype(BF16)


def prepare_level(level, flat_ref, entry_ref, middle_ref, exit_ref, outs, wide):
    e_ref, et_ref, f_ref, ft_ref, wb_ref, wbt_ref, bb_ref = outs
    chans = CH * (level + 1)
    start = 0 if level == 0 else TWO_START
    half, tall = chans // 2, 8 * (level + 1)
    first_in, first_out = (0, 0) if level == 0 else (CH // 2, CH)
    wide[...] = jnp.zeros_like(wide)
    for tap in range(9):
        wide[tap * tall : tap * tall + half, :] = entry_ref[tap, first_in : first_in + half, :]
    row, lane = iotas(LANES)
    for block in range(HID // LANES):
        at = slice(block * LANES, (block + 1) * LANES)
        value = take_flat(flat_ref, start + 4 * chans + block * LANES, LANES)
        for tap in range(3):
            part = value.astype(BF16).astype(F32)
            wide[tap * tall + half : tap * tall + half + 1, at] = part
            value = value - part
        value = take_flat(flat_ref, start + 4 * chans + HID + block * LANES, LANES)
        bb_ref[at, :] = pick(row == lane, value)
    count = 9 * tall
    padded = -(-count // LANES) * LANES
    e_ref[...] = wide[0:count, :].astype(BF16)
    et_ref[...] = wide[0:padded, :].T[:, 0:count].astype(BF16)
    wide[...] = jnp.zeros_like(wide)
    for tap in range(9):
        for side in range(2):
            first = (tap * 2 + side) * tall
            wide[first : first + half, :] = exit_ref[tap, first_out + side * half : first_out + (side + 1) * half, :]
    count = 18 * tall
    padded = -(-count // LANES) * LANES
    f_ref[...] = wide[0:count, :].astype(BF16)
    ft_ref[...] = wide[0:padded, :].T[:, 0:count].astype(BF16)
    wb_ref[...] = middle_ref[level].astype(BF16)
    wbt_ref[...] = middle_ref[level].T.astype(BF16)


def prepare_kernel(
    flat_ref,
    prior_ref,
    entry_far,
    middle_far,
    exit_far,
    chan1_ref,
    m1_ref,
    chan2_ref,
    m2_ref,
    m2t_ref,
    wp_ref,
    wpt_ref,
    pbias_ref,
    *refs,
):
    outs_two, outs_one = refs[:7], refs[7:14]
    lu, wide, entry_ref, middle_ref, exit_ref, sems = refs[14:]
    copies = [
        pltpu.make_async_copy(middle_far.at[1], middle_ref.at[1], sems.at[0]),
        pltpu.make_async_copy(exit_far, exit_ref, sems.at[1]),
        pltpu.make_async_copy(entry_far, entry_ref, sems.at[2]),
        pltpu.make_async_copy(middle_far.at[0], middle_ref.at[0], sems.at[3]),
    ]
    for copy in copies:
        copy.start()
    for level in range(2):
        chans, start, chan, lower, upper = level_tables(flat_ref, level, lu)
        product = high_dot(lower, upper)
        height = 16 * (level + 1)
        row, lane = iotas(height)
        natural, valid = natural_row(level, row)
        spread = ((lane == chans - 1 - natural) & valid).astype(F32)
        matrix = high_dot(spread, product)
        out_bias = pick((lane == natural) & valid, chan[3])
        if level == 0:
            m1_ref[...] = matrix
            shift, scale = pick(lane == row, chan[0]), pick((lane == row) & (row < CH), jnp.exp(chan[1]))
        else:
            source, target = iotas(LANES)
            place, used = natural_keep(target)
            matrix = high_dot(matrix, ((source == place) & used & (target < 32)).astype(F32))
            m2_ref[...] = matrix
            lu[...] = jnp.zeros_like(lu)
            lu[0:32, :] = matrix
            m2t_ref[...] = lu[...].T[0:32, :]
            place, used = natural_keep(row)
            shift = pick((lane == place) & used, chan[0])
            scale = pick((lane == place) & used, jnp.exp(chan[1]))
        chan_ref = chan1_ref if level == 0 else chan2_ref
        chan_ref[...] = (
            jnp.where(lane == 0, shift, 0.0) + jnp.where(lane == 1, scale, 0.0) + jnp.where(lane == 2, out_bias, 0.0)
        )
    places = prior_places()
    blocks = [None] * 3
    for tap in range(9):
        moved = dot_nt(places, prior_ref[tap].astype(BF16)).astype(BF16)
        part = dot(moved, prior_lanes(tap))
        block = tap * 32 // LANES
        blocks[block] = part if blocks[block] is None else blocks[block] + part
    lu[...] = jnp.zeros_like(lu)
    for block, value in enumerate(blocks):
        width = min(LANES, 288 - block * LANES)
        at = slice(block * LANES, block * LANES + width)
        wp_ref[:, at] = value[:, 0:width].astype(BF16)
        lu[0:64, :] = value
        wpt_ref[at, :] = lu[...].T[0:width, 0:64].astype(BF16)
    row, lane = iotas(64)
    natural, valid = natural_keep(lax.rem(row, 32))
    pbias_ref[...] = pick((lane == natural + (row // 32) * 2 * CH) & valid, take_flat(flat_ref, PRIOR_START, 4 * CH))
    for copy in copies[:3]:
        copy.wait()
    prepare_level(1, flat_ref, entry_ref, middle_ref, exit_ref, outs_two, wide)
    copies[3].wait()
    prepare_level(0, flat_ref, entry_ref, middle_ref, exit_ref, outs_one, wide)


def adamw(weight, grad, first, second):
    first_new = BETA_ONE * first + (1.0 - BETA_ONE) * grad
    second_new = BETA_TWO * second + (1.0 - BETA_TWO) * grad * grad
    first_hat = first_new * (1.0 / (1.0 - BETA_ONE**ADAM_STEP))
    second_hat = second_new * (1.0 / (1.0 - BETA_TWO**ADAM_STEP))
    updated = weight - LEARN_RATE * (first_hat / (jnp.sqrt(second_hat) + ADAM_EPS) + WEIGHT_DECAY * weight)
    return (updated, second_new)


def finish_kernel(
    two_ref,
    one_ref,
    rest_ref,
    extra_ref,
    flat_ref,
    flat_first,
    flat_second,
    *refs,
):
    far_in, refs = refs[:12], refs[12:]
    (loss_ref, norm_ref, flat_new, flat_grad, flat_moment), refs = refs[:5], refs[5:]
    far_out, refs = refs[:12], refs[12:]
    bias_ref, two, one, rest, lu = refs[:5]
    held, (in_sems, out_sems) = refs[5:21], refs[21:]
    weights, firsts, seconds, grads = held[0:4], held[4:8], held[8:12], held[12:16]
    entry_grad, _, exit_grad, prior_grad = grads
    jobs = [(1, 0), (1, 1), (2, None), (0, None), (3, None)]

    def part(ref, level):
        return ref if level is None else ref.at[level]

    def copies_in(k):
        group, level = jobs[k]
        return [
            pltpu.make_async_copy(part(far_in[3 * group + j], level), part(near[group], level), in_sems.at[k, j])
            for j, near in enumerate((weights, firsts, seconds))
        ]

    def copies_out(k):
        group, level = jobs[k]
        return [
            pltpu.make_async_copy(part(near[group], level), part(far_out[3 * group + j], level), out_sems.at[k, j])
            for j, near in enumerate((weights, grads, seconds))
        ]

    for k in range(len(jobs)):
        for copy in copies_in(k):
            copy.start()
    extra = extra_ref[...].astype(F32)
    count = jnp.sum(extra[6:9], keepdims=True)
    coef = -1.0 / (CH * count * math.log(2.0))
    factor = -coef
    two[...] = two_ref[WB_ROWS:, :].astype(F32) * factor
    one[...] = one_ref[WB_ROWS:, :].astype(F32) * factor
    rest[...] = rest_ref[...].astype(F32) * factor
    log_total = jnp.sum(extra[0:3], keepdims=True)
    count_two = jnp.sum(extra[3:6], keepdims=True)
    base = WB_ROWS
    squares = []
    pieces = {}
    consts = []
    for level in range(2):
        chans, start, chan, lower, upper = level_tables(flat_ref, level, lu)
        consts.append(jnp.sum(chan[1] + chan[2], keepdims=True))
        weight = coef * count if level == 0 else coef * count_two
        height = 16 * (level + 1)
        small = rest[REST_SMALL : REST_SMALL + 16, :] if level == 0 else two[TWO_SMALL - base : TWO_SMALL - base + 32, :]
        sum_lane = 16 * (level + 1)
        product = high_dot(lower, upper)
        row, lane = iotas(LANES, height)
        natural, valid = natural_row(level, lane)
        turned = high_dot(((row == chans - 1 - natural) & valid).astype(F32), small)
        row, lane = iotas(LANES)
        g_product = jnp.where(lane < sum_lane, turned, 0.0)
        if level == 1:
            place, used = natural_keep(row)
            g_product = high_dot(g_product, ((lane == place) & used & (row < 32)).astype(F32))
        else:
            g_product = jnp.where(lane < chans, g_product, 0.0)
        g_lower = high_dot(g_product, upper, (1, 1))
        g_upper = high_dot(lower.T, g_product)
        g_lu = jnp.where(row > lane, g_lower, 0.0) + jnp.where(row < lane, g_upper, 0.0)
        diagonal = jnp.sum(jnp.where(row == lane, g_upper, 0.0), axis=0, keepdims=True)
        shift = jnp.sum(turned[:, sum_lane : sum_lane + 1] * product, axis=0, keepdims=True)
        scale = jnp.sum(product * g_product, axis=0, keepdims=True)
        row, lane = iotas(height)
        natural, valid = natural_row(level, row)
        out_bias = jnp.where((lane == natural) & valid, small[:, sum_lane + 1 : sum_lane + 2], 0.0)
        put_flat(pieces, start, shift * jnp.exp(chan[1]), chans)
        put_flat(pieces, start + chans, scale + weight, chans)
        put_flat(pieces, start + 2 * chans, diagonal * jnp.exp(chan[2]) + weight, chans)
        put_flat(pieces, start + 3 * chans, jnp.sum(out_bias, axis=0, keepdims=True), chans)
        for i in range(chans):
            put_flat(pieces, start + 4 * chans + 2 * HID + i * chans, g_lu[i : i + 1, :], chans)
        for block in range(HID // LANES):
            if level == 0:
                value_a = rest[REST_A + block : REST_A + block + 1, :]
                value_b = one[ONE_B - base + block : ONE_B - base + block + 1, :]
            else:
                at = TWO_E - base + block * 144 + CH
                value_a = two[at : at + 1, :]
                value_b = two[TWO_B - base + block : TWO_B - base + block + 1, :]
            at = start + 4 * chans + block * LANES
            put_flat(pieces, at, value_a, LANES)
            put_flat(pieces, at + HID, value_b, LANES)
            bias_ref[2 * level : 2 * level + 1, block * LANES : (block + 1) * LANES] = value_a
            bias_ref[2 * level + 1 : 2 * level + 2, block * LANES : (block + 1) * LANES] = value_b
    row, lane = iotas(64)
    natural, valid = natural_keep(lax.rem(row, 32))
    column = one[ONE_P - base : ONE_P - base + 64, CH // 2 : CH // 2 + 1]
    prior_bias = jnp.where((lane == natural + (row // 32) * 2 * CH) & valid, column, 0.0)
    put_flat(pieces, PRIOR_START, jnp.sum(prior_bias, axis=0, keepdims=True), 4 * CH)
    for r in range(FLAT_ROWS):
        parts = pieces.get(r, [jnp.zeros((1, LANES), F32)])
        flat_grad[r : r + 1, :] = functools.reduce(jnp.add, parts)
    for tap in range(9):
        for block in range(HID // LANES):
            at = slice(block * LANES, (block + 1) * LANES)
            first = block * 56 + tap * 6
            entry_grad[tap, 0:6, at] = rest[first : first + 6, :]
            first = TWO_E - base + block * 144 + tap * 16
            entry_grad[tap, 6:18, at] = two[first : first + CH, :]
            first = ONE_F - base + block * 112 + tap * CH
            exit_grad[tap, 0:CH, at] = one[first : first + CH, :]
            first = TWO_F - base + block * 216 + tap * 2 * CH
            exit_grad[tap, CH : 3 * CH, at] = two[first : first + 2 * CH, :]
    places = prior_places()
    for tap in range(9):
        first = ONE_P + (tap * 32 // LANES) * 64
        moved = dot_nt(prior_lanes(tap), one_ref[first : first + 64, :]).astype(BF16)
        prior_grad[tap, :, :] = dot(moved, places) * factor
    for ref in (flat_grad, entry_grad, exit_grad, prior_grad):
        value = ref[...]
        squares.append(jnp.sum(value * value, keepdims=True).reshape(1, 1))
    for ref in (one_ref, two_ref):
        total = jnp.zeros((64, LANES), F32)
        for start in range(0, WB_ROWS, 64):
            value = ref[start : start + 64, :].astype(F32)
            total = total + value * value
        squares.append(jnp.sum(total, keepdims=True) * factor * factor)
    norm = jnp.sqrt(functools.reduce(jnp.add, squares))
    clip = jnp.minimum(1.0, CLIP_NORM / (norm + 1e-06))
    total = log_total + consts[0] * count + count_two * (consts[1] - 2 * CH * LOG_TWO_PI)
    loss_ref[...] = coef * total + 8.0
    norm_ref[...] = norm
    bias_ref[...] = bias_ref[...] * clip

    middle_factor = factor * clip
    value = flat_grad[...] * clip
    flat_grad[...] = value
    flat_new[...], flat_moment[...] = adamw(flat_ref[...], value, flat_first[...], flat_second[...])
    size = 64
    for k, (group, level) in enumerate(jobs):
        for copy in copies_in(k):
            copy.wait()
        weight, first, second, grad = weights[group], firsts[group], seconds[group], grads[group]
        if level is None:
            for tap in range(9):
                value = grad[tap] * clip
                grad[tap] = value
                weight[tap], second[tap] = adamw(weight[tap], value, first[tap], second[tap])
        else:
            slab = (one_ref, two_ref)[level]

            @pl.loop(0, HID // size)
            def _(j):
                rows = pl.ds(pl.multiple_of(j * size, size), size)
                for block in range(HID // LANES):
                    at = (level, rows, slice(block * LANES, (block + 1) * LANES))
                    value = slab[pl.ds(pl.multiple_of(block * HID + j * size, size), size), :].astype(F32) * middle_factor
                    grad[at] = value
                    weight[at], second[at] = adamw(weight[at], value, first[at], second[at])

        for copy in copies_out(k):
            copy.start()
    for k in range(len(jobs)):
        for copy in copies_out(k):
            copy.wait()


def on_device(
    pixels,
    valid_mask,
    vectors,
    vectors_first,
    vectors_second,
    entry_taps,
    entry_first,
    entry_second,
    middle,
    middle_first,
    middle_second,
    exit_taps,
    exit_first,
    exit_second,
    prior_taps,
    prior_first,
    prior_second,
):
    bands = lax.axis_size("rows")
    rows, cols = valid_mask.shape[0], valid_mask.shape[1]
    dims = (rows, cols, bands)
    size = rows * cols * LANES
    part = size // 4
    batches = lax.axis_size("batch")
    devices = batches * bands
    bits = [2**k for k in range((devices - 1).bit_length())]
    index = lax.axis_index("batch") * bands + lax.axis_index("rows")
    own = jnp.stack([lax.axis_index("rows"), index]).astype(jnp.int32)

    def trade(value, bit):
        return lax.ppermute(value, ("batch", "rows"), [(i, i ^ bit) for i in range(devices)])

    def in_hbm(value):
        return pltpu.with_memory_space_constraint(value, pltpu.HBM)

    def after(value, *done):
        return lax.optimization_barrier((value, *done))[0]

    piece_rows = (CH + 1) * rows * cols // bands
    pieces = call(
        functools.partial(pack_kernel, bands),
        (own, pixels.reshape(-1, LANES), valid_mask.reshape(-1, LANES)),
        [shape((piece_rows, LANES), BF16)] * bands,
        [],
        1000,
    )
    bufs = [pieces[0]]
    for d in range(1, bands):
        bufs.append(lax.ppermute(pieces[d], "rows", [(i, i ^ d) for i in range(bands)]))

    def flat(value):
        return jnp.pad(value, (0, FLAT_ROWS * LANES - VEC)).reshape(FLAT_ROWS, LANES)

    vectors_flat = flat(vectors)

    def level_shapes(tall):
        return [
            shape((9 * tall, HID), BF16),
            shape((HID, 9 * tall), BF16),
            shape((18 * tall, HID), BF16),
            shape((HID, 18 * tall), BF16),
            shape((HID, HID), BF16),
            shape((HID, HID), BF16),
            shape((HID, 1)),
        ]

    prior_turned = jnp.swapaxes(prior_taps, 1, 2)
    (
        chan_one, m_one, chan_two, m_two, m_two_t, wp, wpt, prior_bias,
        e_two, e_two_t, f_two, f_two_t, wb_two, wb_two_t, bb_two,
        e_one, e_one_t, f_one, f_one_t, wb_one, wb_one_t, bb_one,
    ) = call(
        prepare_kernel,
        (after(vectors_flat, pieces[0]), prior_turned, in_hbm(entry_taps), in_hbm(middle), in_hbm(exit_taps)),
        [shape((16, LANES)), shape((16, LANES)), shape((32, LANES)), shape((32, LANES)), shape((32, LANES))]
        + [shape((64, 288), BF16), shape((288, 64), BF16), shape((64, 1))]
        + level_shapes(16)
        + level_shapes(8),
        [
            pltpu.VMEM((LANES, LANES), F32),
            pltpu.VMEM((384, HID), F32),
            pltpu.VMEM(entry_taps.shape, F32),
            pltpu.VMEM(middle.shape, F32),
            pltpu.VMEM(exit_taps.shape, F32),
            pltpu.SemaphoreType.DMA((4,)),
        ],
        10**9,
        far_in=(2, 3, 4),
    )


    ext_lanes = (rows // 2 + 2) * (cols // 2 + 2) * LANES
    first_bit, second_bit, third_bit, fourth_bit = bits[0], bits[2], bits[1], bits[3]
    quarter_two = shape((TWO_ROWS // 4, LANES))
    (y1, mixed_one, mask, mask2, keep, loss_two, gkeep_two, kept_u, sent_u, kept_v, sent_v) = call(
        functools.partial(level_two_kernel, dims, (second_bit, third_bit)),
        (
            own, *bufs, chan_one, m_one, chan_two, m_two, m_two_t,
            e_two, e_two_t, f_two, f_two_t, wb_two, wb_two_t, bb_two,
        ),
        [
            shape((16, size)),
            shape((16, size)),
            shape((1, size)),
            shape((1, part)),
            shape((32, part)),
            shape((8, LANES)),
            shape((32, part)),
        ]
        + [quarter_two] * 4,
        [
            pltpu.VMEM((bands, piece_rows, LANES), F32),
            pltpu.VMEM((16, size), F32),
            pltpu.VMEM((32, part), F32),
            pltpu.VMEM((32, part), F32),
            pltpu.VMEM((32, part), F32),
            pltpu.VMEM((16, part), F32),
            pltpu.VMEM((144, part), BF16),
            pltpu.VMEM((HID, part), BF16),
            pltpu.VMEM((HID, part), BF16),
            pltpu.VMEM((16, ext_lanes), F32),
            pltpu.VMEM((32, ext_lanes), F32),
            pltpu.VMEM((32, ext_lanes), F32),
            pltpu.VMEM((16, ext_lanes), F32),
            pltpu.VMEM((32, part), F32),
            pltpu.VMEM((HID, LANES), F32),
            pltpu.VMEM((144, HID), F32),
            pltpu.VMEM((288, HID), F32),
            pltpu.VMEM((32, 32, LANES), F32),
            pltpu.VMEM((TWO_ROWS, LANES), F32),
        ],
        6 * HID * part * (144 + HID + 288),
    )
    whole_lanes = (rows + 2) * (cols + 2) * LANES
    chunk = 1024
    fwd_in = (
        mixed_one,
        mask,
        mask2,
        keep,
        gkeep_two,
        chan_one,
        e_one_t,
        wb_one,
        f_one,
        bb_one,
        wp,
        wpt,
        prior_bias,
    )
    fwd_out = [
        shape((72, size), BF16),
        shape((HID, size), BF16),
        shape((HID, size), BF16),
        shape((8, size)),
        shape((8, size)),
        shape((16, size)),
        shape((64, 288)),
        shape((8, LANES)),
    ]
    (xcol_one, h1_one, h2_one, res_one, t_one, gout_one, gwp, loss_one) = call(
        functools.partial(couple_one_forward, dims, chunk),
        fwd_in,
        fwd_out,
        [
            pltpu.VMEM((8, whole_lanes), F32),
            pltpu.VMEM((16, whole_lanes), F32),
            pltpu.VMEM((32, ext_lanes), F32),
            pltpu.VMEM((288, cols // 2 * LANES), BF16),
            pltpu.VMEM((32, ext_lanes), F32),
            pltpu.VMEM((32, part), F32),
        ],
        2 * HID * size * (72 + HID + 144),
    )
    total_u = kept_u + after(trade(sent_u, second_bit), loss_one)
    total_v = kept_v + after(trade(sent_v, third_bit), loss_one)
    top_in = (own, after(mask, total_u, total_v), res_one, t_one, gout_one, f_one_t, gwp, loss_one, loss_two, h1_one, h2_one)
    half_a, half_b = shape((PART_A // 2, LANES)), shape(((ONE_ROWS - PART_A) // 2, LANES))
    top_out = [shape((HID, size), BF16), half_a, half_a, half_b, half_b, shape((8, size)), shape((16, LANES))]
    (gpre, kept_a, sent_a, kept_b, sent_b, ghalf, gbc) = call(
        functools.partial(one_backward_top, dims, chunk, (second_bit, third_bit)),
        top_in,
        top_out,
        [
            pltpu.VMEM((16, whole_lanes), F32),
            pltpu.VMEM((144, HID), F32),
            pltpu.VMEM((HID, LANES), F32),
            pltpu.VMEM((ONE_ROWS, LANES), F32),
        ],
        2 * HID * size * (144 + HID + 144),
        aliases={10: 0},
    )

    def halve(parts, bit, *beside):
        high = (index // bit) % 2
        halves = [x.shape[0] // 2 for x in parts]
        sent = [lax.dynamic_slice_in_dim(x, (1 - high) * h, h, 0) for x, h in zip(parts, halves)]
        kept = [lax.dynamic_slice_in_dim(x, high * h, h, 0) for x, h in zip(parts, halves)]
        got = after(trade(jnp.concatenate(sent) if len(sent) > 1 else sent[0], bit), *beside)
        results, first = [], 0
        for x, h in zip(kept, halves):
            results.append(x + got[first : first + h])
            first += h
        return results

    def exchange(parts, near_parts, far_parts, near, far_bit):
        code = 2 * ((index // near) % 2) + (index // far_bit) % 2
        sizes = [x.shape[0] // 4 for x in parts]

        def pieces_for(partner):
            return [lax.dynamic_slice_in_dim(x, (code ^ partner) * h, h, 0) for x, h in zip(parts, sizes)]

        totals = pieces_for(0)
        others = []
        for partner, bit, more in ((2, near, near_parts), (1, far_bit, far_parts), (3, near | far_bit, [])):
            high = (index // bit) % 2
            halves = [x.shape[0] // 2 for x in more]
            sent = pieces_for(partner) + [
                lax.dynamic_slice_in_dim(x, (1 - high) * h, h, 0) for x, h in zip(more, halves)
            ]
            got = trade(jnp.concatenate(sent) if len(sent) > 1 else sent[0], bit)
            first = 0
            for k, h in enumerate(sizes):
                totals[k] = totals[k] + got[first : first + h]
                first += h
            for x, h in zip(more, halves):
                others.append(lax.dynamic_slice_in_dim(x, high * h, h, 0) + got[first : first + h])
                first += h
        return totals + others

    (total_u,) = halve([total_u], third_bit, gbc)
    (total_v,) = halve([total_v], second_bit, gbc)
    low_in = (y1, ghalf, after(gbc, total_u, total_v), gout_one, e_one, wb_one_t, xcol_one, h1_one, gpre)
    (slab_rest,) = call(
        functools.partial(one_backward_bottom, dims, chunk),
        low_in,
        [shape((REST_ROWS, LANES))],
        [
            pltpu.VMEM((8, whole_lanes), F32),
            pltpu.VMEM((16, size), F32),
            pltpu.VMEM((72, HID), F32),
            pltpu.VMEM((CH, 16, LANES), F32),
        ],
        2 * HID * size * (72 + HID + 72),
    )

    total_a = kept_a + after(trade(sent_a, second_bit), slab_rest)
    total_b = kept_b + after(trade(sent_b, third_bit), slab_rest)
    total_u, total_v = halve([total_u, total_v], fourth_bit, slab_rest)
    far = bits[3:]
    total_u, total_v, total_a, total_b, total_rest = halve(
        [total_u, total_v, total_a, total_b, after(slab_rest, total_u, total_v)], first_bit
    )
    total_rest, total_a, total_b = exchange([total_rest], [total_a], [total_b], third_bit, second_bit)
    total_a, total_b, total_rest, total_u, total_v = exchange(
        [total_a, total_b, total_rest], [], [total_u, total_v], far[0], far[1]
    )
    shards = [total_u, total_v, total_a, total_b, total_rest]
    for bit in far[2:]:
        shards = halve(shards, bit)
    orders = [
        [second_bit, third_bit, fourth_bit, first_bit] + far[1:],
        [third_bit, second_bit, fourth_bit, first_bit] + far[1:],
        [second_bit, first_bit, third_bit] + far,
        [third_bit, first_bit, second_bit] + far,
        [first_bit, third_bit, second_bit] + far,
    ]
    loss_part = shards[3]
    owner, loss_row = divmod(ONE_LOSS - PART_A, loss_part.shape[0])
    extra = []
    for row in range(3):
        value = loss_part[loss_row + row]
        for _ in range(3):
            high = lax.reduce_precision(value, 8, 7)
            extra.append(high)
            value = value - high
    extra = jnp.pad(jnp.stack(extra), ((0, 7), (0, 0)))
    spread = [jnp.concatenate(shards[:2]).astype(BF16), jnp.concatenate(shards[2:] + [extra]).astype(BF16)]
    near = [[third_bit, second_bit, first_bit], [second_bit, third_bit, first_bit]]
    backs = [far[::-1] + near[0], far[::-1] + near[1]]

    def double(values, bit):
        low = (index // bit) % 2 == 0
        joined = jnp.concatenate(values) if len(values) > 1 else values[0]
        other = trade(joined, bit)
        results, first = [], 0
        for value in values:
            got = other[first : first + value.shape[0]]
            first += value.shape[0]
            results.append(jnp.where(low, jnp.concatenate([value, got]), jnp.concatenate([got, value])))
        return results

    for bit in far[:1:-1]:
        spread = double(spread, bit)
    near_low, far_low = (index // far[0]) % 2 == 0, (index // far[1]) % 2 == 0
    sizes = [value.shape[0] for value in spread]
    joined = jnp.concatenate(spread)
    from_far, from_near, from_both = (trade(joined, bit) for bit in (far[1], far[0], far[0] | far[1]))

    def ordered(low, one, other):
        return jnp.where(low, jnp.concatenate([one, other]), jnp.concatenate([other, one]))

    quads = []
    for first, size_of in ((0, sizes[0]), (sizes[0], sizes[1])):
        own_part, far_part, near_part, both_part = (
            x[first : first + size_of] for x in (joined, from_far, from_near, from_both)
        )
        quads.append(
            ordered(near_low, ordered(far_low, own_part, far_part), ordered(far_low, near_part, both_part))
        )
    spread = quads
    for k in range(3):
        spread = [double([value], order[k])[0] for value, order in zip(spread, near)]
    count_bits = len(bits)
    spread = [value.reshape((2,) * count_bits + (-1, LANES)) for value in spread]

    def reorder(value, back, order):
        axes = [count_bits - 1 - back.index(bit) for bit in order]
        return value.transpose(axes + [count_bits, count_bits + 1]).reshape(-1, LANES)

    totals = []
    first = 0
    for k, (shard, order) in enumerate(zip(shards, orders)):
        first = 0 if k in (0, 2) else first
        side = 0 if k < 2 else 1
        totals.append(reorder(spread[side][..., first : first + shard.shape[0], :], backs[side], order))
        first += shard.shape[0]
    place = [0] * count_bits
    for k, bit in enumerate(orders[3]):
        place[count_bits - 1 - backs[1].index(bit)] = (owner >> (count_bits - 1 - k)) & 1
    extra = spread[1][tuple(place)][first:]
    totals = [jnp.concatenate(totals[:2]), jnp.concatenate(totals[2:4]), totals[4]]
    taps = [
        (entry_taps, entry_first, entry_second),
        (middle, middle_first, middle_second),
        (exit_taps, exit_first, exit_second),
        (prior_turned, jnp.swapaxes(prior_first, 1, 2), jnp.swapaxes(prior_second, 1, 2)),
    ]
    flats = (vectors_flat, flat(vectors_first), flat(vectors_second))
    outs = [shape((1, 1)), shape((1, 1))] + [shape((FLAT_ROWS, LANES))] * 3
    for group in taps:
        outs += [shape(group[0].shape)] * 3
    outs.append(shape((4, HID)))
    results = call(
        finish_kernel,
        (*totals, extra, *flats, *[in_hbm(x) for group in taps for x in group]),
        outs,
        [
            pltpu.VMEM((TWO_ROWS - WB_ROWS, LANES), F32),
            pltpu.VMEM((ONE_ROWS - WB_ROWS, LANES), F32),
            pltpu.VMEM((REST_ROWS, LANES), F32),
            pltpu.VMEM((LANES, LANES), F32),
        ]
        + [pltpu.VMEM(group[0].shape, F32) for _ in range(4) for group in taps]
        + [pltpu.SemaphoreType.DMA((5, 3))] * 2,
        10**8,
        far_in=range(7, 19),
        far_out=range(5, 17),
    )
    results = list(results)
    for k in range(2):
        results[k] = results[k].reshape(())
    for k in range(2, 5):
        results[k] = results[k].reshape(-1)[:VEC]
    for k in range(14, 17):
        results[k] = jnp.swapaxes(results[k], 1, 2)
    return tuple(results)


def solution(mesh):
    replicated = (P(),) * 15
    return jax.shard_map(
        on_device,
        mesh=mesh,
        in_specs=(P(None, "rows", None, "batch"), P("rows", None, "batch")) + replicated,
        out_specs=(P(),) * 18,
        check_vma=False,
    )
```

```python
import functools
import math

import jax
import jax.numpy as jnp
from jax import lax
from jax.experimental import pallas as pl
from jax.experimental.pallas import tpu as pltpu
from jax.sharding import PartitionSpec as P

HID = 512
CH = 12

F32 = jnp.float32
BF16 = jnp.bfloat16
HIGH = lax.Precision.HIGHEST
LOG_TWO_PI = math.log(2.0 * math.pi)
LEARN_RATE = 0.05
BETA_ONE = 0.9
BETA_TWO = 0.999
ADAM_EPS = 1e-08
WEIGHT_DECAY = 0.01
CLIP_NORM = 0.01
ADAM_STEP = 10
LANES = 128
VMEM_LIMIT = 20 * 2**20
ONE_START = 4 * CH
TWO_START = 4 * CH + 2 * HID + CH * CH
PRIOR_START = TWO_START + 8 * CH + 2 * HID + 4 * CH * CH
VEC = PRIOR_START + 4 * CH
FLAT_ROWS = -(-VEC // (8 * LANES)) * 8
WB_ROWS = 4 * HID
TWO_F, TWO_E = WB_ROWS, WB_ROWS + 4 * 216
TWO_B = TWO_E + 4 * 144
TWO_SMALL = TWO_B + 8
TWO_ROWS = 3584
ONE_F = WB_ROWS
ONE_P = ONE_F + 4 * 112
ONE_B = ONE_P + 3 * 64
ONE_LOSS = ONE_B + 8
ONE_ROWS = 2816
PART_A = 768
REST_A = 4 * 56
REST_SMALL = REST_A + 8
REST_ROWS = 256


def dot(left, right):
    return lax.dot_general(left, right, (((1,), (0,)), ((), ())), preferred_element_type=F32)


def dot_nt(left, right):
    return lax.dot_general(left, right, (((1,), (1,)), ((), ())), preferred_element_type=F32)


def lane_band(bands, height=1):
    return lax.broadcasted_iota(jnp.int32, (height, LANES), 1) // (LANES // bands)


def pack_kernel(bands, index_ref, pixels_ref, mask_ref, *out_refs):
    own = index_ref[0]
    width = LANES // bands
    rows = pixels_ref.shape[0] // bands
    extra = mask_ref.shape[0] // bands
    band = lane_band(bands)
    parts = [pixels_ref[pl.ds(e, rows, stride=bands), :].astype(F32) for e in range(bands)]
    masks = [mask_ref[pl.ds(e, extra, stride=bands), :].astype(F32) for e in range(bands)]
    for d, out_ref in enumerate(out_refs):
        target = own ^ d
        for source, first, size in ((parts, 0, rows), (masks, rows, extra)):
            total = jnp.zeros((size, LANES), F32)
            for e in range(bands):
                shift = lax.rem(e - target + bands, bands) * width
                total = jnp.where(band == e, pltpu.roll(source[e], shift, 1), total)
            out_ref[first : first + size, :] = total.astype(BF16)


def fill_ext(ext_ref, field, rows, cols, bands, pattern):
    width = LANES // bands
    band = lane_band(bands)
    stride = (cols + 2) * LANES
    height = ext_ref.shape[0]
    pads = jnp.broadcast_to(pattern, (height, LANES))
    for block in range(ext_ref.shape[1] // LANES):
        ext_ref[:, block * LANES : (block + 1) * LANES] = pads
    for row in range(rows):
        start = (row + 1) * stride + LANES
        ext_ref[:, start : start + cols * LANES] = field[:, row * cols * LANES : (row + 1) * cols * LANES]
    last = (rows - 1) * cols * LANES
    for col in range(cols):
        above = pltpu.roll(field[:, last + col * LANES : last + (col + 1) * LANES], width, 1)
        start = LANES + col * LANES
        ext_ref[:, start : start + LANES] = jnp.where(band >= 1, above, pads)
        below = pltpu.roll(field[:, col * LANES : (col + 1) * LANES], LANES - width, 1)
        start = (rows + 1) * stride + LANES + col * LANES
        ext_ref[:, start : start + LANES] = jnp.where(band < bands - 1, below, pads)


def fold_ext(ext_ref, rows, cols, bands):
    width = LANES // bands
    band = lane_band(bands)
    stride = (cols + 2) * LANES
    pieces = []
    for row in range(rows):
        start = (row + 1) * stride + LANES
        piece = ext_ref[:, start : start + cols * LANES]
        if row == 0:
            blocks = []
            for col in range(cols):
                start = (rows + 1) * stride + LANES + col * LANES
                moved = pltpu.roll(ext_ref[:, start : start + LANES], width, 1)
                blocks.append(jnp.where(band >= 1, moved, 0.0))
            piece = piece + jnp.concatenate(blocks, axis=1)
        if row == rows - 1:
            blocks = []
            for col in range(cols):
                start = LANES + col * LANES
                moved = pltpu.roll(ext_ref[:, start : start + LANES], LANES - width, 1)
                blocks.append(jnp.where(band < bands - 1, moved, 0.0))
            piece = piece + jnp.concatenate(blocks, axis=1)
        pieces.append(piece)
    return pieces


def window(cols, row, first_col, tap, turned=False):
    dy, dx = tap // 3, tap % 3
    if turned:
        dy, dx = 2 - dy, 2 - dx
    return ((row + dy) * (cols + 2) + first_col + dx) * LANES


def place_of(step, chunk, cols):
    per_row = cols * LANES // chunk
    return step // per_row, lax.rem(step, per_row) * (chunk // LANES), pl.ds(pl.multiple_of(step * chunk, chunk), chunk)


def gather_cols(ext_ref, cols, row, first_col, size, turned=False):
    starts = [window(cols, row, first_col, tap, turned) for tap in range(9)]
    starts = [s if isinstance(s, int) else pl.multiple_of(s, LANES) for s in starts]
    return jnp.concatenate([ext_ref[:, pl.ds(s, size)] for s in starts], axis=0).astype(BF16)


def scatter_cols(ext_ref, values, cols, row, first_col, size, turned=False):
    height = ext_ref.shape[0]
    for tap in range(9):
        start = window(cols, row, first_col, tap, turned)
        if not isinstance(start, int):
            start = pl.multiple_of(start, LANES)
        at = pl.ds(start, size)
        ext_ref[:, at] = ext_ref[:, at] + values[tap * height : (tap + 1) * height]


def mix(matrix_ref, field_ref, start, size, pairs):
    total = None
    for j in pairs:
        term = matrix_ref[:, j : j + 1] * field_ref[j : j + 1, start : start + size]
        total = term if total is None else total + term
    return total


def log_sigmoid(value):
    return jnp.minimum(value, 0.0) - jnp.log1p(jnp.exp(-jnp.abs(value)))


def sigmoid_minus(value):
    power = jnp.exp(-jnp.abs(value))
    return jnp.where(value >= 0.0, power, 1.0) / (1.0 + power)


def row_mask(height, period, valid):
    return lax.rem(lax.broadcasted_iota(jnp.int32, (height, 1), 0), period) < valid


def fold_lanes(value):
    total = value[:, :LANES]
    for start in range(LANES, value.shape[1], LANES):
        total = total + value[:, start : start + LANES]
    return total


def unpack_kernel(
    dims,
    index_ref,
    b0,
    b1,
    b2,
    b3,
    chan1_ref,
    m1_ref,
    chan2_ref,
    m2_ref,
    y1_ref,
    mix1_ref,
    mask_ref,
    mask2_ref,
    keep_ref,
    y2_ref,
    mix2_ref,
    bufs,
    xs,
):
    rows, cols, bands = dims
    own = index_ref[0]
    width = LANES // bands
    band = lane_band(bands)
    groups = cols // bands
    for d, ref in enumerate((b0, b1, b2, b3)):
        bufs[d, :, :] = ref[...].astype(F32)
    xs[...] = jnp.zeros_like(xs)
    for s in range(rows):
        for a in range(groups):
            loads = [bufs[d, pl.ds(s * groups + a, CH + 1, stride=rows * groups), :] for d in range(bands)]
            for e in range(bands):
                total = jnp.zeros((CH + 1, LANES), F32)
                for d in range(bands):
                    origin = own ^ d
                    shift = lax.rem(origin - e + bands, bands) * width
                    total = jnp.where(band == origin, pltpu.roll(loads[d], shift, 1), total)
                start = (s * cols + bands * a + e) * LANES
                xs[0 : CH + 1, start : start + LANES] = total
    line = cols * LANES
    for s in range(rows):
        at = slice(s * line, (s + 1) * line)
        mask_ref[:, at] = xs[CH : CH + 1, at]
        raw = xs[:, at]
        source = (raw + 0.5) / 256.0 - 0.5
        y1_ref[:, at] = (source + chan1_ref[:, 0:1]) * chan1_ref[:, 1:2]
    for s in range(rows):
        at = slice(s * line, (s + 1) * line)
        mix1_ref[:, at] = mix(m1_ref, y1_ref, s * line, line, range(CH))
    half_rows, half_cols = rows // 2, cols // 2
    for i in range(half_rows):
        for j in range(half_cols):
            at = slice((i * half_cols + j) * LANES, (i * half_cols + j + 1) * LANES)
            masks = None
            for p in range(4):
                di, dj = p // 2, p % 2
                start = ((2 * i + di) * cols + 2 * j + dj) * LANES
                keep_ref[p * 8 : p * 8 + 8, at] = mix1_ref[0:8, start : start + LANES]
                block = mask_ref[:, start : start + LANES]
                masks = block if masks is None else jnp.minimum(masks, block)
            mask2_ref[:, at] = masks
    size = half_rows * half_cols * LANES
    y2_ref[...] = (keep_ref[...] + chan2_ref[:, 0:1]) * chan2_ref[:, 1:2]
    pairs = [j for j in range(32) if j % 8 < 6]
    mix2_ref[...] = mix(m2_ref, y2_ref, 0, size, pairs)


def couple_two_forward(
    dims,
    mix2_ref,
    mask_ref,
    mask2_ref,
    chan2_ref,
    et_ref,
    wb_ref,
    f_ref,
    bias_ref,
    out2_ref,
    t2_ref,
    xcol_ref,
    h1_ref,
    h2_ref,
    loss_ref,
    ext,
    oacc,
):
    half_rows, half_cols, bands = dims
    mixed = mix2_ref[...]
    out2_ref[0:16, :] = mixed[:16]
    iota = lax.broadcasted_iota(jnp.int32, (16, 1), 0)
    ones = jnp.where(iota == CH, 1.0, 0.0)
    fill_ext(ext, mixed[:16] + ones, half_rows, half_cols, bands, ones)
    oacc[...] = jnp.zeros_like(oacc)
    chunk = half_cols * LANES
    for i in range(half_rows):
        at = slice(i * chunk, (i + 1) * chunk)
        xcol = gather_cols(ext, half_cols, i, 0, chunk)
        xcol_ref[:, at] = xcol
        hidden = jnp.maximum(dot(et_ref[...], xcol), 0.0).astype(BF16)
        h1_ref[:, at] = hidden
        hidden = jnp.maximum(dot(wb_ref[...], hidden) + bias_ref[...], 0.0).astype(BF16)
        h2_ref[:, at] = hidden
        scatter_cols(oacc, dot(f_ref[...], hidden), half_cols, i, 0, chunk, True)
    output = jnp.concatenate(fold_ext(oacc, half_rows, half_cols, bands), axis=1) + chan2_ref[:, 2:3]
    second = output[16:] + 2.0
    t2_ref[...] = second
    scale_log = log_sigmoid(second)
    result = (mixed[16:] + output[:16]) * jnp.exp(scale_log)
    out2_ref[16:, :] = result
    valid = row_mask(16, 16, CH)
    per_pixel = jnp.where(valid, scale_log - 0.5 * (mixed[:16] * mixed[:16] + result * result), 0.0)
    mask2 = mask2_ref[...]
    loss_ref[...] = jnp.zeros_like(loss_ref)
    loss_ref[0:1, :] = jnp.sum(fold_lanes(per_pixel * mask2), axis=0, keepdims=True)
    loss_ref[1:2, :] = fold_lanes(mask2)
    loss_ref[2:3, :] = fold_lanes(mask_ref[...])


def part_out(slab_ref, first, size, index, bit, kept_ref, sent_ref):
    half = size // 2
    high = lax.rem(index // bit, 2)
    kept_ref[...] = slab_ref[pl.ds(pl.multiple_of(first + high * half, 8), half), :]
    sent_ref[...] = slab_ref[pl.ds(pl.multiple_of(first + (1 - high) * half, 8), half), :]


def gram(left, right_ref, pairs, acc_ref):
    for j in pairs:
        acc_ref[j, :, :] = acc_ref[j, :, :] + fold_lanes(left * right_ref[j : j + 1, :])


def couple_two_backward(
    dims,
    bit,
    index_ref,
    mask2_ref,
    y2_ref,
    out2_ref,
    t2_ref,
    xcol_ref,
    h1_ref,
    h2_ref,
    chan2_ref,
    m2t_ref,
    e_ref,
    wbt_ref,
    ft_ref,
    kept_ref,
    sent_ref,
    gkeep_ref,
    ext,
    gacc,
    gmix,
    bacc,
    ge,
    gf,
    acc,
    slab_ref,
):
    rows, cols, bands = dims
    weight = -mask2_ref[...]
    second = t2_ref[...]
    result = out2_ref[16:, :]
    g_result = -weight * result
    g_log = g_result * result + weight
    g_second = g_log * sigmoid_minus(second)
    g_half = g_result * jnp.exp(log_sigmoid(second))
    gmix[0:16, :] = -weight * out2_ref[0:16, :]
    gmix[16:32, :] = g_half
    valid = row_mask(16, 16, CH)
    g_out = jnp.concatenate([g_half, jnp.where(valid, g_second, 0.0)], axis=0)
    g_out = g_out.astype(BF16).astype(F32)
    out_sums = fold_lanes(g_out)
    fill_ext(ext, g_out, rows, cols, bands, jnp.zeros((32, 1), F32))
    gacc[...] = jnp.zeros_like(gacc)
    chunk = cols * LANES
    for i in range(rows):
        at = slice(i * chunk, (i + 1) * chunk)
        gcol = gather_cols(ext, cols, i, 0, chunk, True)
        hidden_two = h2_ref[:, at]
        hidden_one = h1_ref[:, at]
        g_pre = jnp.where(hidden_two > 0, dot(ft_ref[...], gcol), 0.0).astype(BF16)
        g_f = dot_nt(gcol, hidden_two)
        g_wb = dot_nt(g_pre, hidden_one)
        folded = fold_lanes(g_pre.astype(F32))
        g_pre = jnp.where(hidden_one > 0, dot(wbt_ref[...], g_pre), 0.0).astype(BF16)
        g_e = dot_nt(xcol_ref[:, at], g_pre)
        scatter_cols(gacc, dot(e_ref[...], g_pre), cols, i, 0, chunk)
        if i == 0:
            gf[...], ge[...], bacc[...] = g_f, g_e, folded
        else:
            gf[...] += g_f
            ge[...] += g_e
            bacc[...] += folded
        for block in range(HID // LANES):
            at = slice(block * HID, (block + 1) * HID)
            part = g_wb[:, block * LANES : (block + 1) * LANES]
            slab_ref[at, :] = part if i == 0 else slab_ref[at, :] + part
    slab_ref[TWO_B:TWO_ROWS, :] = jnp.zeros((TWO_ROWS - TWO_B, LANES), F32)
    put_rows(slab_ref, lambda block: TWO_B + block, ones_sum(bacc), 0, 1)
    for piece in range(18):
        put_rows(slab_ref, lambda block: TWO_F + block * 216 + piece * CH, gf, piece * 16, CH)
    put_rows(slab_ref, lambda block: TWO_E + block * 144, ge, 0, 144)
    gmix[0:16, :] += jnp.concatenate(fold_ext(gacc, rows, cols, bands), axis=1)
    pairs = [j for j in range(32) if j % 8 < 6]
    g_mixed = gmix[...]
    acc[...] = jnp.zeros_like(acc)
    gram(g_mixed, y2_ref, pairs, acc)
    stack = [(j, acc[j]) for j in pairs] + [(32, fold_lanes(g_mixed)), (33, out_sums)]
    slab_ref[TWO_SMALL : TWO_SMALL + 32, :] = lane_sums(stack, 32)
    part_out(slab_ref, 0, TWO_ROWS, index_ref[1], bit, kept_ref, sent_ref)
    valid_rows = [j for j in range(32) if j % 16 < CH]
    gkeep_ref[...] = mix(m2t_ref, gmix, 0, rows * chunk, valid_rows) * chan2_ref[:, 1:2]


def level_two_kernel(
    dims,
    bit,
    index_ref,
    b0,
    b1,
    b2,
    b3,
    chan1_ref,
    m1_ref,
    chan2_ref,
    m2_ref,
    m2t_ref,
    e_ref,
    et_ref,
    f_ref,
    ft_ref,
    wb_ref,
    wbt_ref,
    bias_ref,
    y1_ref,
    mix1_ref,
    mask_ref,
    mask2_ref,
    keep_ref,
    loss_ref,
    gkeep_ref,
    kept_ref,
    sent_ref,
    bufs,
    xs,
    y2,
    mix2,
    out2,
    t2,
    xcol,
    h1,
    h2,
    ext_in,
    oacc,
    ext_out,
    gacc,
    gmix,
    bacc,
    ge,
    gf,
    acc,
    slab,
):
    rows, cols, bands = dims
    half = (rows // 2, cols // 2, bands)
    unpack_kernel(
        dims, index_ref, b0, b1, b2, b3, chan1_ref, m1_ref, chan2_ref, m2_ref,
        y1_ref, mix1_ref, mask_ref, mask2_ref, keep_ref, y2, mix2, bufs, xs,
    )
    couple_two_forward(
        half, mix2, mask_ref, mask2_ref, chan2_ref, et_ref, wb_ref, f_ref, bias_ref,
        out2, t2, xcol, h1, h2, loss_ref, ext_in, oacc,
    )
    couple_two_backward(
        half, bit, index_ref, mask2_ref, y2, out2, t2, xcol, h1, h2, chan2_ref, m2t_ref, e_ref, wbt_ref, ft_ref,
        kept_ref, sent_ref, gkeep_ref, ext_out, gacc, gmix, bacc, ge, gf, acc, slab,
    )


def couple_one_forward(
    dims,
    chunk,
    mix1_ref,
    mask_ref,
    mask2_ref,
    keep_ref,
    gkeep_in_ref,
    chan1_ref,
    et_ref,
    wb_ref,
    f_ref,
    bias_ref,
    wp_ref,
    wpt_ref,
    pbias_ref,
    xcol_ref,
    h1_ref,
    h2_ref,
    res_ref,
    t_ref,
    gout_ref,
    gwp_ref,
    loss_ref,
    ext,
    oacc,
    kext,
    kcol,
    gkacc,
    drop,
):
    rows, cols, bands = dims
    iota = lax.broadcasted_iota(jnp.int32, (8, 1), 0)
    ones = jnp.where(iota == CH // 2, 1.0, 0.0)
    fill_ext(ext, mix1_ref[0:8, :] + ones, rows, cols, bands, ones)
    oacc[...] = jnp.zeros_like(oacc)

    @pl.loop(0, rows * cols * LANES // chunk)
    def _(step):
        row, col, at = place_of(step, chunk, cols)
        xcol = gather_cols(ext, cols, row, col, chunk)
        xcol_ref[:, at] = xcol
        hidden = jnp.maximum(dot(et_ref[...], xcol), 0.0).astype(BF16)
        h1_ref[:, at] = hidden
        hidden = jnp.maximum(dot(wb_ref[...], hidden) + bias_ref[...], 0.0).astype(BF16)
        h2_ref[:, at] = hidden
        scatter_cols(oacc, dot(f_ref[...], hidden), cols, row, col, chunk, True)

    line = cols * LANES
    valid = row_mask(8, 8, CH // 2)
    step_total = None
    half_rows, half_cols = rows // 2, cols // 2
    for s, piece in enumerate(fold_ext(oacc, rows, cols, bands)):
        at = slice(s * line, (s + 1) * line)
        output = piece + chan1_ref[:, 2:3]
        second = output[8:] + 2.0
        t_ref[:, at] = second
        scale_log = log_sigmoid(second)
        result = (mix1_ref[8:16, at] + output[:8]) * jnp.exp(scale_log)
        res_ref[:, at] = result
        part = fold_lanes(jnp.where(valid, scale_log, 0.0) * mask_ref[:, at])
        step_total = part if step_total is None else step_total + part
    for i in range(half_rows):
        for j in range(half_cols):
            at = slice((i * half_cols + j) * LANES, (i * half_cols + j + 1) * LANES)
            for p in range(4):
                start = ((2 * i + p // 2) * cols + 2 * j + p % 2) * LANES
                drop[p * 8 : p * 8 + 8, at] = res_ref[:, start : start + LANES]
    part_iota = lax.broadcasted_iota(jnp.int32, (32, 1), 0)
    part_ones = jnp.where(part_iota == CH // 2, 1.0, 0.0)
    fill_ext(kext, keep_ref[...] + part_ones, half_rows, half_cols, bands, part_ones)
    part_line = half_cols * LANES
    gkacc[...] = jnp.zeros_like(gkacc)
    weight = -mask2_ref[...]
    valid = row_mask(32, 8, CH // 2)
    prior_total = None
    for i in range(half_rows):
        at = slice(i * part_line, (i + 1) * part_line)
        columns = gather_cols(kext, half_cols, i, 0, part_line)
        kcol[...] = columns
        prior = dot(wp_ref[...], columns) + pbias_ref[...]
        mean, logs = prior[:32], prior[32:]
        inverse = jnp.exp(-logs)
        scaled = (drop[:, at] - mean) * inverse
        part = fold_lanes((-logs - 0.5 * scaled * scaled) * mask2_ref[:, at])
        prior_total = part if prior_total is None else prior_total + part
        g_mean = weight[:, at] * scaled * inverse
        g_logs = jnp.where(valid, weight[:, at] * (scaled * scaled - 1.0), 0.0)
        drop[:, at] = -g_mean
        g_prior = jnp.concatenate([g_mean, g_logs], axis=0).astype(BF16)
        g_wp = dot_nt(g_prior, kcol[...])
        if i == 0:
            gwp_ref[...] = g_wp
        else:
            gwp_ref[...] += g_wp
        scatter_cols(gkacc, dot(wpt_ref[...], g_prior), half_cols, i, 0, part_line)
    loss_ref[...] = jnp.zeros_like(loss_ref)
    loss_ref[0:1, :] = jnp.sum(step_total, axis=0, keepdims=True) + jnp.sum(prior_total, axis=0, keepdims=True)
    for i, piece in enumerate(fold_ext(gkacc, half_rows, half_cols, bands)):
        at = slice(i * part_line, (i + 1) * part_line)
        g_keep = piece + gkeep_in_ref[:, at]
        g_drop = drop[:, at]
        for j in range(half_cols):
            inner = slice(j * LANES, (j + 1) * LANES)
            for p in range(4):
                start = ((2 * i + p // 2) * cols + 2 * j + p % 2) * LANES
                gout_ref[0:8, start : start + LANES] = g_keep[p * 8 : p * 8 + 8, inner]
                gout_ref[8:16, start : start + LANES] = g_drop[p * 8 : p * 8 + 8, inner]


def put_rows(slab_ref, first, values, row, count):
    for block in range(HID // LANES):
        start = first(block)
        slab_ref[start : start + count, :] = values[row : row + count, block * LANES : (block + 1) * LANES]


def lane_sums(stack, width):
    lane = lax.broadcasted_iota(jnp.int32, (1, LANES), 1)
    total = jnp.zeros(stack[0][1].shape, F32)
    for j, value in stack:
        total = total + jnp.where(lane == j, jnp.sum(value, axis=1, keepdims=True), 0.0)
    return total


def ones_sum(value_ref):
    return lax.dot_general(
        jnp.ones((8, LANES), F32), value_ref[...], (((1,), (1,)), ((), ())), precision=HIGH, preferred_element_type=F32
    )


def one_backward_top(
    dims,
    chunk,
    bits,
    index_ref,
    mask_ref,
    res_ref,
    t_ref,
    gout_ref,
    ft_ref,
    gwp_ref,
    loss_one_ref,
    loss_two_ref,
    h1_ref,
    h2_ref,
    gpre_ref,
    kept_a,
    sent_a,
    kept_b,
    sent_b,
    ghalf_ref,
    gbc_ref,
    ext,
    gft,
    gf,
    bacc,
    slab_ref,
):
    rows, cols, bands = dims
    weight = -mask_ref[...]
    second = t_ref[...]
    result = res_ref[...]
    g_result = gout_ref[8:16, :]
    g_log = g_result * result + weight
    g_second = g_log * sigmoid_minus(second)
    g_half = g_result * jnp.exp(log_sigmoid(second))
    ghalf_ref[...] = g_half
    valid = row_mask(8, 8, CH // 2)
    g_out = jnp.concatenate([g_half, jnp.where(valid, g_second, 0.0)], axis=0)
    g_out = g_out.astype(BF16).astype(F32)
    gbc_ref[...] = fold_lanes(g_out)
    fill_ext(ext, g_out, rows, cols, bands, jnp.zeros((16, 1), F32))
    gft[...] = jnp.zeros_like(gft)
    slab_ref[...] = jnp.zeros_like(slab_ref)
    bacc[...] = jnp.zeros_like(bacc)

    @pl.loop(0, rows * cols * LANES // chunk)
    def _(step):
        row, col, at = place_of(step, chunk, cols)
        gcol = gather_cols(ext, cols, row, col, chunk, True)
        hidden_two = h2_ref[:, at]
        g_pre = jnp.where(hidden_two > 0, dot(ft_ref[...], gcol), 0.0).astype(BF16)
        gft[...] += dot_nt(hidden_two, gcol)
        gpre_ref[:, at] = g_pre
        g_wb = dot_nt(g_pre, h1_ref[:, at])
        for block in range(HID // LANES):
            slab_ref[block * HID : (block + 1) * HID, :] += g_wb[:, block * LANES : (block + 1) * LANES]
        bacc[...] += fold_lanes(g_pre.astype(F32))

    for first, count in ((0, LANES), (LANES, 16)):
        gf[first : first + count, :] = gft[:, first : first + count].T
    bias = ones_sum(bacc)
    put_rows(slab_ref, lambda block: ONE_B + block, bias, 0, 1)
    for piece in range(18):
        put_rows(slab_ref, lambda block: ONE_F + block * 112 + piece * 6, gf, piece * 8, 6)
    for block in range(3):
        width = min(LANES, 288 - block * LANES)
        slab_ref[ONE_P + block * 64 : ONE_P + block * 64 + 64, 0:width] = gwp_ref[
            :, block * LANES : block * LANES + width
        ]
    slab_ref[ONE_LOSS : ONE_LOSS + 1, :] = loss_one_ref[0:1, :] + loss_two_ref[0:1, :]
    slab_ref[ONE_LOSS + 1 : ONE_LOSS + 3, :] = loss_two_ref[1:3, :]
    part_out(slab_ref, 0, PART_A, index_ref[1], bits[0], kept_a, sent_a)
    part_out(slab_ref, PART_A, ONE_ROWS - PART_A, index_ref[1], bits[1], kept_b, sent_b)


def one_backward_bottom(
    dims,
    chunk,
    y1_ref,
    ghalf_ref,
    gbc_ref,
    gout_ref,
    e_ref,
    wbt_ref,
    xcol_ref,
    h1_ref,
    gpre_ref,
    slab_ref,
    gacc,
    gmix,
    ge,
    acc,
):
    rows, cols, bands = dims
    gacc[...] = jnp.zeros_like(gacc)
    ge[...] = jnp.zeros_like(ge)
    slab_ref[...] = jnp.zeros_like(slab_ref)

    @pl.loop(0, rows * cols * LANES // chunk)
    def _(step):
        row, col, at = place_of(step, chunk, cols)
        g_pre = jnp.where(h1_ref[:, at] > 0, dot(wbt_ref[...], gpre_ref[:, at]), 0.0).astype(BF16)
        ge[...] += dot_nt(xcol_ref[:, at], g_pre)
        scatter_cols(gacc, dot(e_ref[...], g_pre), cols, row, col, chunk)

    gmix[0:8, :] = gout_ref[0:8, :] + jnp.concatenate(fold_ext(gacc, rows, cols, bands), axis=1)
    gmix[8:16, :] = ghalf_ref[...]
    g_mixed = gmix[...]
    acc[...] = jnp.zeros_like(acc)
    gram(g_mixed, y1_ref, range(CH), acc)
    stack = [(j, acc[j]) for j in range(CH)] + [(16, fold_lanes(g_mixed)), (17, gbc_ref[...])]
    slab_ref[REST_SMALL : REST_SMALL + 16, :] = lane_sums(stack, CH)
    for tap in range(9):
        put_rows(slab_ref, lambda block: block * 56 + tap * 6, ge, tap * 8, 6)
    put_rows(slab_ref, lambda block: REST_A + block, ge, 6, 1)


def call(kernel, inputs, outputs, scratch, flops, aliases=None, far_in=(), far_out=()):
    whole = pl.BlockSpec(memory_space=pltpu.VMEM)
    smem = pl.BlockSpec(memory_space=pltpu.SMEM)
    far = pl.BlockSpec(memory_space=pl.ANY)
    traffic = sum(x.size * x.dtype.itemsize for x in list(inputs) + list(outputs))
    return pl.pallas_call(
        kernel,
        out_shape=outputs,
        in_specs=[
            far if k in far_in else smem if x.dtype == jnp.int32 and x.ndim == 1 else whole for k, x in enumerate(inputs)
        ],
        out_specs=[far if k in far_out else whole for k in range(len(outputs))],
        scratch_shapes=scratch,
        input_output_aliases=aliases or {},
        compiler_params=pltpu.CompilerParams(vmem_limit_bytes=VMEM_LIMIT),
        cost_estimate=pl.CostEstimate(flops=flops, bytes_accessed=traffic, transcendentals=0),
    )(*inputs)


def shape(dims, dtype=F32):
    return jax.ShapeDtypeStruct(tuple(dims), dtype)


def high_dot(left, right, contract=(1, 0)):
    return lax.dot_general(
        left, right, (((contract[0],), (contract[1],)), ((), ())), precision=HIGH, preferred_element_type=F32
    )


def iotas(height, width=LANES):
    return (
        lax.broadcasted_iota(jnp.int32, (height, width), 0),
        lax.broadcasted_iota(jnp.int32, (height, width), 1),
    )


def take_flat(flat_ref, start, length):
    row, offset = divmod(start, LANES)
    lane = lax.broadcasted_iota(jnp.int32, (1, LANES), 1)
    value = flat_ref[row : row + 1, :]
    if offset:
        value = pltpu.roll(value, LANES - offset, 1)
        if offset + length > LANES:
            after = pltpu.roll(flat_ref[row + 1 : row + 2, :], LANES - offset, 1)
            value = jnp.where(lane < LANES - offset, value, after)
    return jnp.where(lane < length, value, 0.0) if length < LANES else value


def put_flat(pieces, start, value, length):
    row, offset = divmod(start, LANES)
    lane = lax.broadcasted_iota(jnp.int32, (1, LANES), 1)
    if length < LANES:
        value = jnp.where(lane < length, value, 0.0)
    if offset:
        value = pltpu.roll(value, offset, 1)
    if offset + length > LANES:
        pieces.setdefault(row + 1, []).append(jnp.where(lane < offset, value, 0.0))
        value = jnp.where(lane >= offset, value, 0.0)
    pieces.setdefault(row, []).append(value)


def level_tables(flat_ref, level, lu):
    chans = CH * (level + 1)
    start = ONE_START - 4 * CH if level == 0 else TWO_START
    chan = [take_flat(flat_ref, start + k * chans, chans) for k in range(4)]
    first = start + 4 * chans + 2 * HID
    lu[...] = jnp.zeros_like(lu)
    for i in range(chans):
        lu[i : i + 1, :] = take_flat(flat_ref, first + i * chans, chans)
    row, lane = iotas(LANES)
    value = lu[...]
    inside = row < chans
    lower = jnp.where(row > lane, value, 0.0) + jnp.where((row == lane) & inside, 1.0, 0.0)
    upper = jnp.where(row < lane, value, 0.0) + jnp.where((row == lane) & inside, jnp.exp(chan[2]), 0.0)
    return chans, start, chan, lower, upper


def natural_row(level, row):
    height, half = (8, CH // 2) if level == 0 else (16, CH)
    return (row // height) * half + lax.rem(row, height), lax.rem(row, height) < half


def natural_keep(row):
    return 4 * lax.rem(row, 8) + row // 8, lax.rem(row, 8) < CH // 2


def pick(condition, value):
    return jnp.sum(jnp.where(condition, value, 0.0), axis=1, keepdims=True)


def prior_places():
    row, lane = iotas(64, 4 * CH)
    inner = lax.rem(row, 32)
    natural, valid = natural_keep(inner)
    return ((lane == natural + (row // 32) * 2 * CH) & valid).astype(F32).astype(BF16)


def prior_lanes(tap):
    row, lane = iotas(2 * CH)
    inner = lane - (tap * 32) % LANES
    natural = 4 * lax.rem(inner, 8) + inner // 8
    valid = (inner >= 0) & (inner < 32) & (lax.rem(inner, 8) < CH // 2)
    return ((row == natural) & valid).astype(F32).astype(BF16)


def prepare_level(level, flat_ref, entry_ref, middle_ref, exit_ref, outs, wide):
    e_ref, et_ref, f_ref, ft_ref, wb_ref, wbt_ref, bb_ref = outs
    chans = CH * (level + 1)
    start = 0 if level == 0 else TWO_START
    half, tall = chans // 2, 8 * (level + 1)
    first_in, first_out = (0, 0) if level == 0 else (CH // 2, CH)
    wide[...] = jnp.zeros_like(wide)
    for tap in range(9):
        wide[tap * tall : tap * tall + half, :] = entry_ref[tap, first_in : first_in + half, :]
    row, lane = iotas(LANES)
    for block in range(HID // LANES):
        at = slice(block * LANES, (block + 1) * LANES)
        value = take_flat(flat_ref, start + 4 * chans + block * LANES, LANES)
        for tap in range(3):
            part = value.astype(BF16).astype(F32)
            wide[tap * tall + half : tap * tall + half + 1, at] = part
            value = value - part
        value = take_flat(flat_ref, start + 4 * chans + HID + block * LANES, LANES)
        bb_ref[at, :] = pick(row == lane, value)
    count = 9 * tall
    padded = -(-count // LANES) * LANES
    e_ref[...] = wide[0:count, :].astype(BF16)
    et_ref[...] = wide[0:padded, :].T[:, 0:count].astype(BF16)
    wide[...] = jnp.zeros_like(wide)
    for tap in range(9):
        for side in range(2):
            first = (tap * 2 + side) * tall
            wide[first : first + half, :] = exit_ref[tap, first_out + side * half : first_out + (side + 1) * half, :]
    count = 18 * tall
    padded = -(-count // LANES) * LANES
    f_ref[...] = wide[0:count, :].astype(BF16)
    ft_ref[...] = wide[0:padded, :].T[:, 0:count].astype(BF16)
    wb_ref[...] = middle_ref[level].astype(BF16)
    wbt_ref[...] = middle_ref[level].T.astype(BF16)


def prepare_kernel(
    flat_ref,
    prior_far,
    entry_far,
    middle_far,
    exit_far,
    chan1_ref,
    m1_ref,
    chan2_ref,
    m2_ref,
    m2t_ref,
    wp_ref,
    wpt_ref,
    pbias_ref,
    *refs,
):
    outs_two, outs_one = refs[:7], refs[7:14]
    lu, wide, entry_ref, middle_ref, exit_ref, prior_ref, sems = refs[14:]
    copies = [
        pltpu.make_async_copy(middle_far.at[1], middle_ref.at[1], sems.at[0]),
        pltpu.make_async_copy(exit_far, exit_ref, sems.at[1]),
        pltpu.make_async_copy(entry_far, entry_ref, sems.at[2]),
        pltpu.make_async_copy(middle_far.at[0], middle_ref.at[0], sems.at[3]),
        pltpu.make_async_copy(prior_far, prior_ref, sems.at[4]),
    ]
    for copy in copies:
        copy.start()
    for level in range(2):
        chans, start, chan, lower, upper = level_tables(flat_ref, level, lu)
        product = high_dot(lower, upper)
        height = 16 * (level + 1)
        row, lane = iotas(height)
        natural, valid = natural_row(level, row)
        spread = ((lane == chans - 1 - natural) & valid).astype(F32)
        matrix = high_dot(spread, product)
        out_bias = pick((lane == natural) & valid, chan[3])
        if level == 0:
            m1_ref[...] = matrix
            shift, scale = pick(lane == row, chan[0]), pick((lane == row) & (row < CH), jnp.exp(chan[1]))
        else:
            source, target = iotas(LANES)
            place, used = natural_keep(target)
            matrix = high_dot(matrix, ((source == place) & used & (target < 32)).astype(F32))
            m2_ref[...] = matrix
            lu[...] = jnp.zeros_like(lu)
            lu[0:32, :] = matrix
            m2t_ref[...] = lu[...].T[0:32, :]
            place, used = natural_keep(row)
            shift = pick((lane == place) & used, chan[0])
            scale = pick((lane == place) & used, jnp.exp(chan[1]))
        chan_ref = chan1_ref if level == 0 else chan2_ref
        chan_ref[...] = (
            jnp.where(lane == 0, shift, 0.0) + jnp.where(lane == 1, scale, 0.0) + jnp.where(lane == 2, out_bias, 0.0)
        )
    copies[4].wait()
    places = prior_places()
    blocks = [None] * 3
    for tap in range(9):
        moved = dot_nt(places, prior_ref[tap].astype(BF16)).astype(BF16)
        part = dot(moved, prior_lanes(tap))
        block = tap * 32 // LANES
        blocks[block] = part if blocks[block] is None else blocks[block] + part
    lu[...] = jnp.zeros_like(lu)
    for block, value in enumerate(blocks):
        width = min(LANES, 288 - block * LANES)
        at = slice(block * LANES, block * LANES + width)
        wp_ref[:, at] = value[:, 0:width].astype(BF16)
        lu[0:64, :] = value
        wpt_ref[at, :] = lu[...].T[0:width, 0:64].astype(BF16)
    row, lane = iotas(64)
    natural, valid = natural_keep(lax.rem(row, 32))
    pbias_ref[...] = pick((lane == natural + (row // 32) * 2 * CH) & valid, take_flat(flat_ref, PRIOR_START, 4 * CH))
    for copy in copies[:3]:
        copy.wait()
    prepare_level(1, flat_ref, entry_ref, middle_ref, exit_ref, outs_two, wide)
    copies[3].wait()
    prepare_level(0, flat_ref, entry_ref, middle_ref, exit_ref, outs_one, wide)


def adamw(weight, grad, first, second):
    first_new = BETA_ONE * first + (1.0 - BETA_ONE) * grad
    second_new = BETA_TWO * second + (1.0 - BETA_TWO) * grad * grad
    first_hat = first_new * (1.0 / (1.0 - BETA_ONE**ADAM_STEP))
    second_hat = second_new * (1.0 / (1.0 - BETA_TWO**ADAM_STEP))
    updated = weight - LEARN_RATE * (first_hat / (jnp.sqrt(second_hat) + ADAM_EPS) + WEIGHT_DECAY * weight)
    return (updated, second_new)


def finish_kernel(
    two_ref,
    one_ref,
    rest_ref,
    extra_ref,
    flat_ref,
    flat_first,
    flat_second,
    *refs,
):
    far_in, refs = refs[:12], refs[12:]
    (loss_ref, norm_ref, flat_new, flat_grad, flat_moment), refs = refs[:5], refs[5:]
    far_out, refs = refs[:12], refs[12:]
    bias_ref, two, one, rest, lu = refs[:5]
    held, (in_sems, out_sems) = refs[5:21], refs[21:]
    weights, firsts, seconds, grads = held[0:4], held[4:8], held[8:12], held[12:16]
    entry_grad, _, exit_grad, prior_grad = grads
    jobs = [(1, 0), (1, 1), (2, None), (0, None), (3, None)]

    def part(ref, level):
        return ref if level is None else ref.at[level]

    def copies_in(k):
        group, level = jobs[k]
        return [
            pltpu.make_async_copy(part(far_in[3 * group + j], level), part(near[group], level), in_sems.at[k, j])
            for j, near in enumerate((weights, firsts, seconds))
        ]

    def copies_out(k):
        group, level = jobs[k]
        return [
            pltpu.make_async_copy(part(near[group], level), part(far_out[3 * group + j], level), out_sems.at[k, j])
            for j, near in enumerate((weights, grads, seconds))
        ]

    for k in range(len(jobs)):
        for copy in copies_in(k):
            copy.start()
    extra = extra_ref[...].astype(F32)
    count = jnp.sum(extra[6:9], keepdims=True)
    coef = -1.0 / (CH * count * math.log(2.0))
    factor = -coef
    two[...] = two_ref[WB_ROWS:, :].astype(F32) * factor
    one[...] = one_ref[WB_ROWS:, :].astype(F32) * factor
    rest[...] = rest_ref[...].astype(F32) * factor
    log_total = jnp.sum(extra[0:3], keepdims=True)
    count_two = jnp.sum(extra[3:6], keepdims=True)
    base = WB_ROWS
    squares = []
    pieces = {}
    consts = []
    for level in range(2):
        chans, start, chan, lower, upper = level_tables(flat_ref, level, lu)
        consts.append(jnp.sum(chan[1] + chan[2], keepdims=True))
        weight = coef * count if level == 0 else coef * count_two
        height = 16 * (level + 1)
        small = rest[REST_SMALL : REST_SMALL + 16, :] if level == 0 else two[TWO_SMALL - base : TWO_SMALL - base + 32, :]
        sum_lane = 16 * (level + 1)
        product = high_dot(lower, upper)
        row, lane = iotas(LANES, height)
        natural, valid = natural_row(level, lane)
        turned = high_dot(((row == chans - 1 - natural) & valid).astype(F32), small)
        row, lane = iotas(LANES)
        g_product = jnp.where(lane < sum_lane, turned, 0.0)
        if level == 1:
            place, used = natural_keep(row)
            g_product = high_dot(g_product, ((lane == place) & used & (row < 32)).astype(F32))
        else:
            g_product = jnp.where(lane < chans, g_product, 0.0)
        g_lower = high_dot(g_product, upper, (1, 1))
        g_upper = high_dot(lower.T, g_product)
        g_lu = jnp.where(row > lane, g_lower, 0.0) + jnp.where(row < lane, g_upper, 0.0)
        diagonal = jnp.sum(jnp.where(row == lane, g_upper, 0.0), axis=0, keepdims=True)
        shift = jnp.sum(turned[:, sum_lane : sum_lane + 1] * product, axis=0, keepdims=True)
        scale = jnp.sum(product * g_product, axis=0, keepdims=True)
        row, lane = iotas(height)
        natural, valid = natural_row(level, row)
        out_bias = jnp.where((lane == natural) & valid, small[:, sum_lane + 1 : sum_lane + 2], 0.0)
        put_flat(pieces, start, shift * jnp.exp(chan[1]), chans)
        put_flat(pieces, start + chans, scale + weight, chans)
        put_flat(pieces, start + 2 * chans, diagonal * jnp.exp(chan[2]) + weight, chans)
        put_flat(pieces, start + 3 * chans, jnp.sum(out_bias, axis=0, keepdims=True), chans)
        for i in range(chans):
            put_flat(pieces, start + 4 * chans + 2 * HID + i * chans, g_lu[i : i + 1, :], chans)
        for block in range(HID // LANES):
            if level == 0:
                value_a = rest[REST_A + block : REST_A + block + 1, :]
                value_b = one[ONE_B - base + block : ONE_B - base + block + 1, :]
            else:
                at = TWO_E - base + block * 144 + CH
                value_a = two[at : at + 1, :]
                value_b = two[TWO_B - base + block : TWO_B - base + block + 1, :]
            at = start + 4 * chans + block * LANES
            put_flat(pieces, at, value_a, LANES)
            put_flat(pieces, at + HID, value_b, LANES)
            bias_ref[2 * level : 2 * level + 1, block * LANES : (block + 1) * LANES] = value_a
            bias_ref[2 * level + 1 : 2 * level + 2, block * LANES : (block + 1) * LANES] = value_b
    row, lane = iotas(64)
    natural, valid = natural_keep(lax.rem(row, 32))
    column = one[ONE_P - base : ONE_P - base + 64, CH // 2 : CH // 2 + 1]
    prior_bias = jnp.where((lane == natural + (row // 32) * 2 * CH) & valid, column, 0.0)
    put_flat(pieces, PRIOR_START, jnp.sum(prior_bias, axis=0, keepdims=True), 4 * CH)
    for r in range(FLAT_ROWS):
        parts = pieces.get(r, [jnp.zeros((1, LANES), F32)])
        flat_grad[r : r + 1, :] = functools.reduce(jnp.add, parts)
    for tap in range(9):
        for block in range(HID // LANES):
            at = slice(block * LANES, (block + 1) * LANES)
            first = block * 56 + tap * 6
            entry_grad[tap, 0:6, at] = rest[first : first + 6, :]
            first = TWO_E - base + block * 144 + tap * 16
            entry_grad[tap, 6:18, at] = two[first : first + CH, :]
            first = ONE_F - base + block * 112 + tap * CH
            exit_grad[tap, 0:CH, at] = one[first : first + CH, :]
            first = TWO_F - base + block * 216 + tap * 2 * CH
            exit_grad[tap, CH : 3 * CH, at] = two[first : first + 2 * CH, :]
    places = prior_places()
    for tap in range(9):
        first = ONE_P + (tap * 32 // LANES) * 64
        moved = dot_nt(prior_lanes(tap), one_ref[first : first + 64, :]).astype(BF16)
        prior_grad[tap, :, :] = dot(moved, places) * factor
    for ref in (flat_grad, entry_grad, exit_grad, prior_grad):
        value = ref[...]
        squares.append(jnp.sum(value * value, keepdims=True).reshape(1, 1))
    for ref in (one_ref, two_ref):
        total = jnp.zeros((64, LANES), F32)
        for start in range(0, WB_ROWS, 64):
            value = ref[start : start + 64, :].astype(F32)
            total = total + value * value
        squares.append(jnp.sum(total, keepdims=True) * factor * factor)
    norm = jnp.sqrt(functools.reduce(jnp.add, squares))
    clip = jnp.minimum(1.0, CLIP_NORM / (norm + 1e-06))
    total = log_total + consts[0] * count + count_two * (consts[1] - 2 * CH * LOG_TWO_PI)
    loss_ref[...] = coef * total + 8.0
    norm_ref[...] = norm
    bias_ref[...] = bias_ref[...] * clip

    middle_factor = factor * clip
    value = flat_grad[...] * clip
    flat_grad[...] = value
    flat_new[...], flat_moment[...] = adamw(flat_ref[...], value, flat_first[...], flat_second[...])
    size = 64
    for k, (group, level) in enumerate(jobs):
        for copy in copies_in(k):
            copy.wait()
        weight, first, second, grad = weights[group], firsts[group], seconds[group], grads[group]
        if level is None:
            for tap in range(9):
                value = grad[tap] * clip
                grad[tap] = value
                weight[tap], second[tap] = adamw(weight[tap], value, first[tap], second[tap])
        else:
            slab = (one_ref, two_ref)[level]

            @pl.loop(0, HID // size)
            def _(j):
                rows = pl.ds(pl.multiple_of(j * size, size), size)
                for block in range(HID // LANES):
                    at = (level, rows, slice(block * LANES, (block + 1) * LANES))
                    value = slab[pl.ds(pl.multiple_of(block * HID + j * size, size), size), :].astype(F32) * middle_factor
                    grad[at] = value
                    weight[at], second[at] = adamw(weight[at], value, first[at], second[at])

        for copy in copies_out(k):
            copy.start()
    for k in range(len(jobs)):
        for copy in copies_out(k):
            copy.wait()


def on_device(
    pixels,
    valid_mask,
    vectors,
    vectors_first,
    vectors_second,
    entry_taps,
    entry_first,
    entry_second,
    middle,
    middle_first,
    middle_second,
    exit_taps,
    exit_first,
    exit_second,
    prior_taps,
    prior_first,
    prior_second,
):
    bands = lax.axis_size("rows")
    rows, cols = valid_mask.shape[0], valid_mask.shape[1]
    dims = (rows, cols, bands)
    size = rows * cols * LANES
    part = size // 4
    batches = lax.axis_size("batch")
    devices = batches * bands
    bits = [2**k for k in range((devices - 1).bit_length())]
    index = lax.axis_index("batch") * bands + lax.axis_index("rows")
    own = jnp.stack([lax.axis_index("rows"), index]).astype(jnp.int32)

    def trade(value, bit):
        return lax.ppermute(value, ("batch", "rows"), [(i, i ^ bit) for i in range(devices)])

    def in_hbm(value):
        return pltpu.with_memory_space_constraint(value, pltpu.HBM)

    def after(value, *done):
        return lax.optimization_barrier((value, *done))[0]

    piece_rows = (CH + 1) * rows * cols // bands
    pieces = call(
        functools.partial(pack_kernel, bands),
        (own, in_hbm(pixels.reshape(-1, LANES)), in_hbm(valid_mask.reshape(-1, LANES))),
        [shape((piece_rows, LANES), BF16)] * bands,
        [],
        1000,
    )
    bufs = [pieces[0]]
    for d in range(1, bands):
        bufs.append(lax.ppermute(pieces[d], "rows", [(i, i ^ d) for i in range(bands)]))

    def flat(value):
        return jnp.pad(value, (0, FLAT_ROWS * LANES - VEC)).reshape(FLAT_ROWS, LANES)

    vectors_flat = flat(vectors)

    def level_shapes(tall):
        return [
            shape((9 * tall, HID), BF16),
            shape((HID, 9 * tall), BF16),
            shape((18 * tall, HID), BF16),
            shape((HID, 18 * tall), BF16),
            shape((HID, HID), BF16),
            shape((HID, HID), BF16),
            shape((HID, 1)),
        ]

    prior_turned = jnp.swapaxes(prior_taps, 1, 2)
    (
        chan_one, m_one, chan_two, m_two, m_two_t, wp, wpt, prior_bias,
        e_two, e_two_t, f_two, f_two_t, wb_two, wb_two_t, bb_two,
        e_one, e_one_t, f_one, f_one_t, wb_one, wb_one_t, bb_one,
    ) = call(
        prepare_kernel,
        (after(vectors_flat, pieces[0]), in_hbm(prior_turned), in_hbm(entry_taps), in_hbm(middle), in_hbm(exit_taps)),
        [shape((16, LANES)), shape((16, LANES)), shape((32, LANES)), shape((32, LANES)), shape((32, LANES))]
        + [shape((64, 288), BF16), shape((288, 64), BF16), shape((64, 1))]
        + level_shapes(16)
        + level_shapes(8),
        [
            pltpu.VMEM((LANES, LANES), F32),
            pltpu.VMEM((384, HID), F32),
            pltpu.VMEM(entry_taps.shape, F32),
            pltpu.VMEM(middle.shape, F32),
            pltpu.VMEM(exit_taps.shape, F32),
            pltpu.VMEM(prior_turned.shape, F32),
            pltpu.SemaphoreType.DMA((5,)),
        ],
        10**9,
        far_in=(1, 2, 3, 4),
    )


    ext_lanes = (rows // 2 + 2) * (cols // 2 + 2) * LANES
    first_bit, second_bit, third_bit, fourth_bit = bits[0], bits[2], bits[1], bits[3]
    half_two = shape((TWO_ROWS // 2, LANES))
    (y1, mixed_one, mask, mask2, keep, loss_two, gkeep_two, kept_two, sent_two) = call(
        functools.partial(level_two_kernel, dims, second_bit),
        (
            own, *bufs, chan_one, m_one, chan_two, m_two, m_two_t,
            e_two, e_two_t, f_two, f_two_t, wb_two, wb_two_t, bb_two,
        ),
        [
            shape((16, size)),
            shape((16, size)),
            shape((1, size)),
            shape((1, part)),
            shape((32, part)),
            shape((8, LANES)),
            shape((32, part)),
        ]
        + [half_two] * 2,
        [
            pltpu.VMEM((bands, piece_rows, LANES), F32),
            pltpu.VMEM((16, size), F32),
            pltpu.VMEM((32, part), F32),
            pltpu.VMEM((32, part), F32),
            pltpu.VMEM((32, part), F32),
            pltpu.VMEM((16, part), F32),
            pltpu.VMEM((144, part), BF16),
            pltpu.VMEM((HID, part), BF16),
            pltpu.VMEM((HID, part), BF16),
            pltpu.VMEM((16, ext_lanes), F32),
            pltpu.VMEM((32, ext_lanes), F32),
            pltpu.VMEM((32, ext_lanes), F32),
            pltpu.VMEM((16, ext_lanes), F32),
            pltpu.VMEM((32, part), F32),
            pltpu.VMEM((HID, LANES), F32),
            pltpu.VMEM((144, HID), F32),
            pltpu.VMEM((288, HID), F32),
            pltpu.VMEM((32, 32, LANES), F32),
            pltpu.VMEM((TWO_ROWS, LANES), F32),
        ],
        6 * HID * part * (144 + HID + 288),
    )
    whole_lanes = (rows + 2) * (cols + 2) * LANES
    chunk = min(2048, size)
    fwd_in = (
        mixed_one,
        mask,
        mask2,
        keep,
        gkeep_two,
        chan_one,
        e_one_t,
        wb_one,
        f_one,
        bb_one,
        wp,
        wpt,
        prior_bias,
    )
    fwd_out = [
        shape((72, size), BF16),
        shape((HID, size), BF16),
        shape((HID, size), BF16),
        shape((8, size)),
        shape((8, size)),
        shape((16, size)),
        shape((64, 288)),
        shape((8, LANES)),
    ]
    (xcol_one, h1_one, h2_one, res_one, t_one, gout_one, gwp, loss_one) = call(
        functools.partial(couple_one_forward, dims, chunk),
        fwd_in,
        fwd_out,
        [
            pltpu.VMEM((8, whole_lanes), F32),
            pltpu.VMEM((16, whole_lanes), F32),
            pltpu.VMEM((32, ext_lanes), F32),
            pltpu.VMEM((288, cols // 2 * LANES), BF16),
            pltpu.VMEM((32, ext_lanes), F32),
            pltpu.VMEM((32, part), F32),
        ],
        2 * HID * size * (72 + HID + 144),
    )
    top_in = (own, mask, res_one, t_one, gout_one, f_one_t, gwp, loss_one, loss_two, h1_one, h2_one)
    half_a, half_b = shape((PART_A // 2, LANES)), shape(((ONE_ROWS - PART_A) // 2, LANES))
    top_out = [shape((HID, size), BF16), half_a, half_a, half_b, half_b, shape((8, size)), shape((16, LANES))]
    (gpre, kept_a, sent_a, kept_b, sent_b, ghalf, gbc) = call(
        functools.partial(one_backward_top, dims, chunk // 2, (second_bit, third_bit)),
        top_in,
        top_out,
        [
            pltpu.VMEM((16, whole_lanes), F32),
            pltpu.VMEM((HID, 144), F32),
            pltpu.VMEM((144, HID), F32),
            pltpu.VMEM((HID, LANES), F32),
            pltpu.VMEM((ONE_ROWS, LANES), F32),
        ],
        2 * HID * size * (144 + HID + 144),
        aliases={10: 0},
    )

    def halve(parts, bit, *beside):
        high = (index // bit) % 2
        halves = [x.shape[0] // 2 for x in parts]
        sent = [lax.dynamic_slice_in_dim(x, (1 - high) * h, h, 0) for x, h in zip(parts, halves)]
        kept = [lax.dynamic_slice_in_dim(x, high * h, h, 0) for x, h in zip(parts, halves)]
        got = after(trade(jnp.concatenate(sent) if len(sent) > 1 else sent[0], bit), *beside)
        results, first = [], 0
        for x, h in zip(kept, halves):
            results.append(x + got[first : first + h])
            first += h
        return results

    def exchange(parts, near_parts, far_parts, near, far_bit):
        code = 2 * ((index // near) % 2) + (index // far_bit) % 2
        sizes = [x.shape[0] // 4 for x in parts]

        def pieces_for(partner):
            return [lax.dynamic_slice_in_dim(x, (code ^ partner) * h, h, 0) for x, h in zip(parts, sizes)]

        totals = pieces_for(0)
        others = []
        for partner, bit, more in ((2, near, near_parts), (1, far_bit, far_parts), (3, near | far_bit, [])):
            high = (index // bit) % 2
            halves = [x.shape[0] // 2 for x in more]
            sent = pieces_for(partner) + [
                lax.dynamic_slice_in_dim(x, (1 - high) * h, h, 0) for x, h in zip(more, halves)
            ]
            got = trade(jnp.concatenate(sent) if len(sent) > 1 else sent[0], bit)
            first = 0
            for k, h in enumerate(sizes):
                totals[k] = totals[k] + got[first : first + h]
                first += h
            for x, h in zip(more, halves):
                others.append(lax.dynamic_slice_in_dim(x, high * h, h, 0) + got[first : first + h])
                first += h
        return totals + others

    total_two = kept_two + after(trade(sent_two, second_bit), gbc)
    low_in = (y1, ghalf, after(gbc, total_two), gout_one, e_one, wb_one_t, xcol_one, h1_one, gpre)
    (slab_rest,) = call(
        functools.partial(one_backward_bottom, dims, chunk),
        low_in,
        [shape((REST_ROWS, LANES))],
        [
            pltpu.VMEM((8, whole_lanes), F32),
            pltpu.VMEM((16, size), F32),
            pltpu.VMEM((72, HID), F32),
            pltpu.VMEM((CH, 16, LANES), F32),
        ],
        2 * HID * size * (72 + HID + 72),
    )

    total_a = kept_a + after(trade(sent_a, second_bit), slab_rest)
    total_b = kept_b + after(trade(sent_b, third_bit), slab_rest)
    (total_two,) = halve([total_two], fourth_bit, slab_rest)
    far = bits[3:]
    total_two, total_a, total_b, total_rest = halve(
        [total_two, total_a, total_b, after(slab_rest, total_two)], first_bit
    )
    total_rest, total_a, total_two, total_b = exchange(
        [total_rest], [total_a, total_two], [total_b], third_bit, second_bit
    )
    total_a, total_b, total_rest, total_two = exchange(
        [total_a, total_b, total_rest], [], [total_two], far[0], far[1]
    )
    shards = [total_two, total_a, total_b, total_rest]
    for bit in far[2:]:
        shards = halve(shards, bit)
    orders = [
        [second_bit, fourth_bit, first_bit, third_bit] + far[1:],
        [second_bit, first_bit, third_bit] + far,
        [third_bit, first_bit, second_bit] + far,
        [first_bit, third_bit, second_bit] + far,
    ]
    loss_part = shards[2]
    owner, loss_row = divmod(ONE_LOSS - PART_A, loss_part.shape[0])
    extra = []
    for row in range(3):
        value = loss_part[loss_row + row]
        for _ in range(3):
            high = lax.reduce_precision(value, 8, 7)
            extra.append(high)
            value = value - high
    extra = jnp.pad(jnp.stack(extra), ((0, 7), (0, 0)))
    spread = [shards[0].astype(BF16), jnp.concatenate(shards[1:] + [extra]).astype(BF16)]
    near = [[third_bit, second_bit, first_bit], [second_bit, third_bit, first_bit]]
    backs = [far[::-1] + near[0], far[::-1] + near[1]]

    def double(values, bit):
        low = (index // bit) % 2 == 0
        joined = jnp.concatenate(values) if len(values) > 1 else values[0]
        other = trade(joined, bit)
        results, first = [], 0
        for value in values:
            got = other[first : first + value.shape[0]]
            first += value.shape[0]
            results.append(jnp.where(low, jnp.concatenate([value, got]), jnp.concatenate([got, value])))
        return results

    for bit in far[:1:-1]:
        spread = double(spread, bit)
    near_low, far_low = (index // far[0]) % 2 == 0, (index // far[1]) % 2 == 0
    sizes = [value.shape[0] for value in spread]
    joined = jnp.concatenate(spread)
    from_far, from_near, from_both = (trade(joined, bit) for bit in (far[1], far[0], far[0] | far[1]))

    def ordered(low, one, other):
        return jnp.where(low, jnp.concatenate([one, other]), jnp.concatenate([other, one]))

    quads = []
    for first, size_of in ((0, sizes[0]), (sizes[0], sizes[1])):
        own_part, far_part, near_part, both_part = (
            x[first : first + size_of] for x in (joined, from_far, from_near, from_both)
        )
        quads.append(
            ordered(near_low, ordered(far_low, own_part, far_part), ordered(far_low, near_part, both_part))
        )
    spread = quads
    for k in range(3):
        spread = [double([value], order[k])[0] for value, order in zip(spread, near)]
    count_bits = len(bits)
    spread = [value.reshape((2,) * count_bits + (-1, LANES)) for value in spread]

    def reorder(value, back, order):
        axes = [count_bits - 1 - back.index(bit) for bit in order]
        return value.transpose(axes + [count_bits, count_bits + 1]).reshape(-1, LANES)

    totals = []
    first = 0
    for k, (shard, order) in enumerate(zip(shards, orders)):
        first = 0 if k < 2 else first
        side = 0 if k < 1 else 1
        totals.append(reorder(spread[side][..., first : first + shard.shape[0], :], backs[side], order))
        first += shard.shape[0]
    place = [0] * count_bits
    for k, bit in enumerate(orders[2]):
        place[count_bits - 1 - backs[1].index(bit)] = (owner >> (count_bits - 1 - k)) & 1
    extra = spread[1][tuple(place)][first:]
    totals = [totals[0], jnp.concatenate(totals[1:3]), totals[3]]
    taps = [
        (entry_taps, entry_first, entry_second),
        (middle, middle_first, middle_second),
        (exit_taps, exit_first, exit_second),
        (prior_turned, jnp.swapaxes(prior_first, 1, 2), jnp.swapaxes(prior_second, 1, 2)),
    ]
    flats = (vectors_flat, flat(vectors_first), flat(vectors_second))
    outs = [shape((1, 1)), shape((1, 1))] + [shape((FLAT_ROWS, LANES))] * 3
    for group in taps:
        outs += [shape(group[0].shape)] * 3
    outs.append(shape((4, HID)))
    results = call(
        finish_kernel,
        (*totals, extra, *flats, *[in_hbm(x) for group in taps for x in group]),
        outs,
        [
            pltpu.VMEM((TWO_ROWS - WB_ROWS, LANES), F32),
            pltpu.VMEM((ONE_ROWS - WB_ROWS, LANES), F32),
            pltpu.VMEM((REST_ROWS, LANES), F32),
            pltpu.VMEM((LANES, LANES), F32),
        ]
        + [pltpu.VMEM(group[0].shape, F32) for _ in range(4) for group in taps]
        + [pltpu.SemaphoreType.DMA((5, 3))] * 2,
        10**8,
        far_in=range(7, 19),
        far_out=range(5, 17),
    )
    results = list(results)
    for k in range(2):
        results[k] = results[k].reshape(())
    for k in range(2, 5):
        results[k] = results[k].reshape(-1)[:VEC]
    for k in range(14, 17):
        results[k] = jnp.swapaxes(results[k], 1, 2)
    return tuple(results)


def solution(mesh):
    replicated = (P(),) * 15
    return jax.shard_map(
        on_device,
        mesh=mesh,
        in_specs=(P(None, "rows", None, "batch"), P("rows", None, "batch")) + replicated,
        out_specs=(P(),) * 18,
        check_vma=False,
    )
```

```python
import functools
import math

import jax
import jax.numpy as jnp
from jax import lax
from jax.experimental import pallas as pl
from jax.experimental.pallas import tpu as pltpu
from jax.sharding import PartitionSpec as P

HID = 512
CH = 12

F32 = jnp.float32
BF16 = jnp.bfloat16
HIGH = lax.Precision.HIGHEST
LOG_TWO_PI = math.log(2.0 * math.pi)
LEARN_RATE = 0.05
BETA_ONE = 0.9
BETA_TWO = 0.999
ADAM_EPS = 1e-08
WEIGHT_DECAY = 0.01
CLIP_NORM = 0.01
ADAM_STEP = 10
LANES = 128
VMEM_LIMIT = 20 * 2**20
ONE_START = 4 * CH
TWO_START = 4 * CH + 2 * HID + CH * CH
PRIOR_START = TWO_START + 8 * CH + 2 * HID + 4 * CH * CH
VEC = PRIOR_START + 4 * CH
FLAT_ROWS = -(-VEC // (8 * LANES)) * 8
WB_ROWS = 4 * HID
TWO_F, TWO_E = WB_ROWS, WB_ROWS + 4 * 216
TWO_B = TWO_E + 4 * 144
TWO_ROWS = 3584
ONE_F = WB_ROWS
ONE_P = ONE_F + 4 * 112
ONE_B = ONE_P + 3 * 64
ONE_LOSS = ONE_B + 8
ONE_ROWS = 2816
PART_A = 768
REST_A = 4 * 56
REST_SMALL = REST_A + 8
REST_ROWS = 256


def dot(left, right):
    return lax.dot_general(left, right, (((1,), (0,)), ((), ())), preferred_element_type=F32)


def dot_nt(left, right):
    return lax.dot_general(left, right, (((1,), (1,)), ((), ())), preferred_element_type=F32)


def lane_band(bands, height=1):
    return lax.broadcasted_iota(jnp.int32, (height, LANES), 1) // (LANES // bands)


def pack_kernel(bands, index_ref, pixels_ref, mask_ref, *out_refs):
    own = index_ref[0]
    width = LANES // bands
    rows = pixels_ref.shape[0] // bands
    extra = mask_ref.shape[0] // bands
    band = lane_band(bands)
    parts = [pixels_ref[pl.ds(e, rows, stride=bands), :].astype(F32) for e in range(bands)]
    masks = [mask_ref[pl.ds(e, extra, stride=bands), :].astype(F32) for e in range(bands)]
    for d, out_ref in enumerate(out_refs):
        target = own ^ d
        for source, first, size in ((parts, 0, rows), (masks, rows, extra)):
            total = jnp.zeros((size, LANES), F32)
            for e in range(bands):
                shift = lax.rem(e - target + bands, bands) * width
                total = jnp.where(band == e, pltpu.roll(source[e], shift, 1), total)
            out_ref[first : first + size, :] = total.astype(BF16)


def fill_ext(ext_ref, field, rows, cols, bands, pattern):
    width = LANES // bands
    band = lane_band(bands)
    stride = (cols + 2) * LANES
    height = ext_ref.shape[0]
    pads = jnp.broadcast_to(pattern, (height, LANES))
    for block in range(ext_ref.shape[1] // LANES):
        ext_ref[:, block * LANES : (block + 1) * LANES] = pads
    for row in range(rows):
        start = (row + 1) * stride + LANES
        ext_ref[:, start : start + cols * LANES] = field[:, row * cols * LANES : (row + 1) * cols * LANES]
    last = (rows - 1) * cols * LANES
    for col in range(cols):
        above = pltpu.roll(field[:, last + col * LANES : last + (col + 1) * LANES], width, 1)
        start = LANES + col * LANES
        ext_ref[:, start : start + LANES] = jnp.where(band >= 1, above, pads)
        below = pltpu.roll(field[:, col * LANES : (col + 1) * LANES], LANES - width, 1)
        start = (rows + 1) * stride + LANES + col * LANES
        ext_ref[:, start : start + LANES] = jnp.where(band < bands - 1, below, pads)


def fold_ext(ext_ref, rows, cols, bands):
    width = LANES // bands
    band = lane_band(bands)
    stride = (cols + 2) * LANES
    pieces = []
    for row in range(rows):
        start = (row + 1) * stride + LANES
        piece = ext_ref[:, start : start + cols * LANES]
        if row == 0:
            blocks = []
            for col in range(cols):
                start = (rows + 1) * stride + LANES + col * LANES
                moved = pltpu.roll(ext_ref[:, start : start + LANES], width, 1)
                blocks.append(jnp.where(band >= 1, moved, 0.0))
            piece = piece + jnp.concatenate(blocks, axis=1)
        if row == rows - 1:
            blocks = []
            for col in range(cols):
                start = LANES + col * LANES
                moved = pltpu.roll(ext_ref[:, start : start + LANES], LANES - width, 1)
                blocks.append(jnp.where(band < bands - 1, moved, 0.0))
            piece = piece + jnp.concatenate(blocks, axis=1)
        pieces.append(piece)
    return pieces


def window(cols, row, first_col, tap, turned=False):
    dy, dx = tap // 3, tap % 3
    if turned:
        dy, dx = 2 - dy, 2 - dx
    return ((row + dy) * (cols + 2) + first_col + dx) * LANES


def place_of(step, chunk, cols):
    per_row = cols * LANES // chunk
    return step // per_row, lax.rem(step, per_row) * (chunk // LANES), pl.ds(pl.multiple_of(step * chunk, chunk), chunk)


def gather_cols(ext_ref, cols, row, first_col, size, turned=False):
    starts = [window(cols, row, first_col, tap, turned) for tap in range(9)]
    starts = [s if isinstance(s, int) else pl.multiple_of(s, LANES) for s in starts]
    return jnp.concatenate([ext_ref[:, pl.ds(s, size)] for s in starts], axis=0).astype(BF16)


def scatter_cols(ext_ref, values, cols, row, first_col, size, turned=False):
    height = ext_ref.shape[0]
    for tap in range(9):
        start = window(cols, row, first_col, tap, turned)
        if not isinstance(start, int):
            start = pl.multiple_of(start, LANES)
        at = pl.ds(start, size)
        ext_ref[:, at] = ext_ref[:, at] + values[tap * height : (tap + 1) * height]


def mix(matrix_ref, field_ref, start, size, pairs):
    total = None
    for j in pairs:
        term = matrix_ref[:, j : j + 1] * field_ref[j : j + 1, start : start + size]
        total = term if total is None else total + term
    return total


def log_sigmoid(value):
    return jnp.minimum(value, 0.0) - jnp.log1p(jnp.exp(-jnp.abs(value)))


def sigmoid_minus(value):
    power = jnp.exp(-jnp.abs(value))
    return jnp.where(value >= 0.0, power, 1.0) / (1.0 + power)


def row_mask(height, period, valid):
    return lax.rem(lax.broadcasted_iota(jnp.int32, (height, 1), 0), period) < valid


def fold_lanes(value):
    total = value[:, :LANES]
    for start in range(LANES, value.shape[1], LANES):
        total = total + value[:, start : start + LANES]
    return total


def unpack_kernel(
    dims,
    index_ref,
    b0,
    b1,
    b2,
    b3,
    chan1_ref,
    m1_ref,
    chan2_ref,
    m2_ref,
    y1_ref,
    mix1_ref,
    mask_ref,
    mask2_ref,
    keep_ref,
    y2_ref,
    mix2_ref,
    bufs,
    xs,
):
    rows, cols, bands = dims
    own = index_ref[0]
    width = LANES // bands
    band = lane_band(bands)
    groups = cols // bands
    for d, ref in enumerate((b0, b1, b2, b3)):
        bufs[d, :, :] = ref[...].astype(F32)
    xs[...] = jnp.zeros_like(xs)
    for s in range(rows):
        for a in range(groups):
            loads = [bufs[d, pl.ds(s * groups + a, CH + 1, stride=rows * groups), :] for d in range(bands)]
            for e in range(bands):
                total = jnp.zeros((CH + 1, LANES), F32)
                for d in range(bands):
                    origin = own ^ d
                    shift = lax.rem(origin - e + bands, bands) * width
                    total = jnp.where(band == origin, pltpu.roll(loads[d], shift, 1), total)
                start = (s * cols + bands * a + e) * LANES
                xs[0 : CH + 1, start : start + LANES] = total
    line = cols * LANES
    for s in range(rows):
        at = slice(s * line, (s + 1) * line)
        mask_ref[:, at] = xs[CH : CH + 1, at]
        raw = xs[:, at]
        source = (raw + 0.5) / 256.0 - 0.5
        y1_ref[:, at] = (source + chan1_ref[:, 0:1]) * chan1_ref[:, 1:2]
    for s in range(rows):
        at = slice(s * line, (s + 1) * line)
        mix1_ref[:, at] = mix(m1_ref, y1_ref, s * line, line, range(CH))
    half_rows, half_cols = rows // 2, cols // 2
    for i in range(half_rows):
        for j in range(half_cols):
            at = slice((i * half_cols + j) * LANES, (i * half_cols + j + 1) * LANES)
            masks = None
            for p in range(4):
                di, dj = p // 2, p % 2
                start = ((2 * i + di) * cols + 2 * j + dj) * LANES
                keep_ref[p * 8 : p * 8 + 8, at] = mix1_ref[0:8, start : start + LANES]
                block = mask_ref[:, start : start + LANES]
                masks = block if masks is None else jnp.minimum(masks, block)
            mask2_ref[:, at] = masks
    size = half_rows * half_cols * LANES
    y2_ref[...] = (keep_ref[...] + chan2_ref[:, 0:1]) * chan2_ref[:, 1:2]
    pairs = [j for j in range(32) if j % 8 < 6]
    mix2_ref[...] = mix(m2_ref, y2_ref, 0, size, pairs)


def couple_two_forward(
    dims,
    mix2_ref,
    mask_ref,
    mask2_ref,
    chan2_ref,
    et_ref,
    wb_ref,
    f_ref,
    bias_ref,
    out2_ref,
    t2_ref,
    xcol_ref,
    h1_ref,
    h2_ref,
    loss_ref,
    ext,
    oacc,
):
    half_rows, half_cols, bands = dims
    mixed = mix2_ref[...]
    out2_ref[0:16, :] = mixed[:16]
    iota = lax.broadcasted_iota(jnp.int32, (16, 1), 0)
    ones = jnp.where(iota == CH, 1.0, 0.0)
    fill_ext(ext, mixed[:16] + ones, half_rows, half_cols, bands, ones)
    oacc[...] = jnp.zeros_like(oacc)
    chunk = half_cols * LANES
    for i in range(half_rows):
        at = slice(i * chunk, (i + 1) * chunk)
        xcol = gather_cols(ext, half_cols, i, 0, chunk)
        xcol_ref[:, at] = xcol
        hidden = jnp.maximum(dot(et_ref[...], xcol).astype(BF16), jnp.zeros((), BF16))
        h1_ref[:, at] = hidden
        hidden = jnp.maximum((dot(wb_ref[...], hidden) + bias_ref[...]).astype(BF16), jnp.zeros((), BF16))
        h2_ref[:, at] = hidden
        scatter_cols(oacc, dot(f_ref[...], hidden), half_cols, i, 0, chunk, True)
    output = jnp.concatenate(fold_ext(oacc, half_rows, half_cols, bands), axis=1) + chan2_ref[:, 2:3]
    second = output[16:] + 2.0
    t2_ref[...] = second
    scale_log = log_sigmoid(second)
    result = (mixed[16:] + output[:16]) * jnp.exp(scale_log)
    out2_ref[16:, :] = result
    valid = row_mask(16, 16, CH)
    per_pixel = jnp.where(valid, scale_log - 0.5 * (mixed[:16] * mixed[:16] + result * result), 0.0)
    mask2 = mask2_ref[...]
    loss_ref[...] = jnp.zeros_like(loss_ref)
    loss_ref[0:1, :] = jnp.sum(fold_lanes(per_pixel * mask2), axis=0, keepdims=True)
    loss_ref[1:2, :] = fold_lanes(mask2)
    loss_ref[2:3, :] = fold_lanes(mask_ref[...])


def part_out(slab_ref, first, size, index, bit, kept_ref, sent_ref):
    half = size // 2
    high = lax.rem(index // bit, 2)
    kept_ref[...] = slab_ref[pl.ds(pl.multiple_of(first + high * half, 8), half), :]
    sent_ref[...] = slab_ref[pl.ds(pl.multiple_of(first + (1 - high) * half, 8), half), :]


def gram(left, right_ref, pairs, acc_ref):
    for j in pairs:
        acc_ref[j, :, :] = acc_ref[j, :, :] + fold_lanes(left * right_ref[j : j + 1, :])


def couple_two_backward(
    dims,
    bit,
    index_ref,
    mask2_ref,
    y2_ref,
    out2_ref,
    t2_ref,
    xcol_ref,
    h1_ref,
    h2_ref,
    chan2_ref,
    m2t_ref,
    e_ref,
    wbt_ref,
    ft_ref,
    kept_ref,
    sent_ref,
    small_ref,
    gkeep_ref,
    ext,
    gacc,
    gmix,
    bacc,
    ge,
    gf,
    acc,
    slab_ref,
):
    rows, cols, bands = dims
    weight = -mask2_ref[...]
    second = t2_ref[...]
    result = out2_ref[16:, :]
    g_result = -weight * result
    g_log = g_result * result + weight
    g_second = g_log * sigmoid_minus(second)
    g_half = g_result * jnp.exp(log_sigmoid(second))
    gmix[0:16, :] = -weight * out2_ref[0:16, :]
    gmix[16:32, :] = g_half
    valid = row_mask(16, 16, CH)
    g_out = jnp.concatenate([g_half, jnp.where(valid, g_second, 0.0)], axis=0)
    g_out = g_out.astype(BF16).astype(F32)
    out_sums = fold_lanes(g_out)
    fill_ext(ext, g_out, rows, cols, bands, jnp.zeros((32, 1), F32))
    gacc[...] = jnp.zeros_like(gacc)
    chunk = cols * LANES
    for i in range(rows):
        at = slice(i * chunk, (i + 1) * chunk)
        gcol = gather_cols(ext, cols, i, 0, chunk, True)
        hidden_two = h2_ref[:, at]
        hidden_one = h1_ref[:, at]
        g_pre = jnp.where(hidden_two > 0, dot(ft_ref[...], gcol).astype(BF16), jnp.zeros((), BF16))
        g_f = dot_nt(gcol, hidden_two)
        g_wb = dot_nt(g_pre, hidden_one)
        folded = fold_lanes(g_pre.astype(F32))
        g_pre = jnp.where(hidden_one > 0, dot(wbt_ref[...], g_pre).astype(BF16), jnp.zeros((), BF16))
        g_e = dot_nt(xcol_ref[:, at], g_pre)
        scatter_cols(gacc, dot(e_ref[...], g_pre), cols, i, 0, chunk)
        if i == 0:
            gf[...], ge[...], bacc[...] = g_f, g_e, folded
        else:
            gf[...] += g_f
            ge[...] += g_e
            bacc[...] += folded
        for block in range(HID // LANES):
            at = slice(block * HID, (block + 1) * HID)
            part = g_wb[:, block * LANES : (block + 1) * LANES]
            slab_ref[at, :] = part if i == 0 else slab_ref[at, :] + part
    slab_ref[TWO_B:TWO_ROWS, :] = jnp.zeros((TWO_ROWS - TWO_B, LANES), F32)
    put_rows(slab_ref, lambda block: TWO_B + block, ones_sum(bacc), 0, 1)
    for piece in range(18):
        put_rows(slab_ref, lambda block: TWO_F + block * 216 + piece * CH, gf, piece * 16, CH)
    put_rows(slab_ref, lambda block: TWO_E + block * 144, ge, 0, 144)
    gmix[0:16, :] += jnp.concatenate(fold_ext(gacc, rows, cols, bands), axis=1)
    pairs = [j for j in range(32) if j % 8 < 6]
    g_mixed = gmix[...]
    acc[...] = jnp.zeros_like(acc)
    gram(g_mixed, y2_ref, pairs, acc)
    stack = [(j, acc[j]) for j in pairs] + [(32, fold_lanes(g_mixed)), (33, out_sums)]
    small_ref[...] = lane_sums(stack, 32)
    part_out(slab_ref, 0, TWO_ROWS, index_ref[1], bit, kept_ref, sent_ref)
    valid_rows = [j for j in range(32) if j % 16 < CH]
    gkeep_ref[...] = mix(m2t_ref, gmix, 0, rows * chunk, valid_rows) * chan2_ref[:, 1:2]


def level_two_kernel(
    dims,
    bit,
    index_ref,
    b0,
    b1,
    b2,
    b3,
    chan1_ref,
    m1_ref,
    chan2_ref,
    m2_ref,
    m2t_ref,
    e_ref,
    et_ref,
    f_ref,
    ft_ref,
    wb_ref,
    wbt_ref,
    bias_ref,
    y1_ref,
    mix1_ref,
    mask_ref,
    mask2_ref,
    keep_ref,
    loss_ref,
    gkeep_ref,
    kept_ref,
    sent_ref,
    small_ref,
    bufs,
    xs,
    y2,
    mix2,
    out2,
    t2,
    xcol,
    h1,
    h2,
    ext_in,
    oacc,
    ext_out,
    gacc,
    gmix,
    bacc,
    ge,
    gf,
    acc,
    slab,
):
    rows, cols, bands = dims
    half = (rows // 2, cols // 2, bands)
    unpack_kernel(
        dims, index_ref, b0, b1, b2, b3, chan1_ref, m1_ref, chan2_ref, m2_ref,
        y1_ref, mix1_ref, mask_ref, mask2_ref, keep_ref, y2, mix2, bufs, xs,
    )
    couple_two_forward(
        half, mix2, mask_ref, mask2_ref, chan2_ref, et_ref, wb_ref, f_ref, bias_ref,
        out2, t2, xcol, h1, h2, loss_ref, ext_in, oacc,
    )
    couple_two_backward(
        half, bit, index_ref, mask2_ref, y2, out2, t2, xcol, h1, h2, chan2_ref, m2t_ref, e_ref, wbt_ref, ft_ref,
        kept_ref, sent_ref, small_ref, gkeep_ref, ext_out, gacc, gmix, bacc, ge, gf, acc, slab,
    )


def couple_one_forward(
    dims,
    chunk,
    mix1_ref,
    mask_ref,
    mask2_ref,
    keep_ref,
    gkeep_in_ref,
    chan1_ref,
    et_ref,
    wb_ref,
    f_ref,
    bias_ref,
    wp_ref,
    wpt_ref,
    pbias_ref,
    xcol_ref,
    h1_ref,
    h2_ref,
    res_ref,
    t_ref,
    gout_ref,
    gwp_ref,
    loss_ref,
    ext,
    oacc,
    kext,
    kcol,
    gkacc,
    drop,
):
    rows, cols, bands = dims
    iota = lax.broadcasted_iota(jnp.int32, (8, 1), 0)
    ones = jnp.where(iota == CH // 2, 1.0, 0.0)
    fill_ext(ext, mix1_ref[0:8, :] + ones, rows, cols, bands, ones)
    oacc[...] = jnp.zeros_like(oacc)

    @pl.loop(0, rows * cols * LANES // chunk)
    def _(step):
        row, col, at = place_of(step, chunk, cols)
        xcol = gather_cols(ext, cols, row, col, chunk)
        xcol_ref[:, at] = xcol
        hidden = jnp.maximum(dot(et_ref[...], xcol).astype(BF16), jnp.zeros((), BF16))
        h1_ref[:, at] = hidden
        hidden = jnp.maximum((dot(wb_ref[...], hidden) + bias_ref[...]).astype(BF16), jnp.zeros((), BF16))
        h2_ref[:, at] = hidden
        scatter_cols(oacc, dot(f_ref[...], hidden), cols, row, col, chunk, True)

    line = cols * LANES
    valid = row_mask(8, 8, CH // 2)
    step_total = None
    half_rows, half_cols = rows // 2, cols // 2
    for s, piece in enumerate(fold_ext(oacc, rows, cols, bands)):
        at = slice(s * line, (s + 1) * line)
        output = piece + chan1_ref[:, 2:3]
        second = output[8:] + 2.0
        t_ref[:, at] = second
        scale_log = log_sigmoid(second)
        result = (mix1_ref[8:16, at] + output[:8]) * jnp.exp(scale_log)
        res_ref[:, at] = result
        part = fold_lanes(jnp.where(valid, scale_log, 0.0) * mask_ref[:, at])
        step_total = part if step_total is None else step_total + part
    for i in range(half_rows):
        for j in range(half_cols):
            at = slice((i * half_cols + j) * LANES, (i * half_cols + j + 1) * LANES)
            for p in range(4):
                start = ((2 * i + p // 2) * cols + 2 * j + p % 2) * LANES
                drop[p * 8 : p * 8 + 8, at] = res_ref[:, start : start + LANES]
    part_iota = lax.broadcasted_iota(jnp.int32, (32, 1), 0)
    part_ones = jnp.where(part_iota == CH // 2, 1.0, 0.0)
    fill_ext(kext, keep_ref[...] + part_ones, half_rows, half_cols, bands, part_ones)
    part_line = half_cols * LANES
    gkacc[...] = jnp.zeros_like(gkacc)
    weight = -mask2_ref[...]
    valid = row_mask(32, 8, CH // 2)
    prior_total = None
    for i in range(half_rows):
        at = slice(i * part_line, (i + 1) * part_line)
        columns = gather_cols(kext, half_cols, i, 0, part_line)
        kcol[...] = columns
        prior = dot(wp_ref[...], columns) + pbias_ref[...]
        mean, logs = prior[:32], prior[32:]
        inverse = jnp.exp(-logs)
        scaled = (drop[:, at] - mean) * inverse
        part = fold_lanes((-logs - 0.5 * scaled * scaled) * mask2_ref[:, at])
        prior_total = part if prior_total is None else prior_total + part
        g_mean = weight[:, at] * scaled * inverse
        g_logs = jnp.where(valid, weight[:, at] * (scaled * scaled - 1.0), 0.0)
        drop[:, at] = -g_mean
        g_prior = jnp.concatenate([g_mean, g_logs], axis=0).astype(BF16)
        g_wp = dot_nt(g_prior, kcol[...])
        if i == 0:
            gwp_ref[...] = g_wp
        else:
            gwp_ref[...] += g_wp
        scatter_cols(gkacc, dot(wpt_ref[...], g_prior), half_cols, i, 0, part_line)
    loss_ref[...] = jnp.zeros_like(loss_ref)
    loss_ref[0:1, :] = jnp.sum(step_total, axis=0, keepdims=True) + jnp.sum(prior_total, axis=0, keepdims=True)
    for i, piece in enumerate(fold_ext(gkacc, half_rows, half_cols, bands)):
        at = slice(i * part_line, (i + 1) * part_line)
        g_keep = piece + gkeep_in_ref[:, at]
        g_drop = drop[:, at]
        for j in range(half_cols):
            inner = slice(j * LANES, (j + 1) * LANES)
            for p in range(4):
                start = ((2 * i + p // 2) * cols + 2 * j + p % 2) * LANES
                gout_ref[0:8, start : start + LANES] = g_keep[p * 8 : p * 8 + 8, inner]
                gout_ref[8:16, start : start + LANES] = g_drop[p * 8 : p * 8 + 8, inner]


def put_rows(slab_ref, first, values, row, count):
    for block in range(HID // LANES):
        start = first(block)
        slab_ref[start : start + count, :] = values[row : row + count, block * LANES : (block + 1) * LANES]


def lane_sums(stack, width):
    lane = lax.broadcasted_iota(jnp.int32, (1, LANES), 1)
    total = jnp.zeros(stack[0][1].shape, F32)
    for j, value in stack:
        total = total + jnp.where(lane == j, jnp.sum(value, axis=1, keepdims=True), 0.0)
    return total


def ones_sum(value_ref):
    return lax.dot_general(
        jnp.ones((8, LANES), F32), value_ref[...], (((1,), (1,)), ((), ())), precision=HIGH, preferred_element_type=F32
    )


def one_backward_top(
    dims,
    chunk,
    bits,
    index_ref,
    mask_ref,
    res_ref,
    t_ref,
    gout_ref,
    ft_ref,
    gwp_ref,
    loss_one_ref,
    loss_two_ref,
    h1_ref,
    h2_ref,
    gpre_ref,
    kept_a,
    sent_a,
    kept_b,
    sent_b,
    ghalf_ref,
    gbc_ref,
    ext,
    gft,
    gf,
    bacc,
    slab_ref,
):
    rows, cols, bands = dims
    weight = -mask_ref[...]
    second = t_ref[...]
    result = res_ref[...]
    g_result = gout_ref[8:16, :]
    g_log = g_result * result + weight
    g_second = g_log * sigmoid_minus(second)
    g_half = g_result * jnp.exp(log_sigmoid(second))
    ghalf_ref[...] = g_half
    valid = row_mask(8, 8, CH // 2)
    g_out = jnp.concatenate([g_half, jnp.where(valid, g_second, 0.0)], axis=0)
    g_out = g_out.astype(BF16).astype(F32)
    gbc_ref[...] = fold_lanes(g_out)
    fill_ext(ext, g_out, rows, cols, bands, jnp.zeros((16, 1), F32))
    gft[...] = jnp.zeros_like(gft)
    slab_ref[...] = jnp.zeros_like(slab_ref)
    bacc[...] = jnp.zeros_like(bacc)

    @pl.loop(0, rows * cols * LANES // chunk)
    def _(step):
        row, col, at = place_of(step, chunk, cols)
        gcol = gather_cols(ext, cols, row, col, chunk, True)
        hidden_two = h2_ref[:, at]
        g_pre = jnp.where(hidden_two > 0, dot(ft_ref[...], gcol).astype(BF16), jnp.zeros((), BF16))
        gft[...] += dot_nt(hidden_two, gcol)
        gpre_ref[:, at] = g_pre
        g_wb = dot_nt(g_pre, h1_ref[:, at])
        for block in range(HID // LANES):
            slab_ref[block * HID : (block + 1) * HID, :] += g_wb[:, block * LANES : (block + 1) * LANES]
        bacc[...] += fold_lanes(g_pre.astype(F32))

    for first, count in ((0, LANES), (LANES, 16)):
        gf[first : first + count, :] = gft[:, first : first + count].T
    bias = ones_sum(bacc)
    put_rows(slab_ref, lambda block: ONE_B + block, bias, 0, 1)
    for piece in range(18):
        put_rows(slab_ref, lambda block: ONE_F + block * 112 + piece * 6, gf, piece * 8, 6)
    for block in range(3):
        width = min(LANES, 288 - block * LANES)
        slab_ref[ONE_P + block * 64 : ONE_P + block * 64 + 64, 0:width] = gwp_ref[
            :, block * LANES : block * LANES + width
        ]
    scalars = [(0, loss_one_ref[0:1, :] + loss_two_ref[0:1, :]), (1, loss_two_ref[1:2, :]), (2, loss_two_ref[2:3, :])]
    slab_ref[ONE_LOSS : ONE_LOSS + 1, :] = lane_sums(scalars, 3)
    part_out(slab_ref, 0, PART_A, index_ref[1], bits[0], kept_a, sent_a)
    part_out(slab_ref, PART_A, ONE_ROWS - PART_A, index_ref[1], bits[1], kept_b, sent_b)


def one_backward_bottom(
    dims,
    chunk,
    y1_ref,
    ghalf_ref,
    gbc_ref,
    gout_ref,
    e_ref,
    wbt_ref,
    xcol_ref,
    h1_ref,
    gpre_ref,
    small_ref,
    slab_ref,
    gacc,
    gmix,
    ge,
    acc,
):
    rows, cols, bands = dims
    gacc[...] = jnp.zeros_like(gacc)
    ge[...] = jnp.zeros_like(ge)
    slab_ref[...] = jnp.zeros_like(slab_ref)

    @pl.loop(0, rows * cols * LANES // chunk)
    def _(step):
        row, col, at = place_of(step, chunk, cols)
        g_pre = jnp.where(h1_ref[:, at] > 0, dot(wbt_ref[...], gpre_ref[:, at]).astype(BF16), jnp.zeros((), BF16))
        ge[...] += dot_nt(xcol_ref[:, at], g_pre)
        scatter_cols(gacc, dot(e_ref[...], g_pre), cols, row, col, chunk)

    gmix[0:8, :] = gout_ref[0:8, :] + jnp.concatenate(fold_ext(gacc, rows, cols, bands), axis=1)
    gmix[8:16, :] = ghalf_ref[...]
    g_mixed = gmix[...]
    acc[...] = jnp.zeros_like(acc)
    gram(g_mixed, y1_ref, range(CH), acc)
    stack = [(j, acc[j]) for j in range(CH)] + [(16, fold_lanes(g_mixed)), (17, gbc_ref[...])]
    slab_ref[REST_SMALL : REST_SMALL + 16, :] = (
        lane_sums(stack, CH) + pltpu.roll(small_ref[0:16, :], 32, 1) + pltpu.roll(small_ref[16:32, :], 66, 1)
    )
    for tap in range(9):
        put_rows(slab_ref, lambda block: block * 56 + tap * 6, ge, tap * 8, 6)
    put_rows(slab_ref, lambda block: REST_A + block, ge, 6, 1)


def call(kernel, inputs, outputs, scratch, flops, aliases=None, far_in=(), far_out=()):
    whole = pl.BlockSpec(memory_space=pltpu.VMEM)
    smem = pl.BlockSpec(memory_space=pltpu.SMEM)
    far = pl.BlockSpec(memory_space=pl.ANY)
    traffic = sum(x.size * x.dtype.itemsize for x in list(inputs) + list(outputs))
    return pl.pallas_call(
        kernel,
        out_shape=outputs,
        in_specs=[
            far if k in far_in else smem if x.dtype == jnp.int32 and x.ndim == 1 else whole for k, x in enumerate(inputs)
        ],
        out_specs=[far if k in far_out else whole for k in range(len(outputs))],
        scratch_shapes=scratch,
        input_output_aliases=aliases or {},
        compiler_params=pltpu.CompilerParams(vmem_limit_bytes=VMEM_LIMIT),
        cost_estimate=pl.CostEstimate(flops=flops, bytes_accessed=traffic, transcendentals=0),
    )(*inputs)


def shape(dims, dtype=F32):
    return jax.ShapeDtypeStruct(tuple(dims), dtype)


def high_dot(left, right, contract=(1, 0)):
    return lax.dot_general(
        left, right, (((contract[0],), (contract[1],)), ((), ())), precision=HIGH, preferred_element_type=F32
    )


def iotas(height, width=LANES):
    return (
        lax.broadcasted_iota(jnp.int32, (height, width), 0),
        lax.broadcasted_iota(jnp.int32, (height, width), 1),
    )


def take_flat(flat_ref, start, length):
    row, offset = divmod(start, LANES)
    lane = lax.broadcasted_iota(jnp.int32, (1, LANES), 1)
    value = flat_ref[row : row + 1, :]
    if offset:
        value = pltpu.roll(value, LANES - offset, 1)
        if offset + length > LANES:
            after = pltpu.roll(flat_ref[row + 1 : row + 2, :], LANES - offset, 1)
            value = jnp.where(lane < LANES - offset, value, after)
    return jnp.where(lane < length, value, 0.0) if length < LANES else value


def put_flat(pieces, start, value, length):
    row, offset = divmod(start, LANES)
    lane = lax.broadcasted_iota(jnp.int32, (1, LANES), 1)
    if length < LANES:
        value = jnp.where(lane < length, value, 0.0)
    if offset:
        value = pltpu.roll(value, offset, 1)
    if offset + length > LANES:
        pieces.setdefault(row + 1, []).append(jnp.where(lane < offset, value, 0.0))
        value = jnp.where(lane >= offset, value, 0.0)
    pieces.setdefault(row, []).append(value)


def level_tables(flat_ref, level, lu):
    chans = CH * (level + 1)
    start = ONE_START - 4 * CH if level == 0 else TWO_START
    chan = [take_flat(flat_ref, start + k * chans, chans) for k in range(4)]
    first = start + 4 * chans + 2 * HID
    lu[...] = jnp.zeros_like(lu)
    for i in range(chans):
        lu[i : i + 1, :] = take_flat(flat_ref, first + i * chans, chans)
    row, lane = iotas(LANES)
    value = lu[...]
    inside = row < chans
    lower = jnp.where(row > lane, value, 0.0) + jnp.where((row == lane) & inside, 1.0, 0.0)
    upper = jnp.where(row < lane, value, 0.0) + jnp.where((row == lane) & inside, jnp.exp(chan[2]), 0.0)
    return chans, start, chan, lower, upper


def natural_row(level, row):
    height, half = (8, CH // 2) if level == 0 else (16, CH)
    return (row // height) * half + lax.rem(row, height), lax.rem(row, height) < half


def natural_keep(row):
    return 4 * lax.rem(row, 8) + row // 8, lax.rem(row, 8) < CH // 2


def pick(condition, value):
    return jnp.sum(jnp.where(condition, value, 0.0), axis=1, keepdims=True)


def prior_places():
    row, lane = iotas(64, 4 * CH)
    inner = lax.rem(row, 32)
    natural, valid = natural_keep(inner)
    return ((lane == natural + (row // 32) * 2 * CH) & valid).astype(F32).astype(BF16)


def prior_lanes(tap):
    row, lane = iotas(2 * CH)
    inner = lane - (tap * 32) % LANES
    natural = 4 * lax.rem(inner, 8) + inner // 8
    valid = (inner >= 0) & (inner < 32) & (lax.rem(inner, 8) < CH // 2)
    return ((row == natural) & valid).astype(F32).astype(BF16)


def prepare_level(level, flat_ref, entry_ref, middle_ref, exit_ref, outs, wide):
    e_ref, et_ref, f_ref, ft_ref, wb_ref, wbt_ref, bb_ref = outs
    chans = CH * (level + 1)
    start = 0 if level == 0 else TWO_START
    half, tall = chans // 2, 8 * (level + 1)
    first_in, first_out = (0, 0) if level == 0 else (CH // 2, CH)
    wide[...] = jnp.zeros_like(wide)
    for tap in range(9):
        wide[tap * tall : tap * tall + half, :] = entry_ref[tap, first_in : first_in + half, :]
    row, lane = iotas(LANES)
    for block in range(HID // LANES):
        at = slice(block * LANES, (block + 1) * LANES)
        value = take_flat(flat_ref, start + 4 * chans + block * LANES, LANES)
        for tap in range(3):
            part = value.astype(BF16).astype(F32)
            wide[tap * tall + half : tap * tall + half + 1, at] = part
            value = value - part
        value = take_flat(flat_ref, start + 4 * chans + HID + block * LANES, LANES)
        bb_ref[at, :] = pick(row == lane, value)
    count = 9 * tall
    padded = -(-count // LANES) * LANES
    e_ref[...] = wide[0:count, :].astype(BF16)
    et_ref[...] = wide[0:padded, :].T[:, 0:count].astype(BF16)
    wide[...] = jnp.zeros_like(wide)
    for tap in range(9):
        for side in range(2):
            first = (tap * 2 + side) * tall
            wide[first : first + half, :] = exit_ref[tap, first_out + side * half : first_out + (side + 1) * half, :]
    count = 18 * tall
    padded = -(-count // LANES) * LANES
    f_ref[...] = wide[0:count, :].astype(BF16)
    ft_ref[...] = wide[0:padded, :].T[:, 0:count].astype(BF16)
    wb_ref[...] = middle_ref[level].astype(BF16)
    wbt_ref[...] = middle_ref[level].T.astype(BF16)


def prepare_kernel(
    flat_ref,
    prior_far,
    entry_far,
    middle_far,
    exit_far,
    chan1_ref,
    m1_ref,
    chan2_ref,
    m2_ref,
    m2t_ref,
    wp_ref,
    wpt_ref,
    pbias_ref,
    *refs,
):
    outs_two, outs_one = refs[:7], refs[7:14]
    lu, wide, entry_ref, middle_ref, exit_ref, prior_ref, sems = refs[14:]
    pieces = [(middle_far, middle_ref, (1, slice(k * LANES, (k + 1) * LANES))) for k in range(4)]
    pieces += [(exit_far, exit_ref, (slice(3 * k, 3 * k + 3),)) for k in range(3)]
    pieces += [(entry_far, entry_ref, (slice(3 * k, 3 * k + 3),)) for k in range(3)]
    pieces += [(middle_far, middle_ref, (0, slice(k * LANES, (k + 1) * LANES))) for k in range(4)]
    pieces += [(prior_far, prior_ref, (slice(0, 9),))]
    copies = [
        pltpu.make_async_copy(source.at[at], target.at[at], sems.at[k]) for k, (source, target, at) in enumerate(pieces)
    ]
    for copy in copies:
        copy.start()
    for level in range(2):
        chans, start, chan, lower, upper = level_tables(flat_ref, level, lu)
        product = high_dot(lower, upper)
        height = 16 * (level + 1)
        row, lane = iotas(height)
        natural, valid = natural_row(level, row)
        spread = ((lane == chans - 1 - natural) & valid).astype(F32)
        matrix = high_dot(spread, product)
        out_bias = pick((lane == natural) & valid, chan[3])
        if level == 0:
            m1_ref[...] = matrix
            shift, scale = pick(lane == row, chan[0]), pick((lane == row) & (row < CH), jnp.exp(chan[1]))
        else:
            source, target = iotas(LANES)
            place, used = natural_keep(target)
            matrix = high_dot(matrix, ((source == place) & used & (target < 32)).astype(F32))
            m2_ref[...] = matrix
            lu[...] = jnp.zeros_like(lu)
            lu[0:32, :] = matrix
            m2t_ref[...] = lu[...].T[0:32, :]
            place, used = natural_keep(row)
            shift = pick((lane == place) & used, chan[0])
            scale = pick((lane == place) & used, jnp.exp(chan[1]))
        chan_ref = chan1_ref if level == 0 else chan2_ref
        chan_ref[...] = (
            jnp.where(lane == 0, shift, 0.0) + jnp.where(lane == 1, scale, 0.0) + jnp.where(lane == 2, out_bias, 0.0)
        )
    copies[14].wait()
    places = prior_places()
    blocks = [None] * 3
    for tap in range(9):
        moved = dot_nt(places, prior_ref[tap].astype(BF16)).astype(BF16)
        part = dot(moved, prior_lanes(tap))
        block = tap * 32 // LANES
        blocks[block] = part if blocks[block] is None else blocks[block] + part
    lu[...] = jnp.zeros_like(lu)
    for block, value in enumerate(blocks):
        width = min(LANES, 288 - block * LANES)
        at = slice(block * LANES, block * LANES + width)
        wp_ref[:, at] = value[:, 0:width].astype(BF16)
        lu[0:64, :] = value
        wpt_ref[at, :] = lu[...].T[0:width, 0:64].astype(BF16)
    row, lane = iotas(64)
    natural, valid = natural_keep(lax.rem(row, 32))
    pbias_ref[...] = pick((lane == natural + (row // 32) * 2 * CH) & valid, take_flat(flat_ref, PRIOR_START, 4 * CH))
    for copy in copies[:10]:
        copy.wait()
    prepare_level(1, flat_ref, entry_ref, middle_ref, exit_ref, outs_two, wide)
    for copy in copies[10:14]:
        copy.wait()
    prepare_level(0, flat_ref, entry_ref, middle_ref, exit_ref, outs_one, wide)


def adamw(weight, grad, first, second):
    first_new = BETA_ONE * first + (1.0 - BETA_ONE) * grad
    second_new = BETA_TWO * second + (1.0 - BETA_TWO) * grad * grad
    first_hat = first_new * (1.0 / (1.0 - BETA_ONE**ADAM_STEP))
    second_hat = second_new * (1.0 / (1.0 - BETA_TWO**ADAM_STEP))
    updated = weight - LEARN_RATE * (first_hat / (jnp.sqrt(second_hat) + ADAM_EPS) + WEIGHT_DECAY * weight)
    return (updated, second_new)


def finish_kernel(
    two_ref,
    one_ref,
    rest_ref,
    low_ref,
    extra_ref,
    flat_ref,
    flat_first,
    flat_second,
    *refs,
):
    far_in, refs = refs[:12], refs[12:]
    (loss_ref, norm_ref, flat_new, flat_grad, flat_moment), refs = refs[:5], refs[5:]
    far_out, refs = refs[:12], refs[12:]
    bias_ref, two, one, rest, lu = refs[:5]
    held, (in_sems, out_sems) = refs[5:21], refs[21:]
    weights, firsts, seconds, grads = held[0:4], held[4:8], held[8:12], held[12:16]
    entry_grad, _, exit_grad, prior_grad = grads
    jobs = [(1, 0), (1, 1), (2, None), (0, None), (3, None)]

    def part(ref, level):
        return ref if level is None else ref.at[level]

    def copies_in(k):
        group, level = jobs[k]
        return [
            pltpu.make_async_copy(part(far_in[3 * group + j], level), part(near[group], level), in_sems.at[k, j])
            for j, near in enumerate((weights, firsts, seconds))
        ]

    def copies_out(k):
        group, level = jobs[k]
        return [
            pltpu.make_async_copy(part(near[group], level), part(far_out[3 * group + j], level), out_sems.at[k, j])
            for j, near in enumerate((weights, grads, seconds))
        ]

    for k in range(len(jobs)):
        for copy in copies_in(k):
            copy.start()
    extra = extra_ref[...].astype(F32)
    _, lane = iotas(extra.shape[0])
    log_total, count_two, count = (jnp.sum(jnp.where(lane == k, extra, 0.0), keepdims=True) for k in range(3))
    coef = -1.0 / (CH * count * math.log(2.0))
    factor = -coef
    two[...] = two_ref[WB_ROWS:, :].astype(F32) * factor
    one[...] = one_ref[WB_ROWS:, :].astype(F32) * factor
    rest[...] = (rest_ref[...].astype(F32) + low_ref[...].astype(F32)) * factor
    base = WB_ROWS
    squares = []
    pieces = {}
    consts = []
    for level in range(2):
        chans, start, chan, lower, upper = level_tables(flat_ref, level, lu)
        consts.append(jnp.sum(chan[1] + chan[2], keepdims=True))
        weight = coef * count if level == 0 else coef * count_two
        height = 16 * (level + 1)
        small = rest[REST_SMALL : REST_SMALL + 16, :]
        if level == 1:
            small = jnp.concatenate([pltpu.roll(small, LANES - 32, 1), pltpu.roll(small, LANES - 66, 1)], axis=0)
        sum_lane = 16 * (level + 1)
        product = high_dot(lower, upper)
        row, lane = iotas(LANES, height)
        natural, valid = natural_row(level, lane)
        turned = high_dot(((row == chans - 1 - natural) & valid).astype(F32), small)
        row, lane = iotas(LANES)
        g_product = jnp.where(lane < sum_lane, turned, 0.0)
        if level == 1:
            place, used = natural_keep(row)
            g_product = high_dot(g_product, ((lane == place) & used & (row < 32)).astype(F32))
        else:
            g_product = jnp.where(lane < chans, g_product, 0.0)
        g_lower = high_dot(g_product, upper, (1, 1))
        g_upper = high_dot(lower.T, g_product)
        g_lu = jnp.where(row > lane, g_lower, 0.0) + jnp.where(row < lane, g_upper, 0.0)
        diagonal = jnp.sum(jnp.where(row == lane, g_upper, 0.0), axis=0, keepdims=True)
        shift = jnp.sum(turned[:, sum_lane : sum_lane + 1] * product, axis=0, keepdims=True)
        scale = jnp.sum(product * g_product, axis=0, keepdims=True)
        row, lane = iotas(height)
        natural, valid = natural_row(level, row)
        out_bias = jnp.where((lane == natural) & valid, small[:, sum_lane + 1 : sum_lane + 2], 0.0)
        put_flat(pieces, start, shift * jnp.exp(chan[1]), chans)
        put_flat(pieces, start + chans, scale + weight, chans)
        put_flat(pieces, start + 2 * chans, diagonal * jnp.exp(chan[2]) + weight, chans)
        put_flat(pieces, start + 3 * chans, jnp.sum(out_bias, axis=0, keepdims=True), chans)
        for i in range(chans):
            put_flat(pieces, start + 4 * chans + 2 * HID + i * chans, g_lu[i : i + 1, :], chans)
        for block in range(HID // LANES):
            if level == 0:
                value_a = rest[REST_A + block : REST_A + block + 1, :]
                value_b = one[ONE_B - base + block : ONE_B - base + block + 1, :]
            else:
                at = TWO_E - base + block * 144 + CH
                value_a = two[at : at + 1, :]
                value_b = two[TWO_B - base + block : TWO_B - base + block + 1, :]
            at = start + 4 * chans + block * LANES
            put_flat(pieces, at, value_a, LANES)
            put_flat(pieces, at + HID, value_b, LANES)
            bias_ref[2 * level : 2 * level + 1, block * LANES : (block + 1) * LANES] = value_a
            bias_ref[2 * level + 1 : 2 * level + 2, block * LANES : (block + 1) * LANES] = value_b
    row, lane = iotas(64)
    natural, valid = natural_keep(lax.rem(row, 32))
    column = one[ONE_P - base : ONE_P - base + 64, CH // 2 : CH // 2 + 1]
    prior_bias = jnp.where((lane == natural + (row // 32) * 2 * CH) & valid, column, 0.0)
    put_flat(pieces, PRIOR_START, jnp.sum(prior_bias, axis=0, keepdims=True), 4 * CH)
    for r in range(FLAT_ROWS):
        parts = pieces.get(r, [jnp.zeros((1, LANES), F32)])
        flat_grad[r : r + 1, :] = functools.reduce(jnp.add, parts)
    for tap in range(9):
        for block in range(HID // LANES):
            at = slice(block * LANES, (block + 1) * LANES)
            first = block * 56 + tap * 6
            entry_grad[tap, 0:6, at] = rest[first : first + 6, :]
            first = TWO_E - base + block * 144 + tap * 16
            entry_grad[tap, 6:18, at] = two[first : first + CH, :]
            first = ONE_F - base + block * 112 + tap * CH
            exit_grad[tap, 0:CH, at] = one[first : first + CH, :]
            first = TWO_F - base + block * 216 + tap * 2 * CH
            exit_grad[tap, CH : 3 * CH, at] = two[first : first + 2 * CH, :]
    places = prior_places()
    for tap in range(9):
        first = ONE_P + (tap * 32 // LANES) * 64
        moved = dot_nt(prior_lanes(tap), one_ref[first : first + 64, :]).astype(BF16)
        prior_grad[tap, :, :] = dot(moved, places) * factor
    for ref in (flat_grad, entry_grad, exit_grad, prior_grad):
        value = ref[...]
        squares.append(jnp.sum(value * value, keepdims=True).reshape(1, 1))
    for ref in (one_ref, two_ref):
        total = jnp.zeros((64, LANES), F32)
        for start in range(0, WB_ROWS, 64):
            value = ref[start : start + 64, :].astype(F32)
            total = total + value * value
        squares.append(jnp.sum(total, keepdims=True) * factor * factor)
    norm = jnp.sqrt(functools.reduce(jnp.add, squares))
    clip = jnp.minimum(1.0, CLIP_NORM / (norm + 1e-06))
    total = log_total + consts[0] * count + count_two * (consts[1] - 2 * CH * LOG_TWO_PI)
    loss_ref[...] = coef * total + 8.0
    norm_ref[...] = norm
    bias_ref[...] = bias_ref[...] * clip

    middle_factor = factor * clip
    value = flat_grad[...] * clip
    flat_grad[...] = value
    flat_new[...], flat_moment[...] = adamw(flat_ref[...], value, flat_first[...], flat_second[...])
    size = 64
    for k, (group, level) in enumerate(jobs):
        for copy in copies_in(k):
            copy.wait()
        weight, first, second, grad = weights[group], firsts[group], seconds[group], grads[group]
        if level is None:
            for tap in range(9):
                value = grad[tap] * clip
                grad[tap] = value
                weight[tap], second[tap] = adamw(weight[tap], value, first[tap], second[tap])
        else:
            slab = (one_ref, two_ref)[level]

            @pl.loop(0, HID // size)
            def _(j):
                rows = pl.ds(pl.multiple_of(j * size, size), size)
                for block in range(HID // LANES):
                    at = (level, rows, slice(block * LANES, (block + 1) * LANES))
                    value = slab[pl.ds(pl.multiple_of(block * HID + j * size, size), size), :].astype(F32) * middle_factor
                    grad[at] = value
                    weight[at], second[at] = adamw(weight[at], value, first[at], second[at])

        for copy in copies_out(k):
            copy.start()
    for k in range(len(jobs)):
        for copy in copies_out(k):
            copy.wait()


def on_device(
    pixels,
    valid_mask,
    vectors,
    vectors_first,
    vectors_second,
    entry_taps,
    entry_first,
    entry_second,
    middle,
    middle_first,
    middle_second,
    exit_taps,
    exit_first,
    exit_second,
    prior_taps,
    prior_first,
    prior_second,
):
    bands = lax.axis_size("rows")
    rows, cols = valid_mask.shape[0], valid_mask.shape[1]
    dims = (rows, cols, bands)
    size = rows * cols * LANES
    part = size // 4
    batches = lax.axis_size("batch")
    devices = batches * bands
    bits = [2**k for k in range((devices - 1).bit_length())]
    index = lax.axis_index("batch") * bands + lax.axis_index("rows")
    own = jnp.stack([lax.axis_index("rows"), index]).astype(jnp.int32)

    def trade(value, bit):
        return lax.ppermute(value, ("batch", "rows"), [(i, i ^ bit) for i in range(devices)])

    def in_hbm(value):
        return pltpu.with_memory_space_constraint(value, pltpu.HBM)

    def after(value, *done):
        return lax.optimization_barrier((value, *done))[0]

    piece_rows = (CH + 1) * rows * cols // bands
    pieces = call(
        functools.partial(pack_kernel, bands),
        (own, in_hbm(pixels.reshape(-1, LANES)), in_hbm(valid_mask.reshape(-1, LANES))),
        [shape((piece_rows, LANES), BF16)] * bands,
        [],
        1000,
    )
    bufs = [pieces[0]]
    for d in range(1, bands):
        bufs.append(lax.ppermute(pieces[d], "rows", [(i, i ^ d) for i in range(bands)]))

    def flat(value):
        return jnp.pad(value, (0, FLAT_ROWS * LANES - VEC)).reshape(FLAT_ROWS, LANES)

    vectors_flat = flat(vectors)

    def level_shapes(tall):
        return [
            shape((9 * tall, HID), BF16),
            shape((HID, 9 * tall), BF16),
            shape((18 * tall, HID), BF16),
            shape((HID, 18 * tall), BF16),
            shape((HID, HID), BF16),
            shape((HID, HID), BF16),
            shape((HID, 1)),
        ]

    prior_turned = jnp.swapaxes(prior_taps, 1, 2)
    (
        chan_one, m_one, chan_two, m_two, m_two_t, wp, wpt, prior_bias,
        e_two, e_two_t, f_two, f_two_t, wb_two, wb_two_t, bb_two,
        e_one, e_one_t, f_one, f_one_t, wb_one, wb_one_t, bb_one,
    ) = call(
        prepare_kernel,
        (after(vectors_flat, pieces[0]), in_hbm(prior_turned), in_hbm(entry_taps), in_hbm(middle), in_hbm(exit_taps)),
        [shape((16, LANES)), shape((16, LANES)), shape((32, LANES)), shape((32, LANES)), shape((32, LANES))]
        + [shape((64, 288), BF16), shape((288, 64), BF16), shape((64, 1))]
        + level_shapes(16)
        + level_shapes(8),
        [
            pltpu.VMEM((LANES, LANES), F32),
            pltpu.VMEM((384, HID), F32),
            pltpu.VMEM(entry_taps.shape, F32),
            pltpu.VMEM(middle.shape, F32),
            pltpu.VMEM(exit_taps.shape, F32),
            pltpu.VMEM(prior_turned.shape, F32),
            pltpu.SemaphoreType.DMA((15,)),
        ],
        10**9,
        far_in=(1, 2, 3, 4),
    )


    ext_lanes = (rows // 2 + 2) * (cols // 2 + 2) * LANES
    first_bit, second_bit, third_bit, fourth_bit = bits[0], bits[2], bits[1], bits[3]
    half_two = shape((TWO_ROWS // 2, LANES))
    (y1, mixed_one, mask, mask2, keep, loss_two, gkeep_two, kept_two, sent_two, small_two) = call(
        functools.partial(level_two_kernel, dims, second_bit),
        (
            own, *bufs, chan_one, m_one, chan_two, m_two, m_two_t,
            e_two, e_two_t, f_two, f_two_t, wb_two, wb_two_t, bb_two,
        ),
        [
            shape((16, size)),
            shape((16, size)),
            shape((1, size)),
            shape((1, part)),
            shape((32, part)),
            shape((8, LANES)),
            shape((32, part)),
        ]
        + [half_two] * 2
        + [shape((32, LANES))],
        [
            pltpu.VMEM((bands, piece_rows, LANES), F32),
            pltpu.VMEM((16, size), F32),
            pltpu.VMEM((32, part), F32),
            pltpu.VMEM((32, part), F32),
            pltpu.VMEM((32, part), F32),
            pltpu.VMEM((16, part), F32),
            pltpu.VMEM((144, part), BF16),
            pltpu.VMEM((HID, part), BF16),
            pltpu.VMEM((HID, part), BF16),
            pltpu.VMEM((16, ext_lanes), F32),
            pltpu.VMEM((32, ext_lanes), F32),
            pltpu.VMEM((32, ext_lanes), F32),
            pltpu.VMEM((16, ext_lanes), F32),
            pltpu.VMEM((32, part), F32),
            pltpu.VMEM((HID, LANES), F32),
            pltpu.VMEM((144, HID), F32),
            pltpu.VMEM((288, HID), F32),
            pltpu.VMEM((32, 32, LANES), F32),
            pltpu.VMEM((TWO_ROWS, LANES), F32),
        ],
        6 * HID * part * (144 + HID + 288),
    )
    whole_lanes = (rows + 2) * (cols + 2) * LANES
    chunk = min(2048, size)
    fwd_in = (
        mixed_one,
        mask,
        mask2,
        keep,
        gkeep_two,
        chan_one,
        e_one_t,
        wb_one,
        f_one,
        bb_one,
        wp,
        wpt,
        prior_bias,
    )
    fwd_out = [
        shape((72, size), BF16),
        shape((HID, size), BF16),
        shape((HID, size), BF16),
        shape((8, size)),
        shape((8, size)),
        shape((16, size)),
        shape((64, 288)),
        shape((8, LANES)),
    ]
    (xcol_one, h1_one, h2_one, res_one, t_one, gout_one, gwp, loss_one) = call(
        functools.partial(couple_one_forward, dims, chunk),
        fwd_in,
        fwd_out,
        [
            pltpu.VMEM((8, whole_lanes), F32),
            pltpu.VMEM((16, whole_lanes), F32),
            pltpu.VMEM((32, ext_lanes), F32),
            pltpu.VMEM((288, cols // 2 * LANES), BF16),
            pltpu.VMEM((32, ext_lanes), F32),
            pltpu.VMEM((32, part), F32),
        ],
        2 * HID * size * (72 + HID + 144),
    )
    top_in = (own, mask, res_one, t_one, gout_one, f_one_t, gwp, loss_one, loss_two, h1_one, h2_one)
    half_a, half_b = shape((PART_A // 2, LANES)), shape(((ONE_ROWS - PART_A) // 2, LANES))
    top_out = [shape((HID, size), BF16), half_a, half_a, half_b, half_b, shape((8, size)), shape((16, LANES))]
    (gpre, kept_a, sent_a, kept_b, sent_b, ghalf, gbc) = call(
        functools.partial(one_backward_top, dims, chunk // 2, (second_bit, third_bit)),
        top_in,
        top_out,
        [
            pltpu.VMEM((16, whole_lanes), F32),
            pltpu.VMEM((HID, 144), F32),
            pltpu.VMEM((144, HID), F32),
            pltpu.VMEM((HID, LANES), F32),
            pltpu.VMEM((ONE_ROWS, LANES), F32),
        ],
        2 * HID * size * (144 + HID + 144),
        aliases={10: 0},
    )

    def halve(parts, bit, *beside):
        high = (index // bit) % 2
        halves = [x.shape[0] // 2 for x in parts]
        sent = [lax.dynamic_slice_in_dim(x, (1 - high) * h, h, 0) for x, h in zip(parts, halves)]
        kept = [lax.dynamic_slice_in_dim(x, high * h, h, 0) for x, h in zip(parts, halves)]
        got = after(trade(jnp.concatenate(sent) if len(sent) > 1 else sent[0], bit), *beside)
        results, first = [], 0
        for x, h in zip(kept, halves):
            results.append(x + got[first : first + h])
            first += h
        return results

    def exchange(parts, near_parts, far_parts, near, far_bit):
        code = 2 * ((index // near) % 2) + (index // far_bit) % 2
        sizes = [x.shape[0] // 4 for x in parts]

        def pieces_for(partner):
            return [lax.dynamic_slice_in_dim(x, (code ^ partner) * h, h, 0) for x, h in zip(parts, sizes)]

        totals = pieces_for(0)
        others = []
        for partner, bit, more in ((2, near, near_parts), (1, far_bit, far_parts), (3, near | far_bit, [])):
            high = (index // bit) % 2
            halves = [x.shape[0] // 2 for x in more]
            sent = pieces_for(partner) + [
                lax.dynamic_slice_in_dim(x, (1 - high) * h, h, 0) for x, h in zip(more, halves)
            ]
            got = trade(jnp.concatenate(sent) if len(sent) > 1 else sent[0], bit)
            first = 0
            for k, h in enumerate(sizes):
                totals[k] = totals[k] + got[first : first + h]
                first += h
            for x, h in zip(more, halves):
                others.append(lax.dynamic_slice_in_dim(x, high * h, h, 0) + got[first : first + h])
                first += h
        return totals + others

    total_two = kept_two + after(trade(sent_two, second_bit), gbc)
    low_in = (y1, ghalf, after(gbc, total_two), gout_one, e_one, wb_one_t, xcol_one, h1_one, gpre, small_two)
    (slab_rest,) = call(
        functools.partial(one_backward_bottom, dims, chunk),
        low_in,
        [shape((REST_ROWS, LANES))],
        [
            pltpu.VMEM((8, whole_lanes), F32),
            pltpu.VMEM((16, size), F32),
            pltpu.VMEM((72, HID), F32),
            pltpu.VMEM((CH, 16, LANES), F32),
        ],
        2 * HID * size * (72 + HID + 72),
    )

    total_a = kept_a + after(trade(sent_a, second_bit), slab_rest)
    total_b = kept_b + after(trade(sent_b, third_bit), slab_rest)
    (total_two,) = halve([total_two], fourth_bit, slab_rest)
    far = bits[3:]
    total_two, total_a, total_b, total_rest = halve(
        [total_two, total_a, total_b, after(slab_rest, total_two)], first_bit
    )
    total_rest, total_a, total_two, total_b = exchange(
        [total_rest], [total_a, total_two], [total_b], third_bit, second_bit
    )
    total_a, total_b, total_rest, total_two = exchange(
        [total_a, total_b, total_rest], [], [total_two], far[0], far[1]
    )
    shards = [total_two, total_a, total_b, total_rest]
    for bit in far[2:]:
        shards = halve(shards, bit)
    orders = [
        [second_bit, fourth_bit, first_bit, third_bit] + far[1:],
        [second_bit, first_bit, third_bit] + far,
        [third_bit, first_bit, second_bit] + far,
        [first_bit, third_bit, second_bit] + far,
    ]
    loss_part = shards[2]
    owner, loss_row = divmod(ONE_LOSS - PART_A, loss_part.shape[0])
    extra = []
    value = loss_part[loss_row : loss_row + 1]
    for _ in range(3):
        high = lax.reduce_precision(value, 8, 7)
        extra.append(high)
        value = value - high
    extra.append(shards[3] - lax.reduce_precision(shards[3], 8, 7))
    extra = jnp.concatenate(extra)
    extra = jnp.pad(extra, ((0, -extra.shape[0] % 16), (0, 0)))
    spread = [shards[0].astype(BF16), jnp.concatenate(shards[1:] + [extra]).astype(BF16)]
    near = [[third_bit, second_bit, first_bit], [second_bit, third_bit, first_bit]]
    backs = [far[::-1] + near[0], far[::-1] + near[1]]

    def double(values, bit):
        low = (index // bit) % 2 == 0
        joined = jnp.concatenate(values) if len(values) > 1 else values[0]
        other = trade(joined, bit)
        results, first = [], 0
        for value in values:
            got = other[first : first + value.shape[0]]
            first += value.shape[0]
            results.append(jnp.where(low, jnp.concatenate([value, got]), jnp.concatenate([got, value])))
        return results

    for bit in far[:1:-1]:
        spread = double(spread, bit)
    near_low, far_low = (index // far[0]) % 2 == 0, (index // far[1]) % 2 == 0
    sizes = [value.shape[0] for value in spread]
    joined = jnp.concatenate(spread)
    from_far, from_near, from_both = (trade(joined, bit) for bit in (far[1], far[0], far[0] | far[1]))

    def ordered(low, one, other):
        return jnp.where(low, jnp.concatenate([one, other]), jnp.concatenate([other, one]))

    quads = []
    for first, size_of in ((0, sizes[0]), (sizes[0], sizes[1])):
        own_part, far_part, near_part, both_part = (
            x[first : first + size_of] for x in (joined, from_far, from_near, from_both)
        )
        quads.append(
            ordered(near_low, ordered(far_low, own_part, far_part), ordered(far_low, near_part, both_part))
        )
    spread = quads
    for k in range(3):
        spread = [double([value], order[k])[0] for value, order in zip(spread, near)]
    count_bits = len(bits)
    spread = [value.reshape((2,) * count_bits + (-1, LANES)) for value in spread]

    def reorder(value, back, order):
        axes = [count_bits - 1 - back.index(bit) for bit in order]
        return value.transpose(axes + [count_bits, count_bits + 1]).reshape(-1, LANES)

    totals = []
    first = 0
    for k, (shard, order) in enumerate(zip(shards, orders)):
        first = 0 if k < 2 else first
        side = 0 if k < 1 else 1
        totals.append(reorder(spread[side][..., first : first + shard.shape[0], :], backs[side], order))
        first += shard.shape[0]
    place = [0] * count_bits
    for k, bit in enumerate(orders[2]):
        place[count_bits - 1 - backs[1].index(bit)] = (owner >> (count_bits - 1 - k)) & 1
    extra = spread[1][tuple(place)][first : first + 3]
    low_rest = reorder(spread[1][..., first + 3 : first + 3 + shards[3].shape[0], :], backs[1], orders[3])
    totals = [totals[0], jnp.concatenate(totals[1:3]), totals[3]]
    taps = [
        (entry_taps, entry_first, entry_second),
        (middle, middle_first, middle_second),
        (exit_taps, exit_first, exit_second),
        (prior_turned, jnp.swapaxes(prior_first, 1, 2), jnp.swapaxes(prior_second, 1, 2)),
    ]
    flats = (vectors_flat, flat(vectors_first), flat(vectors_second))
    outs = [shape((1, 1)), shape((1, 1))] + [shape((FLAT_ROWS, LANES))] * 3
    for group in taps:
        outs += [shape(group[0].shape)] * 3
    outs.append(shape((4, HID)))
    results = call(
        finish_kernel,
        (*totals, low_rest, extra, *flats, *[in_hbm(x) for group in taps for x in group]),
        outs,
        [
            pltpu.VMEM((TWO_ROWS - WB_ROWS, LANES), F32),
            pltpu.VMEM((ONE_ROWS - WB_ROWS, LANES), F32),
            pltpu.VMEM((REST_ROWS, LANES), F32),
            pltpu.VMEM((LANES, LANES), F32),
        ]
        + [pltpu.VMEM(group[0].shape, F32) for _ in range(4) for group in taps]
        + [pltpu.SemaphoreType.DMA((5, 3))] * 2,
        10**8,
        far_in=range(8, 20),
        far_out=range(5, 17),
    )
    results = list(results)
    for k in range(2):
        results[k] = results[k].reshape(())
    for k in range(2, 5):
        results[k] = results[k].reshape(-1)[:VEC]
    for k in range(14, 17):
        results[k] = jnp.swapaxes(results[k], 1, 2)
    return tuple(results)


def solution(mesh):
    replicated = (P(),) * 15
    return jax.shard_map(
        on_device,
        mesh=mesh,
        in_specs=(P(None, "rows", None, "batch"), P("rows", None, "batch")) + replicated,
        out_specs=(P(),) * 18,
        check_vma=False,
    )
```

```python
import functools
import math

import jax
import jax.numpy as jnp
from jax import lax
from jax.experimental import pallas as pl
from jax.experimental.pallas import tpu as pltpu
from jax.sharding import PartitionSpec as P

HID = 512
CH = 12

F32 = jnp.float32
BF16 = jnp.bfloat16
HIGH = lax.Precision.HIGHEST
LOG_TWO_PI = math.log(2.0 * math.pi)
LEARN_RATE = 0.05
BETA_ONE = 0.9
BETA_TWO = 0.999
ADAM_EPS = 1e-08
WEIGHT_DECAY = 0.01
CLIP_NORM = 0.01
ADAM_STEP = 10
LANES = 128
VMEM_LIMIT = 20 * 2**20
ONE_START = 4 * CH
TWO_START = 4 * CH + 2 * HID + CH * CH
PRIOR_START = TWO_START + 8 * CH + 2 * HID + 4 * CH * CH
VEC = PRIOR_START + 4 * CH
FLAT_ROWS = -(-VEC // (8 * LANES)) * 8
WB_ROWS = 4 * HID
TWO_F, TWO_E = WB_ROWS, WB_ROWS + 4 * 216
TWO_B = TWO_E + 4 * 144
TWO_ROWS = 3584
ONE_F = WB_ROWS
ONE_P = ONE_F + 4 * 112
ONE_B = ONE_P + 3 * 64
ONE_LOSS = ONE_B + 8
ONE_ROWS = 2816
PART_A = 768
REST_A = 4 * 56
REST_SMALL = REST_A + 8
REST_ROWS = 256


def dot(left, right):
    return lax.dot_general(left, right, (((1,), (0,)), ((), ())), preferred_element_type=F32)


def dot_nt(left, right):
    return lax.dot_general(left, right, (((1,), (1,)), ((), ())), preferred_element_type=F32)


def lane_band(bands, height=1):
    return lax.broadcasted_iota(jnp.int32, (height, LANES), 1) // (LANES // bands)


def pack_kernel(bands, index_ref, pixels_ref, mask_ref, *out_refs):
    own = index_ref[0]
    width = LANES // bands
    rows = pixels_ref.shape[0] // bands
    extra = mask_ref.shape[0] // bands
    band = lane_band(bands)
    parts = [pixels_ref[pl.ds(e, rows, stride=bands), :].astype(F32) for e in range(bands)]
    masks = [mask_ref[pl.ds(e, extra, stride=bands), :].astype(F32) for e in range(bands)]
    for d, out_ref in enumerate(out_refs):
        target = own ^ d
        for source, first, size in ((parts, 0, rows), (masks, rows, extra)):
            total = jnp.zeros((size, LANES), F32)
            for e in range(bands):
                shift = lax.rem(e - target + bands, bands) * width
                total = jnp.where(band == e, pltpu.roll(source[e], shift, 1), total)
            out_ref[first : first + size, :] = total.astype(BF16)


def fill_ext(ext_ref, field, rows, cols, bands, pattern):
    width = LANES // bands
    band = lane_band(bands)
    stride = (cols + 2) * LANES
    height = ext_ref.shape[0]
    pads = jnp.broadcast_to(pattern, (height, LANES))
    for block in range(ext_ref.shape[1] // LANES):
        ext_ref[:, block * LANES : (block + 1) * LANES] = pads
    for row in range(rows):
        start = (row + 1) * stride + LANES
        ext_ref[:, start : start + cols * LANES] = field[:, row * cols * LANES : (row + 1) * cols * LANES]
    last = (rows - 1) * cols * LANES
    for col in range(cols):
        above = pltpu.roll(field[:, last + col * LANES : last + (col + 1) * LANES], width, 1)
        start = LANES + col * LANES
        ext_ref[:, start : start + LANES] = jnp.where(band >= 1, above, pads)
        below = pltpu.roll(field[:, col * LANES : (col + 1) * LANES], LANES - width, 1)
        start = (rows + 1) * stride + LANES + col * LANES
        ext_ref[:, start : start + LANES] = jnp.where(band < bands - 1, below, pads)


def fold_ext(ext_ref, rows, cols, bands):
    width = LANES // bands
    band = lane_band(bands)
    stride = (cols + 2) * LANES
    pieces = []
    for row in range(rows):
        start = (row + 1) * stride + LANES
        piece = ext_ref[:, start : start + cols * LANES]
        if row == 0:
            blocks = []
            for col in range(cols):
                start = (rows + 1) * stride + LANES + col * LANES
                moved = pltpu.roll(ext_ref[:, start : start + LANES], width, 1)
                blocks.append(jnp.where(band >= 1, moved, 0.0))
            piece = piece + jnp.concatenate(blocks, axis=1)
        if row == rows - 1:
            blocks = []
            for col in range(cols):
                start = LANES + col * LANES
                moved = pltpu.roll(ext_ref[:, start : start + LANES], LANES - width, 1)
                blocks.append(jnp.where(band < bands - 1, moved, 0.0))
            piece = piece + jnp.concatenate(blocks, axis=1)
        pieces.append(piece)
    return pieces


def window(cols, row, first_col, tap, turned=False):
    dy, dx = tap // 3, tap % 3
    if turned:
        dy, dx = 2 - dy, 2 - dx
    return ((row + dy) * (cols + 2) + first_col + dx) * LANES


def place_of(step, chunk, cols):
    per_row = cols * LANES // chunk
    return step // per_row, lax.rem(step, per_row) * (chunk // LANES), pl.ds(pl.multiple_of(step * chunk, chunk), chunk)


def gather_cols(ext_ref, cols, row, first_col, size, turned=False):
    starts = [window(cols, row, first_col, tap, turned) for tap in range(9)]
    starts = [s if isinstance(s, int) else pl.multiple_of(s, LANES) for s in starts]
    return jnp.concatenate([ext_ref[:, pl.ds(s, size)] for s in starts], axis=0).astype(BF16)


def scatter_cols(ext_ref, values, cols, row, first_col, size, turned=False):
    height = ext_ref.shape[0]
    for tap in range(9):
        start = window(cols, row, first_col, tap, turned)
        if not isinstance(start, int):
            start = pl.multiple_of(start, LANES)
        at = pl.ds(start, size)
        ext_ref[:, at] = ext_ref[:, at] + values[tap * height : (tap + 1) * height]


def mix(matrix_ref, field_ref, start, size, pairs):
    total = None
    for j in pairs:
        term = matrix_ref[:, j : j + 1] * field_ref[j : j + 1, start : start + size]
        total = term if total is None else total + term
    return total


def log_sigmoid(value):
    return jnp.minimum(value, 0.0) - jnp.log1p(jnp.exp(-jnp.abs(value)))


def sigmoid_minus(value):
    power = jnp.exp(-jnp.abs(value))
    return jnp.where(value >= 0.0, power, 1.0) / (1.0 + power)


def row_mask(height, period, valid):
    return lax.rem(lax.broadcasted_iota(jnp.int32, (height, 1), 0), period) < valid


def fold_lanes(value):
    total = value[:, :LANES]
    for start in range(LANES, value.shape[1], LANES):
        total = total + value[:, start : start + LANES]
    return total


def unpack_kernel(
    dims,
    index_ref,
    b0,
    b1,
    b2,
    b3,
    chan1_ref,
    m1_ref,
    chan2_ref,
    m2_ref,
    y1_ref,
    mix1_ref,
    mask_ref,
    mask2_ref,
    keep_ref,
    y2_ref,
    mix2_ref,
    bufs,
    xs,
):
    rows, cols, bands = dims
    own = index_ref[0]
    width = LANES // bands
    band = lane_band(bands)
    groups = cols // bands
    for d, ref in enumerate((b0, b1, b2, b3)):
        bufs[d, :, :] = ref[...].astype(F32)
    xs[...] = jnp.zeros_like(xs)
    for s in range(rows):
        for a in range(groups):
            loads = [bufs[d, pl.ds(s * groups + a, CH + 1, stride=rows * groups), :] for d in range(bands)]
            for e in range(bands):
                total = jnp.zeros((CH + 1, LANES), F32)
                for d in range(bands):
                    origin = own ^ d
                    shift = lax.rem(origin - e + bands, bands) * width
                    total = jnp.where(band == origin, pltpu.roll(loads[d], shift, 1), total)
                start = (s * cols + bands * a + e) * LANES
                xs[0 : CH + 1, start : start + LANES] = total
    line = cols * LANES
    for s in range(rows):
        at = slice(s * line, (s + 1) * line)
        mask_ref[:, at] = xs[CH : CH + 1, at]
        raw = xs[:, at]
        source = (raw + 0.5) / 256.0 - 0.5
        y1_ref[:, at] = (source + chan1_ref[:, 0:1]) * chan1_ref[:, 1:2]
    for s in range(rows):
        at = slice(s * line, (s + 1) * line)
        mix1_ref[:, at] = mix(m1_ref, y1_ref, s * line, line, range(CH))
    half_rows, half_cols = rows // 2, cols // 2
    for i in range(half_rows):
        for j in range(half_cols):
            at = slice((i * half_cols + j) * LANES, (i * half_cols + j + 1) * LANES)
            masks = None
            for p in range(4):
                di, dj = p // 2, p % 2
                start = ((2 * i + di) * cols + 2 * j + dj) * LANES
                keep_ref[p * 8 : p * 8 + 8, at] = mix1_ref[0:8, start : start + LANES]
                block = mask_ref[:, start : start + LANES]
                masks = block if masks is None else jnp.minimum(masks, block)
            mask2_ref[:, at] = masks
    size = half_rows * half_cols * LANES
    y2_ref[...] = (keep_ref[...] + chan2_ref[:, 0:1]) * chan2_ref[:, 1:2]
    pairs = [j for j in range(32) if j % 8 < 6]
    mix2_ref[...] = mix(m2_ref, y2_ref, 0, size, pairs)


def couple_two_forward(
    dims,
    mix2_ref,
    mask_ref,
    mask2_ref,
    chan2_ref,
    et_ref,
    wb_ref,
    f_ref,
    bias_ref,
    out2_ref,
    t2_ref,
    xcol_ref,
    h1_ref,
    h2_ref,
    loss_ref,
    ext,
    oacc,
):
    half_rows, half_cols, bands = dims
    mixed = mix2_ref[...]
    out2_ref[0:16, :] = mixed[:16]
    iota = lax.broadcasted_iota(jnp.int32, (16, 1), 0)
    ones = jnp.where(iota == CH, 1.0, 0.0)
    fill_ext(ext, mixed[:16] + ones, half_rows, half_cols, bands, ones)
    oacc[...] = jnp.zeros_like(oacc)
    chunk = half_cols * LANES
    xcol = jnp.concatenate([gather_cols(ext, half_cols, i, 0, chunk) for i in range(half_rows)], axis=1)
    xcol_ref[...] = xcol
    hidden = jnp.maximum(dot(et_ref[...], xcol).astype(BF16), jnp.zeros((), BF16))
    h1_ref[...] = hidden
    hidden = jnp.maximum((dot(wb_ref[...], hidden) + bias_ref[...]).astype(BF16), jnp.zeros((), BF16))
    h2_ref[...] = hidden
    outputs = dot(f_ref[...], hidden)
    for i in range(half_rows):
        scatter_cols(oacc, outputs[:, i * chunk : (i + 1) * chunk], half_cols, i, 0, chunk, True)
    output = jnp.concatenate(fold_ext(oacc, half_rows, half_cols, bands), axis=1) + chan2_ref[:, 2:3]
    second = output[16:] + 2.0
    t2_ref[...] = second
    scale_log = log_sigmoid(second)
    result = (mixed[16:] + output[:16]) * jnp.exp(scale_log)
    out2_ref[16:, :] = result
    valid = row_mask(16, 16, CH)
    per_pixel = jnp.where(valid, scale_log - 0.5 * (mixed[:16] * mixed[:16] + result * result), 0.0)
    mask2 = mask2_ref[...]
    loss_ref[...] = jnp.zeros_like(loss_ref)
    loss_ref[0:1, :] = jnp.sum(fold_lanes(per_pixel * mask2), axis=0, keepdims=True)
    loss_ref[1:2, :] = fold_lanes(mask2)
    loss_ref[2:3, :] = fold_lanes(mask_ref[...])


def part_out(slab_ref, first, size, index, bit, kept_ref, sent_ref):
    half = size // 2
    high = lax.rem(index // bit, 2)
    kept_ref[...] = slab_ref[pl.ds(pl.multiple_of(first + high * half, 8), half), :]
    sent_ref[...] = slab_ref[pl.ds(pl.multiple_of(first + (1 - high) * half, 8), half), :]


def gram(left, right_ref, pairs, acc_ref):
    for j in pairs:
        acc_ref[j, :, :] = acc_ref[j, :, :] + fold_lanes(left * right_ref[j : j + 1, :])


def couple_two_backward(
    dims,
    bit,
    index_ref,
    mask2_ref,
    y2_ref,
    out2_ref,
    t2_ref,
    xcol_ref,
    h1_ref,
    h2_ref,
    chan2_ref,
    m2t_ref,
    e_ref,
    wbt_ref,
    ft_ref,
    kept_ref,
    sent_ref,
    small_ref,
    gkeep_ref,
    ext,
    gacc,
    gmix,
    bacc,
    ge,
    gf,
    acc,
    slab_ref,
):
    rows, cols, bands = dims
    weight = -mask2_ref[...]
    second = t2_ref[...]
    result = out2_ref[16:, :]
    g_result = -weight * result
    g_log = g_result * result + weight
    g_second = g_log * sigmoid_minus(second)
    g_half = g_result * jnp.exp(log_sigmoid(second))
    gmix[0:16, :] = -weight * out2_ref[0:16, :]
    gmix[16:32, :] = g_half
    valid = row_mask(16, 16, CH)
    g_out = jnp.concatenate([g_half, jnp.where(valid, g_second, 0.0)], axis=0)
    g_out = g_out.astype(BF16).astype(F32)
    out_sums = fold_lanes(g_out)
    fill_ext(ext, g_out, rows, cols, bands, jnp.zeros((32, 1), F32))
    gacc[...] = jnp.zeros_like(gacc)
    chunk = cols * LANES
    gcol = jnp.concatenate([gather_cols(ext, cols, i, 0, chunk, True) for i in range(rows)], axis=1)
    hidden_two = h2_ref[...]
    hidden_one = h1_ref[...]
    g_pre = jnp.where(hidden_two > 0, dot(ft_ref[...], gcol).astype(BF16), jnp.zeros((), BF16))
    gf[...] = dot_nt(gcol, hidden_two)
    g_wb = dot_nt(g_pre, hidden_one)
    for block in range(HID // LANES):
        slab_ref[block * HID : (block + 1) * HID, :] = g_wb[:, block * LANES : (block + 1) * LANES]
    bacc[...] = fold_lanes(g_pre.astype(F32))
    g_pre = jnp.where(hidden_one > 0, dot(wbt_ref[...], g_pre).astype(BF16), jnp.zeros((), BF16))
    ge[...] = dot_nt(xcol_ref[...], g_pre)
    inputs = dot(e_ref[...], g_pre)
    for i in range(rows):
        scatter_cols(gacc, inputs[:, i * chunk : (i + 1) * chunk], cols, i, 0, chunk)
    slab_ref[TWO_B:TWO_ROWS, :] = jnp.zeros((TWO_ROWS - TWO_B, LANES), F32)
    put_rows(slab_ref, lambda block: TWO_B + block, ones_sum(bacc), 0, 1)
    for piece in range(18):
        put_rows(slab_ref, lambda block: TWO_F + block * 216 + piece * CH, gf, piece * 16, CH)
    put_rows(slab_ref, lambda block: TWO_E + block * 144, ge, 0, 144)
    gmix[0:16, :] += jnp.concatenate(fold_ext(gacc, rows, cols, bands), axis=1)
    pairs = [j for j in range(32) if j % 8 < 6]
    g_mixed = gmix[...]
    acc[...] = jnp.zeros_like(acc)
    gram(g_mixed, y2_ref, pairs, acc)
    stack = [(j, acc[j]) for j in pairs] + [(32, fold_lanes(g_mixed)), (33, out_sums)]
    small_ref[...] = lane_sums(stack, 32)
    part_out(slab_ref, 0, TWO_ROWS, index_ref[1], bit, kept_ref, sent_ref)
    valid_rows = [j for j in range(32) if j % 16 < CH]
    gkeep_ref[...] = mix(m2t_ref, gmix, 0, rows * chunk, valid_rows) * chan2_ref[:, 1:2]


def level_two_kernel(
    dims,
    bit,
    index_ref,
    b0,
    b1,
    b2,
    b3,
    chan1_ref,
    m1_ref,
    chan2_ref,
    m2_ref,
    m2t_ref,
    e_ref,
    et_ref,
    f_ref,
    ft_ref,
    wb_ref,
    wbt_ref,
    bias_ref,
    y1_ref,
    mix1_ref,
    mask_ref,
    mask2_ref,
    keep_ref,
    loss_ref,
    gkeep_ref,
    kept_ref,
    sent_ref,
    small_ref,
    bufs,
    xs,
    y2,
    mix2,
    out2,
    t2,
    xcol,
    h1,
    h2,
    ext_in,
    oacc,
    ext_out,
    gacc,
    gmix,
    bacc,
    ge,
    gf,
    acc,
    slab,
):
    rows, cols, bands = dims
    half = (rows // 2, cols // 2, bands)
    unpack_kernel(
        dims, index_ref, b0, b1, b2, b3, chan1_ref, m1_ref, chan2_ref, m2_ref,
        y1_ref, mix1_ref, mask_ref, mask2_ref, keep_ref, y2, mix2, bufs, xs,
    )
    couple_two_forward(
        half, mix2, mask_ref, mask2_ref, chan2_ref, et_ref, wb_ref, f_ref, bias_ref,
        out2, t2, xcol, h1, h2, loss_ref, ext_in, oacc,
    )
    couple_two_backward(
        half, bit, index_ref, mask2_ref, y2, out2, t2, xcol, h1, h2, chan2_ref, m2t_ref, e_ref, wbt_ref, ft_ref,
        kept_ref, sent_ref, small_ref, gkeep_ref, ext_out, gacc, gmix, bacc, ge, gf, acc, slab,
    )


def couple_one_forward(
    dims,
    chunk,
    mix1_ref,
    mask_ref,
    mask2_ref,
    keep_ref,
    gkeep_in_ref,
    chan1_ref,
    et_ref,
    wb_ref,
    f_ref,
    bias_ref,
    wp_ref,
    wpt_ref,
    pbias_ref,
    xcol_ref,
    h1_ref,
    h2_ref,
    res_ref,
    t_ref,
    gout_ref,
    gwp_ref,
    loss_ref,
    ext,
    oacc,
    kext,
    kcol,
    gkacc,
    drop,
):
    rows, cols, bands = dims
    iota = lax.broadcasted_iota(jnp.int32, (8, 1), 0)
    ones = jnp.where(iota == CH // 2, 1.0, 0.0)
    fill_ext(ext, mix1_ref[0:8, :] + ones, rows, cols, bands, ones)
    oacc[...] = jnp.zeros_like(oacc)

    @pl.loop(0, rows * cols * LANES // chunk)
    def _(step):
        row, col, at = place_of(step, chunk, cols)
        xcol = gather_cols(ext, cols, row, col, chunk)
        xcol_ref[:, at] = xcol
        hidden = jnp.maximum(dot(et_ref[...], xcol).astype(BF16), jnp.zeros((), BF16))
        h1_ref[:, at] = hidden
        hidden = jnp.maximum((dot(wb_ref[...], hidden) + bias_ref[...]).astype(BF16), jnp.zeros((), BF16))
        h2_ref[:, at] = hidden
        scatter_cols(oacc, dot(f_ref[...], hidden), cols, row, col, chunk, True)

    line = cols * LANES
    valid = row_mask(8, 8, CH // 2)
    step_total = None
    half_rows, half_cols = rows // 2, cols // 2
    for s, piece in enumerate(fold_ext(oacc, rows, cols, bands)):
        at = slice(s * line, (s + 1) * line)
        output = piece + chan1_ref[:, 2:3]
        second = output[8:] + 2.0
        t_ref[:, at] = second
        scale_log = log_sigmoid(second)
        result = (mix1_ref[8:16, at] + output[:8]) * jnp.exp(scale_log)
        res_ref[:, at] = result
        part = fold_lanes(jnp.where(valid, scale_log, 0.0) * mask_ref[:, at])
        step_total = part if step_total is None else step_total + part
    for i in range(half_rows):
        for j in range(half_cols):
            at = slice((i * half_cols + j) * LANES, (i * half_cols + j + 1) * LANES)
            for p in range(4):
                start = ((2 * i + p // 2) * cols + 2 * j + p % 2) * LANES
                drop[p * 8 : p * 8 + 8, at] = res_ref[:, start : start + LANES]
    part_iota = lax.broadcasted_iota(jnp.int32, (32, 1), 0)
    part_ones = jnp.where(part_iota == CH // 2, 1.0, 0.0)
    fill_ext(kext, keep_ref[...] + part_ones, half_rows, half_cols, bands, part_ones)
    part_line = half_cols * LANES
    gkacc[...] = jnp.zeros_like(gkacc)
    weight = -mask2_ref[...]
    valid = row_mask(32, 8, CH // 2)
    prior_total = None
    for i in range(half_rows):
        at = slice(i * part_line, (i + 1) * part_line)
        columns = gather_cols(kext, half_cols, i, 0, part_line)
        kcol[...] = columns
        prior = dot(wp_ref[...], columns) + pbias_ref[...]
        mean, logs = prior[:32], prior[32:]
        inverse = jnp.exp(-logs)
        scaled = (drop[:, at] - mean) * inverse
        part = fold_lanes((-logs - 0.5 * scaled * scaled) * mask2_ref[:, at])
        prior_total = part if prior_total is None else prior_total + part
        g_mean = weight[:, at] * scaled * inverse
        g_logs = jnp.where(valid, weight[:, at] * (scaled * scaled - 1.0), 0.0)
        drop[:, at] = -g_mean
        g_prior = jnp.concatenate([g_mean, g_logs], axis=0).astype(BF16)
        g_wp = dot_nt(g_prior, kcol[...])
        if i == 0:
            gwp_ref[...] = g_wp
        else:
            gwp_ref[...] += g_wp
        scatter_cols(gkacc, dot(wpt_ref[...], g_prior), half_cols, i, 0, part_line)
    loss_ref[...] = jnp.zeros_like(loss_ref)
    loss_ref[0:1, :] = jnp.sum(step_total, axis=0, keepdims=True) + jnp.sum(prior_total, axis=0, keepdims=True)
    for i, piece in enumerate(fold_ext(gkacc, half_rows, half_cols, bands)):
        at = slice(i * part_line, (i + 1) * part_line)
        g_keep = piece + gkeep_in_ref[:, at]
        g_drop = drop[:, at]
        for j in range(half_cols):
            inner = slice(j * LANES, (j + 1) * LANES)
            for p in range(4):
                start = ((2 * i + p // 2) * cols + 2 * j + p % 2) * LANES
                gout_ref[0:8, start : start + LANES] = g_keep[p * 8 : p * 8 + 8, inner]
                gout_ref[8:16, start : start + LANES] = g_drop[p * 8 : p * 8 + 8, inner]


def put_rows(slab_ref, first, values, row, count):
    for block in range(HID // LANES):
        start = first(block)
        slab_ref[start : start + count, :] = values[row : row + count, block * LANES : (block + 1) * LANES]


def lane_sums(stack, width):
    lane = lax.broadcasted_iota(jnp.int32, (1, LANES), 1)
    total = jnp.zeros(stack[0][1].shape, F32)
    for j, value in stack:
        total = total + jnp.where(lane == j, jnp.sum(value, axis=1, keepdims=True), 0.0)
    return total


def ones_sum(value_ref):
    return lax.dot_general(
        jnp.ones((8, LANES), F32), value_ref[...], (((1,), (1,)), ((), ())), precision=HIGH, preferred_element_type=F32
    )


def one_backward_top(
    dims,
    chunk,
    bits,
    index_ref,
    mask_ref,
    res_ref,
    t_ref,
    gout_ref,
    ft_ref,
    gwp_ref,
    loss_one_ref,
    loss_two_ref,
    h1_ref,
    h2_ref,
    gpre_ref,
    kept_a,
    sent_a,
    kept_b,
    sent_b,
    ghalf_ref,
    gbc_ref,
    ext,
    gft,
    gf,
    bacc,
    slab_ref,
):
    rows, cols, bands = dims
    weight = -mask_ref[...]
    second = t_ref[...]
    result = res_ref[...]
    g_result = gout_ref[8:16, :]
    g_log = g_result * result + weight
    g_second = g_log * sigmoid_minus(second)
    g_half = g_result * jnp.exp(log_sigmoid(second))
    ghalf_ref[...] = g_half
    valid = row_mask(8, 8, CH // 2)
    g_out = jnp.concatenate([g_half, jnp.where(valid, g_second, 0.0)], axis=0)
    g_out = g_out.astype(BF16).astype(F32)
    gbc_ref[...] = fold_lanes(g_out)
    fill_ext(ext, g_out, rows, cols, bands, jnp.zeros((16, 1), F32))
    gft[...] = jnp.zeros_like(gft)
    slab_ref[...] = jnp.zeros_like(slab_ref)
    bacc[...] = jnp.zeros_like(bacc)

    @pl.loop(0, rows * cols * LANES // chunk)
    def _(step):
        row, col, at = place_of(step, chunk, cols)
        gcol = gather_cols(ext, cols, row, col, chunk, True)
        hidden_two = h2_ref[:, at]
        g_pre = jnp.where(hidden_two > 0, dot(ft_ref[...], gcol).astype(BF16), jnp.zeros((), BF16))
        gft[...] += dot_nt(hidden_two, gcol)
        gpre_ref[:, at] = g_pre
        g_wb = dot_nt(g_pre, h1_ref[:, at])
        for block in range(HID // LANES):
            slab_ref[block * HID : (block + 1) * HID, :] += g_wb[:, block * LANES : (block + 1) * LANES]
        bacc[...] += fold_lanes(g_pre.astype(F32))

    for first, count in ((0, LANES), (LANES, 16)):
        gf[first : first + count, :] = gft[:, first : first + count].T
    bias = ones_sum(bacc)
    put_rows(slab_ref, lambda block: ONE_B + block, bias, 0, 1)
    for piece in range(18):
        put_rows(slab_ref, lambda block: ONE_F + block * 112 + piece * 6, gf, piece * 8, 6)
    for block in range(3):
        width = min(LANES, 288 - block * LANES)
        slab_ref[ONE_P + block * 64 : ONE_P + block * 64 + 64, 0:width] = gwp_ref[
            :, block * LANES : block * LANES + width
        ]
    scalars = [(0, loss_one_ref[0:1, :] + loss_two_ref[0:1, :]), (1, loss_two_ref[1:2, :]), (2, loss_two_ref[2:3, :])]
    slab_ref[ONE_LOSS : ONE_LOSS + 1, :] = lane_sums(scalars, 3)
    part_out(slab_ref, 0, PART_A, index_ref[1], bits[0], kept_a, sent_a)
    part_out(slab_ref, PART_A, ONE_ROWS - PART_A, index_ref[1], bits[1], kept_b, sent_b)


def one_backward_bottom(
    dims,
    chunk,
    y1_ref,
    ghalf_ref,
    gbc_ref,
    gout_ref,
    e_ref,
    wbt_ref,
    xcol_ref,
    h1_ref,
    gpre_ref,
    small_ref,
    slab_ref,
    gacc,
    gmix,
    ge,
    acc,
):
    rows, cols, bands = dims
    gacc[...] = jnp.zeros_like(gacc)
    ge[...] = jnp.zeros_like(ge)
    slab_ref[...] = jnp.zeros_like(slab_ref)

    @pl.loop(0, rows * cols * LANES // chunk)
    def _(step):
        row, col, at = place_of(step, chunk, cols)
        g_pre = jnp.where(h1_ref[:, at] > 0, dot(wbt_ref[...], gpre_ref[:, at]).astype(BF16), jnp.zeros((), BF16))
        ge[...] += dot_nt(xcol_ref[:, at], g_pre)
        scatter_cols(gacc, dot(e_ref[...], g_pre), cols, row, col, chunk)

    gmix[0:8, :] = gout_ref[0:8, :] + jnp.concatenate(fold_ext(gacc, rows, cols, bands), axis=1)
    gmix[8:16, :] = ghalf_ref[...]
    g_mixed = gmix[...]
    acc[...] = jnp.zeros_like(acc)
    gram(g_mixed, y1_ref, range(CH), acc)
    stack = [(j, acc[j]) for j in range(CH)] + [(16, fold_lanes(g_mixed)), (17, gbc_ref[...])]
    slab_ref[REST_SMALL : REST_SMALL + 16, :] = (
        lane_sums(stack, CH) + pltpu.roll(small_ref[0:16, :], 32, 1) + pltpu.roll(small_ref[16:32, :], 66, 1)
    )
    for tap in range(9):
        put_rows(slab_ref, lambda block: block * 56 + tap * 6, ge, tap * 8, 6)
    put_rows(slab_ref, lambda block: REST_A + block, ge, 6, 1)


def call(kernel, inputs, outputs, scratch, flops, aliases=None, far_in=(), far_out=()):
    whole = pl.BlockSpec(memory_space=pltpu.VMEM)
    smem = pl.BlockSpec(memory_space=pltpu.SMEM)
    far = pl.BlockSpec(memory_space=pl.ANY)
    traffic = sum(x.size * x.dtype.itemsize for x in list(inputs) + list(outputs))
    return pl.pallas_call(
        kernel,
        out_shape=outputs,
        in_specs=[
            far if k in far_in else smem if x.dtype == jnp.int32 and x.ndim == 1 else whole for k, x in enumerate(inputs)
        ],
        out_specs=[far if k in far_out else whole for k in range(len(outputs))],
        scratch_shapes=scratch,
        input_output_aliases=aliases or {},
        compiler_params=pltpu.CompilerParams(vmem_limit_bytes=VMEM_LIMIT),
        cost_estimate=pl.CostEstimate(flops=flops, bytes_accessed=traffic, transcendentals=0),
    )(*inputs)


def shape(dims, dtype=F32):
    return jax.ShapeDtypeStruct(tuple(dims), dtype)


def high_dot(left, right, contract=(1, 0)):
    return lax.dot_general(
        left, right, (((contract[0],), (contract[1],)), ((), ())), precision=HIGH, preferred_element_type=F32
    )


def iotas(height, width=LANES):
    return (
        lax.broadcasted_iota(jnp.int32, (height, width), 0),
        lax.broadcasted_iota(jnp.int32, (height, width), 1),
    )


def take_flat(flat_ref, start, length):
    row, offset = divmod(start, LANES)
    lane = lax.broadcasted_iota(jnp.int32, (1, LANES), 1)
    value = flat_ref[row : row + 1, :]
    if offset:
        value = pltpu.roll(value, LANES - offset, 1)
        if offset + length > LANES:
            after = pltpu.roll(flat_ref[row + 1 : row + 2, :], LANES - offset, 1)
            value = jnp.where(lane < LANES - offset, value, after)
    return jnp.where(lane < length, value, 0.0) if length < LANES else value


def put_flat(pieces, start, value, length):
    row, offset = divmod(start, LANES)
    lane = lax.broadcasted_iota(jnp.int32, (1, LANES), 1)
    if length < LANES:
        value = jnp.where(lane < length, value, 0.0)
    if offset:
        value = pltpu.roll(value, offset, 1)
    if offset + length > LANES:
        pieces.setdefault(row + 1, []).append(jnp.where(lane < offset, value, 0.0))
        value = jnp.where(lane >= offset, value, 0.0)
    pieces.setdefault(row, []).append(value)


def level_tables(flat_ref, level, lu):
    chans = CH * (level + 1)
    start = ONE_START - 4 * CH if level == 0 else TWO_START
    chan = [take_flat(flat_ref, start + k * chans, chans) for k in range(4)]
    first = start + 4 * chans + 2 * HID
    lu[...] = jnp.zeros_like(lu)
    for i in range(chans):
        lu[i : i + 1, :] = take_flat(flat_ref, first + i * chans, chans)
    row, lane = iotas(LANES)
    value = lu[...]
    inside = row < chans
    lower = jnp.where(row > lane, value, 0.0) + jnp.where((row == lane) & inside, 1.0, 0.0)
    upper = jnp.where(row < lane, value, 0.0) + jnp.where((row == lane) & inside, jnp.exp(chan[2]), 0.0)
    return chans, start, chan, lower, upper


def natural_row(level, row):
    height, half = (8, CH // 2) if level == 0 else (16, CH)
    return (row // height) * half + lax.rem(row, height), lax.rem(row, height) < half


def natural_keep(row):
    return 4 * lax.rem(row, 8) + row // 8, lax.rem(row, 8) < CH // 2


def pick(condition, value):
    return jnp.sum(jnp.where(condition, value, 0.0), axis=1, keepdims=True)


def prior_places():
    row, lane = iotas(64, 4 * CH)
    inner = lax.rem(row, 32)
    natural, valid = natural_keep(inner)
    return ((lane == natural + (row // 32) * 2 * CH) & valid).astype(F32).astype(BF16)


def prior_lanes(tap):
    row, lane = iotas(2 * CH)
    inner = lane - (tap * 32) % LANES
    natural = 4 * lax.rem(inner, 8) + inner // 8
    valid = (inner >= 0) & (inner < 32) & (lax.rem(inner, 8) < CH // 2)
    return ((row == natural) & valid).astype(F32).astype(BF16)


def prepare_level(level, flat_ref, entry_ref, middle_ref, exit_ref, outs, wide):
    e_ref, et_ref, f_ref, ft_ref, wb_ref, wbt_ref, bb_ref = outs
    chans = CH * (level + 1)
    start = 0 if level == 0 else TWO_START
    half, tall = chans // 2, 8 * (level + 1)
    first_in, first_out = (0, 0) if level == 0 else (CH // 2, CH)
    wide[...] = jnp.zeros_like(wide)
    for tap in range(9):
        wide[tap * tall : tap * tall + half, :] = entry_ref[tap, first_in : first_in + half, :]
    row, lane = iotas(LANES)
    for block in range(HID // LANES):
        at = slice(block * LANES, (block + 1) * LANES)
        value = take_flat(flat_ref, start + 4 * chans + block * LANES, LANES)
        for tap in range(3):
            part = value.astype(BF16).astype(F32)
            wide[tap * tall + half : tap * tall + half + 1, at] = part
            value = value - part
        value = take_flat(flat_ref, start + 4 * chans + HID + block * LANES, LANES)
        bb_ref[at, :] = pick(row == lane, value)
    count = 9 * tall
    padded = -(-count // LANES) * LANES
    e_ref[...] = wide[0:count, :].astype(BF16)
    et_ref[...] = wide[0:padded, :].T[:, 0:count].astype(BF16)
    wide[...] = jnp.zeros_like(wide)
    for tap in range(9):
        for side in range(2):
            first = (tap * 2 + side) * tall
            wide[first : first + half, :] = exit_ref[tap, first_out + side * half : first_out + (side + 1) * half, :]
    count = 18 * tall
    padded = -(-count // LANES) * LANES
    f_ref[...] = wide[0:count, :].astype(BF16)
    ft_ref[...] = wide[0:padded, :].T[:, 0:count].astype(BF16)
    wb_ref[...] = middle_ref[level].astype(BF16)
    wbt_ref[...] = middle_ref[level].T.astype(BF16)


def prepare_kernel(
    flat_ref,
    prior_far,
    entry_far,
    middle_far,
    exit_far,
    chan1_ref,
    m1_ref,
    chan2_ref,
    m2_ref,
    m2t_ref,
    wp_ref,
    wpt_ref,
    pbias_ref,
    *refs,
):
    outs_two, outs_one = refs[:7], refs[7:14]
    lu, wide, entry_ref, middle_ref, exit_ref, prior_ref, sems = refs[14:]
    pieces = [(middle_far, middle_ref, (1, slice(k * LANES, (k + 1) * LANES))) for k in range(4)]
    pieces += [(exit_far, exit_ref, (slice(3 * k, 3 * k + 3),)) for k in range(3)]
    pieces += [(entry_far, entry_ref, (slice(3 * k, 3 * k + 3),)) for k in range(3)]
    pieces += [(middle_far, middle_ref, (0, slice(k * LANES, (k + 1) * LANES))) for k in range(4)]
    pieces += [(prior_far, prior_ref, (slice(0, 9),))]
    copies = [
        pltpu.make_async_copy(source.at[at], target.at[at], sems.at[k]) for k, (source, target, at) in enumerate(pieces)
    ]
    for copy in copies:
        copy.start()
    for level in range(2):
        chans, start, chan, lower, upper = level_tables(flat_ref, level, lu)
        product = high_dot(lower, upper)
        height = 16 * (level + 1)
        row, lane = iotas(height)
        natural, valid = natural_row(level, row)
        spread = ((lane == chans - 1 - natural) & valid).astype(F32)
        matrix = high_dot(spread, product)
        out_bias = pick((lane == natural) & valid, chan[3])
        if level == 0:
            m1_ref[...] = matrix
            shift, scale = pick(lane == row, chan[0]), pick((lane == row) & (row < CH), jnp.exp(chan[1]))
        else:
            source, target = iotas(LANES)
            place, used = natural_keep(target)
            matrix = high_dot(matrix, ((source == place) & used & (target < 32)).astype(F32))
            m2_ref[...] = matrix
            lu[...] = jnp.zeros_like(lu)
            lu[0:32, :] = matrix
            m2t_ref[...] = lu[...].T[0:32, :]
            place, used = natural_keep(row)
            shift = pick((lane == place) & used, chan[0])
            scale = pick((lane == place) & used, jnp.exp(chan[1]))
        chan_ref = chan1_ref if level == 0 else chan2_ref
        chan_ref[...] = (
            jnp.where(lane == 0, shift, 0.0) + jnp.where(lane == 1, scale, 0.0) + jnp.where(lane == 2, out_bias, 0.0)
        )
    copies[14].wait()
    places = prior_places()
    blocks = [None] * 3
    for tap in range(9):
        moved = dot_nt(places, prior_ref[tap].astype(BF16)).astype(BF16)
        part = dot(moved, prior_lanes(tap))
        block = tap * 32 // LANES
        blocks[block] = part if blocks[block] is None else blocks[block] + part
    lu[...] = jnp.zeros_like(lu)
    for block, value in enumerate(blocks):
        width = min(LANES, 288 - block * LANES)
        at = slice(block * LANES, block * LANES + width)
        wp_ref[:, at] = value[:, 0:width].astype(BF16)
        lu[0:64, :] = value
        wpt_ref[at, :] = lu[...].T[0:width, 0:64].astype(BF16)
    row, lane = iotas(64)
    natural, valid = natural_keep(lax.rem(row, 32))
    pbias_ref[...] = pick((lane == natural + (row // 32) * 2 * CH) & valid, take_flat(flat_ref, PRIOR_START, 4 * CH))
    for copy in copies[:10]:
        copy.wait()
    prepare_level(1, flat_ref, entry_ref, middle_ref, exit_ref, outs_two, wide)
    for copy in copies[10:14]:
        copy.wait()
    prepare_level(0, flat_ref, entry_ref, middle_ref, exit_ref, outs_one, wide)


def adamw(weight, grad, first, second):
    first_new = BETA_ONE * first + (1.0 - BETA_ONE) * grad
    second_new = BETA_TWO * second + (1.0 - BETA_TWO) * grad * grad
    first_hat = first_new * (1.0 / (1.0 - BETA_ONE**ADAM_STEP))
    second_hat = second_new * (1.0 / (1.0 - BETA_TWO**ADAM_STEP))
    updated = weight - LEARN_RATE * (first_hat / (jnp.sqrt(second_hat) + ADAM_EPS) + WEIGHT_DECAY * weight)
    return (updated, second_new)


def finish_kernel(
    two_ref,
    one_ref,
    rest_ref,
    low_ref,
    extra_ref,
    flat_ref,
    flat_first,
    flat_second,
    *refs,
):
    far_in, refs = refs[:12], refs[12:]
    (loss_ref, norm_ref, flat_new, flat_grad, flat_moment), refs = refs[:5], refs[5:]
    far_out, refs = refs[:12], refs[12:]
    bias_ref, two, one, rest, lu = refs[:5]
    held, (in_sems, out_sems) = refs[5:21], refs[21:]
    weights, firsts, seconds, grads = held[0:4], held[4:8], held[8:12], held[12:16]
    entry_grad, _, exit_grad, prior_grad = grads
    jobs = [(1, 0), (1, 1), (2, None), (0, None), (3, None)]

    def part(ref, level):
        return ref if level is None else ref.at[level]

    def copies_in(k):
        group, level = jobs[k]
        return [
            pltpu.make_async_copy(part(far_in[3 * group + j], level), part(near[group], level), in_sems.at[k, j])
            for j, near in enumerate((weights, firsts, seconds))
        ]

    def copies_out(k):
        group, level = jobs[k]
        return [
            pltpu.make_async_copy(part(near[group], level), part(far_out[3 * group + j], level), out_sems.at[k, j])
            for j, near in enumerate((weights, grads, seconds))
        ]

    for k in range(len(jobs)):
        for copy in copies_in(k):
            copy.start()
    extra = extra_ref[...].astype(F32)
    _, lane = iotas(extra.shape[0])
    log_total, count_two, count = (jnp.sum(jnp.where(lane == k, extra, 0.0), keepdims=True) for k in range(3))
    coef = -1.0 / (CH * count * math.log(2.0))
    factor = -coef
    two[...] = two_ref[WB_ROWS:, :].astype(F32) * factor
    one[...] = one_ref[WB_ROWS:, :].astype(F32) * factor
    rest[...] = (rest_ref[...].astype(F32) + low_ref[...].astype(F32)) * factor
    base = WB_ROWS
    squares = []
    pieces = {}
    consts = []
    for level in range(2):
        chans, start, chan, lower, upper = level_tables(flat_ref, level, lu)
        consts.append(jnp.sum(chan[1] + chan[2], keepdims=True))
        weight = coef * count if level == 0 else coef * count_two
        height = 16 * (level + 1)
        small = rest[REST_SMALL : REST_SMALL + 16, :]
        if level == 1:
            small = jnp.concatenate([pltpu.roll(small, LANES - 32, 1), pltpu.roll(small, LANES - 66, 1)], axis=0)
        sum_lane = 16 * (level + 1)
        product = high_dot(lower, upper)
        row, lane = iotas(LANES, height)
        natural, valid = natural_row(level, lane)
        turned = high_dot(((row == chans - 1 - natural) & valid).astype(F32), small)
        row, lane = iotas(LANES)
        g_product = jnp.where(lane < sum_lane, turned, 0.0)
        if level == 1:
            place, used = natural_keep(row)
            g_product = high_dot(g_product, ((lane == place) & used & (row < 32)).astype(F32))
        else:
            g_product = jnp.where(lane < chans, g_product, 0.0)
        g_lower = high_dot(g_product, upper, (1, 1))
        g_upper = high_dot(lower.T, g_product)
        g_lu = jnp.where(row > lane, g_lower, 0.0) + jnp.where(row < lane, g_upper, 0.0)
        diagonal = jnp.sum(jnp.where(row == lane, g_upper, 0.0), axis=0, keepdims=True)
        shift = jnp.sum(turned[:, sum_lane : sum_lane + 1] * product, axis=0, keepdims=True)
        scale = jnp.sum(product * g_product, axis=0, keepdims=True)
        row, lane = iotas(height)
        natural, valid = natural_row(level, row)
        out_bias = jnp.where((lane == natural) & valid, small[:, sum_lane + 1 : sum_lane + 2], 0.0)
        put_flat(pieces, start, shift * jnp.exp(chan[1]), chans)
        put_flat(pieces, start + chans, scale + weight, chans)
        put_flat(pieces, start + 2 * chans, diagonal * jnp.exp(chan[2]) + weight, chans)
        put_flat(pieces, start + 3 * chans, jnp.sum(out_bias, axis=0, keepdims=True), chans)
        for i in range(chans):
            put_flat(pieces, start + 4 * chans + 2 * HID + i * chans, g_lu[i : i + 1, :], chans)
        for block in range(HID // LANES):
            if level == 0:
                value_a = rest[REST_A + block : REST_A + block + 1, :]
                value_b = one[ONE_B - base + block : ONE_B - base + block + 1, :]
            else:
                at = TWO_E - base + block * 144 + CH
                value_a = two[at : at + 1, :]
                value_b = two[TWO_B - base + block : TWO_B - base + block + 1, :]
            at = start + 4 * chans + block * LANES
            put_flat(pieces, at, value_a, LANES)
            put_flat(pieces, at + HID, value_b, LANES)
            bias_ref[2 * level : 2 * level + 1, block * LANES : (block + 1) * LANES] = value_a
            bias_ref[2 * level + 1 : 2 * level + 2, block * LANES : (block + 1) * LANES] = value_b
    row, lane = iotas(64)
    natural, valid = natural_keep(lax.rem(row, 32))
    column = one[ONE_P - base : ONE_P - base + 64, CH // 2 : CH // 2 + 1]
    prior_bias = jnp.where((lane == natural + (row // 32) * 2 * CH) & valid, column, 0.0)
    put_flat(pieces, PRIOR_START, jnp.sum(prior_bias, axis=0, keepdims=True), 4 * CH)
    for r in range(FLAT_ROWS):
        parts = pieces.get(r, [jnp.zeros((1, LANES), F32)])
        flat_grad[r : r + 1, :] = functools.reduce(jnp.add, parts)
    for tap in range(9):
        for block in range(HID // LANES):
            at = slice(block * LANES, (block + 1) * LANES)
            first = block * 56 + tap * 6
            entry_grad[tap, 0:6, at] = rest[first : first + 6, :]
            first = TWO_E - base + block * 144 + tap * 16
            entry_grad[tap, 6:18, at] = two[first : first + CH, :]
            first = ONE_F - base + block * 112 + tap * CH
            exit_grad[tap, 0:CH, at] = one[first : first + CH, :]
            first = TWO_F - base + block * 216 + tap * 2 * CH
            exit_grad[tap, CH : 3 * CH, at] = two[first : first + 2 * CH, :]
    places = prior_places()
    for tap in range(9):
        first = ONE_P + (tap * 32 // LANES) * 64
        moved = dot_nt(prior_lanes(tap), one_ref[first : first + 64, :]).astype(BF16)
        prior_grad[tap, :, :] = dot(moved, places) * factor
    for ref in (flat_grad, entry_grad, exit_grad, prior_grad):
        value = ref[...]
        squares.append(jnp.sum(value * value, keepdims=True).reshape(1, 1))
    for ref in (one_ref, two_ref):
        total = jnp.zeros((64, LANES), F32)
        for start in range(0, WB_ROWS, 64):
            value = ref[start : start + 64, :].astype(F32)
            total = total + value * value
        squares.append(jnp.sum(total, keepdims=True) * factor * factor)
    norm = jnp.sqrt(functools.reduce(jnp.add, squares))
    clip = jnp.minimum(1.0, CLIP_NORM / (norm + 1e-06))
    total = log_total + consts[0] * count + count_two * (consts[1] - 2 * CH * LOG_TWO_PI)
    loss_ref[...] = coef * total + 8.0
    norm_ref[...] = norm
    bias_ref[...] = bias_ref[...] * clip

    middle_factor = factor * clip
    value = flat_grad[...] * clip
    flat_grad[...] = value
    flat_new[...], flat_moment[...] = adamw(flat_ref[...], value, flat_first[...], flat_second[...])
    size = 64
    for k, (group, level) in enumerate(jobs):
        for copy in copies_in(k):
            copy.wait()
        weight, first, second, grad = weights[group], firsts[group], seconds[group], grads[group]
        if level is None:
            for tap in range(9):
                value = grad[tap] * clip
                grad[tap] = value
                weight[tap], second[tap] = adamw(weight[tap], value, first[tap], second[tap])
        else:
            slab = (one_ref, two_ref)[level]

            @pl.loop(0, HID // size)
            def _(j):
                rows = pl.ds(pl.multiple_of(j * size, size), size)
                for block in range(HID // LANES):
                    at = (level, rows, slice(block * LANES, (block + 1) * LANES))
                    value = slab[pl.ds(pl.multiple_of(block * HID + j * size, size), size), :].astype(F32) * middle_factor
                    grad[at] = value
                    weight[at], second[at] = adamw(weight[at], value, first[at], second[at])

        for copy in copies_out(k):
            copy.start()
    for k in range(len(jobs)):
        for copy in copies_out(k):
            copy.wait()


def on_device(
    pixels,
    valid_mask,
    vectors,
    vectors_first,
    vectors_second,
    entry_taps,
    entry_first,
    entry_second,
    middle,
    middle_first,
    middle_second,
    exit_taps,
    exit_first,
    exit_second,
    prior_taps,
    prior_first,
    prior_second,
):
    bands = lax.axis_size("rows")
    rows, cols = valid_mask.shape[0], valid_mask.shape[1]
    dims = (rows, cols, bands)
    size = rows * cols * LANES
    part = size // 4
    batches = lax.axis_size("batch")
    devices = batches * bands
    bits = [2**k for k in range((devices - 1).bit_length())]
    index = lax.axis_index("batch") * bands + lax.axis_index("rows")
    own = jnp.stack([lax.axis_index("rows"), index]).astype(jnp.int32)

    def trade(value, bit):
        return lax.ppermute(value, ("batch", "rows"), [(i, i ^ bit) for i in range(devices)])

    def in_hbm(value):
        return pltpu.with_memory_space_constraint(value, pltpu.HBM)

    def after(value, *done):
        return lax.optimization_barrier((value, *done))[0]

    piece_rows = (CH + 1) * rows * cols // bands
    pieces = call(
        functools.partial(pack_kernel, bands),
        (own, in_hbm(pixels.reshape(-1, LANES)), in_hbm(valid_mask.reshape(-1, LANES))),
        [shape((piece_rows, LANES), BF16)] * bands,
        [],
        1000,
    )
    bufs = [pieces[0]]
    for d in range(1, bands):
        bufs.append(lax.ppermute(pieces[d], "rows", [(i, i ^ d) for i in range(bands)]))

    def flat(value):
        return jnp.pad(value, (0, FLAT_ROWS * LANES - VEC)).reshape(FLAT_ROWS, LANES)

    vectors_flat = flat(vectors)

    def level_shapes(tall):
        return [
            shape((9 * tall, HID), BF16),
            shape((HID, 9 * tall), BF16),
            shape((18 * tall, HID), BF16),
            shape((HID, 18 * tall), BF16),
            shape((HID, HID), BF16),
            shape((HID, HID), BF16),
            shape((HID, 1)),
        ]

    prior_turned = jnp.swapaxes(prior_taps, 1, 2)
    (
        chan_one, m_one, chan_two, m_two, m_two_t, wp, wpt, prior_bias,
        e_two, e_two_t, f_two, f_two_t, wb_two, wb_two_t, bb_two,
        e_one, e_one_t, f_one, f_one_t, wb_one, wb_one_t, bb_one,
    ) = call(
        prepare_kernel,
        (after(vectors_flat, pieces[0]), in_hbm(prior_turned), in_hbm(entry_taps), in_hbm(middle), in_hbm(exit_taps)),
        [shape((16, LANES)), shape((16, LANES)), shape((32, LANES)), shape((32, LANES)), shape((32, LANES))]
        + [shape((64, 288), BF16), shape((288, 64), BF16), shape((64, 1))]
        + level_shapes(16)
        + level_shapes(8),
        [
            pltpu.VMEM((LANES, LANES), F32),
            pltpu.VMEM((384, HID), F32),
            pltpu.VMEM(entry_taps.shape, F32),
            pltpu.VMEM(middle.shape, F32),
            pltpu.VMEM(exit_taps.shape, F32),
            pltpu.VMEM(prior_turned.shape, F32),
            pltpu.SemaphoreType.DMA((15,)),
        ],
        10**9,
        far_in=(1, 2, 3, 4),
    )


    ext_lanes = (rows // 2 + 2) * (cols // 2 + 2) * LANES
    first_bit, second_bit, third_bit, fourth_bit = bits[0], bits[2], bits[1], bits[3]
    half_two = shape((TWO_ROWS // 2, LANES))
    (y1, mixed_one, mask, mask2, keep, loss_two, gkeep_two, kept_two, sent_two, small_two) = call(
        functools.partial(level_two_kernel, dims, second_bit),
        (
            own, *bufs, chan_one, m_one, chan_two, m_two, m_two_t,
            e_two, e_two_t, f_two, f_two_t, wb_two, wb_two_t, bb_two,
        ),
        [
            shape((16, size)),
            shape((16, size)),
            shape((1, size)),
            shape((1, part)),
            shape((32, part)),
            shape((8, LANES)),
            shape((32, part)),
        ]
        + [half_two] * 2
        + [shape((32, LANES))],
        [
            pltpu.VMEM((bands, piece_rows, LANES), F32),
            pltpu.VMEM((16, size), F32),
            pltpu.VMEM((32, part), F32),
            pltpu.VMEM((32, part), F32),
            pltpu.VMEM((32, part), F32),
            pltpu.VMEM((16, part), F32),
            pltpu.VMEM((144, part), BF16),
            pltpu.VMEM((HID, part), BF16),
            pltpu.VMEM((HID, part), BF16),
            pltpu.VMEM((16, ext_lanes), F32),
            pltpu.VMEM((32, ext_lanes), F32),
            pltpu.VMEM((32, ext_lanes), F32),
            pltpu.VMEM((16, ext_lanes), F32),
            pltpu.VMEM((32, part), F32),
            pltpu.VMEM((HID, LANES), F32),
            pltpu.VMEM((144, HID), F32),
            pltpu.VMEM((288, HID), F32),
            pltpu.VMEM((32, 32, LANES), F32),
            pltpu.VMEM((TWO_ROWS, LANES), F32),
        ],
        6 * HID * part * (144 + HID + 288),
    )
    whole_lanes = (rows + 2) * (cols + 2) * LANES
    chunk = min(2048, size)
    fwd_in = (
        mixed_one,
        mask,
        mask2,
        keep,
        gkeep_two,
        chan_one,
        e_one_t,
        wb_one,
        f_one,
        bb_one,
        wp,
        wpt,
        prior_bias,
    )
    fwd_out = [
        shape((72, size), BF16),
        shape((HID, size), BF16),
        shape((HID, size), BF16),
        shape((8, size)),
        shape((8, size)),
        shape((16, size)),
        shape((64, 288)),
        shape((8, LANES)),
    ]
    (xcol_one, h1_one, h2_one, res_one, t_one, gout_one, gwp, loss_one) = call(
        functools.partial(couple_one_forward, dims, chunk),
        fwd_in,
        fwd_out,
        [
            pltpu.VMEM((8, whole_lanes), F32),
            pltpu.VMEM((16, whole_lanes), F32),
            pltpu.VMEM((32, ext_lanes), F32),
            pltpu.VMEM((288, cols // 2 * LANES), BF16),
            pltpu.VMEM((32, ext_lanes), F32),
            pltpu.VMEM((32, part), F32),
        ],
        2 * HID * size * (72 + HID + 144),
    )
    top_in = (own, mask, res_one, t_one, gout_one, f_one_t, gwp, loss_one, loss_two, h1_one, h2_one)
    half_a, half_b = shape((PART_A // 2, LANES)), shape(((ONE_ROWS - PART_A) // 2, LANES))
    top_out = [shape((HID, size), BF16), half_a, half_a, half_b, half_b, shape((8, size)), shape((16, LANES))]
    (gpre, kept_a, sent_a, kept_b, sent_b, ghalf, gbc) = call(
        functools.partial(one_backward_top, dims, chunk, (second_bit, third_bit)),
        top_in,
        top_out,
        [
            pltpu.VMEM((16, whole_lanes), F32),
            pltpu.VMEM((HID, 144), F32),
            pltpu.VMEM((144, HID), F32),
            pltpu.VMEM((HID, LANES), F32),
            pltpu.VMEM((ONE_ROWS, LANES), F32),
        ],
        2 * HID * size * (144 + HID + 144),
        aliases={10: 0},
    )

    def halve(parts, bit, *beside):
        high = (index // bit) % 2
        halves = [x.shape[0] // 2 for x in parts]
        sent = [lax.dynamic_slice_in_dim(x, (1 - high) * h, h, 0) for x, h in zip(parts, halves)]
        kept = [lax.dynamic_slice_in_dim(x, high * h, h, 0) for x, h in zip(parts, halves)]
        got = after(trade(jnp.concatenate(sent) if len(sent) > 1 else sent[0], bit), *beside)
        results, first = [], 0
        for x, h in zip(kept, halves):
            results.append(x + got[first : first + h])
            first += h
        return results

    def exchange(parts, near_parts, far_parts, near, far_bit):
        code = 2 * ((index // near) % 2) + (index // far_bit) % 2
        sizes = [x.shape[0] // 4 for x in parts]

        def pieces_for(partner):
            return [lax.dynamic_slice_in_dim(x, (code ^ partner) * h, h, 0) for x, h in zip(parts, sizes)]

        totals = pieces_for(0)
        others = []
        for partner, bit, more in ((2, near, near_parts), (1, far_bit, far_parts), (3, near | far_bit, [])):
            high = (index // bit) % 2
            halves = [x.shape[0] // 2 for x in more]
            sent = pieces_for(partner) + [
                lax.dynamic_slice_in_dim(x, (1 - high) * h, h, 0) for x, h in zip(more, halves)
            ]
            got = trade(jnp.concatenate(sent) if len(sent) > 1 else sent[0], bit)
            first = 0
            for k, h in enumerate(sizes):
                totals[k] = totals[k] + got[first : first + h]
                first += h
            for x, h in zip(more, halves):
                others.append(lax.dynamic_slice_in_dim(x, high * h, h, 0) + got[first : first + h])
                first += h
        return totals + others

    total_two = kept_two + after(trade(sent_two, second_bit), gbc)
    low_in = (y1, ghalf, after(gbc, total_two), gout_one, e_one, wb_one_t, xcol_one, h1_one, gpre, small_two)
    (slab_rest,) = call(
        functools.partial(one_backward_bottom, dims, chunk),
        low_in,
        [shape((REST_ROWS, LANES))],
        [
            pltpu.VMEM((8, whole_lanes), F32),
            pltpu.VMEM((16, size), F32),
            pltpu.VMEM((72, HID), F32),
            pltpu.VMEM((CH, 16, LANES), F32),
        ],
        2 * HID * size * (72 + HID + 72),
    )

    total_a = kept_a + after(trade(sent_a, second_bit), slab_rest)
    total_b = kept_b + after(trade(sent_b, third_bit), slab_rest)
    (total_two,) = halve([total_two], fourth_bit, slab_rest)
    far = bits[3:]
    total_two, total_a, total_b, total_rest = halve(
        [total_two, total_a, total_b, after(slab_rest, total_two)], first_bit
    )
    total_rest, total_a, total_two, total_b = exchange(
        [total_rest], [total_a, total_two], [total_b], third_bit, second_bit
    )
    total_a, total_b, total_rest, total_two = exchange(
        [total_a, total_b, total_rest], [], [total_two], far[0], far[1]
    )
    shards = [total_two, total_a, total_b, total_rest]
    for bit in far[2:]:
        shards = halve(shards, bit)
    orders = [
        [second_bit, fourth_bit, first_bit, third_bit] + far[1:],
        [second_bit, first_bit, third_bit] + far,
        [third_bit, first_bit, second_bit] + far,
        [first_bit, third_bit, second_bit] + far,
    ]
    loss_part = shards[2]
    owner, loss_row = divmod(ONE_LOSS - PART_A, loss_part.shape[0])
    extra = []
    value = loss_part[loss_row : loss_row + 1]
    for _ in range(3):
        high = lax.reduce_precision(value, 8, 7)
        extra.append(high)
        value = value - high
    extra.append(shards[3] - lax.reduce_precision(shards[3], 8, 7))
    extra = jnp.concatenate(extra)
    extra = jnp.pad(extra, ((0, -extra.shape[0] % 16), (0, 0)))
    spread = [shards[0].astype(BF16), jnp.concatenate(shards[1:] + [extra]).astype(BF16)]
    near = [[third_bit, second_bit, first_bit], [second_bit, third_bit, first_bit]]
    backs = [far[::-1] + near[0], far[::-1] + near[1]]

    def double(values, bit):
        low = (index // bit) % 2 == 0
        joined = jnp.concatenate(values) if len(values) > 1 else values[0]
        other = trade(joined, bit)
        results, first = [], 0
        for value in values:
            got = other[first : first + value.shape[0]]
            first += value.shape[0]
            results.append(jnp.where(low, jnp.concatenate([value, got]), jnp.concatenate([got, value])))
        return results

    for bit in far[:1:-1]:
        spread = double(spread, bit)
    near_low, far_low = (index // far[0]) % 2 == 0, (index // far[1]) % 2 == 0
    sizes = [value.shape[0] for value in spread]
    joined = jnp.concatenate(spread)
    from_far, from_near, from_both = (trade(joined, bit) for bit in (far[1], far[0], far[0] | far[1]))

    def ordered(low, one, other):
        return jnp.where(low, jnp.concatenate([one, other]), jnp.concatenate([other, one]))

    quads = []
    for first, size_of in ((0, sizes[0]), (sizes[0], sizes[1])):
        own_part, far_part, near_part, both_part = (
            x[first : first + size_of] for x in (joined, from_far, from_near, from_both)
        )
        quads.append(
            ordered(near_low, ordered(far_low, own_part, far_part), ordered(far_low, near_part, both_part))
        )
    spread = quads
    for k in range(3):
        spread = [double([value], order[k])[0] for value, order in zip(spread, near)]
    count_bits = len(bits)
    spread = [value.reshape((2,) * count_bits + (-1, LANES)) for value in spread]

    def reorder(value, back, order):
        axes = [count_bits - 1 - back.index(bit) for bit in order]
        return value.transpose(axes + [count_bits, count_bits + 1]).reshape(-1, LANES)

    totals = []
    first = 0
    for k, (shard, order) in enumerate(zip(shards, orders)):
        first = 0 if k < 2 else first
        side = 0 if k < 1 else 1
        totals.append(reorder(spread[side][..., first : first + shard.shape[0], :], backs[side], order))
        first += shard.shape[0]
    place = [0] * count_bits
    for k, bit in enumerate(orders[2]):
        place[count_bits - 1 - backs[1].index(bit)] = (owner >> (count_bits - 1 - k)) & 1
    extra = spread[1][tuple(place)][first : first + 3]
    low_rest = reorder(spread[1][..., first + 3 : first + 3 + shards[3].shape[0], :], backs[1], orders[3])
    totals = [totals[0], jnp.concatenate(totals[1:3]), totals[3]]
    taps = [
        (entry_taps, entry_first, entry_second),
        (middle, middle_first, middle_second),
        (exit_taps, exit_first, exit_second),
        (prior_turned, jnp.swapaxes(prior_first, 1, 2), jnp.swapaxes(prior_second, 1, 2)),
    ]
    flats = (vectors_flat, flat(vectors_first), flat(vectors_second))
    outs = [shape((1, 1)), shape((1, 1))] + [shape((FLAT_ROWS, LANES))] * 3
    for group in taps:
        outs += [shape(group[0].shape)] * 3
    outs.append(shape((4, HID)))
    results = call(
        finish_kernel,
        (*totals, low_rest, extra, *flats, *[in_hbm(x) for group in taps for x in group]),
        outs,
        [
            pltpu.VMEM((TWO_ROWS - WB_ROWS, LANES), F32),
            pltpu.VMEM((ONE_ROWS - WB_ROWS, LANES), F32),
            pltpu.VMEM((REST_ROWS, LANES), F32),
            pltpu.VMEM((LANES, LANES), F32),
        ]
        + [pltpu.VMEM(group[0].shape, F32) for _ in range(4) for group in taps]
        + [pltpu.SemaphoreType.DMA((5, 3))] * 2,
        10**8,
        far_in=range(8, 20),
        far_out=range(5, 17),
    )
    results = list(results)
    for k in range(2):
        results[k] = results[k].reshape(())
    for k in range(2, 5):
        results[k] = results[k].reshape(-1)[:VEC]
    for k in range(14, 17):
        results[k] = jnp.swapaxes(results[k], 1, 2)
    return tuple(results)


def solution(mesh):
    replicated = (P(),) * 15
    return jax.shard_map(
        on_device,
        mesh=mesh,
        in_specs=(P(None, "rows", None, "batch"), P("rows", None, "batch")) + replicated,
        out_specs=(P(),) * 18,
        check_vma=False,
    )
```

```python
import functools
import math

import jax
import jax.numpy as jnp
from jax import lax
from jax.experimental import pallas as pl
from jax.experimental.pallas import tpu as pltpu
from jax.sharding import PartitionSpec as P

HID = 512
CH = 12

F32 = jnp.float32
BF16 = jnp.bfloat16
HIGH = lax.Precision.HIGHEST
LOG_TWO_PI = math.log(2.0 * math.pi)
LEARN_RATE = 0.05
BETA_ONE = 0.9
BETA_TWO = 0.999
ADAM_EPS = 1e-08
WEIGHT_DECAY = 0.01
CLIP_NORM = 0.01
ADAM_STEP = 10
LANES = 128
VMEM_LIMIT = 20 * 2**20
ONE_START = 4 * CH
TWO_START = 4 * CH + 2 * HID + CH * CH
PRIOR_START = TWO_START + 8 * CH + 2 * HID + 4 * CH * CH
VEC = PRIOR_START + 4 * CH
FLAT_ROWS = -(-VEC // (8 * LANES)) * 8
WB_ROWS = 4 * HID
TWO_F, TWO_E = WB_ROWS, WB_ROWS + 4 * 216
TWO_B = TWO_E + 4 * 144
TWO_ROWS = 3584
ONE_F = WB_ROWS
ONE_P = ONE_F + 4 * 112
ONE_B = ONE_P + 3 * 64
ONE_LOSS = ONE_B + 8
ONE_ROWS = 2816
PART_A = 768
REST_A = 4 * 56
REST_SMALL = REST_A + 8
REST_ROWS = 256


def dot(left, right):
    return lax.dot_general(left, right, (((1,), (0,)), ((), ())), preferred_element_type=F32)


def dot_nt(left, right):
    return lax.dot_general(left, right, (((1,), (1,)), ((), ())), preferred_element_type=F32)


def lane_band(bands, height=1):
    return lax.broadcasted_iota(jnp.int32, (height, LANES), 1) // (LANES // bands)


def pack_kernel(bands, index_ref, pixels_ref, mask_ref, *out_refs):
    own = index_ref[0]
    width = LANES // bands
    rows = pixels_ref.shape[0] // bands
    extra = mask_ref.shape[0] // bands
    band = lane_band(bands)
    parts = [pixels_ref[pl.ds(e, rows, stride=bands), :].astype(F32) for e in range(bands)]
    masks = [mask_ref[pl.ds(e, extra, stride=bands), :].astype(F32) for e in range(bands)]
    for d, out_ref in enumerate(out_refs):
        target = own ^ d
        for source, first, size in ((parts, 0, rows), (masks, rows, extra)):
            total = jnp.zeros((size, LANES), F32)
            for e in range(bands):
                shift = lax.rem(e - target + bands, bands) * width
                total = jnp.where(band == e, pltpu.roll(source[e], shift, 1), total)
            out_ref[first : first + size, :] = total.astype(BF16)


def fill_ext(ext_ref, field, rows, cols, bands, pattern):
    width = LANES // bands
    band = lane_band(bands)
    stride = (cols + 2) * LANES
    height = ext_ref.shape[0]
    pads = jnp.broadcast_to(pattern, (height, LANES))
    for block in range(ext_ref.shape[1] // LANES):
        ext_ref[:, block * LANES : (block + 1) * LANES] = pads
    for row in range(rows):
        start = (row + 1) * stride + LANES
        ext_ref[:, start : start + cols * LANES] = field[:, row * cols * LANES : (row + 1) * cols * LANES]
    last = (rows - 1) * cols * LANES
    for col in range(cols):
        above = pltpu.roll(field[:, last + col * LANES : last + (col + 1) * LANES], width, 1)
        start = LANES + col * LANES
        ext_ref[:, start : start + LANES] = jnp.where(band >= 1, above, pads)
        below = pltpu.roll(field[:, col * LANES : (col + 1) * LANES], LANES - width, 1)
        start = (rows + 1) * stride + LANES + col * LANES
        ext_ref[:, start : start + LANES] = jnp.where(band < bands - 1, below, pads)


def fold_ext(ext_ref, rows, cols, bands):
    width = LANES // bands
    band = lane_band(bands)
    stride = (cols + 2) * LANES
    pieces = []
    for row in range(rows):
        start = (row + 1) * stride + LANES
        piece = ext_ref[:, start : start + cols * LANES]
        if row == 0:
            blocks = []
            for col in range(cols):
                start = (rows + 1) * stride + LANES + col * LANES
                moved = pltpu.roll(ext_ref[:, start : start + LANES], width, 1)
                blocks.append(jnp.where(band >= 1, moved, 0.0))
            piece = piece + jnp.concatenate(blocks, axis=1)
        if row == rows - 1:
            blocks = []
            for col in range(cols):
                start = LANES + col * LANES
                moved = pltpu.roll(ext_ref[:, start : start + LANES], LANES - width, 1)
                blocks.append(jnp.where(band < bands - 1, moved, 0.0))
            piece = piece + jnp.concatenate(blocks, axis=1)
        pieces.append(piece)
    return pieces


def window(cols, row, first_col, tap, turned=False):
    dy, dx = tap // 3, tap % 3
    if turned:
        dy, dx = 2 - dy, 2 - dx
    return ((row + dy) * (cols + 2) + first_col + dx) * LANES


def place_of(step, chunk, cols):
    per_row = cols * LANES // chunk
    return step // per_row, lax.rem(step, per_row) * (chunk // LANES), pl.ds(pl.multiple_of(step * chunk, chunk), chunk)


def gather_cols(ext_ref, cols, row, first_col, size, turned=False):
    starts = [window(cols, row, first_col, tap, turned) for tap in range(9)]
    starts = [s if isinstance(s, int) else pl.multiple_of(s, LANES) for s in starts]
    return jnp.concatenate([ext_ref[:, pl.ds(s, size)] for s in starts], axis=0).astype(BF16)


def scatter_cols(ext_ref, values, cols, row, first_col, size, turned=False):
    height = ext_ref.shape[0]
    for tap in range(9):
        start = window(cols, row, first_col, tap, turned)
        if not isinstance(start, int):
            start = pl.multiple_of(start, LANES)
        at = pl.ds(start, size)
        ext_ref[:, at] = ext_ref[:, at] + values[tap * height : (tap + 1) * height]


def mix(matrix_ref, field_ref, start, size, pairs):
    total = None
    for j in pairs:
        term = matrix_ref[:, j : j + 1] * field_ref[j : j + 1, start : start + size]
        total = term if total is None else total + term
    return total


def log_sigmoid(value):
    return jnp.minimum(value, 0.0) - jnp.log1p(jnp.exp(-jnp.abs(value)))


def sigmoid_minus(value):
    power = jnp.exp(-jnp.abs(value))
    return jnp.where(value >= 0.0, power, 1.0) / (1.0 + power)


def row_mask(height, period, valid):
    return lax.rem(lax.broadcasted_iota(jnp.int32, (height, 1), 0), period) < valid


def fold_lanes(value):
    total = value[:, :LANES]
    for start in range(LANES, value.shape[1], LANES):
        total = total + value[:, start : start + LANES]
    return total


def unpack_kernel(
    dims,
    index_ref,
    b0,
    b1,
    b2,
    b3,
    chan1_ref,
    m1_ref,
    chan2_ref,
    m2_ref,
    y1_ref,
    mix1_ref,
    mask_ref,
    mask2_ref,
    keep_ref,
    y2_ref,
    mix2_ref,
    bufs,
    xs,
):
    rows, cols, bands = dims
    own = index_ref[0]
    width = LANES // bands
    band = lane_band(bands)
    groups = cols // bands
    for d, ref in enumerate((b0, b1, b2, b3)):
        bufs[d, :, :] = ref[...].astype(F32)
    xs[...] = jnp.zeros_like(xs)
    for s in range(rows):
        for a in range(groups):
            loads = [bufs[d, pl.ds(s * groups + a, CH + 1, stride=rows * groups), :] for d in range(bands)]
            for e in range(bands):
                total = jnp.zeros((CH + 1, LANES), F32)
                for d in range(bands):
                    origin = own ^ d
                    shift = lax.rem(origin - e + bands, bands) * width
                    total = jnp.where(band == origin, pltpu.roll(loads[d], shift, 1), total)
                start = (s * cols + bands * a + e) * LANES
                xs[0 : CH + 1, start : start + LANES] = total
    line = cols * LANES
    for s in range(rows):
        at = slice(s * line, (s + 1) * line)
        mask_ref[:, at] = xs[CH : CH + 1, at]
        raw = xs[:, at]
        source = (raw + 0.5) / 256.0 - 0.5
        y1_ref[:, at] = (source + chan1_ref[:, 0:1]) * chan1_ref[:, 1:2]
    for s in range(rows):
        at = slice(s * line, (s + 1) * line)
        mix1_ref[:, at] = mix(m1_ref, y1_ref, s * line, line, range(CH))
    half_rows, half_cols = rows // 2, cols // 2
    for i in range(half_rows):
        for j in range(half_cols):
            at = slice((i * half_cols + j) * LANES, (i * half_cols + j + 1) * LANES)
            masks = None
            for p in range(4):
                di, dj = p // 2, p % 2
                start = ((2 * i + di) * cols + 2 * j + dj) * LANES
                keep_ref[p * 8 : p * 8 + 8, at] = mix1_ref[0:8, start : start + LANES]
                block = mask_ref[:, start : start + LANES]
                masks = block if masks is None else jnp.minimum(masks, block)
            mask2_ref[:, at] = masks
    size = half_rows * half_cols * LANES
    y2_ref[...] = (keep_ref[...] + chan2_ref[:, 0:1]) * chan2_ref[:, 1:2]
    pairs = [j for j in range(32) if j % 8 < 6]
    mix2_ref[...] = mix(m2_ref, y2_ref, 0, size, pairs)


def couple_two_forward(
    dims,
    mix2_ref,
    mask_ref,
    mask2_ref,
    chan2_ref,
    et_ref,
    wb_ref,
    f_ref,
    bias_ref,
    out2_ref,
    t2_ref,
    xcol_ref,
    h1_ref,
    h2_ref,
    loss_ref,
    ext,
    oacc,
):
    half_rows, half_cols, bands = dims
    mixed = mix2_ref[...]
    out2_ref[0:16, :] = mixed[:16]
    iota = lax.broadcasted_iota(jnp.int32, (16, 1), 0)
    ones = jnp.where(iota == CH, 1.0, 0.0)
    fill_ext(ext, mixed[:16] + ones, half_rows, half_cols, bands, ones)
    oacc[...] = jnp.zeros_like(oacc)
    chunk = half_cols * LANES
    xcol = jnp.concatenate([gather_cols(ext, half_cols, i, 0, chunk) for i in range(half_rows)], axis=1)
    xcol_ref[...] = xcol
    hidden = jnp.maximum(dot(et_ref[...], xcol).astype(BF16), jnp.zeros((), BF16))
    h1_ref[...] = hidden
    hidden = jnp.maximum((dot(wb_ref[...], hidden) + bias_ref[...]).astype(BF16), jnp.zeros((), BF16))
    h2_ref[...] = hidden
    outputs = dot(f_ref[...], hidden)
    for i in range(half_rows):
        scatter_cols(oacc, outputs[:, i * chunk : (i + 1) * chunk], half_cols, i, 0, chunk, True)
    output = jnp.concatenate(fold_ext(oacc, half_rows, half_cols, bands), axis=1) + chan2_ref[:, 2:3]
    second = output[16:] + 2.0
    t2_ref[...] = second
    scale_log = log_sigmoid(second)
    result = (mixed[16:] + output[:16]) * jnp.exp(scale_log)
    out2_ref[16:, :] = result
    valid = row_mask(16, 16, CH)
    per_pixel = jnp.where(valid, scale_log - 0.5 * (mixed[:16] * mixed[:16] + result * result), 0.0)
    mask2 = mask2_ref[...]
    loss_ref[...] = jnp.zeros_like(loss_ref)
    loss_ref[0:1, :] = jnp.sum(fold_lanes(per_pixel * mask2), axis=0, keepdims=True)
    loss_ref[1:2, :] = fold_lanes(mask2)
    loss_ref[2:3, :] = fold_lanes(mask_ref[...])


def part_out(slab_ref, first, size, index, bit, kept_ref, sent_ref):
    half = size // 2
    high = lax.rem(index // bit, 2)
    kept_ref[...] = slab_ref[pl.ds(pl.multiple_of(first + high * half, 8), half), :]
    sent_ref[...] = slab_ref[pl.ds(pl.multiple_of(first + (1 - high) * half, 8), half), :]


def gram(left, right_ref, pairs, acc_ref):
    for j in pairs:
        acc_ref[j, :, :] = acc_ref[j, :, :] + fold_lanes(left * right_ref[j : j + 1, :])


def couple_two_backward(
    dims,
    bit,
    index_ref,
    mask2_ref,
    y2_ref,
    out2_ref,
    t2_ref,
    xcol_ref,
    h1_ref,
    h2_ref,
    chan2_ref,
    m2t_ref,
    e_ref,
    wbt_ref,
    ft_ref,
    kept_ref,
    sent_ref,
    small_ref,
    gkeep_ref,
    ext,
    gacc,
    gmix,
    bacc,
    ge,
    gf,
    acc,
    slab_ref,
):
    rows, cols, bands = dims
    weight = -mask2_ref[...]
    second = t2_ref[...]
    result = out2_ref[16:, :]
    g_result = -weight * result
    g_log = g_result * result + weight
    g_second = g_log * sigmoid_minus(second)
    g_half = g_result * jnp.exp(log_sigmoid(second))
    gmix[0:16, :] = -weight * out2_ref[0:16, :]
    gmix[16:32, :] = g_half
    valid = row_mask(16, 16, CH)
    g_out = jnp.concatenate([g_half, jnp.where(valid, g_second, 0.0)], axis=0)
    g_out = g_out.astype(BF16).astype(F32)
    out_sums = fold_lanes(g_out)
    fill_ext(ext, g_out, rows, cols, bands, jnp.zeros((32, 1), F32))
    gacc[...] = jnp.zeros_like(gacc)
    chunk = cols * LANES
    gcol = jnp.concatenate([gather_cols(ext, cols, i, 0, chunk, True) for i in range(rows)], axis=1)
    hidden_two = h2_ref[...]
    hidden_one = h1_ref[...]
    g_pre = jnp.where(hidden_two > 0, dot(ft_ref[...], gcol).astype(BF16), jnp.zeros((), BF16))
    gf[...] = dot_nt(gcol, hidden_two)
    g_wb = dot_nt(g_pre, hidden_one)
    for block in range(HID // LANES):
        slab_ref[block * HID : (block + 1) * HID, :] = g_wb[:, block * LANES : (block + 1) * LANES]
    bacc[...] = fold_lanes(g_pre.astype(F32))
    g_pre = jnp.where(hidden_one > 0, dot(wbt_ref[...], g_pre).astype(BF16), jnp.zeros((), BF16))
    ge[...] = dot_nt(xcol_ref[...], g_pre)
    inputs = dot(e_ref[...], g_pre)
    for i in range(rows):
        scatter_cols(gacc, inputs[:, i * chunk : (i + 1) * chunk], cols, i, 0, chunk)
    slab_ref[TWO_B:TWO_ROWS, :] = jnp.zeros((TWO_ROWS - TWO_B, LANES), F32)
    put_rows(slab_ref, lambda block: TWO_B + block, ones_sum(bacc), 0, 1)
    for piece in range(18):
        put_rows(slab_ref, lambda block: TWO_F + block * 216 + piece * CH, gf, piece * 16, CH)
    put_rows(slab_ref, lambda block: TWO_E + block * 144, ge, 0, 144)
    gmix[0:16, :] += jnp.concatenate(fold_ext(gacc, rows, cols, bands), axis=1)
    pairs = [j for j in range(32) if j % 8 < 6]
    g_mixed = gmix[...]
    acc[...] = jnp.zeros_like(acc)
    gram(g_mixed, y2_ref, pairs, acc)
    stack = [(j, acc[j]) for j in pairs] + [(32, fold_lanes(g_mixed)), (33, out_sums)]
    small_ref[...] = lane_sums(stack, 32)
    part_out(slab_ref, 0, TWO_ROWS, index_ref[1], bit, kept_ref, sent_ref)
    valid_rows = [j for j in range(32) if j % 16 < CH]
    gkeep_ref[...] = mix(m2t_ref, gmix, 0, rows * chunk, valid_rows) * chan2_ref[:, 1:2]


def level_two_kernel(
    dims,
    bit,
    index_ref,
    b0,
    b1,
    b2,
    b3,
    chan1_ref,
    m1_ref,
    chan2_ref,
    m2_ref,
    m2t_ref,
    e_ref,
    et_ref,
    f_ref,
    ft_ref,
    wb_ref,
    wbt_ref,
    bias_ref,
    y1_ref,
    mix1_ref,
    mask_ref,
    mask2_ref,
    keep_ref,
    loss_ref,
    gkeep_ref,
    kept_ref,
    sent_ref,
    small_ref,
    bufs,
    xs,
    y2,
    mix2,
    out2,
    t2,
    xcol,
    h1,
    h2,
    ext_in,
    oacc,
    ext_out,
    gacc,
    gmix,
    bacc,
    ge,
    gf,
    acc,
    slab,
):
    rows, cols, bands = dims
    half = (rows // 2, cols // 2, bands)
    unpack_kernel(
        dims, index_ref, b0, b1, b2, b3, chan1_ref, m1_ref, chan2_ref, m2_ref,
        y1_ref, mix1_ref, mask_ref, mask2_ref, keep_ref, y2, mix2, bufs, xs,
    )
    couple_two_forward(
        half, mix2, mask_ref, mask2_ref, chan2_ref, et_ref, wb_ref, f_ref, bias_ref,
        out2, t2, xcol, h1, h2, loss_ref, ext_in, oacc,
    )
    couple_two_backward(
        half, bit, index_ref, mask2_ref, y2, out2, t2, xcol, h1, h2, chan2_ref, m2t_ref, e_ref, wbt_ref, ft_ref,
        kept_ref, sent_ref, small_ref, gkeep_ref, ext_out, gacc, gmix, bacc, ge, gf, acc, slab,
    )


def couple_one_forward(
    dims,
    chunk,
    mix1_ref,
    mask_ref,
    mask2_ref,
    keep_ref,
    gkeep_in_ref,
    chan1_ref,
    et_ref,
    wb_ref,
    f_ref,
    bias_ref,
    wp_ref,
    wpt_ref,
    pbias_ref,
    xcol_ref,
    h1_ref,
    h2_ref,
    res_ref,
    t_ref,
    gout_ref,
    gwp_ref,
    loss_ref,
    ext,
    oacc,
    kext,
    kcol,
    gkacc,
    drop,
):
    rows, cols, bands = dims
    iota = lax.broadcasted_iota(jnp.int32, (8, 1), 0)
    ones = jnp.where(iota == CH // 2, 1.0, 0.0)
    fill_ext(ext, mix1_ref[0:8, :] + ones, rows, cols, bands, ones)
    oacc[...] = jnp.zeros_like(oacc)

    @pl.loop(0, rows * cols * LANES // chunk)
    def _(step):
        row, col, at = place_of(step, chunk, cols)
        xcol = gather_cols(ext, cols, row, col, chunk)
        xcol_ref[:, at] = xcol
        hidden = jnp.maximum(dot(et_ref[...], xcol).astype(BF16), jnp.zeros((), BF16))
        h1_ref[:, at] = hidden
        hidden = jnp.maximum((dot(wb_ref[...], hidden) + bias_ref[...]).astype(BF16), jnp.zeros((), BF16))
        h2_ref[:, at] = hidden
        scatter_cols(oacc, dot(f_ref[...], hidden), cols, row, col, chunk, True)

    line = cols * LANES
    valid = row_mask(8, 8, CH // 2)
    step_total = None
    half_rows, half_cols = rows // 2, cols // 2
    for s, piece in enumerate(fold_ext(oacc, rows, cols, bands)):
        at = slice(s * line, (s + 1) * line)
        output = piece + chan1_ref[:, 2:3]
        second = output[8:] + 2.0
        t_ref[:, at] = second
        scale_log = log_sigmoid(second)
        result = (mix1_ref[8:16, at] + output[:8]) * jnp.exp(scale_log)
        res_ref[:, at] = result
        part = fold_lanes(jnp.where(valid, scale_log, 0.0) * mask_ref[:, at])
        step_total = part if step_total is None else step_total + part
    for i in range(half_rows):
        for j in range(half_cols):
            at = slice((i * half_cols + j) * LANES, (i * half_cols + j + 1) * LANES)
            for p in range(4):
                start = ((2 * i + p // 2) * cols + 2 * j + p % 2) * LANES
                drop[p * 8 : p * 8 + 8, at] = res_ref[:, start : start + LANES]
    part_iota = lax.broadcasted_iota(jnp.int32, (32, 1), 0)
    part_ones = jnp.where(part_iota == CH // 2, 1.0, 0.0)
    fill_ext(kext, keep_ref[...] + part_ones, half_rows, half_cols, bands, part_ones)
    part_line = half_cols * LANES
    gkacc[...] = jnp.zeros_like(gkacc)
    weight = -mask2_ref[...]
    valid = row_mask(32, 8, CH // 2)
    prior_total = None
    for i in range(half_rows):
        at = slice(i * part_line, (i + 1) * part_line)
        columns = gather_cols(kext, half_cols, i, 0, part_line)
        kcol[...] = columns
        prior = dot(wp_ref[...], columns) + pbias_ref[...]
        mean, logs = prior[:32], prior[32:]
        inverse = jnp.exp(-logs)
        scaled = (drop[:, at] - mean) * inverse
        part = fold_lanes((-logs - 0.5 * scaled * scaled) * mask2_ref[:, at])
        prior_total = part if prior_total is None else prior_total + part
        g_mean = weight[:, at] * scaled * inverse
        g_logs = jnp.where(valid, weight[:, at] * (scaled * scaled - 1.0), 0.0)
        drop[:, at] = -g_mean
        g_prior = jnp.concatenate([g_mean, g_logs], axis=0).astype(BF16)
        g_wp = dot_nt(g_prior, kcol[...])
        if i == 0:
            gwp_ref[...] = g_wp
        else:
            gwp_ref[...] += g_wp
        scatter_cols(gkacc, dot(wpt_ref[...], g_prior), half_cols, i, 0, part_line)
    loss_ref[...] = jnp.zeros_like(loss_ref)
    loss_ref[0:1, :] = jnp.sum(step_total, axis=0, keepdims=True) + jnp.sum(prior_total, axis=0, keepdims=True)
    for i, piece in enumerate(fold_ext(gkacc, half_rows, half_cols, bands)):
        at = slice(i * part_line, (i + 1) * part_line)
        g_keep = piece + gkeep_in_ref[:, at]
        g_drop = drop[:, at]
        for j in range(half_cols):
            inner = slice(j * LANES, (j + 1) * LANES)
            for p in range(4):
                start = ((2 * i + p // 2) * cols + 2 * j + p % 2) * LANES
                gout_ref[0:8, start : start + LANES] = g_keep[p * 8 : p * 8 + 8, inner]
                gout_ref[8:16, start : start + LANES] = g_drop[p * 8 : p * 8 + 8, inner]


def put_rows(slab_ref, first, values, row, count):
    for block in range(HID // LANES):
        start = first(block)
        slab_ref[start : start + count, :] = values[row : row + count, block * LANES : (block + 1) * LANES]


def lane_sums(stack, width):
    lane = lax.broadcasted_iota(jnp.int32, (1, LANES), 1)
    total = jnp.zeros(stack[0][1].shape, F32)
    for j, value in stack:
        total = total + jnp.where(lane == j, jnp.sum(value, axis=1, keepdims=True), 0.0)
    return total


def ones_sum(value_ref):
    return lax.dot_general(
        jnp.ones((8, LANES), F32), value_ref[...], (((1,), (1,)), ((), ())), precision=HIGH, preferred_element_type=F32
    )


def one_backward_top(
    dims,
    chunk,
    bits,
    index_ref,
    mask_ref,
    res_ref,
    t_ref,
    gout_ref,
    ft_ref,
    gwp_ref,
    loss_one_ref,
    loss_two_ref,
    h1_ref,
    h2_ref,
    gpre_ref,
    kept_a,
    sent_a,
    kept_b,
    sent_b,
    ghalf_ref,
    gbc_ref,
    ext,
    gft,
    gf,
    bacc,
    slab_ref,
):
    rows, cols, bands = dims
    weight = -mask_ref[...]
    second = t_ref[...]
    result = res_ref[...]
    g_result = gout_ref[8:16, :]
    g_log = g_result * result + weight
    g_second = g_log * sigmoid_minus(second)
    g_half = g_result * jnp.exp(log_sigmoid(second))
    ghalf_ref[...] = g_half
    valid = row_mask(8, 8, CH // 2)
    g_out = jnp.concatenate([g_half, jnp.where(valid, g_second, 0.0)], axis=0)
    g_out = g_out.astype(BF16).astype(F32)
    gbc_ref[...] = fold_lanes(g_out)
    fill_ext(ext, g_out, rows, cols, bands, jnp.zeros((16, 1), F32))
    gft[...] = jnp.zeros_like(gft)
    slab_ref[...] = jnp.zeros_like(slab_ref)
    bacc[...] = jnp.zeros_like(bacc)

    @pl.loop(0, rows * cols * LANES // chunk)
    def _(step):
        row, col, at = place_of(step, chunk, cols)
        gcol = gather_cols(ext, cols, row, col, chunk, True)
        hidden_two = h2_ref[:, at]
        g_pre = jnp.where(hidden_two > 0, dot(ft_ref[...], gcol).astype(BF16), jnp.zeros((), BF16))
        gft[...] += dot_nt(hidden_two, gcol)
        gpre_ref[:, at] = g_pre
        g_wb = dot_nt(g_pre, h1_ref[:, at])
        for block in range(HID // LANES):
            slab_ref[block * HID : (block + 1) * HID, :] += g_wb[:, block * LANES : (block + 1) * LANES]
        bacc[...] += fold_lanes(g_pre.astype(F32))

    for first, count in ((0, LANES), (LANES, 16)):
        gf[first : first + count, :] = gft[:, first : first + count].T
    bias = ones_sum(bacc)
    put_rows(slab_ref, lambda block: ONE_B + block, bias, 0, 1)
    for piece in range(18):
        put_rows(slab_ref, lambda block: ONE_F + block * 112 + piece * 6, gf, piece * 8, 6)
    for block in range(3):
        width = min(LANES, 288 - block * LANES)
        slab_ref[ONE_P + block * 64 : ONE_P + block * 64 + 64, 0:width] = gwp_ref[
            :, block * LANES : block * LANES + width
        ]
    scalars = [(0, loss_one_ref[0:1, :] + loss_two_ref[0:1, :]), (1, loss_two_ref[1:2, :]), (2, loss_two_ref[2:3, :])]
    slab_ref[ONE_LOSS : ONE_LOSS + 1, :] = lane_sums(scalars, 3)
    part_out(slab_ref, 0, PART_A, index_ref[1], bits[0], kept_a, sent_a)
    part_out(slab_ref, PART_A, ONE_ROWS - PART_A, index_ref[1], bits[1], kept_b, sent_b)


def one_backward_bottom(
    dims,
    chunk,
    y1_ref,
    ghalf_ref,
    gbc_ref,
    gout_ref,
    e_ref,
    wbt_ref,
    xcol_ref,
    h1_ref,
    gpre_ref,
    small_ref,
    slab_ref,
    gacc,
    gmix,
    ge,
    acc,
):
    rows, cols, bands = dims
    gacc[...] = jnp.zeros_like(gacc)
    ge[...] = jnp.zeros_like(ge)
    slab_ref[...] = jnp.zeros_like(slab_ref)

    @pl.loop(0, rows * cols * LANES // chunk)
    def _(step):
        row, col, at = place_of(step, chunk, cols)
        g_pre = jnp.where(h1_ref[:, at] > 0, dot(wbt_ref[...], gpre_ref[:, at]).astype(BF16), jnp.zeros((), BF16))
        ge[...] += dot_nt(xcol_ref[:, at], g_pre)
        scatter_cols(gacc, dot(e_ref[...], g_pre), cols, row, col, chunk)

    gmix[0:8, :] = gout_ref[0:8, :] + jnp.concatenate(fold_ext(gacc, rows, cols, bands), axis=1)
    gmix[8:16, :] = ghalf_ref[...]
    g_mixed = gmix[...]
    acc[...] = jnp.zeros_like(acc)
    gram(g_mixed, y1_ref, range(CH), acc)
    stack = [(j, acc[j]) for j in range(CH)] + [(16, fold_lanes(g_mixed)), (17, gbc_ref[...])]
    slab_ref[REST_SMALL : REST_SMALL + 16, :] = (
        lane_sums(stack, CH) + pltpu.roll(small_ref[0:16, :], 32, 1) + pltpu.roll(small_ref[16:32, :], 66, 1)
    )
    for tap in range(9):
        put_rows(slab_ref, lambda block: block * 56 + tap * 6, ge, tap * 8, 6)
    put_rows(slab_ref, lambda block: REST_A + block, ge, 6, 1)


def call(kernel, inputs, outputs, scratch, flops, aliases=None, far_in=(), far_out=()):
    whole = pl.BlockSpec(memory_space=pltpu.VMEM)
    smem = pl.BlockSpec(memory_space=pltpu.SMEM)
    far = pl.BlockSpec(memory_space=pl.ANY)
    traffic = sum(x.size * x.dtype.itemsize for x in list(inputs) + list(outputs))
    return pl.pallas_call(
        kernel,
        out_shape=outputs,
        in_specs=[
            far if k in far_in else smem if x.dtype == jnp.int32 and x.ndim == 1 else whole for k, x in enumerate(inputs)
        ],
        out_specs=[far if k in far_out else whole for k in range(len(outputs))],
        scratch_shapes=scratch,
        input_output_aliases=aliases or {},
        compiler_params=pltpu.CompilerParams(vmem_limit_bytes=VMEM_LIMIT),
        cost_estimate=pl.CostEstimate(flops=flops, bytes_accessed=traffic, transcendentals=0),
    )(*inputs)


def shape(dims, dtype=F32):
    return jax.ShapeDtypeStruct(tuple(dims), dtype)


def high_dot(left, right, contract=(1, 0)):
    return lax.dot_general(
        left, right, (((contract[0],), (contract[1],)), ((), ())), precision=HIGH, preferred_element_type=F32
    )


def iotas(height, width=LANES):
    return (
        lax.broadcasted_iota(jnp.int32, (height, width), 0),
        lax.broadcasted_iota(jnp.int32, (height, width), 1),
    )


def take_flat(flat_ref, start, length):
    row, offset = divmod(start, LANES)
    lane = lax.broadcasted_iota(jnp.int32, (1, LANES), 1)
    value = flat_ref[row : row + 1, :]
    if offset:
        value = pltpu.roll(value, LANES - offset, 1)
        if offset + length > LANES:
            after = pltpu.roll(flat_ref[row + 1 : row + 2, :], LANES - offset, 1)
            value = jnp.where(lane < LANES - offset, value, after)
    return jnp.where(lane < length, value, 0.0) if length < LANES else value


def put_flat(pieces, start, value, length):
    row, offset = divmod(start, LANES)
    lane = lax.broadcasted_iota(jnp.int32, (1, LANES), 1)
    if length < LANES:
        value = jnp.where(lane < length, value, 0.0)
    if offset:
        value = pltpu.roll(value, offset, 1)
    if offset + length > LANES:
        pieces.setdefault(row + 1, []).append(jnp.where(lane < offset, value, 0.0))
        value = jnp.where(lane >= offset, value, 0.0)
    pieces.setdefault(row, []).append(value)


def level_rows(flat_ref, level):
    chans = CH * (level + 1)
    start = ONE_START - 4 * CH if level == 0 else TWO_START
    return chans, start, [take_flat(flat_ref, start + k * chans, chans) for k in range(4)]


def level_tables(flat_ref, level, lu):
    chans, start, chan = level_rows(flat_ref, level)
    first = start + 4 * chans + 2 * HID
    lu[...] = jnp.zeros_like(lu)
    for i in range(chans):
        lu[i : i + 1, :] = take_flat(flat_ref, first + i * chans, chans)
    row, lane = iotas(LANES)
    value = lu[...]
    inside = row < chans
    lower = jnp.where(row > lane, value, 0.0) + jnp.where((row == lane) & inside, 1.0, 0.0)
    upper = jnp.where(row < lane, value, 0.0) + jnp.where((row == lane) & inside, jnp.exp(chan[2]), 0.0)
    return chans, start, chan, lower, upper


def natural_row(level, row):
    height, half = (8, CH // 2) if level == 0 else (16, CH)
    return (row // height) * half + lax.rem(row, height), lax.rem(row, height) < half


def natural_keep(row):
    return 4 * lax.rem(row, 8) + row // 8, lax.rem(row, 8) < CH // 2


def pick(condition, value):
    return jnp.sum(jnp.where(condition, value, 0.0), axis=1, keepdims=True)


def prior_places():
    row, lane = iotas(64, 4 * CH)
    inner = lax.rem(row, 32)
    natural, valid = natural_keep(inner)
    return ((lane == natural + (row // 32) * 2 * CH) & valid).astype(F32).astype(BF16)


def prior_lanes(tap):
    row, lane = iotas(2 * CH)
    inner = lane - (tap * 32) % LANES
    natural = 4 * lax.rem(inner, 8) + inner // 8
    valid = (inner >= 0) & (inner < 32) & (lax.rem(inner, 8) < CH // 2)
    return ((row == natural) & valid).astype(F32).astype(BF16)


def prepare_level(level, flat_ref, entry_ref, middle_ref, exit_ref, outs, wide):
    e_ref, et_ref, f_ref, ft_ref, wb_ref, wbt_ref, bb_ref = outs
    chans = CH * (level + 1)
    start = 0 if level == 0 else TWO_START
    half, tall = chans // 2, 8 * (level + 1)
    first_in, first_out = (0, 0) if level == 0 else (CH // 2, CH)
    wide[...] = jnp.zeros_like(wide)
    for tap in range(9):
        wide[tap * tall : tap * tall + half, :] = entry_ref[tap, first_in : first_in + half, :]
    row, lane = iotas(LANES)
    for block in range(HID // LANES):
        at = slice(block * LANES, (block + 1) * LANES)
        value = take_flat(flat_ref, start + 4 * chans + block * LANES, LANES)
        for tap in range(3):
            part = value.astype(BF16).astype(F32)
            wide[tap * tall + half : tap * tall + half + 1, at] = part
            value = value - part
        value = take_flat(flat_ref, start + 4 * chans + HID + block * LANES, LANES)
        bb_ref[at, :] = pick(row == lane, value)
    count = 9 * tall
    padded = -(-count // LANES) * LANES
    e_ref[...] = wide[0:count, :].astype(BF16)
    et_ref[...] = wide[0:padded, :].T[:, 0:count].astype(BF16)
    wide[...] = jnp.zeros_like(wide)
    for tap in range(9):
        for side in range(2):
            first = (tap * 2 + side) * tall
            wide[first : first + half, :] = exit_ref[tap, first_out + side * half : first_out + (side + 1) * half, :]
    count = 18 * tall
    padded = -(-count // LANES) * LANES
    f_ref[...] = wide[0:count, :].astype(BF16)
    ft_ref[...] = wide[0:padded, :].T[:, 0:count].astype(BF16)
    wb_ref[...] = middle_ref[level].astype(BF16)
    wbt_ref[...] = middle_ref[level].T.astype(BF16)


def prepare_kernel(
    flat_ref,
    prior_far,
    entry_far,
    middle_far,
    exit_far,
    chan1_ref,
    m1_ref,
    chan2_ref,
    m2_ref,
    m2t_ref,
    wp_ref,
    wpt_ref,
    pbias_ref,
    tables_ref,
    *refs,
):
    outs_two, outs_one = refs[:7], refs[7:14]
    lu, wide, entry_ref, middle_ref, exit_ref, prior_ref, sems = refs[14:]
    pieces = [(middle_far, middle_ref, (1, slice(k * LANES, (k + 1) * LANES))) for k in range(4)]
    pieces += [(exit_far, exit_ref, (slice(3 * k, 3 * k + 3),)) for k in range(3)]
    pieces += [(entry_far, entry_ref, (slice(3 * k, 3 * k + 3),)) for k in range(3)]
    pieces += [(middle_far, middle_ref, (0, slice(k * LANES, (k + 1) * LANES))) for k in range(4)]
    pieces += [(prior_far, prior_ref, (slice(0, 9),))]
    copies = [
        pltpu.make_async_copy(source.at[at], target.at[at], sems.at[k]) for k, (source, target, at) in enumerate(pieces)
    ]
    for copy in copies:
        copy.start()
    for level in range(2):
        chans, start, chan, lower, upper = level_tables(flat_ref, level, lu)
        product = high_dot(lower, upper)
        for k, table in enumerate((product, lower.T, upper)):
            tables_ref[3 * level + k] = table
        height = 16 * (level + 1)
        row, lane = iotas(height)
        natural, valid = natural_row(level, row)
        spread = ((lane == chans - 1 - natural) & valid).astype(F32)
        matrix = high_dot(spread, product)
        out_bias = pick((lane == natural) & valid, chan[3])
        if level == 0:
            m1_ref[...] = matrix
            shift, scale = pick(lane == row, chan[0]), pick((lane == row) & (row < CH), jnp.exp(chan[1]))
        else:
            source, target = iotas(LANES)
            place, used = natural_keep(target)
            matrix = high_dot(matrix, ((source == place) & used & (target < 32)).astype(F32))
            m2_ref[...] = matrix
            lu[...] = jnp.zeros_like(lu)
            lu[0:32, :] = matrix
            m2t_ref[...] = lu[...].T[0:32, :]
            place, used = natural_keep(row)
            shift = pick((lane == place) & used, chan[0])
            scale = pick((lane == place) & used, jnp.exp(chan[1]))
        chan_ref = chan1_ref if level == 0 else chan2_ref
        chan_ref[...] = (
            jnp.where(lane == 0, shift, 0.0) + jnp.where(lane == 1, scale, 0.0) + jnp.where(lane == 2, out_bias, 0.0)
        )
    copies[14].wait()
    places = prior_places()
    blocks = [None] * 3
    for tap in range(9):
        moved = dot_nt(places, prior_ref[tap].astype(BF16)).astype(BF16)
        part = dot(moved, prior_lanes(tap))
        block = tap * 32 // LANES
        blocks[block] = part if blocks[block] is None else blocks[block] + part
    lu[...] = jnp.zeros_like(lu)
    for block, value in enumerate(blocks):
        width = min(LANES, 288 - block * LANES)
        at = slice(block * LANES, block * LANES + width)
        wp_ref[:, at] = value[:, 0:width].astype(BF16)
        lu[0:64, :] = value
        wpt_ref[at, :] = lu[...].T[0:width, 0:64].astype(BF16)
    row, lane = iotas(64)
    natural, valid = natural_keep(lax.rem(row, 32))
    pbias_ref[...] = pick((lane == natural + (row // 32) * 2 * CH) & valid, take_flat(flat_ref, PRIOR_START, 4 * CH))
    for copy in copies[:10]:
        copy.wait()
    prepare_level(1, flat_ref, entry_ref, middle_ref, exit_ref, outs_two, wide)
    for copy in copies[10:14]:
        copy.wait()
    prepare_level(0, flat_ref, entry_ref, middle_ref, exit_ref, outs_one, wide)


def adamw(weight, grad, first, second):
    first_new = BETA_ONE * first + (1.0 - BETA_ONE) * grad
    second_new = BETA_TWO * second + (1.0 - BETA_TWO) * grad * grad
    first_hat = first_new * (1.0 / (1.0 - BETA_ONE**ADAM_STEP))
    second_hat = second_new * (1.0 / (1.0 - BETA_TWO**ADAM_STEP))
    updated = weight - LEARN_RATE * (first_hat / (jnp.sqrt(second_hat) + ADAM_EPS) + WEIGHT_DECAY * weight)
    return (updated, second_new)


def finish_kernel(
    two_ref,
    one_ref,
    rest_ref,
    low_ref,
    extra_ref,
    tables_ref,
    flat_ref,
    flat_first,
    flat_second,
    *refs,
):
    far_in, refs = refs[:12], refs[12:]
    (loss_ref, norm_ref, flat_new, flat_grad, flat_moment), refs = refs[:5], refs[5:]
    far_out, refs = refs[:12], refs[12:]
    bias_ref, two, one, rest = refs[:4]
    held, (in_sems, out_sems) = refs[4:20], refs[20:]
    weights, firsts, seconds, grads = held[0:4], held[4:8], held[8:12], held[12:16]
    entry_grad, _, exit_grad, prior_grad = grads
    jobs = [(1, 0), (1, 1), (2, None), (0, None), (3, None)]

    def part(ref, level):
        return ref if level is None else ref.at[level]

    def copies_in(k):
        group, level = jobs[k]
        return [
            pltpu.make_async_copy(part(far_in[3 * group + j], level), part(near[group], level), in_sems.at[k, j])
            for j, near in enumerate((weights, firsts, seconds))
        ]

    def copies_out(k):
        group, level = jobs[k]
        return [
            pltpu.make_async_copy(part(near[group], level), part(far_out[3 * group + j], level), out_sems.at[k, j])
            for j, near in enumerate((weights, grads, seconds))
        ]

    for k in range(len(jobs)):
        for copy in copies_in(k):
            copy.start()
    extra = extra_ref[...].astype(F32)
    _, lane = iotas(extra.shape[0])
    log_total, count_two, count = (jnp.sum(jnp.where(lane == k, extra, 0.0), keepdims=True) for k in range(3))
    coef = -1.0 / (CH * count * math.log(2.0))
    factor = -coef
    two[...] = two_ref[WB_ROWS:, :].astype(F32) * factor
    one[...] = one_ref[WB_ROWS:, :].astype(F32) * factor
    rest[...] = (rest_ref[...].astype(F32) + low_ref[...].astype(F32)) * factor
    base = WB_ROWS
    squares = []
    pieces = {}
    consts = []
    for level in range(2):
        chans, start, chan = level_rows(flat_ref, level)
        product, lower_turned, upper = (tables_ref[3 * level + k] for k in range(3))
        consts.append(jnp.sum(chan[1] + chan[2], keepdims=True))
        weight = coef * count if level == 0 else coef * count_two
        height = 16 * (level + 1)
        small = rest[REST_SMALL : REST_SMALL + 16, :]
        if level == 1:
            small = jnp.concatenate([pltpu.roll(small, LANES - 32, 1), pltpu.roll(small, LANES - 66, 1)], axis=0)
        sum_lane = 16 * (level + 1)
        row, lane = iotas(LANES, height)
        natural, valid = natural_row(level, lane)
        turned = high_dot(((row == chans - 1 - natural) & valid).astype(F32), small)
        row, lane = iotas(LANES)
        g_product = jnp.where(lane < sum_lane, turned, 0.0)
        if level == 1:
            place, used = natural_keep(row)
            g_product = high_dot(g_product, ((lane == place) & used & (row < 32)).astype(F32))
        else:
            g_product = jnp.where(lane < chans, g_product, 0.0)
        g_lower = high_dot(g_product, upper, (1, 1))
        g_upper = high_dot(lower_turned, g_product)
        g_lu = jnp.where(row > lane, g_lower, 0.0) + jnp.where(row < lane, g_upper, 0.0)
        diagonal = jnp.sum(jnp.where(row == lane, g_upper, 0.0), axis=0, keepdims=True)
        shift = jnp.sum(turned[:, sum_lane : sum_lane + 1] * product, axis=0, keepdims=True)
        scale = jnp.sum(product * g_product, axis=0, keepdims=True)
        row, lane = iotas(height)
        natural, valid = natural_row(level, row)
        out_bias = jnp.where((lane == natural) & valid, small[:, sum_lane + 1 : sum_lane + 2], 0.0)
        put_flat(pieces, start, shift * jnp.exp(chan[1]), chans)
        put_flat(pieces, start + chans, scale + weight, chans)
        put_flat(pieces, start + 2 * chans, diagonal * jnp.exp(chan[2]) + weight, chans)
        put_flat(pieces, start + 3 * chans, jnp.sum(out_bias, axis=0, keepdims=True), chans)
        for i in range(chans):
            put_flat(pieces, start + 4 * chans + 2 * HID + i * chans, g_lu[i : i + 1, :], chans)
        for block in range(HID // LANES):
            if level == 0:
                value_a = rest[REST_A + block : REST_A + block + 1, :]
                value_b = one[ONE_B - base + block : ONE_B - base + block + 1, :]
            else:
                at = TWO_E - base + block * 144 + CH
                value_a = two[at : at + 1, :]
                value_b = two[TWO_B - base + block : TWO_B - base + block + 1, :]
            at = start + 4 * chans + block * LANES
            put_flat(pieces, at, value_a, LANES)
            put_flat(pieces, at + HID, value_b, LANES)
            bias_ref[2 * level : 2 * level + 1, block * LANES : (block + 1) * LANES] = value_a
            bias_ref[2 * level + 1 : 2 * level + 2, block * LANES : (block + 1) * LANES] = value_b
    row, lane = iotas(64)
    natural, valid = natural_keep(lax.rem(row, 32))
    column = one[ONE_P - base : ONE_P - base + 64, CH // 2 : CH // 2 + 1]
    prior_bias = jnp.where((lane == natural + (row // 32) * 2 * CH) & valid, column, 0.0)
    put_flat(pieces, PRIOR_START, jnp.sum(prior_bias, axis=0, keepdims=True), 4 * CH)
    for r in range(FLAT_ROWS):
        parts = pieces.get(r, [jnp.zeros((1, LANES), F32)])
        flat_grad[r : r + 1, :] = functools.reduce(jnp.add, parts)
    for tap in range(9):
        for block in range(HID // LANES):
            at = slice(block * LANES, (block + 1) * LANES)
            first = block * 56 + tap * 6
            entry_grad[tap, 0:6, at] = rest[first : first + 6, :]
            first = TWO_E - base + block * 144 + tap * 16
            entry_grad[tap, 6:18, at] = two[first : first + CH, :]
            first = ONE_F - base + block * 112 + tap * CH
            exit_grad[tap, 0:CH, at] = one[first : first + CH, :]
            first = TWO_F - base + block * 216 + tap * 2 * CH
            exit_grad[tap, CH : 3 * CH, at] = two[first : first + 2 * CH, :]
    places = prior_places()
    for block in range(3):
        taps = [tap for tap in range(9) if tap * 32 // LANES == block]
        lanes = jnp.concatenate([prior_lanes(tap).astype(F32) for tap in taps], axis=0).astype(BF16)
        moved = dot_nt(lanes, one_ref[ONE_P + block * 64 : ONE_P + block * 64 + 64, :]).astype(BF16)
        moved = dot(moved, places) * factor
        for k, tap in enumerate(taps):
            prior_grad[tap, :, :] = moved[k * 2 * CH : (k + 1) * 2 * CH]
    for ref in (flat_grad, entry_grad, exit_grad, prior_grad):
        value = ref[...]
        squares.append(jnp.sum(value * value, keepdims=True).reshape(1, 1))
    for ref in (one_ref, two_ref):
        total = jnp.zeros((64, LANES), F32)
        for start in range(0, WB_ROWS, 64):
            value = ref[start : start + 64, :].astype(F32)
            total = total + value * value
        squares.append(jnp.sum(total, keepdims=True) * factor * factor)
    norm = jnp.sqrt(functools.reduce(jnp.add, squares))
    clip = jnp.minimum(1.0, CLIP_NORM / (norm + 1e-06))
    total = log_total + consts[0] * count + count_two * (consts[1] - 2 * CH * LOG_TWO_PI)
    loss_ref[...] = coef * total + 8.0
    norm_ref[...] = norm
    bias_ref[...] = bias_ref[...] * clip

    middle_factor = factor * clip
    value = flat_grad[...] * clip
    flat_grad[...] = value
    flat_new[...], flat_moment[...] = adamw(flat_ref[...], value, flat_first[...], flat_second[...])
    size = 64
    for k, (group, level) in enumerate(jobs):
        for copy in copies_in(k):
            copy.wait()
        weight, first, second, grad = weights[group], firsts[group], seconds[group], grads[group]
        if level is None:

            @pl.loop(0, 9)
            def _(tap):
                value = grad[tap] * clip
                grad[tap] = value
                weight[tap], second[tap] = adamw(weight[tap], value, first[tap], second[tap])

        else:
            slab = (one_ref, two_ref)[level]

            @pl.loop(0, HID // size)
            def _(j):
                rows = pl.ds(pl.multiple_of(j * size, size), size)
                for block in range(HID // LANES):
                    at = (level, rows, slice(block * LANES, (block + 1) * LANES))
                    value = slab[pl.ds(pl.multiple_of(block * HID + j * size, size), size), :].astype(F32) * middle_factor
                    grad[at] = value
                    weight[at], second[at] = adamw(weight[at], value, first[at], second[at])

        for copy in copies_out(k):
            copy.start()
    for k in range(len(jobs)):
        for copy in copies_out(k):
            copy.wait()


def on_device(
    pixels,
    valid_mask,
    vectors,
    vectors_first,
    vectors_second,
    entry_taps,
    entry_first,
    entry_second,
    middle,
    middle_first,
    middle_second,
    exit_taps,
    exit_first,
    exit_second,
    prior_taps,
    prior_first,
    prior_second,
):
    bands = lax.axis_size("rows")
    rows, cols = valid_mask.shape[0], valid_mask.shape[1]
    dims = (rows, cols, bands)
    size = rows * cols * LANES
    part = size // 4
    batches = lax.axis_size("batch")
    devices = batches * bands
    bits = [2**k for k in range((devices - 1).bit_length())]
    index = lax.axis_index("batch") * bands + lax.axis_index("rows")
    own = jnp.stack([lax.axis_index("rows"), index]).astype(jnp.int32)

    def trade(value, bit):
        return lax.ppermute(value, ("batch", "rows"), [(i, i ^ bit) for i in range(devices)])

    def in_hbm(value):
        return pltpu.with_memory_space_constraint(value, pltpu.HBM)

    def after(value, *done):
        return lax.optimization_barrier((value, *done))[0]

    piece_rows = (CH + 1) * rows * cols // bands
    pieces = call(
        functools.partial(pack_kernel, bands),
        (own, in_hbm(pixels.reshape(-1, LANES)), in_hbm(valid_mask.reshape(-1, LANES))),
        [shape((piece_rows, LANES), BF16)] * bands,
        [],
        1000,
    )
    bufs = [pieces[0]]
    for d in range(1, bands):
        bufs.append(lax.ppermute(pieces[d], "rows", [(i, i ^ d) for i in range(bands)]))

    def flat(value):
        return jnp.pad(value, (0, FLAT_ROWS * LANES - VEC)).reshape(FLAT_ROWS, LANES)

    vectors_flat = flat(vectors)

    def level_shapes(tall):
        return [
            shape((9 * tall, HID), BF16),
            shape((HID, 9 * tall), BF16),
            shape((18 * tall, HID), BF16),
            shape((HID, 18 * tall), BF16),
            shape((HID, HID), BF16),
            shape((HID, HID), BF16),
            shape((HID, 1)),
        ]

    prior_turned = jnp.swapaxes(prior_taps, 1, 2)
    (
        chan_one, m_one, chan_two, m_two, m_two_t, wp, wpt, prior_bias, tables,
        e_two, e_two_t, f_two, f_two_t, wb_two, wb_two_t, bb_two,
        e_one, e_one_t, f_one, f_one_t, wb_one, wb_one_t, bb_one,
    ) = call(
        prepare_kernel,
        (after(vectors_flat, pieces[0]), in_hbm(prior_turned), in_hbm(entry_taps), in_hbm(middle), in_hbm(exit_taps)),
        [shape((16, LANES)), shape((16, LANES)), shape((32, LANES)), shape((32, LANES)), shape((32, LANES))]
        + [shape((64, 288), BF16), shape((288, 64), BF16), shape((64, 1)), shape((6, LANES, LANES))]
        + level_shapes(16)
        + level_shapes(8),
        [
            pltpu.VMEM((LANES, LANES), F32),
            pltpu.VMEM((384, HID), F32),
            pltpu.VMEM(entry_taps.shape, F32),
            pltpu.VMEM(middle.shape, F32),
            pltpu.VMEM(exit_taps.shape, F32),
            pltpu.VMEM(prior_turned.shape, F32),
            pltpu.SemaphoreType.DMA((15,)),
        ],
        10**9,
        far_in=(1, 2, 3, 4),
    )


    ext_lanes = (rows // 2 + 2) * (cols // 2 + 2) * LANES
    first_bit, second_bit, third_bit, fourth_bit = bits[0], bits[2], bits[1], bits[3]
    half_two = shape((TWO_ROWS // 2, LANES))
    (y1, mixed_one, mask, mask2, keep, loss_two, gkeep_two, kept_two, sent_two, small_two) = call(
        functools.partial(level_two_kernel, dims, second_bit),
        (
            own, *bufs, chan_one, m_one, chan_two, m_two, m_two_t,
            e_two, e_two_t, f_two, f_two_t, wb_two, wb_two_t, bb_two,
        ),
        [
            shape((16, size)),
            shape((16, size)),
            shape((1, size)),
            shape((1, part)),
            shape((32, part)),
            shape((8, LANES)),
            shape((32, part)),
        ]
        + [half_two] * 2
        + [shape((32, LANES))],
        [
            pltpu.VMEM((bands, piece_rows, LANES), F32),
            pltpu.VMEM((16, size), F32),
            pltpu.VMEM((32, part), F32),
            pltpu.VMEM((32, part), F32),
            pltpu.VMEM((32, part), F32),
            pltpu.VMEM((16, part), F32),
            pltpu.VMEM((144, part), BF16),
            pltpu.VMEM((HID, part), BF16),
            pltpu.VMEM((HID, part), BF16),
            pltpu.VMEM((16, ext_lanes), F32),
            pltpu.VMEM((32, ext_lanes), F32),
            pltpu.VMEM((32, ext_lanes), F32),
            pltpu.VMEM((16, ext_lanes), F32),
            pltpu.VMEM((32, part), F32),
            pltpu.VMEM((HID, LANES), F32),
            pltpu.VMEM((144, HID), F32),
            pltpu.VMEM((288, HID), F32),
            pltpu.VMEM((32, 32, LANES), F32),
            pltpu.VMEM((TWO_ROWS, LANES), F32),
        ],
        6 * HID * part * (144 + HID + 288),
    )
    whole_lanes = (rows + 2) * (cols + 2) * LANES
    chunk = min(2048, size)
    fwd_in = (
        mixed_one,
        mask,
        mask2,
        keep,
        gkeep_two,
        chan_one,
        e_one_t,
        wb_one,
        f_one,
        bb_one,
        wp,
        wpt,
        prior_bias,
    )
    fwd_out = [
        shape((72, size), BF16),
        shape((HID, size), BF16),
        shape((HID, size), BF16),
        shape((8, size)),
        shape((8, size)),
        shape((16, size)),
        shape((64, 288)),
        shape((8, LANES)),
    ]
    (xcol_one, h1_one, h2_one, res_one, t_one, gout_one, gwp, loss_one) = call(
        functools.partial(couple_one_forward, dims, chunk),
        fwd_in,
        fwd_out,
        [
            pltpu.VMEM((8, whole_lanes), F32),
            pltpu.VMEM((16, whole_lanes), F32),
            pltpu.VMEM((32, ext_lanes), F32),
            pltpu.VMEM((288, cols // 2 * LANES), BF16),
            pltpu.VMEM((32, ext_lanes), F32),
            pltpu.VMEM((32, part), F32),
        ],
        2 * HID * size * (72 + HID + 144),
    )
    top_in = (own, mask, res_one, t_one, gout_one, f_one_t, gwp, loss_one, loss_two, h1_one, h2_one)
    half_a, half_b = shape((PART_A // 2, LANES)), shape(((ONE_ROWS - PART_A) // 2, LANES))
    top_out = [shape((HID, size), BF16), half_a, half_a, half_b, half_b, shape((8, size)), shape((16, LANES))]
    (gpre, kept_a, sent_a, kept_b, sent_b, ghalf, gbc) = call(
        functools.partial(one_backward_top, dims, chunk, (second_bit, third_bit)),
        top_in,
        top_out,
        [
            pltpu.VMEM((16, whole_lanes), F32),
            pltpu.VMEM((HID, 144), F32),
            pltpu.VMEM((144, HID), F32),
            pltpu.VMEM((HID, LANES), F32),
            pltpu.VMEM((ONE_ROWS, LANES), F32),
        ],
        2 * HID * size * (144 + HID + 144),
        aliases={10: 0},
    )

    def halve(parts, bit, *beside):
        high = (index // bit) % 2
        halves = [x.shape[0] // 2 for x in parts]
        sent = [lax.dynamic_slice_in_dim(x, (1 - high) * h, h, 0) for x, h in zip(parts, halves)]
        kept = [lax.dynamic_slice_in_dim(x, high * h, h, 0) for x, h in zip(parts, halves)]
        got = after(trade(jnp.concatenate(sent) if len(sent) > 1 else sent[0], bit), *beside)
        results, first = [], 0
        for x, h in zip(kept, halves):
            results.append(x + got[first : first + h])
            first += h
        return results

    def exchange(parts, near_parts, far_parts, near, far_bit):
        code = 2 * ((index // near) % 2) + (index // far_bit) % 2
        sizes = [x.shape[0] // 4 for x in parts]

        def pieces_for(partner):
            return [lax.dynamic_slice_in_dim(x, (code ^ partner) * h, h, 0) for x, h in zip(parts, sizes)]

        totals = pieces_for(0)
        others = []
        for partner, bit, more in ((2, near, near_parts), (1, far_bit, far_parts), (3, near | far_bit, [])):
            high = (index // bit) % 2
            halves = [x.shape[0] // 2 for x in more]
            sent = pieces_for(partner) + [
                lax.dynamic_slice_in_dim(x, (1 - high) * h, h, 0) for x, h in zip(more, halves)
            ]
            got = trade(jnp.concatenate(sent) if len(sent) > 1 else sent[0], bit)
            first = 0
            for k, h in enumerate(sizes):
                totals[k] = totals[k] + got[first : first + h]
                first += h
            for x, h in zip(more, halves):
                others.append(lax.dynamic_slice_in_dim(x, high * h, h, 0) + got[first : first + h])
                first += h
        return totals + others

    total_two = kept_two + after(trade(sent_two, second_bit), gbc)
    low_in = (y1, ghalf, after(gbc, total_two), gout_one, e_one, wb_one_t, xcol_one, h1_one, gpre, small_two)
    (slab_rest,) = call(
        functools.partial(one_backward_bottom, dims, chunk),
        low_in,
        [shape((REST_ROWS, LANES))],
        [
            pltpu.VMEM((8, whole_lanes), F32),
            pltpu.VMEM((16, size), F32),
            pltpu.VMEM((72, HID), F32),
            pltpu.VMEM((CH, 16, LANES), F32),
        ],
        2 * HID * size * (72 + HID + 72),
    )

    total_a = kept_a + after(trade(sent_a, second_bit), slab_rest)
    total_b = kept_b + after(trade(sent_b, third_bit), slab_rest)
    (total_two,) = halve([total_two], fourth_bit, slab_rest)
    far = bits[3:]
    total_two, total_a, total_b, total_rest = halve(
        [total_two, total_a, total_b, after(slab_rest, total_two)], first_bit
    )
    total_rest, total_a, total_two, total_b = exchange(
        [total_rest], [total_a, total_two], [total_b], third_bit, second_bit
    )
    total_a, total_b, total_rest, total_two = exchange(
        [total_a, total_b, total_rest], [], [total_two], far[0], far[1]
    )
    shards = [total_two, total_a, total_b, total_rest]
    for bit in far[2:]:
        shards = halve(shards, bit)
    orders = [
        [second_bit, fourth_bit, first_bit, third_bit] + far[1:],
        [second_bit, first_bit, third_bit] + far,
        [third_bit, first_bit, second_bit] + far,
        [first_bit, third_bit, second_bit] + far,
    ]
    loss_part = shards[2]
    owner, loss_row = divmod(ONE_LOSS - PART_A, loss_part.shape[0])
    extra = []
    value = loss_part[loss_row : loss_row + 1]
    for _ in range(3):
        high = lax.reduce_precision(value, 8, 7)
        extra.append(high)
        value = value - high
    extra.append(shards[3] - lax.reduce_precision(shards[3], 8, 7))
    extra = jnp.concatenate(extra)
    extra = jnp.pad(extra, ((0, -extra.shape[0] % 16), (0, 0)))
    spread = [shards[0].astype(BF16), jnp.concatenate(shards[1:] + [extra]).astype(BF16)]
    near = [[third_bit, second_bit, first_bit], [second_bit, third_bit, first_bit]]
    backs = [far[::-1] + near[0], far[::-1] + near[1]]

    def double(values, bit):
        low = (index // bit) % 2 == 0
        joined = jnp.concatenate(values) if len(values) > 1 else values[0]
        other = trade(joined, bit)
        results, first = [], 0
        for value in values:
            got = other[first : first + value.shape[0]]
            first += value.shape[0]
            results.append(jnp.where(low, jnp.concatenate([value, got]), jnp.concatenate([got, value])))
        return results

    for bit in far[:1:-1]:
        spread = double(spread, bit)
    near_low, far_low = (index // far[0]) % 2 == 0, (index // far[1]) % 2 == 0
    sizes = [value.shape[0] for value in spread]
    joined = jnp.concatenate(spread)
    from_far, from_near, from_both = (trade(joined, bit) for bit in (far[1], far[0], far[0] | far[1]))

    def ordered(low, one, other):
        return jnp.where(low, jnp.concatenate([one, other]), jnp.concatenate([other, one]))

    quads = []
    for first, size_of in ((0, sizes[0]), (sizes[0], sizes[1])):
        own_part, far_part, near_part, both_part = (
            x[first : first + size_of] for x in (joined, from_far, from_near, from_both)
        )
        quads.append(
            ordered(near_low, ordered(far_low, own_part, far_part), ordered(far_low, near_part, both_part))
        )
    spread = quads
    for k in range(3):
        spread = [double([value], order[k])[0] for value, order in zip(spread, near)]
    count_bits = len(bits)
    spread = [value.reshape((2,) * count_bits + (-1, LANES)) for value in spread]

    def reorder(value, back, order):
        axes = [count_bits - 1 - back.index(bit) for bit in order]
        return value.transpose(axes + [count_bits, count_bits + 1]).reshape(-1, LANES)

    totals = []
    first = 0
    for k, (shard, order) in enumerate(zip(shards, orders)):
        first = 0 if k < 2 else first
        side = 0 if k < 1 else 1
        totals.append(reorder(spread[side][..., first : first + shard.shape[0], :], backs[side], order))
        first += shard.shape[0]
    place = [0] * count_bits
    for k, bit in enumerate(orders[2]):
        place[count_bits - 1 - backs[1].index(bit)] = (owner >> (count_bits - 1 - k)) & 1
    extra = spread[1][tuple(place)][first : first + 3]
    low_rest = reorder(spread[1][..., first + 3 : first + 3 + shards[3].shape[0], :], backs[1], orders[3])
    totals = [totals[0], jnp.concatenate(totals[1:3]), totals[3]]
    taps = [
        (entry_taps, entry_first, entry_second),
        (middle, middle_first, middle_second),
        (exit_taps, exit_first, exit_second),
        (prior_turned, jnp.swapaxes(prior_first, 1, 2), jnp.swapaxes(prior_second, 1, 2)),
    ]
    flats = (vectors_flat, flat(vectors_first), flat(vectors_second))
    outs = [shape((1, 1)), shape((1, 1))] + [shape((FLAT_ROWS, LANES))] * 3
    for group in taps:
        outs += [shape(group[0].shape)] * 3
    outs.append(shape((4, HID)))
    results = call(
        finish_kernel,
        (*totals, low_rest, extra, tables, *flats, *[in_hbm(x) for group in taps for x in group]),
        outs,
        [
            pltpu.VMEM((TWO_ROWS - WB_ROWS, LANES), F32),
            pltpu.VMEM((ONE_ROWS - WB_ROWS, LANES), F32),
            pltpu.VMEM((REST_ROWS, LANES), F32),
        ]
        + [pltpu.VMEM(group[0].shape, F32) for _ in range(4) for group in taps]
        + [pltpu.SemaphoreType.DMA((5, 3))] * 2,
        10**8,
        far_in=range(9, 21),
        far_out=range(5, 17),
    )
    results = list(results)
    for k in range(2):
        results[k] = results[k].reshape(())
    for k in range(2, 5):
        results[k] = results[k].reshape(-1)[:VEC]
    for k in range(14, 17):
        results[k] = jnp.swapaxes(results[k], 1, 2)
    return tuple(results)


def solution(mesh):
    replicated = (P(),) * 15
    return jax.shard_map(
        on_device,
        mesh=mesh,
        in_specs=(P(None, "rows", None, "batch"), P("rows", None, "batch")) + replicated,
        out_specs=(P(),) * 18,
        check_vma=False,
    )
```
